32 devices in a mesh: groups: 2 (over y), fsdp: 8 (over z, x), seq: 2 (over core).
Axes of the slice: x: 2, y: 2, z: 4, core: 2. Of those that a mesh axis runs over, the one named last changes fastest.
Arguments:
- tokens: bfloat16 [2048, 8192], P(('groups', 'fsdp', 'seq')), parts along dimension 0, may hold values from -6 to 6
- gate_blocks: bfloat16 [1280, 4096], P('fsdp'), may hold values from -0.09375 to 0.09375
- gate_slot: int32 [1280], P('fsdp'), may hold values from 0 to 256, as said below
- up_blocks: bfloat16 [1280, 4096], P('fsdp'), may hold values from -0.09375 to 0.09375
- up_slot: int32 [1280], P('fsdp'), may hold values from 0 to 256, as said below
- down_blocks: bfloat16 [1280, 4096], P('fsdp'), may hold values from -0.25 to 0.25
- down_slot: int32 [1280], P('fsdp'), may hold values from 0 to 256, as said below
- sketch: bfloat16 [32, 8192], P(None, 'fsdp'), may hold values from -0.0625 to 0.0625
- probe_index: int32 [16, 256], replicated, may hold values from 0 to 8191
- probe_value: float32 [16, 256], replicated, may hold values from -32 to 32
Outputs:
- products: float32 [32, 8192], P('groups', 'fsdp'), parts along dimension 0
The draws below stay inside these ranges and needn't reach their ends.
There are 2 independent parts, one for each index of `groups`. The reference program is written for one: setup_inputs(seed, part) draws one part's arguments, and reference() takes and returns one part's arrays. A program takes and returns all parts, laid end to end along the dimension named above; an argument that names none is the same for every part. Nothing has to cross between parts.
Inputs may be any that keep to these rules, and one draw needn't show every extreme that they name: `gate_slot`: slots j * 160 to (j + 1) * 160 - 1 belong to fsdp owner j; they hold distinct block numbers below 256, filled slots first, then the value 256 for empty slots. Every owner fills 3 * 32 slots or more, and in every draw some owner fills all 160. `up_slot`: as for gate_slot, drawn independently. `down_slot`: as for gate_slot, drawn independently.
All inputs are finite; a program needn't handle non-finite values.
Results may differ from the reference program's by a relative error of at most 0.0038.
Values may be sent and summed in bfloat16 or wider, within the bound.
No kernel may reach another device: no remote copies, remote signals or barrier semaphores. Data moves between devices by JAX's collectives and lax.ppermute only.
A program may use at most 128 MiB of HBM per device.

```python
import jax
import jax.numpy as jnp
from jax import lax

D = 8192
BLK = 64
P_SIZE = 16
Q = 256
K = 32
TOKENS = 1024
FF = 1024
RB = 16
FB = 16
CELLS = 256
CAP = 160
SLOTS = 1280
N_FSDP = 8


def slot_table(key):
    owners = SLOTS // CAP
    parts_keys = jax.random.split(key, 3)
    filled_count = jax.random.randint(parts_keys[0], (owners,), 3 * CELLS // 8, CAP + 1)
    fullest = jax.random.randint(parts_keys[1], (), 0, owners)
    filled_count = jnp.where(jnp.arange(owners) == fullest, CAP, filled_count)
    scores = jax.random.randint(parts_keys[2], (owners, CELLS), 0, CELLS) * CELLS + jnp.arange(CELLS, dtype=jnp.int32)[None, :]
    order = jnp.argsort(scores, axis=1, stable=True).astype(jnp.int32)[:, :CAP]
    filled = jnp.arange(CAP, dtype=jnp.int32)[None, :] < filled_count[:, None]
    return jnp.where(filled, order, CELLS).reshape(owners * CAP).astype(jnp.int32)


def draw_gate_slot(key, part):
    return slot_table(jax.random.fold_in(key, 11))


def draw_up_slot(key, part):
    return slot_table(jax.random.fold_in(key, 12))


def draw_down_slot(key, part):
    return slot_table(jax.random.fold_in(key, 13))


def with_ends(entries, rng, low, top_value):
    place = [jax.random.randint(jax.random.fold_in(rng, axis), (), 0, length) for axis, length in enumerate(entries.shape)]
    widest = entries.shape.index(max(entries.shape))
    next_to = place[:widest] + [(place[widest] + 1) % entries.shape[widest]] + place[widest + 1:]
    return entries.at[tuple(place)].set(low).at[tuple(next_to)].set(top_value)


def shard_levels(own_key, shape, cuts, low, high):
    loudness, own = 1.0, jax.random.fold_in(own_key, 6)
    for dim, parts in cuts:
        steps = jnp.exp(jax.random.uniform(jax.random.fold_in(own, dim), (parts,), jnp.float32, low / len(cuts), high / len(cuts)))
        loudness = loudness * jnp.repeat(steps, shape[dim] // parts).reshape([-1 if axis == dim else 1 for axis in range(len(shape))])
    return loudness


def noise(rng, shape, spread, reach, shards=(), kind=jnp.bfloat16):
    values = jax.random.normal(rng, shape, jnp.float32) * spread
    if len(shards) > 0:
        values = shard_levels(rng, shape, shards, -0.22, 0.18) * values
    return jnp.clip(values, min=-reach, max=reach).astype(kind)


def setup_inputs(seed: int = 0, part: int = 0) -> dict:
    seeds = jax.random.split(jax.random.key(seed), 11)
    part_splits = jax.random.split(jax.random.fold_in(seeds[10], part), 11)
    tokens = noise(part_splits[0], (TOKENS, D), 1.0, 6.0, ((0, 16),))
    gate_blocks = noise(seeds[1], (SLOTS, BLK * BLK), (D // 2) ** -0.5, 0.09375, ((0, 8),))
    gate_slot = draw_gate_slot(jax.random.fold_in(seeds[10], 71), part)
    up_blocks = noise(seeds[3], (SLOTS, BLK * BLK), (D // 2) ** -0.5, 0.09375, ((0, 8),))
    up_slot = draw_up_slot(jax.random.fold_in(seeds[10], 71), part)
    down_blocks = noise(seeds[5], (SLOTS, BLK * BLK), (FF // 2) ** -0.5, 0.25, ((0, 8),))
    down_slot = draw_down_slot(jax.random.fold_in(seeds[10], 71), part)
    sketch = noise(seeds[7], (K, D), D ** -0.5, 0.0625, ((1, 8),))
    probe_index = with_ends(jax.random.randint(seeds[8], (P_SIZE, Q), 0, D), jax.random.fold_in(seeds[8], 1), 0, D - 1).astype(jnp.int32)
    probe_value = noise(seeds[9], (P_SIZE, Q), ((D // Q) ** 0.5), 32.0, (), jnp.float32)
    return dict(tokens=tokens, gate_blocks=gate_blocks, gate_slot=gate_slot, up_blocks=up_blocks, up_slot=up_slot, down_blocks=down_blocks, down_slot=down_slot, sketch=sketch, probe_index=probe_index, probe_value=probe_value)


def dense_slots(blocks, slot_ids):
    owners = slot_ids.shape[0] // CAP
    blocks = blocks.reshape(owners, CAP, BLK * BLK)
    slot_ids = slot_ids.reshape(owners, CAP)
    holder = jnp.zeros((owners, CELLS + 1, BLK * BLK), blocks.dtype)
    owner_ids = jnp.arange(owners, dtype=jnp.int32)[:, None]
    return holder.at[owner_ids, slot_ids].set(blocks)[:, :CELLS]


def gate_matrix(blocks, slot_ids):
    holder = dense_slots(blocks, slot_ids).reshape(N_FSDP, RB, FB, BLK, BLK)
    return holder.transpose(0, 1, 3, 2, 4).reshape(D, FF)


def down_matrix(blocks, slot_ids):
    holder = dense_slots(blocks, slot_ids).reshape(N_FSDP, FB, RB, BLK, BLK)
    return holder.transpose(1, 3, 0, 2, 4).reshape(FF, D)


def reference(tokens, gate_blocks, gate_slot, up_blocks, up_slot, down_blocks, down_slot, sketch, probe_index, probe_value):
    gate_weight = gate_matrix(gate_blocks, gate_slot)
    up_weight = gate_matrix(up_blocks, up_slot)
    down_weight = down_matrix(down_blocks, down_slot)
    probe_rows = jnp.arange(P_SIZE, dtype=jnp.int32)[:, None]
    omega = jnp.zeros((P_SIZE, D), jnp.float32).at[probe_rows, probe_index].add(probe_value.astype(jnp.float32))
    probe_gate = jnp.dot(omega, gate_weight.astype(jnp.float32), precision=lax.Precision.HIGHEST)
    probe_up = jnp.dot(omega, up_weight.astype(jnp.float32), precision=lax.Precision.HIGHEST)
    projected = jnp.dot(down_weight, sketch.T, preferred_element_type=jnp.float32).astype(jnp.bfloat16)
    gate_pre = jnp.dot(tokens, gate_weight, preferred_element_type=jnp.float32)
    up_pre = jnp.dot(tokens, up_weight, preferred_element_type=jnp.float32)
    span = 128 if TOKENS % 128 == 0 else TOKENS
    gate_split = gate_pre.reshape(TOKENS // span, span, FF)
    up_split = up_pre.reshape(TOKENS // span, span, FF)

    def visit(carry, pieces):
        gate_part, up_part = pieces
        sigmoid_g = jax.nn.sigmoid(gate_part)
        activated = gate_part * sigmoid_g
        slope_g = sigmoid_g * (1.0 + gate_part * (1.0 - sigmoid_g))
        lead_term = slope_g * up_part
        tangent = (lead_term[:, None, :] * probe_gate[None] + activated[:, None, :] * probe_up[None]).astype(jnp.bfloat16)
        row_total = tangent.shape[0] * P_SIZE
        sketch_rows = jnp.dot(tangent.reshape(row_total, FF), projected, preferred_element_type=jnp.float32).astype(jnp.bfloat16)
        backward = jnp.dot(sketch_rows, projected.T, preferred_element_type=jnp.float32).reshape(-1, P_SIZE, FF)
        gate_acc = carry[0] + jnp.sum(backward * lead_term[:, None, :], axis=0)
        up_acc = carry[1] + jnp.sum(backward * activated[:, None, :], axis=0)
        return (gate_acc, up_acc), None

    initial = (jnp.zeros((P_SIZE, FF), jnp.float32), jnp.zeros((P_SIZE, FF), jnp.float32))
    totals, unused = lax.scan(visit, initial, (gate_split, up_split))
    gate_sum = totals[0].astype(jnp.bfloat16)
    up_sum = totals[1].astype(jnp.bfloat16)
    products = jnp.dot(gate_sum, gate_weight.T, preferred_element_type=jnp.float32)
    products = products + jnp.dot(up_sum, up_weight.T, preferred_element_type=jnp.float32)
    return products
```

```python
import functools

import jax
import jax.numpy as jnp
from jax import lax
from jax.experimental import pallas as pl
from jax.experimental.pallas import tpu as pltpu
from jax.sharding import PartitionSpec as P

HID_DEV = 128
BLK = 64
P_SIZE = 16
K = 32

BF = jnp.bfloat16
F32 = jnp.float32
VMEM = pl.BlockSpec(memory_space=pltpu.VMEM)
SMEM = pl.BlockSpec(memory_space=pltpu.SMEM)
PARAMS = pltpu.CompilerParams(vmem_limit_bytes=56 * 1024 * 1024)


def unpack(blocks, slot_ids, cell_total):
    holder = jnp.zeros((cell_total + 1, blocks.shape[1]), blocks.dtype)
    return holder.at[slot_ids].set(blocks)[:cell_total]


def contract_last(first_mat, second_mat):
    return lax.dot_general(
        first_mat, second_mat, (((1,), (1,)), ((), ())), preferred_element_type=jnp.float32
    )


def hidden_split(
    tokens,
    gate_blocks,
    gate_slot,
    up_blocks,
    up_slot,
    down_blocks,
    down_slot,
    sketch,
    probe_index,
    probe_value,
):
    owners = lax.axis_size("fsdp")
    model_width = tokens.shape[1]
    local_width = model_width // owners
    block_rows = local_width // BLK
    hidden = HID_DEV
    col_blocks = hidden * owners // BLK
    cell_total = block_rows * col_blocks
    gate_dense = unpack(gate_blocks, gate_slot, cell_total).reshape(
        block_rows, col_blocks, BLK, BLK
    )
    up_dense = unpack(up_blocks, up_slot, cell_total).reshape(block_rows, col_blocks, BLK, BLK)
    stacked = jnp.stack([gate_dense, up_dense], axis=1)
    stacked = stacked.reshape(block_rows, 2, owners, hidden // BLK, BLK, BLK)
    stacked = stacked.transpose(0, 4, 2, 1, 3, 5).reshape(local_width, owners * 2 * hidden)
    both_weights = lax.all_to_all(stacked, "fsdp", split_axis=1, concat_axis=0, tiled=True)
    picked = both_weights[probe_index].astype(jnp.float32)
    probe_both = jnp.sum(picked * probe_value[:, :, None], axis=1)
    preact = jnp.dot(
        lax.all_gather(tokens, "fsdp", axis=0, tiled=True),
        both_weights,
        preferred_element_type=jnp.float32,
    )
    row_count = preact.shape[0]
    gate_pre = preact[:, :hidden]
    up_pre = preact[:, hidden:]
    down_dense = unpack(down_blocks, down_slot, cell_total).reshape(
        col_blocks, block_rows, BLK, BLK
    )
    down_dense = down_dense.transpose(0, 2, 1, 3).reshape(col_blocks * BLK, local_width)
    down_rows = lax.all_to_all(down_dense, "fsdp", split_axis=0, concat_axis=1, tiled=True)
    full_sketch = lax.all_gather(sketch, "fsdp", axis=1, tiled=True)
    projected = contract_last(down_rows, full_sketch)
    projected = projected.astype(jnp.bfloat16)
    sigmoid_g = jax.nn.sigmoid(gate_pre)
    activated = gate_pre * sigmoid_g
    slope_g = sigmoid_g * (1.0 + gate_pre * (1.0 - sigmoid_g))
    lead_term = slope_g * up_pre
    tangent = (
        lead_term[:, None, :] * probe_both[None, :, :hidden]
        + activated[:, None, :] * probe_both[None, :, hidden:]
    )
    tangent = tangent.astype(jnp.bfloat16)
    partial_sketch = jnp.dot(
        tangent.reshape(row_count * P_SIZE, hidden), projected, preferred_element_type=jnp.float32
    )
    partial_sketch = partial_sketch.reshape(row_count, P_SIZE * K)
    sketch_rows = lax.psum(partial_sketch, "fsdp").astype(jnp.bfloat16)
    backward = contract_last(sketch_rows.reshape(row_count * P_SIZE, K), projected).reshape(
        row_count, P_SIZE, hidden
    )
    summed = jnp.concatenate(
        [
            jnp.sum(backward * lead_term[:, None, :], axis=0),
            jnp.sum(backward * activated[:, None, :], axis=0),
        ],
        axis=1,
    )
    summed = lax.psum(summed, "seq").astype(jnp.bfloat16)
    products = contract_last(summed, both_weights)
    return lax.psum_scatter(products, "fsdp", scatter_dimension=1, tiled=True)


def dot(a, b):
    return jnp.dot(a, b, preferred_element_type=F32)


def split3(value):
    high = value.astype(BF)
    rest = value - high.astype(F32)
    mid = rest.astype(BF)
    low = (rest - mid.astype(F32)).astype(BF)
    return high, mid, low


def shuffled(natural):
    return (natural // BLK) * BLK + (natural % 2) * (BLK // 2) + (natural % BLK) // 2


def shuffle_matrix(size):
    rows = lax.broadcasted_iota(jnp.int32, (size, size), 0)
    cols = lax.broadcasted_iota(jnp.int32, (size, size), 1)
    return jnp.where(shuffled(rows) == cols, 1.0, 0.0).astype(BF)


def unshuffle_matrix(size):
    rows = lax.broadcasted_iota(jnp.int32, (size, size), 0)
    cols = lax.broadcasted_iota(jnp.int32, (size, size), 1)
    return jnp.where(shuffled(cols) == rows, 1.0, 0.0).astype(BF)


def stage_blocks(blocks_ref, tiles_ref, first_slot):
    @pl.loop(0, blocks_ref.shape[0] // 16)
    def _(step):
        row = pl.multiple_of(step * 16, 16)
        target = (first_slot + row) * 32
        for chunk in range(32):
            piece = blocks_ref[pl.ds(row, 16), 128 * chunk : 128 * (chunk + 1)].astype(F32)
            tiles_ref[pl.ds(target + chunk, 16, stride=32), :] = piece


def assembled_pair(tiles_ref, left_slot, right_slot):
    left = tiles_ref[pl.ds(pl.multiple_of(left_slot * 32, 32), 32), :]
    right = tiles_ref[pl.ds(pl.multiple_of(right_slot * 32, 32), 32), :]
    low_half = lax.broadcasted_iota(jnp.int32, (32, 128), 1) < BLK
    even = jnp.where(low_half, left, pltpu.roll(right, BLK, 1))
    odd = jnp.where(low_half, pltpu.roll(left, BLK, 1), right)
    return even.astype(BF), odd.astype(BF)


def assemble_columns(inv_ref, inv_row, tiles_ref, put):
    @pl.loop(0, 16)
    def _(block_row):
        for pair in range(8):
            cell = block_row * 16 + 2 * pair
            even, odd = assembled_pair(
                tiles_ref, inv_ref[inv_row, cell], inv_ref[inv_row, cell + 1]
            )
            row = pl.multiple_of(block_row * BLK, BLK)
            put(pair, row, even)
            put(pair, row + BLK // 2, odd)


def own_kernel(
    place_ref,
    inv_ref,
    gate_ref,
    up_ref,
    down_ref,
    sketch_ref,
    index_ref,
    value_ref,
    weight_ref,
    payload_ref,
    tiles_ref,
    omega_ref,
    split_ref,
    down_dense_ref,
):
    owner = place_ref[0]
    quarter = place_ref[1]
    tiles_ref[pl.ds(160 * 32, 32), :] = jnp.zeros((32, 128), F32)

    for which, blocks_ref in enumerate((gate_ref, up_ref)):
        stage_blocks(blocks_ref, tiles_ref, 0)

        def put(pair, row, piece):
            lane = (pair % 2) * 128
            weight_ref[4 * which + pair // 2, pl.ds(row, 32), lane : lane + 128] = piece

        assemble_columns(inv_ref, which, tiles_ref, put)

    stage_blocks(down_ref, tiles_ref, 0)
    for local_row in range(4):
        for pair in range(8):
            cell = (quarter * 4 + local_row) * 16 + 2 * pair
            even, odd = assembled_pair(tiles_ref, inv_ref[2, cell], inv_ref[2, cell + 1])
            row = local_row * BLK
            down_dense_ref[row : row + 32, 128 * pair : 128 * (pair + 1)] = even
            down_dense_ref[row + 32 : row + 64, 128 * pair : 128 * (pair + 1)] = odd
    payload_ref[32:64, :] = contract_last(sketch_ref[...], down_dense_ref[...])

    local = index_ref[...] - owner * 1024
    inside = (local >= 0) & (local < 1024)
    safe = jnp.where(inside, local, 0)
    spot = shuffled(safe)
    high_part = jnp.where(inside, spot // 128, -1)
    low_part = spot % 128
    values = value_ref[...]
    high_iota = lax.broadcasted_iota(jnp.int32, (8, 256), 0)
    low_iota = lax.broadcasted_iota(jnp.int32, (128, 256), 0)
    for probe in range(P_SIZE):
        picked = jnp.where(
            high_iota == high_part[probe : probe + 1, :], values[probe : probe + 1, :], 0.0
        )
        one_hot = jnp.where(low_iota == low_part[probe : probe + 1, :], 1.0, 0.0).astype(BF)
        total = None
        for part in split3(picked):
            term = contract_last(part, one_hot)
            total = term if total is None else total + term
        omega_ref[8 * probe : 8 * (probe + 1), :] = total
    for high in range(8):
        piece = omega_ref[pl.ds(high, 16, stride=8), :]
        for part_index, part in enumerate(split3(piece)):
            split_ref[
                16 * part_index : 16 * (part_index + 1), 128 * high : 128 * (high + 1)
            ] = part
    for which in range(2):
        triple = dot(split_ref[...], weight_ref[4 * which + quarter])
        payload_ref[16 * which : 16 * (which + 1), :] = triple[:16] + triple[16:32] + triple[32:]


def partial_kernel(
    inv_row,
    place_ref,
    inv_ref,
    first_ref,
    second_ref,
    own_weight_ref,
    tok0_ref,
    tok1_ref,
    tok2_ref,
    tok3_ref,
    keep_ref,
    out1_ref,
    out2_ref,
    out3_ref,
    tiles_ref,
    weight_ref,
    tokens_ref,
):
    side = place_ref[2]
    core = place_ref[3]
    tiles_ref[pl.ds(160 * 32, 32), :] = jnp.zeros((32, 128), F32)
    stage_blocks(first_ref, tiles_ref, core * 80)
    stage_blocks(second_ref, tiles_ref, (1 - core) * 80)

    def put(pair, row, piece):
        lane = (pair % 2) * 128
        weight_ref[pair // 2, pl.ds(row, 32), lane : lane + 128] = piece

    assemble_columns(inv_ref, inv_row, tiles_ref, put)
    shuffle = shuffle_matrix(256)
    for source, tok_ref in enumerate((tok0_ref, tok1_ref, tok2_ref, tok3_ref)):
        for group in range(8):
            moved = dot(tok_ref[:, 256 * group : 256 * (group + 1)], shuffle).astype(BF)
            half = lax.rem(group // 4 + side, 2)
            tokens_ref[
                half, 64 * source : 64 * (source + 1), 256 * (group % 4) : 256 * (group % 4 + 1)
            ] = moved
    for chunk in range(4):
        total = dot(tokens_ref[0], own_weight_ref[chunk]) + dot(tokens_ref[1], weight_ref[chunk])
        cols = slice(256 * chunk, 256 * (chunk + 1))
        keep_ref[:, cols] = total[:64]
        out1_ref[:, cols] = total[64:128].astype(BF)
        out2_ref[:, cols] = total[128:192].astype(BF)
        out3_ref[:, cols] = total[192:].astype(BF)


def middle_kernel(
    place_ref,
    gate0_ref,
    gate1_ref,
    gate2_ref,
    gate3_ref,
    up0_ref,
    up1_ref,
    up2_ref,
    up3_ref,
    pay0_ref,
    pay1_ref,
    pay2_ref,
    pay3_ref,
    out_ref,
    lead_ref,
    act_ref,
    pay_ref,
    proj_ref,
    tangent_ref,
):
    quarter = place_ref[1]
    low_bit = quarter % 2
    high_bit = quarter // 2
    unshuffle = unshuffle_matrix(256)
    for flip, ref in enumerate((pay0_ref, pay1_ref, pay2_ref, pay3_ref)):
        spot = lax.rem(low_bit + flip % 2, 2) + 2 * lax.rem(high_bit + flip // 2, 2)
        pay_ref[spot] = ref[...]
    for chunk in range(4):
        cols = slice(256 * chunk, 256 * (chunk + 1))
        proj_ref[:, cols] = dot(pay_ref[chunk, 32:64, :].astype(BF), unshuffle).astype(BF)
        gate_pre = (
            gate0_ref[:, cols]
            + gate1_ref[:, cols].astype(F32)
            + gate2_ref[:, cols].astype(F32)
            + gate3_ref[:, cols].astype(F32)
        )
        up_pre = (
            up0_ref[:, cols]
            + up1_ref[:, cols].astype(F32)
            + up2_ref[:, cols].astype(F32)
            + up3_ref[:, cols].astype(F32)
        )
        sigmoid_g = jax.nn.sigmoid(gate_pre)
        activated = gate_pre * sigmoid_g
        slope_g = sigmoid_g * (1.0 + gate_pre * (1.0 - sigmoid_g))
        lead = slope_g * up_pre
        lead_ref[:, cols] = lead
        act_ref[:, cols] = activated
        for probe in range(P_SIZE):
            probe_gate = pay_ref[chunk, probe : probe + 1, :]
            probe_up = pay_ref[chunk, 16 + probe : 17 + probe, :]
            tangent_ref[64 * probe : 64 * (probe + 1), cols] = (
                lead * probe_gate + activated * probe_up
            ).astype(BF)
    sketch_rows = contract_last(tangent_ref[...], proj_ref[...]).astype(BF)
    for probe in range(P_SIZE):
        rows = sketch_rows[64 * probe : 64 * (probe + 1), :]
        backward = dot(rows, proj_ref[...])
        out_ref[probe : probe + 1, :1024] = jnp.sum(backward * lead_ref[...], axis=0, keepdims=True)
        out_ref[probe : probe + 1, 1024:] = jnp.sum(backward * act_ref[...], axis=0, keepdims=True)


def product_kernel(sum_ref, weight_ref, out_ref):
    sums = sum_ref[...].astype(BF)
    total = None
    for chunk in range(8):
        term = contract_last(sums[:, 256 * chunk : 256 * (chunk + 1)], weight_ref[chunk])
        total = term if total is None else total + term
    unshuffle = unshuffle_matrix(256)
    for group in range(4):
        cols = slice(256 * group, 256 * (group + 1))
        high, mid, low = split3(total[:, cols])
        out_ref[:, cols] = dot(high, unshuffle) + dot(mid, unshuffle) + dot(low, unshuffle)


def pair_split(
    tokens,
    gate_blocks,
    gate_slot,
    up_blocks,
    up_slot,
    down_blocks,
    down_slot,
    sketch,
    probe_index,
    probe_value,
):
    owner = lax.axis_index("fsdp")
    core = lax.axis_index("seq")
    group = lax.axis_index("groups")
    zone = owner // 2
    side = owner % 2
    place = jnp.stack([owner, 2 * group + core, side, core]).astype(jnp.int32)

    def owner_flip(value, bits):
        return lax.ppermute(value, "fsdp", [(i, i ^ bits) for i in range(8)])

    def core_flip(value):
        return lax.ppermute(value, "seq", [(0, 1), (1, 0)])

    def token_slice(target_zone):
        return lax.dynamic_slice(tokens, (0, target_zone * 2048), (64, 2048))

    slots = jnp.stack([gate_slot, up_slot, down_slot])
    cells = lax.broadcasted_iota(jnp.int32, (3, 160, 256), 2)
    slot_numbers = lax.broadcasted_iota(jnp.int32, (3, 160, 256), 1)
    inv = jnp.min(jnp.where(slots[:, :, None] == cells, slot_numbers, 160), axis=1)

    tok_parts = [token_slice(zone)]
    for flip in (1, 2, 3):
        tok_parts.append(owner_flip(token_slice(zone ^ flip), 2 * flip))

    near_inv = owner_flip(inv, 1)
    near_gate = owner_flip(lax.dynamic_slice(gate_blocks, (core * 80, 0), (80, 4096)), 1)
    near_up = owner_flip(lax.dynamic_slice(up_blocks, (core * 80, 0), (80, 4096)), 1)

    weights, payload = pl.pallas_call(
        own_kernel,
        out_shape=(
            jax.ShapeDtypeStruct((8, 1024, 256), BF),
            jax.ShapeDtypeStruct((64, 256), F32),
        ),
        in_specs=[SMEM, SMEM] + [VMEM] * 6,
        out_specs=(VMEM, VMEM),
        scratch_shapes=[
            pltpu.VMEM((161 * 32, 128), F32),
            pltpu.VMEM((128, 128), F32),
            pltpu.VMEM((48, 1024), BF),
            pltpu.VMEM((256, 1024), BF),
        ],
        compiler_params=PARAMS,
        name="own_blocks",
    )(place, inv, gate_blocks, up_blocks, down_blocks, sketch, probe_index, probe_value)

    for bits in (1, 2, 4):
        payload = payload + owner_flip(payload, bits)
    pay_parts = [
        payload,
        core_flip(payload),
        lax.ppermute(payload, "groups", [(0, 1), (1, 0)]),
        lax.ppermute(payload, ("groups", "seq"), [(i, i ^ 3) for i in range(4)]),
    ]

    def partial_sums(which, near):
        return pl.pallas_call(
            functools.partial(partial_kernel, which),
            out_shape=(jax.ShapeDtypeStruct((64, 1024), F32),)
            + (jax.ShapeDtypeStruct((64, 1024), BF),) * 3,
            grid=(1,),
            in_specs=[SMEM, SMEM, VMEM, VMEM]
            + [pl.BlockSpec((4, 1024, 256), lambda i: (which, 0, 0))]
            + [VMEM] * 4,
            out_specs=(VMEM,) * 4,
            scratch_shapes=[
                pltpu.VMEM((161 * 32, 128), F32),
                pltpu.VMEM((4, 1024, 256), BF),
                pltpu.VMEM((2, 256, 1024), BF),
            ],
            compiler_params=PARAMS,
            name="partial_sums",
        )(place, near_inv, near, core_flip(near), weights, *tok_parts)

    middle_args = []
    for which, near in enumerate((near_gate, near_up)):
        keep, *sent = partial_sums(which, near)
        middle_args.append(keep)
        for flip in (1, 2, 3):
            middle_args.append(owner_flip(sent[flip - 1], 2 * flip))

    sums = pl.pallas_call(
        middle_kernel,
        out_shape=jax.ShapeDtypeStruct((P_SIZE, 2048), F32),
        in_specs=[SMEM] + [VMEM] * 12,
        out_specs=VMEM,
        scratch_shapes=[
            pltpu.VMEM((64, 1024), F32),
            pltpu.VMEM((64, 1024), F32),
            pltpu.VMEM((4, 64, 256), F32),
            pltpu.VMEM((K, 1024), BF),
            pltpu.VMEM((64 * P_SIZE, 1024), BF),
        ],
        compiler_params=PARAMS,
        name="token_sums",
    )(place, *middle_args, *pay_parts)

    sums = sums + core_flip(sums)
    for bits in (1, 2, 4):
        sums = sums + owner_flip(sums, bits)

    return pl.pallas_call(
        product_kernel,
        out_shape=jax.ShapeDtypeStruct((P_SIZE, 1024), F32),
        in_specs=[VMEM, VMEM],
        out_specs=VMEM,
        compiler_params=PARAMS,
        name="products",
    )(sums, weights)


def per_device(tokens, gate_blocks, *rest):
    fits = (
        lax.axis_size("fsdp") == 8
        and lax.axis_size("seq") == 2
        and lax.axis_size("groups") == 2
        and tokens.shape == (64, 8192)
        and gate_blocks.shape == (160, 4096)
        and rest[-2].shape == (P_SIZE, 256)
    )
    return (pair_split if fits else hidden_split)(tokens, gate_blocks, *rest)


def solution(mesh):
    in_specs = (
        P(("groups", "fsdp", "seq"), None),
        P("fsdp", None),
        P("fsdp"),
        P("fsdp", None),
        P("fsdp"),
        P("fsdp", None),
        P("fsdp"),
        P(None, "fsdp"),
        P(),
        P(),
    )
    out_specs = P("groups", "fsdp")
    return jax.shard_map(
        per_device, mesh=mesh, in_specs=in_specs, out_specs=out_specs, check_vma=False
    )
```

```python
import functools

import jax
import jax.numpy as jnp
from jax import lax
from jax.experimental import pallas as pl
from jax.experimental.pallas import tpu as pltpu
from jax.sharding import PartitionSpec as P

HID_DEV = 128
BLK = 64
P_SIZE = 16
K = 32

BF = jnp.bfloat16
F32 = jnp.float32
VMEM = pl.BlockSpec(memory_space=pltpu.VMEM)
SMEM = pl.BlockSpec(memory_space=pltpu.SMEM)

PARAMS = pltpu.CompilerParams(vmem_limit_bytes=56 * 1024 * 1024)


def unpack(blocks, slot_ids, cell_total):
    holder = jnp.zeros((cell_total + 1, blocks.shape[1]), blocks.dtype)
    return holder.at[slot_ids].set(blocks)[:cell_total]


def contract_last(first_mat, second_mat):
    return lax.dot_general(
        first_mat, second_mat, (((1,), (1,)), ((), ())), preferred_element_type=jnp.float32
    )


def hidden_split(
    tokens,
    gate_blocks,
    gate_slot,
    up_blocks,
    up_slot,
    down_blocks,
    down_slot,
    sketch,
    probe_index,
    probe_value,
):
    owners = lax.axis_size("fsdp")
    model_width = tokens.shape[1]
    local_width = model_width // owners
    block_rows = local_width // BLK
    hidden = HID_DEV
    col_blocks = hidden * owners // BLK
    cell_total = block_rows * col_blocks
    gate_dense = unpack(gate_blocks, gate_slot, cell_total).reshape(
        block_rows, col_blocks, BLK, BLK
    )
    up_dense = unpack(up_blocks, up_slot, cell_total).reshape(block_rows, col_blocks, BLK, BLK)
    stacked = jnp.stack([gate_dense, up_dense], axis=1)
    stacked = stacked.reshape(block_rows, 2, owners, hidden // BLK, BLK, BLK)
    stacked = stacked.transpose(0, 4, 2, 1, 3, 5).reshape(local_width, owners * 2 * hidden)
    both_weights = lax.all_to_all(stacked, "fsdp", split_axis=1, concat_axis=0, tiled=True)
    picked = both_weights[probe_index].astype(jnp.float32)
    probe_both = jnp.sum(picked * probe_value[:, :, None], axis=1)
    preact = jnp.dot(
        lax.all_gather(tokens, "fsdp", axis=0, tiled=True),
        both_weights,
        preferred_element_type=jnp.float32,
    )
    row_count = preact.shape[0]
    gate_pre = preact[:, :hidden]
    up_pre = preact[:, hidden:]
    down_dense = unpack(down_blocks, down_slot, cell_total).reshape(
        col_blocks, block_rows, BLK, BLK
    )
    down_dense = down_dense.transpose(0, 2, 1, 3).reshape(col_blocks * BLK, local_width)
    down_rows = lax.all_to_all(down_dense, "fsdp", split_axis=0, concat_axis=1, tiled=True)
    full_sketch = lax.all_gather(sketch, "fsdp", axis=1, tiled=True)
    projected = contract_last(down_rows, full_sketch)
    projected = projected.astype(jnp.bfloat16)
    sigmoid_g = jax.nn.sigmoid(gate_pre)
    activated = gate_pre * sigmoid_g
    slope_g = sigmoid_g * (1.0 + gate_pre * (1.0 - sigmoid_g))
    lead_term = slope_g * up_pre
    tangent = (
        lead_term[:, None, :] * probe_both[None, :, :hidden]
        + activated[:, None, :] * probe_both[None, :, hidden:]
    )
    tangent = tangent.astype(jnp.bfloat16)
    partial_sketch = jnp.dot(
        tangent.reshape(row_count * P_SIZE, hidden), projected, preferred_element_type=jnp.float32
    )
    partial_sketch = partial_sketch.reshape(row_count, P_SIZE * K)
    sketch_rows = lax.psum(partial_sketch, "fsdp").astype(jnp.bfloat16)
    backward = contract_last(sketch_rows.reshape(row_count * P_SIZE, K), projected).reshape(
        row_count, P_SIZE, hidden
    )
    summed = jnp.concatenate(
        [
            jnp.sum(backward * lead_term[:, None, :], axis=0),
            jnp.sum(backward * activated[:, None, :], axis=0),
        ],
        axis=1,
    )
    summed = lax.psum(summed, "seq").astype(jnp.bfloat16)
    products = contract_last(summed, both_weights)
    return lax.psum_scatter(products, "fsdp", scatter_dimension=1, tiled=True)


def dot(a, b):
    return jnp.dot(a, b, preferred_element_type=F32)


def split3(value):
    high = value.astype(BF)
    rest = value - high.astype(F32)
    mid = rest.astype(BF)
    low = (rest - mid.astype(F32)).astype(BF)
    return high, mid, low


def shuffled(natural):
    return (natural // BLK) * BLK + (natural % 2) * (BLK // 2) + (natural % BLK) // 2


def shuffle_matrix(size):
    rows = lax.broadcasted_iota(jnp.int32, (size, size), 0)
    cols = lax.broadcasted_iota(jnp.int32, (size, size), 1)
    return jnp.where(shuffled(rows) == cols, 1.0, 0.0).astype(BF)


def unshuffle_matrix(size):
    rows = lax.broadcasted_iota(jnp.int32, (size, size), 0)
    cols = lax.broadcasted_iota(jnp.int32, (size, size), 1)
    return jnp.where(shuffled(cols) == rows, 1.0, 0.0).astype(BF)


def stage_blocks(blocks_ref, tiles_ref, first_slot):
    @pl.loop(0, blocks_ref.shape[0] // 16)
    def _(step):
        row = pl.multiple_of(step * 16, 16)
        target = (first_slot + row) * 32
        for chunk in range(32):
            piece = blocks_ref[pl.ds(row, 16), 128 * chunk : 128 * (chunk + 1)].astype(F32)
            tiles_ref[pl.ds(target + chunk, 16, stride=32), :] = piece


def assembled_pair(tiles_ref, left_slot, right_slot):
    left = tiles_ref[pl.ds(pl.multiple_of(left_slot * 32, 32), 32), :]
    right = tiles_ref[pl.ds(pl.multiple_of(right_slot * 32, 32), 32), :]
    low_half = lax.broadcasted_iota(jnp.int32, (32, 128), 1) < BLK
    even = jnp.where(low_half, left, pltpu.roll(right, BLK, 1))
    odd = jnp.where(low_half, pltpu.roll(left, BLK, 1), right)
    return even.astype(BF), odd.astype(BF)


def assemble_columns(inv_ref, inv_row, tiles_ref, put):
    @pl.loop(0, 16)
    def _(block_row):
        for pair in range(8):
            cell = block_row * 16 + 2 * pair
            even, odd = assembled_pair(
                tiles_ref, inv_ref[inv_row, cell], inv_ref[inv_row, cell + 1]
            )
            row = pl.multiple_of(block_row * BLK, BLK)
            put(pair, row, even)
            put(pair, row + BLK // 2, odd)


def own_kernel(
    place_ref,
    inv_ref,
    gate_ref,
    up_ref,
    down_ref,
    sketch_ref,
    index_ref,
    value_ref,
    weight_ref,
    payload_ref,
    tiles_ref,
    omega_ref,
    split_ref,
    down_dense_ref,
):
    owner = place_ref[0]
    quarter = place_ref[1]
    tiles_ref[pl.ds(160 * 32, 32), :] = jnp.zeros((32, 128), F32)

    for which, blocks_ref in enumerate((gate_ref, up_ref)):
        stage_blocks(blocks_ref, tiles_ref, 0)

        def put(pair, row, piece):
            lane = (pair % 2) * 128
            weight_ref[4 * which + pair // 2, pl.ds(row, 32), lane : lane + 128] = piece

        assemble_columns(inv_ref, which, tiles_ref, put)

    stage_blocks(down_ref, tiles_ref, 0)
    for local_row in range(4):
        for pair in range(8):
            cell = (quarter * 4 + local_row) * 16 + 2 * pair
            even, odd = assembled_pair(tiles_ref, inv_ref[2, cell], inv_ref[2, cell + 1])
            row = local_row * BLK
            down_dense_ref[row : row + 32, 128 * pair : 128 * (pair + 1)] = even
            down_dense_ref[row + 32 : row + 64, 128 * pair : 128 * (pair + 1)] = odd
    payload_ref[32:64, :] = contract_last(sketch_ref[...], down_dense_ref[...])

    local = index_ref[...] - owner * 1024
    inside = (local >= 0) & (local < 1024)
    safe = jnp.where(inside, local, 0)
    spot = shuffled(safe)
    high_part = jnp.where(inside, spot // 128, -1)
    low_part = spot % 128
    values = value_ref[...]
    high_iota = lax.broadcasted_iota(jnp.int32, (8, 256), 0)
    low_iota = lax.broadcasted_iota(jnp.int32, (128, 256), 0)
    for probe in range(P_SIZE):
        picked = jnp.where(
            high_iota == high_part[probe : probe + 1, :], values[probe : probe + 1, :], 0.0
        )
        one_hot = jnp.where(low_iota == low_part[probe : probe + 1, :], 1.0, 0.0).astype(BF)
        total = None
        for part in split3(picked):
            term = contract_last(part, one_hot)
            total = term if total is None else total + term
        omega_ref[8 * probe : 8 * (probe + 1), :] = total
    for high in range(8):
        piece = omega_ref[pl.ds(high, 16, stride=8), :]
        for part_index, part in enumerate(split3(piece)):
            split_ref[
                16 * part_index : 16 * (part_index + 1), 128 * high : 128 * (high + 1)
            ] = part
    for which in range(2):
        triple = dot(split_ref[...], weight_ref[4 * which + quarter])
        payload_ref[16 * which : 16 * (which + 1), :] = triple[:16] + triple[16:32] + triple[32:]


def near_kernel(inv_row, place_ref, inv_ref, first_ref, second_ref, weight_ref, tiles_ref):
    core = place_ref[3]
    tiles_ref[pl.ds(160 * 32, 32), :] = jnp.zeros((32, 128), F32)
    stage_blocks(first_ref, tiles_ref, core * 80)
    stage_blocks(second_ref, tiles_ref, (1 - core) * 80)

    def put(pair, row, piece):
        lane = (pair % 2) * 128
        weight_ref[pair // 2, pl.ds(row, 32), lane : lane + 128] = piece

    assemble_columns(inv_ref, inv_row, tiles_ref, put)


def partial_kernel(
    place_ref,
    own_weight_ref,
    weight_ref,
    tok_ref,
    keep_ref,
    out1_ref,
    out2_ref,
    out3_ref,
    tokens_ref,
):
    side = place_ref[2]
    zone = place_ref[0] // 2
    shuffle = shuffle_matrix(256)
    low_bit = lax.rem(zone, 2)
    high_bit = zone // 2
    for source in range(4):
        spot = lax.rem(low_bit + source % 2, 2) + 2 * lax.rem(high_bit + source // 2, 2)
        for group in range(8):
            piece = tok_ref[spot, :, 256 * group : 256 * (group + 1)]
            moved = dot(piece, shuffle).astype(BF)
            half = lax.rem(group // 4 + side, 2)
            tokens_ref[
                half, 64 * source : 64 * (source + 1), 256 * (group % 4) : 256 * (group % 4 + 1)
            ] = moved
    for chunk in range(4):
        total = dot(tokens_ref[0], own_weight_ref[chunk]) + dot(tokens_ref[1], weight_ref[chunk])
        cols = slice(256 * chunk, 256 * (chunk + 1))
        keep_ref[:, cols] = total[:64]
        out1_ref[:, cols] = total[64:128].astype(BF)
        out2_ref[:, cols] = total[128:192].astype(BF)
        out3_ref[:, cols] = total[192:].astype(BF)


def middle_kernel(
    place_ref,
    gate0_ref,
    gate1_ref,
    gate2_ref,
    gate3_ref,
    up0_ref,
    up1_ref,
    up2_ref,
    up3_ref,
    pay0_ref,
    pay1_ref,
    pay2_ref,
    pay3_ref,
    out_ref,
    lead_ref,
    act_ref,
    pay_ref,
    proj_ref,
    tangent_ref,
):
    quarter = place_ref[1]
    low_bit = quarter % 2
    high_bit = quarter // 2
    unshuffle = unshuffle_matrix(256)
    for flip, ref in enumerate((pay0_ref, pay1_ref, pay2_ref, pay3_ref)):
        spot = lax.rem(low_bit + flip % 2, 2) + 2 * lax.rem(high_bit + flip // 2, 2)
        pay_ref[spot] = ref[...]
    for chunk in range(4):
        cols = slice(256 * chunk, 256 * (chunk + 1))
        proj_ref[:, cols] = dot(pay_ref[chunk, 32:64, :].astype(BF), unshuffle).astype(BF)
        gate_pre = (
            gate0_ref[:, cols]
            + gate1_ref[:, cols].astype(F32)
            + gate2_ref[:, cols].astype(F32)
            + gate3_ref[:, cols].astype(F32)
        )
        up_pre = (
            up0_ref[:, cols]
            + up1_ref[:, cols].astype(F32)
            + up2_ref[:, cols].astype(F32)
            + up3_ref[:, cols].astype(F32)
        )
        sigmoid_g = jax.nn.sigmoid(gate_pre)
        activated = gate_pre * sigmoid_g
        slope_g = sigmoid_g * (1.0 + gate_pre * (1.0 - sigmoid_g))
        lead = slope_g * up_pre
        lead_ref[:, cols] = lead
        act_ref[:, cols] = activated
        for probe in range(P_SIZE):
            probe_gate = pay_ref[chunk, probe : probe + 1, :]
            probe_up = pay_ref[chunk, 16 + probe : 17 + probe, :]
            tangent_ref[64 * probe : 64 * (probe + 1), cols] = (
                lead * probe_gate + activated * probe_up
            ).astype(BF)
    sketch_rows = contract_last(tangent_ref[...], proj_ref[...]).astype(BF)
    for probe in range(P_SIZE):
        rows = sketch_rows[64 * probe : 64 * (probe + 1), :]
        backward = dot(rows, proj_ref[...])
        out_ref[probe : probe + 1, :1024] = jnp.sum(backward * lead_ref[...], axis=0, keepdims=True)
        out_ref[probe : probe + 1, 1024:] = jnp.sum(backward * act_ref[...], axis=0, keepdims=True)


def product_kernel(sum_ref, weight_ref, out_ref):
    sums = sum_ref[...].astype(BF)
    total = None
    for chunk in range(8):
        term = contract_last(sums[:, 256 * chunk : 256 * (chunk + 1)], weight_ref[chunk])
        total = term if total is None else total + term
    unshuffle = unshuffle_matrix(256)
    for group in range(4):
        cols = slice(256 * group, 256 * (group + 1))
        high, mid, low = split3(total[:, cols])
        out_ref[:, cols] = dot(high, unshuffle) + dot(mid, unshuffle) + dot(low, unshuffle)


def pair_split(
    tokens,
    gate_blocks,
    gate_slot,
    up_blocks,
    up_slot,
    down_blocks,
    down_slot,
    sketch,
    probe_index,
    probe_value,
):
    owner = lax.axis_index("fsdp")
    core = lax.axis_index("seq")
    group = lax.axis_index("groups")
    zone = owner // 2
    side = owner % 2
    place = jnp.stack([owner, 2 * group + core, side, core]).astype(jnp.int32)

    def owner_flip(value, bits):
        return lax.ppermute(value, "fsdp", [(i, i ^ bits) for i in range(8)])

    def core_flip(value):
        return lax.ppermute(value, "seq", [(0, 1), (1, 0)])

    slots = jnp.stack([gate_slot, up_slot, down_slot])
    cells = lax.broadcasted_iota(jnp.int32, (3, 160, 256), 2)
    slot_numbers = lax.broadcasted_iota(jnp.int32, (3, 160, 256), 1)
    inv = jnp.min(jnp.where(slots[:, :, None] == cells, slot_numbers, 160), axis=1)

    by_zone = tokens.reshape(64, 4, 2048).transpose(1, 0, 2)
    gathered = lax.all_to_all(
        by_zone,
        "fsdp",
        split_axis=0,
        concat_axis=0,
        tiled=True,
        axis_index_groups=[[0, 2, 4, 6], [1, 3, 5, 7]],
    )

    near_inv = owner_flip(inv, 1)
    near_gate = owner_flip(lax.dynamic_slice(gate_blocks, (core * 80, 0), (80, 4096)), 1)
    near_up = owner_flip(lax.dynamic_slice(up_blocks, (core * 80, 0), (80, 4096)), 1)

    weights, payload = pl.pallas_call(
        own_kernel,
        out_shape=(
            jax.ShapeDtypeStruct((8, 1024, 256), BF),
            jax.ShapeDtypeStruct((64, 256), F32),
        ),
        in_specs=[SMEM, SMEM] + [VMEM] * 6,
        out_specs=(VMEM, VMEM),
        scratch_shapes=[
            pltpu.VMEM((161 * 32, 128), F32),
            pltpu.VMEM((128, 128), F32),
            pltpu.VMEM((48, 1024), BF),
            pltpu.VMEM((256, 1024), BF),
        ],
        compiler_params=PARAMS,
        name="own_blocks",
    )(place, inv, gate_blocks, up_blocks, down_blocks, sketch, probe_index, probe_value)

    for bits in (1, 2, 4):
        payload = payload + owner_flip(payload, bits)
    pay_parts = [
        payload,
        core_flip(payload),
        lax.ppermute(payload, "groups", [(0, 1), (1, 0)]),
        lax.ppermute(payload, ("groups", "seq"), [(i, i ^ 3) for i in range(4)]),
    ]

    def near_weights(which, near):
        return pl.pallas_call(
            functools.partial(near_kernel, which),
            out_shape=jax.ShapeDtypeStruct((4, 1024, 256), BF),
            in_specs=[SMEM, SMEM, VMEM, VMEM],
            out_specs=VMEM,
            scratch_shapes=[pltpu.VMEM((161 * 32, 128), F32)],
            compiler_params=PARAMS,
            name="near_blocks",
        )(place, near_inv, near, core_flip(near))

    def partial_sums(which, near):
        near_dense = near_weights(which, near)
        return pl.pallas_call(
            partial_kernel,
            out_shape=(jax.ShapeDtypeStruct((64, 1024), F32),)
            + (jax.ShapeDtypeStruct((64, 1024), BF),) * 3,
            grid=(1,),
            in_specs=[SMEM]
            + [pl.BlockSpec((4, 1024, 256), lambda i: (which, 0, 0))]
            + [VMEM] * 2,
            out_specs=(VMEM,) * 4,
            scratch_shapes=[pltpu.VMEM((2, 256, 1024), BF)],
            compiler_params=PARAMS,
            name="partial_sums",
        )(place, weights, near_dense, gathered)

    middle_args = []
    for which, near in enumerate((near_gate, near_up)):
        keep, *sent = partial_sums(which, near)
        middle_args.append(keep)
        for flip in (1, 2, 3):
            middle_args.append(owner_flip(sent[flip - 1], 2 * flip))

    sums = pl.pallas_call(
        middle_kernel,
        out_shape=jax.ShapeDtypeStruct((P_SIZE, 2048), F32),
        in_specs=[SMEM] + [VMEM] * 12,
        out_specs=VMEM,
        scratch_shapes=[
            pltpu.VMEM((64, 1024), F32),
            pltpu.VMEM((64, 1024), F32),
            pltpu.VMEM((4, 64, 256), F32),
            pltpu.VMEM((K, 1024), BF),
            pltpu.VMEM((64 * P_SIZE, 1024), BF),
        ],
        compiler_params=PARAMS,
        name="token_sums",
    )(place, *middle_args, *pay_parts)

    sums = sums + core_flip(sums)
    for bits in (1, 2, 4):
        sums = sums + owner_flip(sums, bits)

    return pl.pallas_call(
        product_kernel,
        out_shape=jax.ShapeDtypeStruct((P_SIZE, 1024), F32),
        in_specs=[VMEM, VMEM],
        out_specs=VMEM,
        compiler_params=PARAMS,
        name="products",
    )(sums, weights)


def per_device(tokens, gate_blocks, *rest):
    fits = (
        lax.axis_size("fsdp") == 8
        and lax.axis_size("seq") == 2
        and lax.axis_size("groups") == 2
        and tokens.shape == (64, 8192)
        and gate_blocks.shape == (160, 4096)
        and rest[-2].shape == (P_SIZE, 256)
    )
    return (pair_split if fits else hidden_split)(tokens, gate_blocks, *rest)


def solution(mesh):
    in_specs = (
        P(("groups", "fsdp", "seq"), None),
        P("fsdp", None),
        P("fsdp"),
        P("fsdp", None),
        P("fsdp"),
        P("fsdp", None),
        P("fsdp"),
        P(None, "fsdp"),
        P(),
        P(),
    )
    out_specs = P("groups", "fsdp")
    return jax.shard_map(
        per_device, mesh=mesh, in_specs=in_specs, out_specs=out_specs, check_vma=False
    )
```

```python
import functools

import jax
import jax.numpy as jnp
from jax import lax
from jax.experimental import pallas as pl
from jax.experimental.pallas import tpu as pltpu
from jax.sharding import PartitionSpec as P

HID_DEV = 128
BLK = 64
P_SIZE = 16
K = 32

BF = jnp.bfloat16
F32 = jnp.float32
VMEM = pl.BlockSpec(memory_space=pltpu.VMEM)
SMEM = pl.BlockSpec(memory_space=pltpu.SMEM)

STRIDE = 168


def params(mebibytes):
    return pltpu.CompilerParams(vmem_limit_bytes=mebibytes * 1024 * 1024)


def unpack(blocks, slot_ids, cell_total):
    holder = jnp.zeros((cell_total + 1, blocks.shape[1]), blocks.dtype)
    return holder.at[slot_ids].set(blocks)[:cell_total]


def contract_last(first_mat, second_mat):
    return lax.dot_general(
        first_mat, second_mat, (((1,), (1,)), ((), ())), preferred_element_type=jnp.float32
    )


def hidden_split(
    tokens,
    gate_blocks,
    gate_slot,
    up_blocks,
    up_slot,
    down_blocks,
    down_slot,
    sketch,
    probe_index,
    probe_value,
):
    owners = lax.axis_size("fsdp")
    model_width = tokens.shape[1]
    local_width = model_width // owners
    block_rows = local_width // BLK
    hidden = HID_DEV
    col_blocks = hidden * owners // BLK
    cell_total = block_rows * col_blocks
    gate_dense = unpack(gate_blocks, gate_slot, cell_total).reshape(
        block_rows, col_blocks, BLK, BLK
    )
    up_dense = unpack(up_blocks, up_slot, cell_total).reshape(block_rows, col_blocks, BLK, BLK)
    stacked = jnp.stack([gate_dense, up_dense], axis=1)
    stacked = stacked.reshape(block_rows, 2, owners, hidden // BLK, BLK, BLK)
    stacked = stacked.transpose(0, 4, 2, 1, 3, 5).reshape(local_width, owners * 2 * hidden)
    both_weights = lax.all_to_all(stacked, "fsdp", split_axis=1, concat_axis=0, tiled=True)
    picked = both_weights[probe_index].astype(jnp.float32)
    probe_both = jnp.sum(picked * probe_value[:, :, None], axis=1)
    preact = jnp.dot(
        lax.all_gather(tokens, "fsdp", axis=0, tiled=True),
        both_weights,
        preferred_element_type=jnp.float32,
    )
    row_count = preact.shape[0]
    gate_pre = preact[:, :hidden]
    up_pre = preact[:, hidden:]
    down_dense = unpack(down_blocks, down_slot, cell_total).reshape(
        col_blocks, block_rows, BLK, BLK
    )
    down_dense = down_dense.transpose(0, 2, 1, 3).reshape(col_blocks * BLK, local_width)
    down_rows = lax.all_to_all(down_dense, "fsdp", split_axis=0, concat_axis=1, tiled=True)
    full_sketch = lax.all_gather(sketch, "fsdp", axis=1, tiled=True)
    projected = contract_last(down_rows, full_sketch)
    projected = projected.astype(jnp.bfloat16)
    sigmoid_g = jax.nn.sigmoid(gate_pre)
    activated = gate_pre * sigmoid_g
    slope_g = sigmoid_g * (1.0 + gate_pre * (1.0 - sigmoid_g))
    lead_term = slope_g * up_pre
    tangent = (
        lead_term[:, None, :] * probe_both[None, :, :hidden]
        + activated[:, None, :] * probe_both[None, :, hidden:]
    )
    tangent = tangent.astype(jnp.bfloat16)
    partial_sketch = jnp.dot(
        tangent.reshape(row_count * P_SIZE, hidden), projected, preferred_element_type=jnp.float32
    )
    partial_sketch = partial_sketch.reshape(row_count, P_SIZE * K)
    sketch_rows = lax.psum(partial_sketch, "fsdp").astype(jnp.bfloat16)
    backward = contract_last(sketch_rows.reshape(row_count * P_SIZE, K), projected).reshape(
        row_count, P_SIZE, hidden
    )
    summed = jnp.concatenate(
        [
            jnp.sum(backward * lead_term[:, None, :], axis=0),
            jnp.sum(backward * activated[:, None, :], axis=0),
        ],
        axis=1,
    )
    summed = lax.psum(summed, "seq").astype(jnp.bfloat16)
    products = contract_last(summed, both_weights)
    return lax.psum_scatter(products, "fsdp", scatter_dimension=1, tiled=True)


def dot(a, b):
    return jnp.dot(a, b, preferred_element_type=F32)


def split3(value):
    high = value.astype(BF)
    rest = value - high.astype(F32)
    mid = rest.astype(BF)
    low = (rest - mid.astype(F32)).astype(BF)
    return high, mid, low


def shuffled(natural):
    return (natural // BLK) * BLK + (natural % 2) * (BLK // 2) + (natural % BLK) // 2


def shuffle_matrix(size):
    rows = lax.broadcasted_iota(jnp.int32, (size, size), 0)
    cols = lax.broadcasted_iota(jnp.int32, (size, size), 1)
    return jnp.where(shuffled(rows) == cols, 1.0, 0.0).astype(BF)


def unshuffle_matrix(size):
    rows = lax.broadcasted_iota(jnp.int32, (size, size), 0)
    cols = lax.broadcasted_iota(jnp.int32, (size, size), 1)
    return jnp.where(shuffled(cols) == rows, 1.0, 0.0).astype(BF)


def stage_blocks(blocks_ref, tiles_ref, first_slot):
    @pl.loop(0, blocks_ref.shape[0] // 16)
    def _(step):
        row = pl.multiple_of(step * 16, 16)
        target = pl.multiple_of(first_slot + row, 16)
        for chunk in range(32):
            piece = blocks_ref[pl.ds(row, 16), 128 * chunk : 128 * (chunk + 1)].astype(F32)
            tiles_ref[pl.ds(target + chunk * STRIDE, 16), :] = piece


def clear_empty_slot(tiles_ref):
    for chunk in range(32):
        tiles_ref[pl.ds(chunk * STRIDE + 160, 8), :] = jnp.zeros((8, 128), F32)


def assembled_pair(tiles_ref, left_slot, right_slot):
    left = tiles_ref[pl.ds(left_slot, 32, stride=STRIDE), :]
    right = tiles_ref[pl.ds(right_slot, 32, stride=STRIDE), :]
    low_half = lax.broadcasted_iota(jnp.int32, (32, 128), 1) < BLK
    straight = jnp.where(low_half, left, right)
    crossed = pltpu.roll(jnp.where(low_half, right, left), BLK, 1)
    even = jnp.where(low_half, straight, crossed)
    odd = jnp.where(low_half, crossed, straight)
    return even.astype(BF), odd.astype(BF)


def assemble_columns(inv_ref, inv_row, tiles_ref, put):
    @pl.loop(0, 16)
    def _(block_row):
        for pair in range(8):
            cell = block_row * 16 + 2 * pair
            even, odd = assembled_pair(
                tiles_ref, inv_ref[inv_row, cell], inv_ref[inv_row, cell + 1]
            )
            row = pl.multiple_of(block_row * BLK, BLK)
            put(pair, row, even)
            put(pair, row + BLK // 2, odd)


def own_kernel(
    place_ref,
    inv_ref,
    gate_ref,
    up_ref,
    down_ref,
    sketch_ref,
    index_ref,
    value_ref,
    weight_ref,
    payload_ref,
    tiles_ref,
    omega_ref,
    split_ref,
    down_dense_ref,
):
    owner = place_ref[0]
    quarter = place_ref[1]
    clear_empty_slot(tiles_ref)

    for which, blocks_ref in enumerate((gate_ref, up_ref)):
        stage_blocks(blocks_ref, tiles_ref, 0)

        def put(pair, row, piece):
            lane = (pair % 2) * 128
            weight_ref[4 * which + pair // 2, pl.ds(row, 32), lane : lane + 128] = piece

        assemble_columns(inv_ref, which, tiles_ref, put)

    stage_blocks(down_ref, tiles_ref, 0)
    for local_row in range(4):
        for pair in range(8):
            cell = (quarter * 4 + local_row) * 16 + 2 * pair
            even, odd = assembled_pair(tiles_ref, inv_ref[2, cell], inv_ref[2, cell + 1])
            row = local_row * BLK
            down_dense_ref[row : row + 32, 128 * pair : 128 * (pair + 1)] = even
            down_dense_ref[row + 32 : row + 64, 128 * pair : 128 * (pair + 1)] = odd
    payload_ref[32:64, :] = contract_last(sketch_ref[...], down_dense_ref[...])

    local = index_ref[...] - owner * 1024
    inside = (local >= 0) & (local < 1024)
    safe = jnp.where(inside, local, 0)
    spot = shuffled(safe)
    high_part = jnp.where(inside, spot // 128, -1)
    low_part = spot % 128
    values = value_ref[...]
    high_iota = lax.broadcasted_iota(jnp.int32, (8, 256), 0)
    low_iota = lax.broadcasted_iota(jnp.int32, (128, 256), 0)
    for probe in range(P_SIZE):
        picked = jnp.where(
            high_iota == high_part[probe : probe + 1, :], values[probe : probe + 1, :], 0.0
        )
        one_hot = jnp.where(low_iota == low_part[probe : probe + 1, :], 1.0, 0.0).astype(BF)
        total = None
        for part in split3(picked):
            term = contract_last(part, one_hot)
            total = term if total is None else total + term
        omega_ref[8 * probe : 8 * (probe + 1), :] = total
    for high in range(8):
        piece = omega_ref[pl.ds(high, 16, stride=8), :]
        for part_index, part in enumerate(split3(piece)):
            split_ref[
                16 * part_index : 16 * (part_index + 1), 128 * high : 128 * (high + 1)
            ] = part
    for which in range(2):
        triple = dot(split_ref[...], weight_ref[4 * which + quarter])
        payload_ref[16 * which : 16 * (which + 1), :] = triple[:16] + triple[16:32] + triple[32:]


def flipped(two_bits, flip):
    low_bit = lax.rem(two_bits + flip % 2, 2)
    return low_bit + 2 * lax.rem(two_bits // 2 + flip // 2, 2)


def near_kernel(place_ref, inv_ref, blocks_ref, weight_ref, tiles_ref):
    clear_empty_slot(tiles_ref)
    stage_blocks(blocks_ref, tiles_ref, 0)

    def put(pair, row, piece):
        lane = (pair % 2) * 128
        weight_ref[pair // 2, pl.ds(row, 32), lane : lane + 128] = piece

    assemble_columns(inv_ref, place_ref[3], tiles_ref, put)


def partial_kernel(stacked, place_ref, own_ref, near_ref, tok_ref, keep_ref, *rest):
    tokens_ref = rest[-1]
    side = place_ref[2]
    zone = place_ref[0] // 2
    shuffle = shuffle_matrix(256)
    for source in range(4):
        spot = flipped(zone, source)
        for group in range(8):
            piece = tok_ref[spot, :, 256 * group : 256 * (group + 1)]
            moved = dot(piece, shuffle).astype(BF)
            half = lax.rem(group // 4 + side, 2)
            tokens_ref[
                half, 64 * source : 64 * (source + 1), 256 * (group % 4) : 256 * (group % 4 + 1)
            ] = moved
    for chunk in range(4):
        total = dot(tokens_ref[0], own_ref[chunk]) + dot(tokens_ref[1], near_ref[chunk])
        cols = slice(256 * chunk, 256 * (chunk + 1))
        keep_ref[:, cols] = total[:64]
        for flip in range(0 if stacked else 1, 4):
            sent = total[64 * flip : 64 * (flip + 1)].astype(BF)
            if stacked:
                rest[0][flipped(zone, flip), :, cols] = sent
            else:
                rest[flip - 1][:, cols] = sent


def middle_kernel(
    place_ref,
    first_keep_ref,
    first_ref,
    second_keep_ref,
    second1_ref,
    second2_ref,
    second3_ref,
    pay0_ref,
    pay1_ref,
    pay2_ref,
    pay3_ref,
    mine_ref,
    theirs_ref,
    lead_ref,
    act_ref,
    pay_ref,
    proj_ref,
    tangent_ref,
    rows_ref,
):
    zone = place_ref[0] // 2
    quarter = place_ref[1]
    core = place_ref[3]
    unshuffle = unshuffle_matrix(256)
    for flip, ref in enumerate((pay0_ref, pay1_ref, pay2_ref, pay3_ref)):
        pay_ref[flipped(quarter, flip)] = ref[...]
    for chunk in range(4):
        cols = slice(256 * chunk, 256 * (chunk + 1))
        proj_ref[:, cols] = dot(pay_ref[chunk, 32:64, :].astype(BF), unshuffle).astype(BF)
        first = first_keep_ref[:, cols]
        for flip in (1, 2, 3):
            first = first + first_ref[flipped(zone, flip), :, cols].astype(F32)
        second = second_keep_ref[:, cols]
        for ref in (second1_ref, second2_ref, second3_ref):
            second = second + ref[:, cols].astype(F32)
        gate_pre = jnp.where(core == 0, first, second)
        up_pre = jnp.where(core == 0, second, first)
        sigmoid_g = jax.nn.sigmoid(gate_pre)
        activated = gate_pre * sigmoid_g
        slope_g = sigmoid_g * (1.0 + gate_pre * (1.0 - sigmoid_g))
        lead = slope_g * up_pre
        lead_ref[:, cols] = lead
        act_ref[:, cols] = activated
        for probe in range(P_SIZE):
            probe_gate = pay_ref[chunk, probe : probe + 1, :]
            probe_up = pay_ref[chunk, 16 + probe : 17 + probe, :]
            tangent_ref[64 * probe : 64 * (probe + 1), cols] = (
                lead * probe_gate + activated * probe_up
            ).astype(BF)
    rows_ref[...] = contract_last(tangent_ref[...], proj_ref[...]).astype(BF)
    for step in range(P_SIZE):
        probe = lax.rem(step + 8 * core, P_SIZE)
        backward = dot(rows_ref[pl.ds(pl.multiple_of(probe * 64, 64), 64), :], proj_ref[...])
        target = mine_ref if step < 8 else theirs_ref
        row = slice(step % 8, step % 8 + 1)
        target[row, :1024] = jnp.sum(backward * lead_ref[...], axis=0, keepdims=True)
        target[row, 1024:] = jnp.sum(backward * act_ref[...], axis=0, keepdims=True)


def product_kernel(place_ref, mine_ref, theirs_ref, weight_ref, out_ref, sum_ref):
    core = place_ref[3]
    sum_ref[core] = mine_ref[...]
    sum_ref[1 - core] = theirs_ref[...]
    sums = jnp.concatenate([sum_ref[0], sum_ref[1]], axis=0).astype(BF)
    total = None
    for chunk in range(8):
        term = contract_last(sums[:, 256 * chunk : 256 * (chunk + 1)], weight_ref[chunk])
        total = term if total is None else total + term
    unshuffle = unshuffle_matrix(256)
    for group in range(4):
        cols = slice(256 * group, 256 * (group + 1))
        high, mid, low = split3(total[:, cols])
        out_ref[:, cols] = dot(high, unshuffle) + dot(mid, unshuffle) + dot(low, unshuffle)


def pair_split(
    tokens,
    gate_blocks,
    gate_slot,
    up_blocks,
    up_slot,
    down_blocks,
    down_slot,
    sketch,
    probe_index,
    probe_value,
):
    owner = lax.axis_index("fsdp")
    core = lax.axis_index("seq")
    group = lax.axis_index("groups")
    place = jnp.stack([owner, 2 * group + core, owner % 2, core]).astype(jnp.int32)

    def owner_flip(value, bits):
        return lax.ppermute(value, "fsdp", [(i, i ^ bits) for i in range(8)])

    def core_flip(value):
        return lax.ppermute(value, "seq", [(0, 1), (1, 0)])

    def zone_exchange(value):
        return lax.all_to_all(
            value,
            "fsdp",
            split_axis=0,
            concat_axis=0,
            tiled=True,
            axis_index_groups=[[0, 2, 4, 6], [1, 3, 5, 7]],
        )

    by_zone = tokens.reshape(64, 4, 2048).transpose(1, 0, 2)
    by_zone, gate_source, up_source = lax.optimization_barrier((by_zone, gate_blocks, up_blocks))
    gathered = core_flip(zone_exchange(by_zone))
    near = owner_flip(jnp.where(core == 0, gate_source, up_source), 1)

    slots = jnp.stack([gate_slot, up_slot, down_slot])
    cells = lax.broadcasted_iota(jnp.int32, (3, 160, 256), 2)
    slot_numbers = lax.broadcasted_iota(jnp.int32, (3, 160, 256), 1)
    inv = jnp.min(jnp.where(slots[:, :, None] == cells, slot_numbers, 160), axis=1)
    near_inv = owner_flip(inv, 1)

    weights, payload = pl.pallas_call(
        own_kernel,
        out_shape=(
            jax.ShapeDtypeStruct((8, 1024, 256), BF),
            jax.ShapeDtypeStruct((64, 256), F32),
        ),
        in_specs=[SMEM, SMEM] + [VMEM] * 6,
        out_specs=(VMEM, VMEM),
        scratch_shapes=[
            pltpu.VMEM((32 * STRIDE, 128), F32),
            pltpu.VMEM((128, 128), F32),
            pltpu.VMEM((48, 1024), BF),
            pltpu.VMEM((256, 1024), BF),
        ],
        compiler_params=params(20),
        name="own_blocks",
    )(place, inv, gate_blocks, up_blocks, down_blocks, sketch, probe_index, probe_value)

    for bits in (1, 2, 4):
        payload = payload + owner_flip(payload, bits)
    near, near_inv, payload = lax.optimization_barrier((near, near_inv, payload))
    pay_parts = [
        payload,
        core_flip(payload),
        lax.ppermute(payload, "groups", [(0, 1), (1, 0)]),
        lax.ppermute(payload, ("groups", "seq"), [(i, i ^ 3) for i in range(4)]),
    ]

    near_weights = pl.pallas_call(
        near_kernel,
        out_shape=jax.ShapeDtypeStruct((4, 1024, 256), BF),
        in_specs=[SMEM, SMEM, VMEM],
        out_specs=VMEM,
        scratch_shapes=[pltpu.VMEM((32 * STRIDE, 128), F32)],
        compiler_params=params(12),
        name="near_blocks",
    )(place, near_inv, near)

    def partial_sums(stacked, near_dense):
        def own_index(i, place_ref):
            return (place_ref[3] if stacked else 1 - place_ref[3], 0, 0)

        sent_shapes = (
            (jax.ShapeDtypeStruct((4, 64, 1024), BF),)
            if stacked
            else (jax.ShapeDtypeStruct((64, 1024), BF),) * 3
        )
        return pl.pallas_call(
            functools.partial(partial_kernel, stacked),
            out_shape=(jax.ShapeDtypeStruct((64, 1024), F32),) + sent_shapes,
            grid_spec=pltpu.PrefetchScalarGridSpec(
                num_scalar_prefetch=1,
                grid=(1,),
                in_specs=[pl.BlockSpec((4, 1024, 256), own_index), VMEM, VMEM],
                out_specs=(VMEM,) * (1 + len(sent_shapes)),
                scratch_shapes=[pltpu.VMEM((2, 256, 1024), BF)],
            ),
            compiler_params=params(16),
            name="partial_sums",
        )(place, weights, near_dense, gathered)

    first_keep, first_sent = partial_sums(True, near_weights)
    first_back = zone_exchange(first_sent)
    second_keep, *second_sent = partial_sums(False, core_flip(near_weights))
    second_back = [owner_flip(second_sent[flip - 1], 2 * flip) for flip in (1, 2, 3)]

    mine, theirs = pl.pallas_call(
        middle_kernel,
        out_shape=(jax.ShapeDtypeStruct((8, 2048), F32),) * 2,
        in_specs=[SMEM] + [VMEM] * 10,
        out_specs=(VMEM, VMEM),
        scratch_shapes=[
            pltpu.VMEM((64, 1024), F32),
            pltpu.VMEM((64, 1024), F32),
            pltpu.VMEM((4, 64, 256), F32),
            pltpu.VMEM((K, 1024), BF),
            pltpu.VMEM((64 * P_SIZE, 1024), BF),
            pltpu.VMEM((64 * P_SIZE, K), BF),
        ],
        compiler_params=params(16),
        name="token_sums",
    )(place, first_keep, first_back, second_keep, *second_back, *pay_parts)

    sums = mine + core_flip(theirs)
    for bits in (1, 2, 4):
        sums = sums + owner_flip(sums, bits)

    return pl.pallas_call(
        product_kernel,
        out_shape=jax.ShapeDtypeStruct((P_SIZE, 1024), F32),
        in_specs=[SMEM, VMEM, VMEM, VMEM],
        out_specs=VMEM,
        scratch_shapes=[pltpu.VMEM((2, 8, 2048), F32)],
        compiler_params=params(12),
        name="products",
    )(place, sums, core_flip(sums), weights)


def per_device(tokens, gate_blocks, *rest):
    fits = (
        lax.axis_size("fsdp") == 8
        and lax.axis_size("seq") == 2
        and lax.axis_size("groups") == 2
        and tokens.shape == (64, 8192)
        and gate_blocks.shape == (160, 4096)
        and rest[-2].shape == (P_SIZE, 256)
    )
    return (pair_split if fits else hidden_split)(tokens, gate_blocks, *rest)


def solution(mesh):
    in_specs = (
        P(("groups", "fsdp", "seq"), None),
        P("fsdp", None),
        P("fsdp"),
        P("fsdp", None),
        P("fsdp"),
        P("fsdp", None),
        P("fsdp"),
        P(None, "fsdp"),
        P(),
        P(),
    )
    out_specs = P("groups", "fsdp")
    return jax.shard_map(
        per_device, mesh=mesh, in_specs=in_specs, out_specs=out_specs, check_vma=False
    )
```

```python
import functools

import jax
import jax.numpy as jnp
from jax import lax
from jax.experimental import pallas as pl
from jax.experimental.pallas import tpu as pltpu
from jax.sharding import PartitionSpec as P

HID_DEV = 128
BLK = 64
P_SIZE = 16
K = 32

BF = jnp.bfloat16
F32 = jnp.float32
VMEM = pl.BlockSpec(memory_space=pltpu.VMEM)
SMEM = pl.BlockSpec(memory_space=pltpu.SMEM)
HBM = pl.BlockSpec(memory_space=pltpu.HBM)

STRIDE = 168


def params(mebibytes):
    return pltpu.CompilerParams(vmem_limit_bytes=mebibytes * 1024 * 1024)


def unpack(blocks, slot_ids, cell_total):
    holder = jnp.zeros((cell_total + 1, blocks.shape[1]), blocks.dtype)
    return holder.at[slot_ids].set(blocks)[:cell_total]


def contract_last(first_mat, second_mat):
    return lax.dot_general(
        first_mat, second_mat, (((1,), (1,)), ((), ())), preferred_element_type=jnp.float32
    )


def hidden_split(
    tokens,
    gate_blocks,
    gate_slot,
    up_blocks,
    up_slot,
    down_blocks,
    down_slot,
    sketch,
    probe_index,
    probe_value,
):
    owners = lax.axis_size("fsdp")
    model_width = tokens.shape[1]
    local_width = model_width // owners
    block_rows = local_width // BLK
    hidden = HID_DEV
    col_blocks = hidden * owners // BLK
    cell_total = block_rows * col_blocks
    gate_dense = unpack(gate_blocks, gate_slot, cell_total).reshape(
        block_rows, col_blocks, BLK, BLK
    )
    up_dense = unpack(up_blocks, up_slot, cell_total).reshape(block_rows, col_blocks, BLK, BLK)
    stacked = jnp.stack([gate_dense, up_dense], axis=1)
    stacked = stacked.reshape(block_rows, 2, owners, hidden // BLK, BLK, BLK)
    stacked = stacked.transpose(0, 4, 2, 1, 3, 5).reshape(local_width, owners * 2 * hidden)
    both_weights = lax.all_to_all(stacked, "fsdp", split_axis=1, concat_axis=0, tiled=True)
    picked = both_weights[probe_index].astype(jnp.float32)
    probe_both = jnp.sum(picked * probe_value[:, :, None], axis=1)
    preact = jnp.dot(
        lax.all_gather(tokens, "fsdp", axis=0, tiled=True),
        both_weights,
        preferred_element_type=jnp.float32,
    )
    row_count = preact.shape[0]
    gate_pre = preact[:, :hidden]
    up_pre = preact[:, hidden:]
    down_dense = unpack(down_blocks, down_slot, cell_total).reshape(
        col_blocks, block_rows, BLK, BLK
    )
    down_dense = down_dense.transpose(0, 2, 1, 3).reshape(col_blocks * BLK, local_width)
    down_rows = lax.all_to_all(down_dense, "fsdp", split_axis=0, concat_axis=1, tiled=True)
    full_sketch = lax.all_gather(sketch, "fsdp", axis=1, tiled=True)
    projected = contract_last(down_rows, full_sketch)
    projected = projected.astype(jnp.bfloat16)
    sigmoid_g = jax.nn.sigmoid(gate_pre)
    activated = gate_pre * sigmoid_g
    slope_g = sigmoid_g * (1.0 + gate_pre * (1.0 - sigmoid_g))
    lead_term = slope_g * up_pre
    tangent = (
        lead_term[:, None, :] * probe_both[None, :, :hidden]
        + activated[:, None, :] * probe_both[None, :, hidden:]
    )
    tangent = tangent.astype(jnp.bfloat16)
    partial_sketch = jnp.dot(
        tangent.reshape(row_count * P_SIZE, hidden), projected, preferred_element_type=jnp.float32
    )
    partial_sketch = partial_sketch.reshape(row_count, P_SIZE * K)
    sketch_rows = lax.psum(partial_sketch, "fsdp").astype(jnp.bfloat16)
    backward = contract_last(sketch_rows.reshape(row_count * P_SIZE, K), projected).reshape(
        row_count, P_SIZE, hidden
    )
    summed = jnp.concatenate(
        [
            jnp.sum(backward * lead_term[:, None, :], axis=0),
            jnp.sum(backward * activated[:, None, :], axis=0),
        ],
        axis=1,
    )
    summed = lax.psum(summed, "seq").astype(jnp.bfloat16)
    products = contract_last(summed, both_weights)
    return lax.psum_scatter(products, "fsdp", scatter_dimension=1, tiled=True)


def dot(a, b):
    return jnp.dot(a, b, preferred_element_type=F32)


def split3(value):
    high = value.astype(BF)
    rest = value - high.astype(F32)
    mid = rest.astype(BF)
    low = (rest - mid.astype(F32)).astype(BF)
    return high, mid, low


def shuffled(natural):
    return (natural // BLK) * BLK + (natural % 2) * (BLK // 2) + (natural % BLK) // 2


def shuffle_matrix(size):
    rows = lax.broadcasted_iota(jnp.int32, (size, size), 0)
    cols = lax.broadcasted_iota(jnp.int32, (size, size), 1)
    return jnp.where(shuffled(rows) == cols, 1.0, 0.0).astype(BF)


def unshuffle_matrix(size):
    rows = lax.broadcasted_iota(jnp.int32, (size, size), 0)
    cols = lax.broadcasted_iota(jnp.int32, (size, size), 1)
    return jnp.where(shuffled(cols) == rows, 1.0, 0.0).astype(BF)


def stage_blocks(blocks_ref, tiles_ref, first_slot):
    @pl.loop(0, blocks_ref.shape[0] // 16)
    def _(step):
        row = pl.multiple_of(step * 16, 16)
        target = pl.multiple_of(first_slot + row, 16)
        for chunk in range(32):
            piece = blocks_ref[pl.ds(row, 16), 128 * chunk : 128 * (chunk + 1)].astype(F32)
            tiles_ref[pl.ds(target + chunk * STRIDE, 16), :] = piece


def clear_empty_slot(tiles_ref):
    for chunk in range(32):
        tiles_ref[pl.ds(chunk * STRIDE + 160, 8), :] = jnp.zeros((8, 128), F32)


def assembled_pair(tiles_ref, left_slot, right_slot):
    left = tiles_ref[pl.ds(left_slot, 32, stride=STRIDE), :]
    right = tiles_ref[pl.ds(right_slot, 32, stride=STRIDE), :]
    low_half = lax.broadcasted_iota(jnp.int32, (32, 128), 1) < BLK
    straight = jnp.where(low_half, left, right)
    crossed = pltpu.roll(jnp.where(low_half, right, left), BLK, 1)
    even = jnp.where(low_half, straight, crossed)
    odd = jnp.where(low_half, crossed, straight)
    return even.astype(BF), odd.astype(BF)


def assemble_columns(inv_ref, inv_row, tiles_ref, put):
    @pl.loop(0, 16)
    def _(block_row):
        for pair in range(8):
            cell = block_row * 16 + 2 * pair
            even, odd = assembled_pair(
                tiles_ref, inv_ref[inv_row, cell], inv_ref[inv_row, cell + 1]
            )
            row = pl.multiple_of(block_row * BLK, BLK)
            put(pair, row, even)
            put(pair, row + BLK // 2, odd)


def own_kernel(
    place_ref,
    inv_ref,
    gate_ref,
    up_ref,
    down_ref,
    sketch_ref,
    index_ref,
    value_ref,
    weight_out_ref,
    payload_ref,
    tiles_ref,
    omega_ref,
    split_ref,
    down_dense_ref,
    blocks_ref,
    weight_ref,
    in_sem,
    out_sem,
):
    owner = place_ref[0]
    quarter = place_ref[1]
    loads = [
        pltpu.make_async_copy(source, blocks_ref.at[i], in_sem.at[i])
        for i, source in enumerate((gate_ref, up_ref, down_ref))
    ]
    stores = [
        pltpu.make_async_copy(
            weight_ref.at[pl.ds(4 * i, 4)], weight_out_ref.at[pl.ds(4 * i, 4)], out_sem.at[i]
        )
        for i in range(2)
    ]
    for load in loads:
        load.start()
    clear_empty_slot(tiles_ref)

    for which in range(2):
        loads[which].wait()
        stage_blocks(blocks_ref.at[which], tiles_ref, 0)

        def put(pair, row, piece):
            lane = (pair % 2) * 128
            weight_ref[4 * which + pair // 2, pl.ds(row, 32), lane : lane + 128] = piece

        assemble_columns(inv_ref, which, tiles_ref, put)
        stores[which].start()

    loads[2].wait()
    stage_blocks(blocks_ref.at[2], tiles_ref, 0)
    for local_row in range(4):
        for pair in range(8):
            cell = (quarter * 4 + local_row) * 16 + 2 * pair
            even, odd = assembled_pair(tiles_ref, inv_ref[2, cell], inv_ref[2, cell + 1])
            row = local_row * BLK
            down_dense_ref[row : row + 32, 128 * pair : 128 * (pair + 1)] = even
            down_dense_ref[row + 32 : row + 64, 128 * pair : 128 * (pair + 1)] = odd
    payload_ref[32:64, :] = contract_last(sketch_ref[...], down_dense_ref[...])

    local = index_ref[...] - owner * 1024
    inside = (local >= 0) & (local < 1024)
    safe = jnp.where(inside, local, 0)
    spot = shuffled(safe)
    high_part = jnp.where(inside, spot // 128, -1)
    low_part = spot % 128
    values = value_ref[...]
    high_iota = lax.broadcasted_iota(jnp.int32, (8, 256), 0)
    low_iota = lax.broadcasted_iota(jnp.int32, (128, 256), 0)
    for probe in range(P_SIZE):
        picked = jnp.where(
            high_iota == high_part[probe : probe + 1, :], values[probe : probe + 1, :], 0.0
        )
        one_hot = jnp.where(low_iota == low_part[probe : probe + 1, :], 1.0, 0.0).astype(BF)
        total = None
        for part in split3(picked):
            term = contract_last(part, one_hot)
            total = term if total is None else total + term
        omega_ref[8 * probe : 8 * (probe + 1), :] = total
    for high in range(8):
        piece = omega_ref[pl.ds(high, 16, stride=8), :]
        for part_index, part in enumerate(split3(piece)):
            split_ref[
                16 * part_index : 16 * (part_index + 1), 128 * high : 128 * (high + 1)
            ] = part
    for which in range(2):
        triple = dot(split_ref[...], weight_ref[4 * which + quarter])
        payload_ref[16 * which : 16 * (which + 1), :] = triple[:16] + triple[16:32] + triple[32:]
    for store in stores:
        store.wait()


def flipped(two_bits, flip):
    low_bit = lax.rem(two_bits + flip % 2, 2)
    return low_bit + 2 * lax.rem(two_bits // 2 + flip // 2, 2)


def shuffle_tokens(zone, side, tok_ref, tokens_ref):
    shuffle = shuffle_matrix(256)
    for source in range(4):
        spot = flipped(zone, source)
        for group in range(8):
            piece = tok_ref[spot, :, 256 * group : 256 * (group + 1)]
            moved = dot(piece, shuffle).astype(BF)
            half = lax.rem(group // 4 + side, 2)
            tokens_ref[
                half, 64 * source : 64 * (source + 1), 256 * (group % 4) : 256 * (group % 4 + 1)
            ] = moved


def first_kernel(
    place_ref,
    inv_ref,
    blocks_in_ref,
    weight_in_ref,
    tok_in_ref,
    keep_ref,
    sent_out_ref,
    near_out_ref,
    blocks_ref,
    tiles_ref,
    near_ref,
    own_ref,
    tok_ref,
    tokens_ref,
    sent_ref,
    in_sem,
    near_sem,
    sent_sem,
):
    zone = place_ref[0] // 2
    side = place_ref[2]
    core = place_ref[3]
    loads = [
        pltpu.make_async_copy(blocks_in_ref, blocks_ref, in_sem.at[0]),
        pltpu.make_async_copy(tok_in_ref, tok_ref, in_sem.at[1]),
        pltpu.make_async_copy(weight_in_ref.at[pl.ds(4 * core, 4)], own_ref, in_sem.at[2]),
    ]
    for load in loads:
        load.start()
    clear_empty_slot(tiles_ref)
    loads[0].wait()
    stage_blocks(blocks_ref, tiles_ref, 0)

    def put(pair, row, piece):
        lane = (pair % 2) * 128
        near_ref[pair // 2, pl.ds(row, 32), lane : lane + 128] = piece

    assemble_columns(inv_ref, core, tiles_ref, put)
    near_store = pltpu.make_async_copy(near_ref, near_out_ref, near_sem)
    near_store.start()
    loads[1].wait()
    shuffle_tokens(zone, side, tok_ref, tokens_ref)
    loads[2].wait()
    stores = []
    for chunk in range(4):
        total = dot(tokens_ref[0], own_ref[chunk]) + dot(tokens_ref[1], near_ref[chunk])
        cols = slice(256 * chunk, 256 * (chunk + 1))
        keep_ref[:, cols] = total[:64]
        for flip in range(4):
            sent_ref[flipped(zone, flip), :, cols] = total[64 * flip : 64 * (flip + 1)].astype(BF)
        lanes = pl.ds(256 * chunk, 256)
        store = pltpu.make_async_copy(
            sent_ref.at[:, :, lanes], sent_out_ref.at[:, :, lanes], sent_sem.at[chunk]
        )
        store.start()
        stores.append(store)
    for store in stores:
        store.wait()
    near_store.wait()


def second_kernel(
    place_ref,
    near_in_ref,
    weight_in_ref,
    tok_in_ref,
    keep_ref,
    out1_ref,
    out2_ref,
    out3_ref,
    near_ref,
    own_ref,
    tok_ref,
    tokens_ref,
    in_sem,
):
    zone = place_ref[0] // 2
    side = place_ref[2]
    core = place_ref[3]
    loads = [
        pltpu.make_async_copy(tok_in_ref, tok_ref, in_sem.at[0]),
        pltpu.make_async_copy(weight_in_ref.at[pl.ds(4 - 4 * core, 4)], own_ref, in_sem.at[1]),
        pltpu.make_async_copy(near_in_ref, near_ref, in_sem.at[2]),
    ]
    for load in loads:
        load.start()
    loads[0].wait()
    shuffle_tokens(zone, side, tok_ref, tokens_ref)
    loads[1].wait()
    loads[2].wait()
    for chunk in range(4):
        total = dot(tokens_ref[0], own_ref[chunk]) + dot(tokens_ref[1], near_ref[chunk])
        cols = slice(256 * chunk, 256 * (chunk + 1))
        keep_ref[:, cols] = total[:64]
        for flip, ref in enumerate((out1_ref, out2_ref, out3_ref), 1):
            ref[:, cols] = total[64 * flip : 64 * (flip + 1)].astype(BF)


def middle_kernel(
    place_ref,
    first_keep_ref,
    first_ref,
    second_keep_ref,
    second1_ref,
    second2_ref,
    second3_ref,
    pay0_ref,
    pay1_ref,
    pay2_ref,
    pay3_ref,
    mine_ref,
    theirs_ref,
    lead_ref,
    act_ref,
    pay_ref,
    proj_ref,
    tangent_ref,
    rows_ref,
):
    zone = place_ref[0] // 2
    quarter = place_ref[1]
    core = place_ref[3]
    unshuffle = unshuffle_matrix(256)
    for flip, ref in enumerate((pay0_ref, pay1_ref, pay2_ref, pay3_ref)):
        pay_ref[flipped(quarter, flip)] = ref[...]
    for chunk in range(4):
        cols = slice(256 * chunk, 256 * (chunk + 1))
        proj_ref[:, cols] = dot(pay_ref[chunk, 32:64, :].astype(BF), unshuffle).astype(BF)
        first = first_keep_ref[:, cols]
        for flip in (1, 2, 3):
            first = first + first_ref[flipped(zone, flip), :, cols].astype(F32)
        second = second_keep_ref[:, cols]
        for ref in (second1_ref, second2_ref, second3_ref):
            second = second + ref[:, cols].astype(F32)
        gate_pre = jnp.where(core == 0, first, second)
        up_pre = jnp.where(core == 0, second, first)
        sigmoid_g = jax.nn.sigmoid(gate_pre)
        activated = gate_pre * sigmoid_g
        slope_g = sigmoid_g * (1.0 + gate_pre * (1.0 - sigmoid_g))
        lead = slope_g * up_pre
        lead_ref[:, cols] = lead
        act_ref[:, cols] = activated
        for probe in range(P_SIZE):
            probe_gate = pay_ref[chunk, probe : probe + 1, :]
            probe_up = pay_ref[chunk, 16 + probe : 17 + probe, :]
            tangent_ref[64 * probe : 64 * (probe + 1), cols] = (
                lead * probe_gate + activated * probe_up
            ).astype(BF)
    rows_ref[...] = contract_last(tangent_ref[...], proj_ref[...]).astype(BF)
    for step in range(P_SIZE):
        probe = lax.rem(step + 8 * core, P_SIZE)
        backward = dot(rows_ref[pl.ds(pl.multiple_of(probe * 64, 64), 64), :], proj_ref[...])
        target = mine_ref if step < 8 else theirs_ref
        row = slice(step % 8, step % 8 + 1)
        target[row, :1024] = jnp.sum(backward * lead_ref[...], axis=0, keepdims=True)
        target[row, 1024:] = jnp.sum(backward * act_ref[...], axis=0, keepdims=True)


def product_kernel(place_ref, mine_ref, theirs_ref, weight_ref, out_ref, sum_ref, held_ref, sem):
    core = place_ref[3]
    loads = [
        pltpu.make_async_copy(weight_ref.at[chunk], held_ref.at[chunk], sem.at[chunk])
        for chunk in range(8)
    ]
    for load in loads:
        load.start()
    sum_ref[core] = mine_ref[...]
    sum_ref[1 - core] = theirs_ref[...]
    sums = jnp.concatenate([sum_ref[0], sum_ref[1]], axis=0).astype(BF)
    total = None
    for chunk in range(8):
        loads[chunk].wait()
        term = contract_last(sums[:, 256 * chunk : 256 * (chunk + 1)], held_ref[chunk])
        total = term if total is None else total + term
    unshuffle = unshuffle_matrix(256)
    for group in range(4):
        cols = slice(256 * group, 256 * (group + 1))
        high, mid, low = split3(total[:, cols])
        out_ref[:, cols] = dot(high, unshuffle) + dot(mid, unshuffle) + dot(low, unshuffle)


def pair_split(
    tokens,
    gate_blocks,
    gate_slot,
    up_blocks,
    up_slot,
    down_blocks,
    down_slot,
    sketch,
    probe_index,
    probe_value,
):
    owner = lax.axis_index("fsdp")
    core = lax.axis_index("seq")
    group = lax.axis_index("groups")
    place = jnp.stack([owner, 2 * group + core, owner % 2, core]).astype(jnp.int32)

    def owner_flip(value, bits):
        return lax.ppermute(value, "fsdp", [(i, i ^ bits) for i in range(8)])

    def core_flip(value):
        return lax.ppermute(value, "seq", [(0, 1), (1, 0)])

    def zone_exchange(value):
        return lax.all_to_all(
            value,
            "fsdp",
            split_axis=0,
            concat_axis=0,
            tiled=True,
            axis_index_groups=[[0, 2, 4, 6], [1, 3, 5, 7]],
        )

    by_zone = tokens.reshape(64, 4, 2048).transpose(1, 0, 2)
    by_zone, gate_source, up_source = lax.optimization_barrier((by_zone, gate_blocks, up_blocks))
    gathered = zone_exchange(by_zone)
    near = owner_flip(jnp.where(core == 0, gate_source, up_source), 1)

    slots = jnp.stack([gate_slot, up_slot, down_slot])
    cells = lax.broadcasted_iota(jnp.int32, (3, 160, 256), 2)
    slot_numbers = lax.broadcasted_iota(jnp.int32, (3, 160, 256), 1)
    inv = jnp.min(jnp.where(slots[:, :, None] == cells, slot_numbers, 160), axis=1)
    near_inv = owner_flip(inv, 1)

    weights, payload = pl.pallas_call(
        own_kernel,
        out_shape=(
            jax.ShapeDtypeStruct((8, 1024, 256), BF),
            jax.ShapeDtypeStruct((64, 256), F32),
        ),
        in_specs=[SMEM, SMEM] + [HBM] * 3 + [VMEM] * 3,
        out_specs=(HBM, VMEM),
        scratch_shapes=[
            pltpu.VMEM((32 * STRIDE, 128), F32),
            pltpu.VMEM((128, 128), F32),
            pltpu.VMEM((48, 1024), BF),
            pltpu.VMEM((256, 1024), BF),
            pltpu.VMEM((3, 160, 4096), BF),
            pltpu.VMEM((8, 1024, 256), BF),
            pltpu.SemaphoreType.DMA((3,)),
            pltpu.SemaphoreType.DMA((2,)),
        ],
        compiler_params=params(60),
        name="own_blocks",
    )(place, inv, gate_blocks, up_blocks, down_blocks, sketch, probe_index, probe_value)

    for bits in (2, 4):
        payload = payload + owner_flip(payload, bits)
    near, near_inv, payload, gathered = lax.optimization_barrier(
        (near, near_inv, payload, gathered)
    )
    payload = payload + owner_flip(payload, 1)
    pay_parts = [
        payload,
        core_flip(payload),
        lax.ppermute(payload, "groups", [(0, 1), (1, 0)]),
        lax.ppermute(payload, ("groups", "seq"), [(i, i ^ 3) for i in range(4)]),
    ]

    first_keep, first_sent, near_weights = pl.pallas_call(
        first_kernel,
        out_shape=(
            jax.ShapeDtypeStruct((64, 1024), F32),
            jax.ShapeDtypeStruct((4, 64, 1024), BF),
            jax.ShapeDtypeStruct((4, 1024, 256), BF),
        ),
        in_specs=[SMEM, SMEM, HBM, HBM, HBM],
        out_specs=(VMEM, HBM, HBM),
        scratch_shapes=[
            pltpu.VMEM((160, 4096), BF),
            pltpu.VMEM((32 * STRIDE, 128), F32),
            pltpu.VMEM((4, 1024, 256), BF),
            pltpu.VMEM((4, 1024, 256), BF),
            pltpu.VMEM((4, 64, 2048), BF),
            pltpu.VMEM((2, 256, 1024), BF),
            pltpu.VMEM((4, 64, 1024), BF),
            pltpu.SemaphoreType.DMA((3,)),
            pltpu.SemaphoreType.DMA,
            pltpu.SemaphoreType.DMA((4,)),
        ],
        compiler_params=params(60),
        name="first_partial",
    )(place, near_inv, near, weights, gathered)
    first_back = zone_exchange(first_sent)

    second_keep, *second_sent = pl.pallas_call(
        second_kernel,
        out_shape=(jax.ShapeDtypeStruct((64, 1024), F32),)
        + (jax.ShapeDtypeStruct((64, 1024), BF),) * 3,
        in_specs=[SMEM, HBM, HBM, HBM],
        out_specs=(VMEM,) * 4,
        scratch_shapes=[
            pltpu.VMEM((4, 1024, 256), BF),
            pltpu.VMEM((4, 1024, 256), BF),
            pltpu.VMEM((4, 64, 2048), BF),
            pltpu.VMEM((2, 256, 1024), BF),
            pltpu.SemaphoreType.DMA((3,)),
        ],
        compiler_params=params(59),
        name="second_partial",
    )(place, core_flip(near_weights), weights, gathered)
    second_back = [owner_flip(second_sent[flip - 1], 2 * flip) for flip in (1, 2, 3)]

    mine, theirs = pl.pallas_call(
        middle_kernel,
        out_shape=(jax.ShapeDtypeStruct((8, 2048), F32),) * 2,
        in_specs=[SMEM] + [VMEM] * 10,
        out_specs=(VMEM, VMEM),
        scratch_shapes=[
            pltpu.VMEM((64, 1024), F32),
            pltpu.VMEM((64, 1024), F32),
            pltpu.VMEM((4, 64, 256), F32),
            pltpu.VMEM((K, 1024), BF),
            pltpu.VMEM((64 * P_SIZE, 1024), BF),
            pltpu.VMEM((64 * P_SIZE, K), BF),
        ],
        compiler_params=params(16),
        name="token_sums",
    )(place, first_keep, first_back, second_keep, *second_back, *pay_parts)

    sums = mine + core_flip(theirs)
    for bits in (1, 2, 4):
        sums = sums + owner_flip(sums, bits)

    return pl.pallas_call(
        product_kernel,
        out_shape=jax.ShapeDtypeStruct((P_SIZE, 1024), F32),
        in_specs=[SMEM, VMEM, VMEM, HBM],
        out_specs=VMEM,
        scratch_shapes=[
            pltpu.VMEM((2, 8, 2048), F32),
            pltpu.VMEM((8, 1024, 256), BF),
            pltpu.SemaphoreType.DMA((8,)),
        ],
        compiler_params=params(59),
        name="products",
    )(place, sums, core_flip(sums), weights)


def per_device(tokens, gate_blocks, *rest):
    fits = (
        lax.axis_size("fsdp") == 8
        and lax.axis_size("seq") == 2
        and lax.axis_size("groups") == 2
        and tokens.shape == (64, 8192)
        and gate_blocks.shape == (160, 4096)
        and rest[-2].shape == (P_SIZE, 256)
    )
    return (pair_split if fits else hidden_split)(tokens, gate_blocks, *rest)


def solution(mesh):
    in_specs = (
        P(("groups", "fsdp", "seq"), None),
        P("fsdp", None),
        P("fsdp"),
        P("fsdp", None),
        P("fsdp"),
        P("fsdp", None),
        P("fsdp"),
        P(None, "fsdp"),
        P(),
        P(),
    )
    out_specs = P("groups", "fsdp")
    return jax.shard_map(
        per_device, mesh=mesh, in_specs=in_specs, out_specs=out_specs, check_vma=False
    )
```

```python
import functools

import jax
import jax.numpy as jnp
from jax import lax
from jax.experimental import pallas as pl
from jax.experimental.pallas import tpu as pltpu
from jax.sharding import PartitionSpec as P

HID_DEV = 128
BLK = 64
P_SIZE = 16
K = 32

BF = jnp.bfloat16
F32 = jnp.float32
VMEM = pl.BlockSpec(memory_space=pltpu.VMEM)
SMEM = pl.BlockSpec(memory_space=pltpu.SMEM)
HBM = pl.BlockSpec(memory_space=pltpu.HBM)
ANY = pl.BlockSpec(memory_space=pl.ANY)

STRIDE = 168


def params(mebibytes):
    return pltpu.CompilerParams(vmem_limit_bytes=int(mebibytes * 1024 * 1024))


def unpack(blocks, slot_ids, cell_total):
    holder = jnp.zeros((cell_total + 1, blocks.shape[1]), blocks.dtype)
    return holder.at[slot_ids].set(blocks)[:cell_total]


def contract_last(first_mat, second_mat):
    return lax.dot_general(
        first_mat, second_mat, (((1,), (1,)), ((), ())), preferred_element_type=jnp.float32
    )


def hidden_split(
    tokens,
    gate_blocks,
    gate_slot,
    up_blocks,
    up_slot,
    down_blocks,
    down_slot,
    sketch,
    probe_index,
    probe_value,
):
    owners = lax.axis_size("fsdp")
    model_width = tokens.shape[1]
    local_width = model_width // owners
    block_rows = local_width // BLK
    hidden = HID_DEV
    col_blocks = hidden * owners // BLK
    cell_total = block_rows * col_blocks
    gate_dense = unpack(gate_blocks, gate_slot, cell_total).reshape(
        block_rows, col_blocks, BLK, BLK
    )
    up_dense = unpack(up_blocks, up_slot, cell_total).reshape(block_rows, col_blocks, BLK, BLK)
    stacked = jnp.stack([gate_dense, up_dense], axis=1)
    stacked = stacked.reshape(block_rows, 2, owners, hidden // BLK, BLK, BLK)
    stacked = stacked.transpose(0, 4, 2, 1, 3, 5).reshape(local_width, owners * 2 * hidden)
    both_weights = lax.all_to_all(stacked, "fsdp", split_axis=1, concat_axis=0, tiled=True)
    picked = both_weights[probe_index].astype(jnp.float32)
    probe_both = jnp.sum(picked * probe_value[:, :, None], axis=1)
    preact = jnp.dot(
        lax.all_gather(tokens, "fsdp", axis=0, tiled=True),
        both_weights,
        preferred_element_type=jnp.float32,
    )
    row_count = preact.shape[0]
    gate_pre = preact[:, :hidden]
    up_pre = preact[:, hidden:]
    down_dense = unpack(down_blocks, down_slot, cell_total).reshape(
        col_blocks, block_rows, BLK, BLK
    )
    down_dense = down_dense.transpose(0, 2, 1, 3).reshape(col_blocks * BLK, local_width)
    down_rows = lax.all_to_all(down_dense, "fsdp", split_axis=0, concat_axis=1, tiled=True)
    full_sketch = lax.all_gather(sketch, "fsdp", axis=1, tiled=True)
    projected = contract_last(down_rows, full_sketch)
    projected = projected.astype(jnp.bfloat16)
    sigmoid_g = jax.nn.sigmoid(gate_pre)
    activated = gate_pre * sigmoid_g
    slope_g = sigmoid_g * (1.0 + gate_pre * (1.0 - sigmoid_g))
    lead_term = slope_g * up_pre
    tangent = (
        lead_term[:, None, :] * probe_both[None, :, :hidden]
        + activated[:, None, :] * probe_both[None, :, hidden:]
    )
    tangent = tangent.astype(jnp.bfloat16)
    partial_sketch = jnp.dot(
        tangent.reshape(row_count * P_SIZE, hidden), projected, preferred_element_type=jnp.float32
    )
    partial_sketch = partial_sketch.reshape(row_count, P_SIZE * K)
    sketch_rows = lax.psum(partial_sketch, "fsdp").astype(jnp.bfloat16)
    backward = contract_last(sketch_rows.reshape(row_count * P_SIZE, K), projected).reshape(
        row_count, P_SIZE, hidden
    )
    summed = jnp.concatenate(
        [
            jnp.sum(backward * lead_term[:, None, :], axis=0),
            jnp.sum(backward * activated[:, None, :], axis=0),
        ],
        axis=1,
    )
    summed = lax.psum(summed, "seq").astype(jnp.bfloat16)
    products = contract_last(summed, both_weights)
    return lax.psum_scatter(products, "fsdp", scatter_dimension=1, tiled=True)


def dot(a, b):
    return jnp.dot(a, b, preferred_element_type=F32)


def split3(value):
    high = value.astype(BF)
    rest = value - high.astype(F32)
    mid = rest.astype(BF)
    low = (rest - mid.astype(F32)).astype(BF)
    return high, mid, low


def shuffled(natural):
    return (natural // BLK) * BLK + (natural % 2) * (BLK // 2) + (natural % BLK) // 2


def shuffle_matrix(size):
    rows = lax.broadcasted_iota(jnp.int32, (size, size), 0)
    cols = lax.broadcasted_iota(jnp.int32, (size, size), 1)
    return jnp.where(shuffled(rows) == cols, 1.0, 0.0).astype(BF)


def unshuffle_matrix(size):
    rows = lax.broadcasted_iota(jnp.int32, (size, size), 0)
    cols = lax.broadcasted_iota(jnp.int32, (size, size), 1)
    return jnp.where(shuffled(cols) == rows, 1.0, 0.0).astype(BF)


def stage_blocks(blocks_ref, tiles_ref, first_slot):
    @pl.loop(0, blocks_ref.shape[0] // 16)
    def _(step):
        row = pl.multiple_of(step * 16, 16)
        target = pl.multiple_of(first_slot + row, 16)
        for chunk in range(32):
            piece = blocks_ref[pl.ds(row, 16), 128 * chunk : 128 * (chunk + 1)].astype(F32)
            tiles_ref[pl.ds(target + chunk * STRIDE, 16), :] = piece


def clear_empty_slot(tiles_ref):
    for chunk in range(32):
        tiles_ref[pl.ds(chunk * STRIDE + 160, 8), :] = jnp.zeros((8, 128), F32)


def assembled_pair(tiles_ref, left_slot, right_slot):
    left = tiles_ref[pl.ds(left_slot, 32, stride=STRIDE), :]
    right = tiles_ref[pl.ds(right_slot, 32, stride=STRIDE), :]
    low_half = lax.broadcasted_iota(jnp.int32, (32, 128), 1) < BLK
    straight = jnp.where(low_half, left, right)
    crossed = pltpu.roll(jnp.where(low_half, right, left), BLK, 1)
    even = jnp.where(low_half, straight, crossed)
    odd = jnp.where(low_half, crossed, straight)
    return even.astype(BF), odd.astype(BF)


def assemble_columns(inv_ref, inv_row, tiles_ref, put):
    @pl.loop(0, 16)
    def _(block_row):
        for pair in range(8):
            cell = block_row * 16 + 2 * pair
            even, odd = assembled_pair(
                tiles_ref, inv_ref[inv_row, cell], inv_ref[inv_row, cell + 1]
            )
            row = pl.multiple_of(block_row * BLK, BLK)
            put(pair, row, even)
            put(pair, row + BLK // 2, odd)


def head_kernel(
    place_ref, tok_in_ref, gate_ref, up_ref, zone_out_ref, kind_out_ref, tok_ref, blocks_ref, sem
):
    core = place_ref[3]

    @pl.when(core == 0)
    def _():
        pltpu.make_async_copy(gate_ref, blocks_ref, sem.at[0]).start()

    @pl.when(core != 0)
    def _():
        pltpu.make_async_copy(up_ref, blocks_ref, sem.at[0]).start()

    loads, stores = [], []
    for zone in range(4):
        held = tok_ref.at[zone]
        lanes = pl.ds(2048 * zone, 2048)
        loads.append(pltpu.make_async_copy(tok_in_ref.at[:, lanes], held, sem.at[2 + zone]))
        stores.append(pltpu.make_async_copy(held, zone_out_ref.at[zone], sem.at[6 + zone]))
    for load in loads:
        load.start()
    pltpu.make_async_copy(gate_ref, blocks_ref, sem.at[0]).wait()
    kind_store = pltpu.make_async_copy(blocks_ref, kind_out_ref, sem.at[1])
    kind_store.start()
    for load, store in zip(loads, stores):
        load.wait()
        store.start()
    for store in stores:
        store.wait()
    kind_store.wait()


def own_kernel(
    place_ref,
    inv_ref,
    gate_ref,
    up_ref,
    down_ref,
    sketch_ref,
    index_ref,
    value_ref,
    weight_out_ref,
    payload_ref,
    tiles_ref,
    omega_ref,
    split_ref,
    down_dense_ref,
    blocks_ref,
    weight_ref,
    in_sem,
    out_sem,
):
    owner = place_ref[0]
    quarter = place_ref[1]
    loads = [
        pltpu.make_async_copy(source, blocks_ref.at[i], in_sem.at[i])
        for i, source in enumerate((gate_ref, up_ref, down_ref))
    ]
    stores = [
        pltpu.make_async_copy(
            weight_ref.at[pl.ds(4 * i, 4)], weight_out_ref.at[pl.ds(4 * i, 4)], out_sem.at[i]
        )
        for i in range(2)
    ]
    for load in loads:
        load.start()
    clear_empty_slot(tiles_ref)

    for which in range(2):
        loads[which].wait()
        stage_blocks(blocks_ref.at[which], tiles_ref, 0)

        def put(pair, row, piece):
            lane = (pair % 2) * 128
            weight_ref[4 * which + pair // 2, pl.ds(row, 32), lane : lane + 128] = piece

        assemble_columns(inv_ref, which, tiles_ref, put)
        stores[which].start()

    loads[2].wait()
    stage_blocks(blocks_ref.at[2], tiles_ref, 0)
    for local_row in range(4):
        for pair in range(8):
            cell = (quarter * 4 + local_row) * 16 + 2 * pair
            even, odd = assembled_pair(tiles_ref, inv_ref[2, cell], inv_ref[2, cell + 1])
            row = local_row * BLK
            down_dense_ref[row : row + 32, 128 * pair : 128 * (pair + 1)] = even
            down_dense_ref[row + 32 : row + 64, 128 * pair : 128 * (pair + 1)] = odd
    payload_ref[32:64, :] = contract_last(sketch_ref[...], down_dense_ref[...])

    local = index_ref[...] - owner * 1024
    inside = (local >= 0) & (local < 1024)
    safe = jnp.where(inside, local, 0)
    spot = shuffled(safe)
    high_part = jnp.where(inside, spot // 128, -1)
    low_part = spot % 128
    values = value_ref[...]
    high_iota = lax.broadcasted_iota(jnp.int32, (8, 256), 0)
    low_iota = lax.broadcasted_iota(jnp.int32, (128, 256), 0)
    for probe in range(P_SIZE):
        picked = jnp.where(
            high_iota == high_part[probe : probe + 1, :], values[probe : probe + 1, :], 0.0
        )
        one_hot = jnp.where(low_iota == low_part[probe : probe + 1, :], 1.0, 0.0).astype(BF)
        total = None
        for part in split3(picked):
            term = contract_last(part, one_hot)
            total = term if total is None else total + term
        omega_ref[8 * probe : 8 * (probe + 1), :] = total
    for high in range(8):
        piece = omega_ref[pl.ds(high, 16, stride=8), :]
        for part_index, part in enumerate(split3(piece)):
            split_ref[
                16 * part_index : 16 * (part_index + 1), 128 * high : 128 * (high + 1)
            ] = part
    for which in range(2):
        triple = dot(split_ref[...], weight_ref[4 * which + quarter])
        payload_ref[16 * which : 16 * (which + 1), :] = triple[:16] + triple[16:32] + triple[32:]
    for store in stores:
        store.wait()


def flipped(two_bits, flip):
    low_bit = lax.rem(two_bits + flip % 2, 2)
    return low_bit + 2 * lax.rem(two_bits // 2 + flip // 2, 2)


def shuffle_tokens(side, tok_ref, tokens_ref):
    shuffle = shuffle_matrix(256)
    for group in range(8):
        piece = tok_ref[:, :, 256 * group : 256 * (group + 1)].reshape(256, 256)
        half = lax.rem(group // 4 + side, 2)
        tokens_ref[half, :, 256 * (group % 4) : 256 * (group % 4 + 1)] = dot(piece, shuffle).astype(
            BF
        )


def first_kernel(
    place_ref,
    inv_ref,
    blocks_in_ref,
    weight_in_ref,
    tok_in_ref,
    keep_ref,
    sent_out_ref,
    near_out_ref,
    blocks_ref,
    tiles_ref,
    near_ref,
    own_ref,
    tok_ref,
    tokens_ref,
    sent_ref,
    total_ref,
    in_sem,
    near_sem,
    sent_sem,
):
    zone = place_ref[0] // 2
    side = place_ref[2]
    core = place_ref[3]
    loads = [
        pltpu.make_async_copy(blocks_in_ref, blocks_ref, in_sem.at[0]),
        pltpu.make_async_copy(tok_in_ref, tok_ref, in_sem.at[1]),
        pltpu.make_async_copy(weight_in_ref.at[pl.ds(4 * core, 4)], own_ref, in_sem.at[2]),
    ]
    for load in loads:
        load.start()
    clear_empty_slot(tiles_ref)
    loads[0].wait()
    stage_blocks(blocks_ref, tiles_ref, 0)

    def put(pair, row, piece):
        lane = (pair % 2) * 128
        near_ref[pair // 2, pl.ds(row, 32), lane : lane + 128] = piece

    assemble_columns(inv_ref, core, tiles_ref, put)
    near_store = pltpu.make_async_copy(near_ref, near_out_ref, near_sem)
    near_store.start()
    loads[1].wait()
    shuffle_tokens(side, tok_ref, tokens_ref)
    loads[2].wait()
    stores = []
    for chunk in range(4):
        total = dot(tokens_ref[0], own_ref[chunk]) + dot(tokens_ref[1], near_ref[chunk])
        cols = slice(256 * chunk, 256 * (chunk + 1))
        total_ref[...] = total
        keep_ref[:, cols] = total_ref[pl.ds(pl.multiple_of(64 * zone, 64), 64), :]
        sent_ref[:, :, cols] = total.astype(BF).reshape(4, 64, 256)
        lanes = pl.ds(256 * chunk, 256)
        store = pltpu.make_async_copy(
            sent_ref.at[:, :, lanes], sent_out_ref.at[:, :, lanes], sent_sem.at[chunk]
        )
        store.start()
        stores.append(store)
    for store in stores:
        store.wait()
    near_store.wait()


def second_kernel(
    place_ref,
    near_in_ref,
    weight_in_ref,
    tok_in_ref,
    keep_ref,
    out1_ref,
    out2_ref,
    out3_ref,
    near_ref,
    own_ref,
    tok_ref,
    tokens_ref,
    total_ref,
    in_sem,
):
    zone = place_ref[0] // 2
    side = place_ref[2]
    core = place_ref[3]
    loads = [
        pltpu.make_async_copy(tok_in_ref, tok_ref, in_sem.at[0]),
        pltpu.make_async_copy(weight_in_ref.at[pl.ds(4 - 4 * core, 4)], own_ref, in_sem.at[1]),
        pltpu.make_async_copy(near_in_ref, near_ref, in_sem.at[2]),
    ]
    for load in loads:
        load.start()
    loads[0].wait()
    shuffle_tokens(side, tok_ref, tokens_ref)
    loads[1].wait()
    loads[2].wait()
    for chunk in range(4):
        total = dot(tokens_ref[0], own_ref[chunk]) + dot(tokens_ref[1], near_ref[chunk])
        cols = slice(256 * chunk, 256 * (chunk + 1))
        total_ref[...] = total
        keep_ref[:, cols] = total_ref[pl.ds(pl.multiple_of(64 * zone, 64), 64), :]
        for flip, ref in enumerate((out1_ref, out2_ref, out3_ref), 1):
            row = pl.multiple_of(64 * flipped(zone, flip), 64)
            ref[:, cols] = total_ref[pl.ds(row, 64), :].astype(BF)


def middle_kernel(
    place_ref,
    first_keep_ref,
    first_ref,
    second_keep_ref,
    second1_ref,
    second2_ref,
    second3_ref,
    pay0_ref,
    pay1_ref,
    pay2_ref,
    pay3_ref,
    weight_in_ref,
    mine_ref,
    theirs_ref,
    weight_out_ref,
    lead_ref,
    act_ref,
    pay_ref,
    proj_ref,
    tangent_ref,
    rows_ref,
    weight_sem,
):
    weight_copy = pltpu.make_async_copy(weight_in_ref, weight_out_ref, weight_sem)
    weight_copy.start()
    zone = place_ref[0] // 2
    quarter = place_ref[1]
    core = place_ref[3]
    unshuffle = unshuffle_matrix(256)
    for flip, ref in enumerate((pay0_ref, pay1_ref, pay2_ref, pay3_ref)):
        pay_ref[flipped(quarter, flip)] = ref[...]
    for chunk in range(4):
        cols = slice(256 * chunk, 256 * (chunk + 1))
        proj_ref[:, cols] = dot(pay_ref[chunk, 32:64, :].astype(BF), unshuffle).astype(BF)
        first = first_keep_ref[:, cols]
        for flip in (1, 2, 3):
            first = first + first_ref[flipped(zone, flip), :, cols].astype(F32)
        second = second_keep_ref[:, cols]
        for ref in (second1_ref, second2_ref, second3_ref):
            second = second + ref[:, cols].astype(F32)
        gate_pre = jnp.where(core == 0, first, second)
        up_pre = jnp.where(core == 0, second, first)
        sigmoid_g = jax.nn.sigmoid(gate_pre)
        activated = gate_pre * sigmoid_g
        slope_g = sigmoid_g * (1.0 + gate_pre * (1.0 - sigmoid_g))
        lead = slope_g * up_pre
        lead_ref[:, cols] = lead
        act_ref[:, cols] = activated
        for probe in range(P_SIZE):
            probe_gate = pay_ref[chunk, probe : probe + 1, :]
            probe_up = pay_ref[chunk, 16 + probe : 17 + probe, :]
            tangent_ref[64 * probe : 64 * (probe + 1), cols] = (
                lead * probe_gate + activated * probe_up
            ).astype(BF)
    rows_ref[...] = contract_last(tangent_ref[...], proj_ref[...]).astype(BF)
    for step in range(P_SIZE):
        probe = lax.rem(step + 8 * core, P_SIZE)
        backward = dot(rows_ref[pl.ds(pl.multiple_of(probe * 64, 64), 64), :], proj_ref[...])
        target = mine_ref if step < 8 else theirs_ref
        row = slice(step % 8, step % 8 + 1)
        target[row, :1024] = jnp.sum(backward * lead_ref[...], axis=0, keepdims=True)
        target[row, 1024:] = jnp.sum(backward * act_ref[...], axis=0, keepdims=True)
    weight_copy.wait()


def product_kernel(place_ref, mine_ref, theirs_ref, weight_ref, out_ref, sum_ref):
    core = place_ref[3]
    sum_ref[core] = mine_ref[...]
    sum_ref[1 - core] = theirs_ref[...]
    sums = jnp.concatenate([sum_ref[0], sum_ref[1]], axis=0).astype(BF)
    total = None
    for chunk in range(8):
        term = contract_last(sums[:, 256 * chunk : 256 * (chunk + 1)], weight_ref[chunk])
        total = term if total is None else total + term
    unshuffle = unshuffle_matrix(256)
    for group in range(4):
        cols = slice(256 * group, 256 * (group + 1))
        high, mid, low = split3(total[:, cols])
        out_ref[:, cols] = dot(high, unshuffle) + dot(mid, unshuffle) + dot(low, unshuffle)


def pair_split(
    tokens,
    gate_blocks,
    gate_slot,
    up_blocks,
    up_slot,
    down_blocks,
    down_slot,
    sketch,
    probe_index,
    probe_value,
):
    owner = lax.axis_index("fsdp")
    core = lax.axis_index("seq")
    group = lax.axis_index("groups")
    place = jnp.stack([owner, 2 * group + core, owner % 2, core]).astype(jnp.int32)

    def owner_flip(value, bits):
        return lax.ppermute(value, "fsdp", [(i, i ^ bits) for i in range(8)])

    def core_flip(value):
        return lax.ppermute(value, "seq", [(0, 1), (1, 0)])

    def zone_exchange(value):
        return lax.all_to_all(
            value,
            "fsdp",
            split_axis=0,
            concat_axis=0,
            tiled=True,
            axis_index_groups=[[0, 2, 4, 6], [1, 3, 5, 7]],
        )

    by_zone, kind = pl.pallas_call(
        head_kernel,
        out_shape=(
            jax.ShapeDtypeStruct((4, 64, 2048), BF),
            jax.ShapeDtypeStruct((160, 4096), BF),
        ),
        in_specs=[SMEM, HBM, HBM, HBM],
        out_specs=(HBM, HBM),
        scratch_shapes=[
            pltpu.VMEM((4, 64, 2048), BF),
            pltpu.VMEM((160, 4096), BF),
            pltpu.SemaphoreType.DMA((10,)),
        ],
        compiler_params=params(60),
        name="head",
    )(place, tokens, gate_blocks, up_blocks)
    near = owner_flip(kind, 1)
    gathered = zone_exchange(by_zone)

    slots = jnp.stack([gate_slot, up_slot, down_slot])
    cells = lax.broadcasted_iota(jnp.int32, (3, 160, 256), 2)
    slot_numbers = lax.broadcasted_iota(jnp.int32, (3, 160, 256), 1)
    inv = jnp.min(jnp.where(slots[:, :, None] == cells, slot_numbers, 160), axis=1)
    near_inv = owner_flip(inv, 1)

    weights, payload = pl.pallas_call(
        own_kernel,
        out_shape=(
            jax.ShapeDtypeStruct((8, 1024, 256), BF),
            jax.ShapeDtypeStruct((64, 256), F32),
        ),
        in_specs=[SMEM, SMEM] + [HBM] * 3 + [VMEM] * 3,
        out_specs=(HBM, VMEM),
        scratch_shapes=[
            pltpu.VMEM((32 * STRIDE, 128), F32),
            pltpu.VMEM((128, 128), F32),
            pltpu.VMEM((48, 1024), BF),
            pltpu.VMEM((256, 1024), BF),
            pltpu.VMEM((3, 160, 4096), BF),
            pltpu.VMEM((8, 1024, 256), BF),
            pltpu.SemaphoreType.DMA((3,)),
            pltpu.SemaphoreType.DMA((2,)),
        ],
        compiler_params=params(60),
        name="own_blocks",
    )(place, inv, gate_blocks, up_blocks, down_blocks, sketch, probe_index, probe_value)

    for bits in (2, 4):
        payload = payload + owner_flip(payload, bits)
    near, near_inv, payload, gathered = lax.optimization_barrier(
        (near, near_inv, payload, gathered)
    )
    first_keep, first_sent, near_weights = pl.pallas_call(
        first_kernel,
        out_shape=(
            jax.ShapeDtypeStruct((64, 1024), F32),
            jax.ShapeDtypeStruct((4, 64, 1024), BF),
            jax.ShapeDtypeStruct((4, 1024, 256), BF),
        ),
        in_specs=[SMEM, SMEM, ANY, HBM, ANY],
        out_specs=(VMEM, HBM, HBM),
        scratch_shapes=[
            pltpu.VMEM((160, 4096), BF),
            pltpu.VMEM((32 * STRIDE, 128), F32),
            pltpu.VMEM((4, 1024, 256), BF),
            pltpu.VMEM((4, 1024, 256), BF),
            pltpu.VMEM((4, 64, 2048), BF),
            pltpu.VMEM((2, 256, 1024), BF),
            pltpu.VMEM((4, 64, 1024), BF),
            pltpu.VMEM((256, 256), F32),
            pltpu.SemaphoreType.DMA((3,)),
            pltpu.SemaphoreType.DMA,
            pltpu.SemaphoreType.DMA((4,)),
        ],
        compiler_params=params(50),
        name="first_partial",
    )(place, near_inv, near, weights, gathered)
    first_back = zone_exchange(first_sent)

    second_keep, *second_sent = pl.pallas_call(
        second_kernel,
        out_shape=(jax.ShapeDtypeStruct((64, 1024), F32),)
        + (jax.ShapeDtypeStruct((64, 1024), BF),) * 3,
        in_specs=[SMEM, ANY, HBM, ANY],
        out_specs=(VMEM,) * 4,
        scratch_shapes=[
            pltpu.VMEM((4, 1024, 256), BF),
            pltpu.VMEM((4, 1024, 256), BF),
            pltpu.VMEM((4, 64, 2048), BF),
            pltpu.VMEM((2, 256, 1024), BF),
            pltpu.VMEM((256, 256), F32),
            pltpu.SemaphoreType.DMA((3,)),
        ],
        compiler_params=params(50),
        name="second_partial",
    )(place, core_flip(near_weights), weights, gathered)
    second_back = [owner_flip(second_sent[flip - 1], 2 * flip) for flip in (1, 2, 3)]

    second_back[0], payload = lax.optimization_barrier((second_back[0], payload))
    payload = payload + owner_flip(payload, 1)
    pay_parts = [
        payload,
        core_flip(payload),
        lax.ppermute(payload, "groups", [(0, 1), (1, 0)]),
        lax.ppermute(payload, ("groups", "seq"), [(i, i ^ 3) for i in range(4)]),
    ]

    mine, theirs, weights_at_hand = pl.pallas_call(
        middle_kernel,
        out_shape=(jax.ShapeDtypeStruct((8, 2048), F32),) * 2
        + (jax.ShapeDtypeStruct((8, 1024, 256), BF),),
        in_specs=[SMEM] + [VMEM] * 10 + [HBM],
        out_specs=(VMEM,) * 3,
        scratch_shapes=[
            pltpu.VMEM((64, 1024), F32),
            pltpu.VMEM((64, 1024), F32),
            pltpu.VMEM((4, 64, 256), F32),
            pltpu.VMEM((K, 1024), BF),
            pltpu.VMEM((64 * P_SIZE, 1024), BF),
            pltpu.VMEM((64 * P_SIZE, K), BF),
            pltpu.SemaphoreType.DMA,
        ],
        compiler_params=params(48),
        name="token_sums",
    )(place, first_keep, first_back, second_keep, *second_back, *pay_parts, weights)

    sums = mine + core_flip(theirs)
    for bits in (1, 2, 4):
        sums = sums + owner_flip(sums, bits)

    return pl.pallas_call(
        product_kernel,
        out_shape=jax.ShapeDtypeStruct((P_SIZE, 1024), F32),
        in_specs=[SMEM, VMEM, VMEM, VMEM],
        out_specs=VMEM,
        scratch_shapes=[pltpu.VMEM((2, 8, 2048), F32)],
        compiler_params=params(30),
        name="products",
    )(place, sums, core_flip(sums), weights_at_hand)


def per_device(tokens, gate_blocks, *rest):
    fits = (
        lax.axis_size("fsdp") == 8
        and lax.axis_size("seq") == 2
        and lax.axis_size("groups") == 2
        and tokens.shape == (64, 8192)
        and gate_blocks.shape == (160, 4096)
        and rest[-2].shape == (P_SIZE, 256)
    )
    return (pair_split if fits else hidden_split)(tokens, gate_blocks, *rest)


def solution(mesh):
    in_specs = (
        P(("groups", "fsdp", "seq"), None),
        P("fsdp", None),
        P("fsdp"),
        P("fsdp", None),
        P("fsdp"),
        P("fsdp", None),
        P("fsdp"),
        P(None, "fsdp"),
        P(),
        P(),
    )
    out_specs = P("groups", "fsdp")
    return jax.shard_map(
        per_device, mesh=mesh, in_specs=in_specs, out_specs=out_specs, check_vma=False
    )
```

```python
import functools

import jax
import jax.numpy as jnp
from jax import lax
from jax.experimental import pallas as pl
from jax.experimental.pallas import tpu as pltpu
from jax.sharding import PartitionSpec as P

HID_DEV = 128
BLK = 64
P_SIZE = 16
K = 32

BF = jnp.bfloat16
F32 = jnp.float32
VMEM = pl.BlockSpec(memory_space=pltpu.VMEM)
SMEM = pl.BlockSpec(memory_space=pltpu.SMEM)
HBM = pl.BlockSpec(memory_space=pltpu.HBM)
ANY = pl.BlockSpec(memory_space=pl.ANY)

STRIDE = 168


def params(mebibytes):
    return pltpu.CompilerParams(vmem_limit_bytes=int(mebibytes * 1024 * 1024))


def unpack(blocks, slot_ids, cell_total):
    holder = jnp.zeros((cell_total + 1, blocks.shape[1]), blocks.dtype)
    return holder.at[slot_ids].set(blocks)[:cell_total]


def contract_last(first_mat, second_mat):
    return lax.dot_general(
        first_mat, second_mat, (((1,), (1,)), ((), ())), preferred_element_type=jnp.float32
    )


def hidden_split(
    tokens,
    gate_blocks,
    gate_slot,
    up_blocks,
    up_slot,
    down_blocks,
    down_slot,
    sketch,
    probe_index,
    probe_value,
):
    owners = lax.axis_size("fsdp")
    model_width = tokens.shape[1]
    local_width = model_width // owners
    block_rows = local_width // BLK
    hidden = HID_DEV
    col_blocks = hidden * owners // BLK
    cell_total = block_rows * col_blocks
    gate_dense = unpack(gate_blocks, gate_slot, cell_total).reshape(
        block_rows, col_blocks, BLK, BLK
    )
    up_dense = unpack(up_blocks, up_slot, cell_total).reshape(block_rows, col_blocks, BLK, BLK)
    stacked = jnp.stack([gate_dense, up_dense], axis=1)
    stacked = stacked.reshape(block_rows, 2, owners, hidden // BLK, BLK, BLK)
    stacked = stacked.transpose(0, 4, 2, 1, 3, 5).reshape(local_width, owners * 2 * hidden)
    both_weights = lax.all_to_all(stacked, "fsdp", split_axis=1, concat_axis=0, tiled=True)
    picked = both_weights[probe_index].astype(jnp.float32)
    probe_both = jnp.sum(picked * probe_value[:, :, None], axis=1)
    preact = jnp.dot(
        lax.all_gather(tokens, "fsdp", axis=0, tiled=True),
        both_weights,
        preferred_element_type=jnp.float32,
    )
    row_count = preact.shape[0]
    gate_pre = preact[:, :hidden]
    up_pre = preact[:, hidden:]
    down_dense = unpack(down_blocks, down_slot, cell_total).reshape(
        col_blocks, block_rows, BLK, BLK
    )
    down_dense = down_dense.transpose(0, 2, 1, 3).reshape(col_blocks * BLK, local_width)
    down_rows = lax.all_to_all(down_dense, "fsdp", split_axis=0, concat_axis=1, tiled=True)
    full_sketch = lax.all_gather(sketch, "fsdp", axis=1, tiled=True)
    projected = contract_last(down_rows, full_sketch)
    projected = projected.astype(jnp.bfloat16)
    sigmoid_g = jax.nn.sigmoid(gate_pre)
    activated = gate_pre * sigmoid_g
    slope_g = sigmoid_g * (1.0 + gate_pre * (1.0 - sigmoid_g))
    lead_term = slope_g * up_pre
    tangent = (
        lead_term[:, None, :] * probe_both[None, :, :hidden]
        + activated[:, None, :] * probe_both[None, :, hidden:]
    )
    tangent = tangent.astype(jnp.bfloat16)
    partial_sketch = jnp.dot(
        tangent.reshape(row_count * P_SIZE, hidden), projected, preferred_element_type=jnp.float32
    )
    partial_sketch = partial_sketch.reshape(row_count, P_SIZE * K)
    sketch_rows = lax.psum(partial_sketch, "fsdp").astype(jnp.bfloat16)
    backward = contract_last(sketch_rows.reshape(row_count * P_SIZE, K), projected).reshape(
        row_count, P_SIZE, hidden
    )
    summed = jnp.concatenate(
        [
            jnp.sum(backward * lead_term[:, None, :], axis=0),
            jnp.sum(backward * activated[:, None, :], axis=0),
        ],
        axis=1,
    )
    summed = lax.psum(summed, "seq").astype(jnp.bfloat16)
    products = contract_last(summed, both_weights)
    return lax.psum_scatter(products, "fsdp", scatter_dimension=1, tiled=True)


def dot(a, b):
    return jnp.dot(a, b, preferred_element_type=F32)


def split3(value):
    high = value.astype(BF)
    rest = value - high.astype(F32)
    mid = rest.astype(BF)
    low = (rest - mid.astype(F32)).astype(BF)
    return high, mid, low


def shuffled(natural):
    return (natural // BLK) * BLK + (natural % 2) * (BLK // 2) + (natural % BLK) // 2


def shuffle_matrix(size):
    rows = lax.broadcasted_iota(jnp.int32, (size, size), 0)
    cols = lax.broadcasted_iota(jnp.int32, (size, size), 1)
    return jnp.where(shuffled(rows) == cols, 1.0, 0.0).astype(BF)


def unshuffle_matrix(size):
    rows = lax.broadcasted_iota(jnp.int32, (size, size), 0)
    cols = lax.broadcasted_iota(jnp.int32, (size, size), 1)
    return jnp.where(shuffled(cols) == rows, 1.0, 0.0).astype(BF)


def stage_blocks(blocks_ref, tiles_ref, first_slot):
    @pl.loop(0, blocks_ref.shape[0] // 16)
    def _(step):
        row = pl.multiple_of(step * 16, 16)
        target = pl.multiple_of(first_slot + row, 16)
        for chunk in range(32):
            piece = blocks_ref[pl.ds(row, 16), 128 * chunk : 128 * (chunk + 1)].astype(F32)
            tiles_ref[pl.ds(target + chunk * STRIDE, 16), :] = piece


def clear_empty_slot(tiles_ref):
    for chunk in range(32):
        tiles_ref[pl.ds(chunk * STRIDE + 160, 8), :] = jnp.zeros((8, 128), F32)


def assembled_pair(tiles_ref, left_slot, right_slot):
    left = tiles_ref[pl.ds(left_slot, 32, stride=STRIDE), :]
    right = tiles_ref[pl.ds(right_slot, 32, stride=STRIDE), :]
    low_half = lax.broadcasted_iota(jnp.int32, (32, 128), 1) < BLK
    straight = jnp.where(low_half, left, right)
    crossed = pltpu.roll(jnp.where(low_half, right, left), BLK, 1)
    even = jnp.where(low_half, straight, crossed)
    odd = jnp.where(low_half, crossed, straight)
    return even.astype(BF), odd.astype(BF)


def assemble_columns(inv_ref, inv_row, tiles_ref, put):
    @pl.loop(0, 16)
    def _(block_row):
        for pair in range(8):
            cell = block_row * 16 + 2 * pair
            even, odd = assembled_pair(
                tiles_ref, inv_ref[inv_row, cell], inv_ref[inv_row, cell + 1]
            )
            row = pl.multiple_of(block_row * BLK, BLK)
            put(pair, row, even)
            put(pair, row + BLK // 2, odd)


def head_kernel(
    place_ref, tok_in_ref, gate_ref, up_ref, zone_out_ref, kind_out_ref, tok_ref, blocks_ref, sem
):
    core = place_ref[3]

    @pl.when(core == 0)
    def _():
        pltpu.make_async_copy(gate_ref, blocks_ref, sem.at[0]).start()

    @pl.when(core != 0)
    def _():
        pltpu.make_async_copy(up_ref, blocks_ref, sem.at[0]).start()

    loads, stores = [], []
    for zone in range(4):
        held = tok_ref.at[zone]
        lanes = pl.ds(2048 * zone, 2048)
        loads.append(pltpu.make_async_copy(tok_in_ref.at[:, lanes], held, sem.at[2 + zone]))
        stores.append(pltpu.make_async_copy(held, zone_out_ref.at[zone], sem.at[6 + zone]))
    for load in loads:
        load.start()
    pltpu.make_async_copy(gate_ref, blocks_ref, sem.at[0]).wait()
    kind_store = pltpu.make_async_copy(blocks_ref, kind_out_ref, sem.at[1])
    kind_store.start()
    for load, store in zip(loads, stores):
        load.wait()
        store.start()
    for store in stores:
        store.wait()
    kind_store.wait()


def own_kernel(
    place_ref,
    inv_ref,
    gate_ref,
    up_ref,
    down_ref,
    sketch_ref,
    index_ref,
    value_ref,
    weight_out_ref,
    payload_ref,
    tiles_ref,
    omega_ref,
    split_ref,
    down_dense_ref,
    blocks_ref,
    weight_ref,
    in_sem,
    out_sem,
):
    owner = place_ref[0]
    quarter = place_ref[1]
    loads = [
        pltpu.make_async_copy(source, blocks_ref.at[i], in_sem.at[i])
        for i, source in enumerate((gate_ref, up_ref, down_ref))
    ]
    stores = [
        pltpu.make_async_copy(
            weight_ref.at[pl.ds(4 * i, 4)], weight_out_ref.at[pl.ds(4 * i, 4)], out_sem.at[i]
        )
        for i in range(2)
    ]
    for load in loads:
        load.start()
    clear_empty_slot(tiles_ref)

    for which in range(2):
        loads[which].wait()
        stage_blocks(blocks_ref.at[which], tiles_ref, 0)

        def put(pair, row, piece):
            lane = (pair % 2) * 128
            weight_ref[4 * which + pair // 2, pl.ds(row, 32), lane : lane + 128] = piece

        assemble_columns(inv_ref, which, tiles_ref, put)
        stores[which].start()

    loads[2].wait()
    stage_blocks(blocks_ref.at[2], tiles_ref, 0)
    for local_row in range(4):
        for pair in range(8):
            cell = (quarter * 4 + local_row) * 16 + 2 * pair
            even, odd = assembled_pair(tiles_ref, inv_ref[2, cell], inv_ref[2, cell + 1])
            row = local_row * BLK
            down_dense_ref[row : row + 32, 128 * pair : 128 * (pair + 1)] = even
            down_dense_ref[row + 32 : row + 64, 128 * pair : 128 * (pair + 1)] = odd
    payload_ref[32:64, :] = contract_last(sketch_ref[...], down_dense_ref[...])

    local = index_ref[...] - owner * 1024
    inside = (local >= 0) & (local < 1024)
    safe = jnp.where(inside, local, 0)
    spot = shuffled(safe)
    high_part = jnp.where(inside, spot // 128, -1)
    low_part = spot % 128
    values = value_ref[...]
    high_iota = lax.broadcasted_iota(jnp.int32, (8, 256), 0)
    low_iota = lax.broadcasted_iota(jnp.int32, (128, 256), 0)
    for probe in range(P_SIZE):
        picked = jnp.where(
            high_iota == high_part[probe : probe + 1, :], values[probe : probe + 1, :], 0.0
        )
        one_hot = jnp.where(low_iota == low_part[probe : probe + 1, :], 1.0, 0.0).astype(BF)
        total = None
        for part in split3(picked):
            term = contract_last(part, one_hot)
            total = term if total is None else total + term
        omega_ref[8 * probe : 8 * (probe + 1), :] = total
    for high in range(8):
        piece = omega_ref[pl.ds(high, 16, stride=8), :]
        for part_index, part in enumerate(split3(piece)):
            split_ref[
                16 * part_index : 16 * (part_index + 1), 128 * high : 128 * (high + 1)
            ] = part
    for which in range(2):
        triple = dot(split_ref[...], weight_ref[4 * which + quarter])
        payload_ref[16 * which : 16 * (which + 1), :] = triple[:16] + triple[16:32] + triple[32:]
    for store in stores:
        store.wait()


def flipped(two_bits, flip):
    low_bit = lax.rem(two_bits + flip % 2, 2)
    return low_bit + 2 * lax.rem(two_bits // 2 + flip // 2, 2)


def shuffle_tokens(side, tok_ref, tokens_ref):
    shuffle = shuffle_matrix(256)
    for group in range(8):
        piece = tok_ref[:, :, 256 * group : 256 * (group + 1)].reshape(256, 256)
        half = lax.rem(group // 4 + side, 2)
        tokens_ref[half, :, 256 * (group % 4) : 256 * (group % 4 + 1)] = dot(piece, shuffle).astype(
            BF
        )


def first_kernel(
    place_ref,
    inv_ref,
    blocks_in_ref,
    weight_in_ref,
    tok_in_ref,
    keep_ref,
    sent_out_ref,
    near_out_ref,
    blocks_ref,
    tiles_ref,
    near_ref,
    own_ref,
    tok_ref,
    tokens_ref,
    sent_ref,
    total_ref,
    in_sem,
    near_sem,
    sent_sem,
):
    zone = place_ref[0] // 2
    side = place_ref[2]
    core = place_ref[3]
    loads = [
        pltpu.make_async_copy(blocks_in_ref, blocks_ref, in_sem.at[0]),
        pltpu.make_async_copy(tok_in_ref, tok_ref, in_sem.at[1]),
        pltpu.make_async_copy(weight_in_ref.at[pl.ds(4 * core, 4)], own_ref, in_sem.at[2]),
    ]
    for load in loads:
        load.start()
    clear_empty_slot(tiles_ref)
    loads[0].wait()
    stage_blocks(blocks_ref, tiles_ref, 0)

    def put(pair, row, piece):
        lane = (pair % 2) * 128
        near_ref[pair // 2, pl.ds(row, 32), lane : lane + 128] = piece

    assemble_columns(inv_ref, core, tiles_ref, put)
    near_store = pltpu.make_async_copy(near_ref, near_out_ref, near_sem)
    near_store.start()
    loads[1].wait()
    shuffle_tokens(side, tok_ref, tokens_ref)
    loads[2].wait()
    stores = []
    for chunk in range(4):
        total = dot(tokens_ref[0], own_ref[chunk]) + dot(tokens_ref[1], near_ref[chunk])
        cols = slice(256 * chunk, 256 * (chunk + 1))
        total_ref[...] = total
        keep_ref[:, cols] = total_ref[pl.ds(pl.multiple_of(64 * zone, 64), 64), :]
        sent_ref[:, :, cols] = total.astype(BF).reshape(4, 64, 256)
        lanes = pl.ds(256 * chunk, 256)
        store = pltpu.make_async_copy(
            sent_ref.at[:, :, lanes], sent_out_ref.at[:, :, lanes], sent_sem.at[chunk]
        )
        store.start()
        stores.append(store)
    for store in stores:
        store.wait()
    near_store.wait()


def second_kernel(
    place_ref,
    near_in_ref,
    weight_in_ref,
    tok_in_ref,
    keep_ref,
    out1_ref,
    out2_ref,
    out3_ref,
    near_ref,
    own_ref,
    tok_ref,
    tokens_ref,
    total_ref,
    in_sem,
):
    zone = place_ref[0] // 2
    side = place_ref[2]
    core = place_ref[3]
    loads = [
        pltpu.make_async_copy(tok_in_ref, tok_ref, in_sem.at[0]),
        pltpu.make_async_copy(weight_in_ref.at[pl.ds(4 - 4 * core, 4)], own_ref, in_sem.at[1]),
        pltpu.make_async_copy(near_in_ref, near_ref, in_sem.at[2]),
    ]
    for load in loads:
        load.start()
    loads[0].wait()
    shuffle_tokens(side, tok_ref, tokens_ref)
    loads[1].wait()
    loads[2].wait()
    for chunk in range(4):
        total = dot(tokens_ref[0], own_ref[chunk]) + dot(tokens_ref[1], near_ref[chunk])
        cols = slice(256 * chunk, 256 * (chunk + 1))
        total_ref[...] = total
        keep_ref[:, cols] = total_ref[pl.ds(pl.multiple_of(64 * zone, 64), 64), :]
        for flip, ref in enumerate((out1_ref, out2_ref, out3_ref), 1):
            row = pl.multiple_of(64 * flipped(zone, flip), 64)
            ref[:, cols] = total_ref[pl.ds(row, 64), :].astype(BF)


def middle_kernel(
    place_ref,
    first_keep_ref,
    first_ref,
    second_keep_ref,
    second1_ref,
    second2_ref,
    second3_ref,
    pay0_ref,
    pay1_ref,
    pay2_ref,
    pay3_ref,
    across0_ref,
    across1_ref,
    across2_ref,
    across3_ref,
    mine_ref,
    theirs_ref,
    lead_ref,
    act_ref,
    pay_ref,
    proj_ref,
    tangent_ref,
    rows_ref,
):
    zone = place_ref[0] // 2
    quarter = place_ref[1]
    core = place_ref[3]
    unshuffle = unshuffle_matrix(256)
    near_parts = (pay0_ref, pay1_ref, pay2_ref, pay3_ref)
    across_parts = (across0_ref, across1_ref, across2_ref, across3_ref)
    for flip in range(4):
        pay_ref[flipped(quarter, flip)] = near_parts[flip][...] + across_parts[flip][...]
    for chunk in range(4):
        cols = slice(256 * chunk, 256 * (chunk + 1))
        proj_ref[:, cols] = dot(pay_ref[chunk, 32:64, :].astype(BF), unshuffle).astype(BF)
        first = first_keep_ref[:, cols]
        for flip in (1, 2, 3):
            first = first + first_ref[flipped(zone, flip), :, cols].astype(F32)
        second = second_keep_ref[:, cols]
        for ref in (second1_ref, second2_ref, second3_ref):
            second = second + ref[:, cols].astype(F32)
        gate_pre = jnp.where(core == 0, first, second)
        up_pre = jnp.where(core == 0, second, first)
        sigmoid_g = jax.nn.sigmoid(gate_pre)
        activated = gate_pre * sigmoid_g
        slope_g = sigmoid_g * (1.0 + gate_pre * (1.0 - sigmoid_g))
        lead = slope_g * up_pre
        lead_ref[:, cols] = lead
        act_ref[:, cols] = activated
        for probe in range(P_SIZE):
            probe_gate = pay_ref[chunk, probe : probe + 1, :]
            probe_up = pay_ref[chunk, 16 + probe : 17 + probe, :]
            tangent_ref[64 * probe : 64 * (probe + 1), cols] = (
                lead * probe_gate + activated * probe_up
            ).astype(BF)
    rows_ref[...] = contract_last(tangent_ref[...], proj_ref[...]).astype(BF)
    for step in range(P_SIZE):
        probe = lax.rem(step + 8 * core, P_SIZE)
        backward = dot(rows_ref[pl.ds(pl.multiple_of(probe * 64, 64), 64), :], proj_ref[...])
        target = mine_ref if step < 8 else theirs_ref
        row = slice(step % 8, step % 8 + 1)
        target[row, :1024] = jnp.sum(backward * lead_ref[...], axis=0, keepdims=True)
        target[row, 1024:] = jnp.sum(backward * act_ref[...], axis=0, keepdims=True)


def fetch_kernel(weight_in_ref, weight_out_ref, sem):
    copy = pltpu.make_async_copy(weight_in_ref, weight_out_ref, sem)
    copy.start()
    copy.wait()


def product_kernel(place_ref, mine_ref, theirs_ref, weight_ref, out_ref, sum_ref):
    core = place_ref[3]
    sum_ref[core] = mine_ref[...]
    sum_ref[1 - core] = theirs_ref[...]
    sums = jnp.concatenate([sum_ref[0], sum_ref[1]], axis=0).astype(BF)
    total = None
    for chunk in range(8):
        term = contract_last(sums[:, 256 * chunk : 256 * (chunk + 1)], weight_ref[chunk])
        total = term if total is None else total + term
    unshuffle = unshuffle_matrix(256)
    for group in range(4):
        cols = slice(256 * group, 256 * (group + 1))
        high, mid, low = split3(total[:, cols])
        out_ref[:, cols] = dot(high, unshuffle) + dot(mid, unshuffle) + dot(low, unshuffle)


def pair_split(
    tokens,
    gate_blocks,
    gate_slot,
    up_blocks,
    up_slot,
    down_blocks,
    down_slot,
    sketch,
    probe_index,
    probe_value,
):
    owner = lax.axis_index("fsdp")
    core = lax.axis_index("seq")
    group = lax.axis_index("groups")
    place = jnp.stack([owner, 2 * group + core, owner % 2, core]).astype(jnp.int32)

    def owner_flip(value, bits):
        return lax.ppermute(value, "fsdp", [(i, i ^ bits) for i in range(8)])

    def core_flip(value):
        return lax.ppermute(value, "seq", [(0, 1), (1, 0)])

    def zone_exchange(value):
        return lax.all_to_all(
            value,
            "fsdp",
            split_axis=0,
            concat_axis=0,
            tiled=True,
            axis_index_groups=[[0, 2, 4, 6], [1, 3, 5, 7]],
        )

    by_zone, kind = pl.pallas_call(
        head_kernel,
        out_shape=(
            jax.ShapeDtypeStruct((4, 64, 2048), BF),
            jax.ShapeDtypeStruct((160, 4096), BF),
        ),
        in_specs=[SMEM, HBM, HBM, HBM],
        out_specs=(HBM, HBM),
        scratch_shapes=[
            pltpu.VMEM((4, 64, 2048), BF),
            pltpu.VMEM((160, 4096), BF),
            pltpu.SemaphoreType.DMA((10,)),
        ],
        compiler_params=params(60),
        name="head",
    )(place, tokens, gate_blocks, up_blocks)
    near = owner_flip(kind, 1)
    gathered = zone_exchange(by_zone)

    slots = jnp.stack([gate_slot, up_slot, down_slot])
    cells = lax.broadcasted_iota(jnp.int32, (3, 160, 256), 2)
    slot_numbers = lax.broadcasted_iota(jnp.int32, (3, 160, 256), 1)
    inv = jnp.min(jnp.where(slots[:, :, None] == cells, slot_numbers, 160), axis=1)
    near_inv = owner_flip(inv, 1)

    weights, payload = pl.pallas_call(
        own_kernel,
        out_shape=(
            jax.ShapeDtypeStruct((8, 1024, 256), BF),
            jax.ShapeDtypeStruct((64, 256), F32),
        ),
        in_specs=[SMEM, SMEM] + [HBM] * 3 + [VMEM] * 3,
        out_specs=(HBM, VMEM),
        scratch_shapes=[
            pltpu.VMEM((32 * STRIDE, 128), F32),
            pltpu.VMEM((128, 128), F32),
            pltpu.VMEM((48, 1024), BF),
            pltpu.VMEM((256, 1024), BF),
            pltpu.VMEM((3, 160, 4096), BF),
            pltpu.VMEM((8, 1024, 256), BF),
            pltpu.SemaphoreType.DMA((3,)),
            pltpu.SemaphoreType.DMA((2,)),
        ],
        compiler_params=params(60),
        name="own_blocks",
    )(place, inv, gate_blocks, up_blocks, down_blocks, sketch, probe_index, probe_value)

    from_zones = [owner_flip(payload, bits) for bits in (4, 6, 2)]
    payload = payload + from_zones[0] + from_zones[1] + from_zones[2]
    pay_parts = [
        payload,
        core_flip(payload),
        lax.ppermute(payload, "groups", [(0, 1), (1, 0)]),
        lax.ppermute(payload, ("groups", "seq"), [(i, i ^ 3) for i in range(4)]),
    ]
    near, near_inv, gathered, pay_parts = lax.optimization_barrier(
        (near, near_inv, gathered, pay_parts)
    )

    first_keep, first_sent, near_weights = pl.pallas_call(
        first_kernel,
        out_shape=(
            jax.ShapeDtypeStruct((64, 1024), F32),
            jax.ShapeDtypeStruct((4, 64, 1024), BF),
            jax.ShapeDtypeStruct((4, 1024, 256), BF),
        ),
        in_specs=[SMEM, SMEM, ANY, HBM, ANY],
        out_specs=(VMEM, HBM, HBM),
        scratch_shapes=[
            pltpu.VMEM((160, 4096), BF),
            pltpu.VMEM((32 * STRIDE, 128), F32),
            pltpu.VMEM((4, 1024, 256), BF),
            pltpu.VMEM((4, 1024, 256), BF),
            pltpu.VMEM((4, 64, 2048), BF),
            pltpu.VMEM((2, 256, 1024), BF),
            pltpu.VMEM((4, 64, 1024), BF),
            pltpu.VMEM((256, 256), F32),
            pltpu.SemaphoreType.DMA((3,)),
            pltpu.SemaphoreType.DMA,
            pltpu.SemaphoreType.DMA((4,)),
        ],
        compiler_params=params(50),
        name="first_partial",
    )(place, near_inv, near, weights, gathered)
    first_back = zone_exchange(first_sent)

    second_keep, *second_sent = pl.pallas_call(
        second_kernel,
        out_shape=(jax.ShapeDtypeStruct((64, 1024), F32),)
        + (jax.ShapeDtypeStruct((64, 1024), BF),) * 3,
        in_specs=[SMEM, ANY, HBM, ANY],
        out_specs=(VMEM,) * 4,
        scratch_shapes=[
            pltpu.VMEM((4, 1024, 256), BF),
            pltpu.VMEM((4, 1024, 256), BF),
            pltpu.VMEM((4, 64, 2048), BF),
            pltpu.VMEM((2, 256, 1024), BF),
            pltpu.VMEM((256, 256), F32),
            pltpu.SemaphoreType.DMA((3,)),
        ],
        compiler_params=params(50),
        name="second_partial",
    )(place, core_flip(near_weights), weights, gathered)
    second_back = [owner_flip(second_sent[flip - 1], 2 * flip) for flip in (1, 2, 3)]

    pay_parts = pay_parts + [owner_flip(part, 1) for part in pay_parts]

    first_back, weights = lax.optimization_barrier((first_back, weights))
    weights_at_hand = pl.pallas_call(
        fetch_kernel,
        out_shape=jax.ShapeDtypeStruct((8, 1024, 256), BF),
        in_specs=[HBM],
        out_specs=VMEM,
        scratch_shapes=[pltpu.SemaphoreType.DMA],
        compiler_params=params(48),
        name="fetch_weights",
    )(weights)
    pay_parts[0], weights_at_hand = lax.optimization_barrier((pay_parts[0], weights_at_hand))

    mine, theirs = pl.pallas_call(
        middle_kernel,
        out_shape=(jax.ShapeDtypeStruct((8, 2048), F32),) * 2,
        in_specs=[SMEM] + [VMEM] * 14,
        out_specs=(VMEM,) * 2,
        scratch_shapes=[
            pltpu.VMEM((64, 1024), F32),
            pltpu.VMEM((64, 1024), F32),
            pltpu.VMEM((4, 64, 256), F32),
            pltpu.VMEM((K, 1024), BF),
            pltpu.VMEM((64 * P_SIZE, 1024), BF),
            pltpu.VMEM((64 * P_SIZE, K), BF),
        ],
        compiler_params=params(48),
        name="token_sums",
    )(place, first_keep, first_back, second_keep, *second_back, *pay_parts)

    sums = mine + core_flip(theirs)
    for bits in (1, 2, 4):
        sums = sums + owner_flip(sums, bits)

    return pl.pallas_call(
        product_kernel,
        out_shape=jax.ShapeDtypeStruct((P_SIZE, 1024), F32),
        in_specs=[SMEM, VMEM, VMEM, VMEM],
        out_specs=VMEM,
        scratch_shapes=[pltpu.VMEM((2, 8, 2048), F32)],
        compiler_params=params(30),
        name="products",
    )(place, sums, core_flip(sums), weights_at_hand)


def per_device(tokens, gate_blocks, *rest):
    fits = (
        lax.axis_size("fsdp") == 8
        and lax.axis_size("seq") == 2
        and lax.axis_size("groups") == 2
        and tokens.shape == (64, 8192)
        and gate_blocks.shape == (160, 4096)
        and rest[-2].shape == (P_SIZE, 256)
    )
    return (pair_split if fits else hidden_split)(tokens, gate_blocks, *rest)


def solution(mesh):
    in_specs = (
        P(("groups", "fsdp", "seq"), None),
        P("fsdp", None),
        P("fsdp"),
        P("fsdp", None),
        P("fsdp"),
        P("fsdp", None),
        P("fsdp"),
        P(None, "fsdp"),
        P(),
        P(),
    )
    out_specs = P("groups", "fsdp")
    return jax.shard_map(
        per_device, mesh=mesh, in_specs=in_specs, out_specs=out_specs, check_vma=False
    )
```

```python
import functools

import jax
import jax.numpy as jnp
from jax import lax
from jax.experimental import pallas as pl
from jax.experimental.pallas import tpu as pltpu
from jax.sharding import PartitionSpec as P

HID_DEV = 128
BLK = 64
P_SIZE = 16
K = 32

BF = jnp.bfloat16
F32 = jnp.float32
VMEM = pl.BlockSpec(memory_space=pltpu.VMEM)
SMEM = pl.BlockSpec(memory_space=pltpu.SMEM)
HBM = pl.BlockSpec(memory_space=pltpu.HBM)
ANY = pl.BlockSpec(memory_space=pl.ANY)

STRIDE = 168
SHARED = 48


def params(mebibytes):
    return pltpu.CompilerParams(vmem_limit_bytes=int(mebibytes * 1024 * 1024))


def unpack(blocks, slot_ids, cell_total):
    holder = jnp.zeros((cell_total + 1, blocks.shape[1]), blocks.dtype)
    return holder.at[slot_ids].set(blocks)[:cell_total]


def contract_last(first_mat, second_mat):
    return lax.dot_general(
        first_mat, second_mat, (((1,), (1,)), ((), ())), preferred_element_type=jnp.float32
    )


def hidden_split(
    tokens,
    gate_blocks,
    gate_slot,
    up_blocks,
    up_slot,
    down_blocks,
    down_slot,
    sketch,
    probe_index,
    probe_value,
):
    owners = lax.axis_size("fsdp")
    model_width = tokens.shape[1]
    local_width = model_width // owners
    block_rows = local_width // BLK
    hidden = HID_DEV
    col_blocks = hidden * owners // BLK
    cell_total = block_rows * col_blocks
    gate_dense = unpack(gate_blocks, gate_slot, cell_total).reshape(
        block_rows, col_blocks, BLK, BLK
    )
    up_dense = unpack(up_blocks, up_slot, cell_total).reshape(block_rows, col_blocks, BLK, BLK)
    stacked = jnp.stack([gate_dense, up_dense], axis=1)
    stacked = stacked.reshape(block_rows, 2, owners, hidden // BLK, BLK, BLK)
    stacked = stacked.transpose(0, 4, 2, 1, 3, 5).reshape(local_width, owners * 2 * hidden)
    both_weights = lax.all_to_all(stacked, "fsdp", split_axis=1, concat_axis=0, tiled=True)
    picked = both_weights[probe_index].astype(jnp.float32)
    probe_both = jnp.sum(picked * probe_value[:, :, None], axis=1)
    preact = jnp.dot(
        lax.all_gather(tokens, "fsdp", axis=0, tiled=True),
        both_weights,
        preferred_element_type=jnp.float32,
    )
    row_count = preact.shape[0]
    gate_pre = preact[:, :hidden]
    up_pre = preact[:, hidden:]
    down_dense = unpack(down_blocks, down_slot, cell_total).reshape(
        col_blocks, block_rows, BLK, BLK
    )
    down_dense = down_dense.transpose(0, 2, 1, 3).reshape(col_blocks * BLK, local_width)
    down_rows = lax.all_to_all(down_dense, "fsdp", split_axis=0, concat_axis=1, tiled=True)
    full_sketch = lax.all_gather(sketch, "fsdp", axis=1, tiled=True)
    projected = contract_last(down_rows, full_sketch)
    projected = projected.astype(jnp.bfloat16)
    sigmoid_g = jax.nn.sigmoid(gate_pre)
    activated = gate_pre * sigmoid_g
    slope_g = sigmoid_g * (1.0 + gate_pre * (1.0 - sigmoid_g))
    lead_term = slope_g * up_pre
    tangent = (
        lead_term[:, None, :] * probe_both[None, :, :hidden]
        + activated[:, None, :] * probe_both[None, :, hidden:]
    )
    tangent = tangent.astype(jnp.bfloat16)
    partial_sketch = jnp.dot(
        tangent.reshape(row_count * P_SIZE, hidden), projected, preferred_element_type=jnp.float32
    )
    partial_sketch = partial_sketch.reshape(row_count, P_SIZE * K)
    sketch_rows = lax.psum(partial_sketch, "fsdp").astype(jnp.bfloat16)
    backward = contract_last(sketch_rows.reshape(row_count * P_SIZE, K), projected).reshape(
        row_count, P_SIZE, hidden
    )
    summed = jnp.concatenate(
        [
            jnp.sum(backward * lead_term[:, None, :], axis=0),
            jnp.sum(backward * activated[:, None, :], axis=0),
        ],
        axis=1,
    )
    summed = lax.psum(summed, "seq").astype(jnp.bfloat16)
    products = contract_last(summed, both_weights)
    return lax.psum_scatter(products, "fsdp", scatter_dimension=1, tiled=True)


def dot(a, b):
    return jnp.dot(a, b, preferred_element_type=F32)


def split3(value):
    high = value.astype(BF)
    rest = value - high.astype(F32)
    mid = rest.astype(BF)
    low = (rest - mid.astype(F32)).astype(BF)
    return high, mid, low


def shuffled(natural):
    return (natural // BLK) * BLK + (natural % 2) * (BLK // 2) + (natural % BLK) // 2


def shuffle_matrix(size):
    rows = lax.broadcasted_iota(jnp.int32, (size, size), 0)
    cols = lax.broadcasted_iota(jnp.int32, (size, size), 1)
    return jnp.where(shuffled(rows) == cols, 1.0, 0.0).astype(BF)


def unshuffle_matrix(size):
    rows = lax.broadcasted_iota(jnp.int32, (size, size), 0)
    cols = lax.broadcasted_iota(jnp.int32, (size, size), 1)
    return jnp.where(shuffled(cols) == rows, 1.0, 0.0).astype(BF)


def stage_blocks(blocks_ref, tiles_ref, first_slot):
    @pl.loop(0, blocks_ref.shape[0] // 16)
    def _(step):
        row = pl.multiple_of(step * 16, 16)
        target = pl.multiple_of(first_slot + row, 16)
        for chunk in range(32):
            piece = blocks_ref[pl.ds(row, 16), 128 * chunk : 128 * (chunk + 1)].astype(F32)
            tiles_ref[pl.ds(target + chunk * STRIDE, 16), :] = piece


def clear_empty_slot(tiles_ref):
    for chunk in range(32):
        tiles_ref[pl.ds(chunk * STRIDE + 160, 8), :] = jnp.zeros((8, 128), F32)


def assembled_pair(tiles_ref, left_slot, right_slot):
    left = tiles_ref[pl.ds(left_slot, 32, stride=STRIDE), :]
    right = tiles_ref[pl.ds(right_slot, 32, stride=STRIDE), :]
    low_half = lax.broadcasted_iota(jnp.int32, (32, 128), 1) < BLK
    straight = jnp.where(low_half, left, right)
    crossed = pltpu.roll(jnp.where(low_half, right, left), BLK, 1)
    even = jnp.where(low_half, straight, crossed)
    odd = jnp.where(low_half, crossed, straight)
    return even.astype(BF), odd.astype(BF)


def assemble_columns(inv_ref, inv_row, tiles_ref, put, first_row=0, row_count=16):
    @pl.loop(first_row, first_row + row_count)
    def _(block_row):
        for pair in range(8):
            cell = block_row * 16 + 2 * pair
            even, odd = assembled_pair(
                tiles_ref, inv_ref[inv_row, cell], inv_ref[inv_row, cell + 1]
            )
            row = pl.multiple_of(block_row * BLK, BLK)
            put(pair, row, even)
            put(pair, row + BLK // 2, odd)


def head_kernel(
    place_ref, tok_in_ref, gate_ref, up_ref, zone_out_ref, a_out_ref, b_out_ref, tok_ref, blocks_ref, sem
):
    group = place_ref[1] // 2
    core = place_ref[3]

    @pl.when(core == 0)
    def _():
        pltpu.make_async_copy(gate_ref, blocks_ref, sem.at[0]).start()

    @pl.when(core != 0)
    def _():
        pltpu.make_async_copy(up_ref, blocks_ref, sem.at[0]).start()

    loads, stores = [], []
    for zone in range(4):
        held = tok_ref.at[zone]
        lanes = pl.ds(2048 * zone, 2048)
        loads.append(pltpu.make_async_copy(tok_in_ref.at[:, lanes], held, sem.at[3 + zone]))
        stores.append(pltpu.make_async_copy(held, zone_out_ref.at[zone], sem.at[7 + zone]))
    for load in loads:
        load.start()
    pltpu.make_async_copy(gate_ref, blocks_ref, sem.at[0]).wait()
    first = pl.multiple_of(SHARED * group, 16)
    stores.append(
        pltpu.make_async_copy(blocks_ref.at[pl.ds(first, SHARED)], a_out_ref, sem.at[1])
    )
    stores.append(
        pltpu.make_async_copy(
            blocks_ref.at[pl.ds(2 * SHARED, 160 - 2 * SHARED)], b_out_ref, sem.at[2]
        )
    )
    stores[4].start()
    stores[5].start()
    for load, store in zip(loads, stores[:4]):
        load.wait()
        store.start()
    for store in stores:
        store.wait()


def own_kernel(
    inv_ref, gate_ref, up_ref, weight_out_ref, tiles_ref, blocks_ref, weight_ref, in_sem, out_sem
):
    loads = [
        pltpu.make_async_copy(source, blocks_ref.at[i], in_sem.at[i])
        for i, source in enumerate((gate_ref, up_ref))
    ]
    for load in loads:
        load.start()
    clear_empty_slot(tiles_ref)
    stores = []
    for which in range(2):
        loads[which].wait()
        stage_blocks(blocks_ref.at[which], tiles_ref, 0)

        def put(pair, row, piece):
            lane = (pair % 2) * 128
            weight_ref[4 * which + pair // 2, pl.ds(row, 32), lane : lane + 128] = piece

        for half in range(2):
            assemble_columns(inv_ref, which, tiles_ref, put, 8 * half, 8)
            source = weight_ref.at[pl.ds(4 * which, 4), pl.ds(512 * half, 512)]
            target = weight_out_ref.at[pl.ds(4 * which, 4), pl.ds(512 * half, 512)]
            store = pltpu.make_async_copy(source, target, out_sem.at[2 * which + half])
            store.start()
            stores.append(store)
    for store in stores:
        store.wait()


def payload_kernel(
    place_ref,
    inv_ref,
    gate_ref,
    up_ref,
    down_ref,
    sketch_ref,
    index_ref,
    value_ref,
    payload_ref,
    tiles_ref,
    omega_ref,
    split_ref,
    down_dense_ref,
    blocks_ref,
    weight_ref,
    in_sem,
):
    owner = place_ref[0]
    quarter = place_ref[1]
    loads = [
        pltpu.make_async_copy(source, blocks_ref.at[i], in_sem.at[i])
        for i, source in enumerate((gate_ref, up_ref, down_ref))
    ]
    for load in loads:
        load.start()
    clear_empty_slot(tiles_ref)

    local = index_ref[...] - owner * 1024
    inside = (local >= 0) & (local < 1024)
    safe = jnp.where(inside, local, 0)
    spot = shuffled(safe)
    high_part = jnp.where(inside, spot // 128, -1)
    low_part = spot % 128
    values = value_ref[...]
    high_iota = lax.broadcasted_iota(jnp.int32, (8, 256), 0)
    low_iota = lax.broadcasted_iota(jnp.int32, (128, 256), 0)
    for probe in range(P_SIZE):
        picked = jnp.where(
            high_iota == high_part[probe : probe + 1, :], values[probe : probe + 1, :], 0.0
        )
        one_hot = jnp.where(low_iota == low_part[probe : probe + 1, :], 1.0, 0.0).astype(BF)
        total = None
        for part in split3(picked):
            term = contract_last(part, one_hot)
            total = term if total is None else total + term
        omega_ref[8 * probe : 8 * (probe + 1), :] = total
    for high in range(8):
        piece = omega_ref[pl.ds(high, 16, stride=8), :]
        for part_index, part in enumerate(split3(piece)):
            split_ref[
                16 * part_index : 16 * (part_index + 1), 128 * high : 128 * (high + 1)
            ] = part

    for which in range(2):
        loads[which].wait()
        stage_blocks(blocks_ref.at[which], tiles_ref, 0)

        @pl.loop(0, 16)
        def _(block_row):
            for pair in range(2):
                cell = block_row * 16 + 4 * quarter + 2 * pair
                even, odd = assembled_pair(
                    tiles_ref, inv_ref[which, cell], inv_ref[which, cell + 1]
                )
                row = pl.multiple_of(block_row * BLK, BLK)
                weight_ref[pl.ds(row, 32), 128 * pair : 128 * (pair + 1)] = even
                weight_ref[pl.ds(row + 32, 32), 128 * pair : 128 * (pair + 1)] = odd

        triple = dot(split_ref[...], weight_ref[...])
        payload_ref[16 * which : 16 * (which + 1), :] = triple[:16] + triple[16:32] + triple[32:]

    loads[2].wait()
    stage_blocks(blocks_ref.at[2], tiles_ref, 0)
    for local_row in range(4):
        for pair in range(8):
            cell = (quarter * 4 + local_row) * 16 + 2 * pair
            even, odd = assembled_pair(tiles_ref, inv_ref[2, cell], inv_ref[2, cell + 1])
            row = local_row * BLK
            down_dense_ref[row : row + 32, 128 * pair : 128 * (pair + 1)] = even
            down_dense_ref[row + 32 : row + 64, 128 * pair : 128 * (pair + 1)] = odd
    payload_ref[32:64, :] = contract_last(sketch_ref[...], down_dense_ref[...])


def flipped(two_bits, flip):
    low_bit = lax.rem(two_bits + flip % 2, 2)
    return low_bit + 2 * lax.rem(two_bits // 2 + flip // 2, 2)


def shuffle_tokens(side, tok_ref, tokens_ref):
    shuffle = shuffle_matrix(256)
    for group in range(8):
        piece = tok_ref[:, :, 256 * group : 256 * (group + 1)].reshape(256, 256)
        half = lax.rem(group // 4 + side, 2)
        tokens_ref[half, :, 256 * (group % 4) : 256 * (group % 4 + 1)] = dot(piece, shuffle).astype(
            BF
        )


def first_kernel(
    place_ref,
    inv_ref,
    a_in_ref,
    b_in_ref,
    a_other_ref,
    weight_in_ref,
    tok_in_ref,
    keep_ref,
    sent_out_ref,
    near_out_ref,
    blocks_ref,
    tiles_ref,
    near_ref,
    own_ref,
    tok_ref,
    tokens_ref,
    sent_ref,
    total_ref,
    in_sem,
    near_sem,
    sent_sem,
):
    zone = place_ref[0] // 2
    side = place_ref[2]
    core = place_ref[3]
    group = place_ref[1] // 2
    mine = pl.multiple_of(SHARED * group, 16)
    other = pl.multiple_of(SHARED * (1 - group), 16)
    loads = [
        pltpu.make_async_copy(a_in_ref, blocks_ref.at[pl.ds(mine, SHARED)], in_sem.at[0]),
        pltpu.make_async_copy(a_other_ref, blocks_ref.at[pl.ds(other, SHARED)], in_sem.at[1]),
        pltpu.make_async_copy(
            b_in_ref, blocks_ref.at[pl.ds(2 * SHARED, 160 - 2 * SHARED)], in_sem.at[2]
        ),
        pltpu.make_async_copy(tok_in_ref, tok_ref, in_sem.at[3]),
        pltpu.make_async_copy(weight_in_ref.at[pl.ds(4 * core, 4)], own_ref, in_sem.at[4]),
    ]
    for load in loads:
        load.start()
    clear_empty_slot(tiles_ref)
    for load in loads[:3]:
        load.wait()
    stage_blocks(blocks_ref, tiles_ref, 0)

    def put(pair, row, piece):
        lane = (pair % 2) * 128
        near_ref[pair // 2, pl.ds(row, 32), lane : lane + 128] = piece

    assemble_columns(inv_ref, core, tiles_ref, put)
    near_store = pltpu.make_async_copy(near_ref, near_out_ref, near_sem)
    near_store.start()
    loads[3].wait()
    shuffle_tokens(side, tok_ref, tokens_ref)
    loads[4].wait()
    stores = []
    for chunk in range(4):
        total = dot(tokens_ref[0], own_ref[chunk]) + dot(tokens_ref[1], near_ref[chunk])
        cols = slice(256 * chunk, 256 * (chunk + 1))
        total_ref[...] = total
        keep_ref[:, cols] = total_ref[pl.ds(pl.multiple_of(64 * zone, 64), 64), :]
        sent_ref[:, :, cols] = total.astype(BF).reshape(4, 64, 256)
        lanes = pl.ds(256 * chunk, 256)
        store = pltpu.make_async_copy(
            sent_ref.at[:, :, lanes], sent_out_ref.at[:, :, lanes], sent_sem.at[chunk]
        )
        store.start()
        stores.append(store)
    for store in stores:
        store.wait()
    near_store.wait()


def second_kernel(
    place_ref,
    near_in_ref,
    weight_in_ref,
    tok_in_ref,
    keep_ref,
    out1_ref,
    out2_ref,
    out3_ref,
    near_ref,
    own_ref,
    tok_ref,
    tokens_ref,
    total_ref,
    in_sem,
):
    zone = place_ref[0] // 2
    side = place_ref[2]
    core = place_ref[3]
    loads = [
        pltpu.make_async_copy(tok_in_ref, tok_ref, in_sem.at[0]),
        pltpu.make_async_copy(weight_in_ref.at[pl.ds(4 - 4 * core, 4)], own_ref, in_sem.at[1]),
        pltpu.make_async_copy(near_in_ref, near_ref, in_sem.at[2]),
    ]
    for load in loads:
        load.start()
    loads[0].wait()
    shuffle_tokens(side, tok_ref, tokens_ref)
    loads[1].wait()
    loads[2].wait()
    for chunk in range(4):
        total = dot(tokens_ref[0], own_ref[chunk]) + dot(tokens_ref[1], near_ref[chunk])
        cols = slice(256 * chunk, 256 * (chunk + 1))
        total_ref[...] = total
        keep_ref[:, cols] = total_ref[pl.ds(pl.multiple_of(64 * zone, 64), 64), :]
        for flip, ref in enumerate((out1_ref, out2_ref, out3_ref), 1):
            row = pl.multiple_of(64 * flipped(zone, flip), 64)
            ref[:, cols] = total_ref[pl.ds(row, 64), :].astype(BF)


def middle_kernel(
    place_ref,
    first_keep_ref,
    first_ref,
    second_keep_ref,
    second1_ref,
    second2_ref,
    second3_ref,
    pay0_ref,
    pay1_ref,
    pay2_ref,
    pay3_ref,
    mine_ref,
    theirs_ref,
    lead_ref,
    act_ref,
    pay_ref,
    proj_ref,
    tangent_ref,
    rows_ref,
):
    zone = place_ref[0] // 2
    quarter = place_ref[1]
    core = place_ref[3]
    unshuffle = unshuffle_matrix(256)
    for flip, ref in enumerate((pay0_ref, pay1_ref, pay2_ref, pay3_ref)):
        pay_ref[flipped(quarter, flip)] = ref[...]
    for chunk in range(4):
        cols = slice(256 * chunk, 256 * (chunk + 1))
        proj_ref[:, cols] = dot(pay_ref[chunk, 32:64, :].astype(BF), unshuffle).astype(BF)
        first = first_keep_ref[:, cols]
        for flip in (1, 2, 3):
            first = first + first_ref[flipped(zone, flip), :, cols].astype(F32)
        second = second_keep_ref[:, cols]
        for ref in (second1_ref, second2_ref, second3_ref):
            second = second + ref[:, cols].astype(F32)
        gate_pre = jnp.where(core == 0, first, second)
        up_pre = jnp.where(core == 0, second, first)
        sigmoid_g = jax.nn.sigmoid(gate_pre)
        activated = gate_pre * sigmoid_g
        slope_g = sigmoid_g * (1.0 + gate_pre * (1.0 - sigmoid_g))
        lead = slope_g * up_pre
        lead_ref[:, cols] = lead
        act_ref[:, cols] = activated
        for probe in range(P_SIZE):
            probe_gate = pay_ref[chunk, probe : probe + 1, :]
            probe_up = pay_ref[chunk, 16 + probe : 17 + probe, :]
            tangent_ref[64 * probe : 64 * (probe + 1), cols] = (
                lead * probe_gate + activated * probe_up
            ).astype(BF)
    rows_ref[...] = contract_last(tangent_ref[...], proj_ref[...]).astype(BF)
    for step in range(P_SIZE):
        probe = lax.rem(step + 8 * core, P_SIZE)
        backward = dot(rows_ref[pl.ds(pl.multiple_of(probe * 64, 64), 64), :], proj_ref[...])
        target = mine_ref if step < 8 else theirs_ref
        row = slice(step % 8, step % 8 + 1)
        target[row, :1024] = jnp.sum(backward * lead_ref[...], axis=0, keepdims=True)
        target[row, 1024:] = jnp.sum(backward * act_ref[...], axis=0, keepdims=True)


def fetch_kernel(weight_in_ref, weight_out_ref, sem):
    copy = pltpu.make_async_copy(weight_in_ref, weight_out_ref, sem)
    copy.start()
    copy.wait()


def product_kernel(place_ref, mine_ref, theirs_ref, weight_ref, out_ref, sum_ref):
    core = place_ref[3]
    sum_ref[core] = mine_ref[...]
    sum_ref[1 - core] = theirs_ref[...]
    sums = jnp.concatenate([sum_ref[0], sum_ref[1]], axis=0).astype(BF)
    total = None
    for chunk in range(8):
        term = contract_last(sums[:, 256 * chunk : 256 * (chunk + 1)], weight_ref[chunk])
        total = term if total is None else total + term
    unshuffle = unshuffle_matrix(256)
    for group in range(4):
        cols = slice(256 * group, 256 * (group + 1))
        high, mid, low = split3(total[:, cols])
        out_ref[:, cols] = dot(high, unshuffle) + dot(mid, unshuffle) + dot(low, unshuffle)


def pair_split(
    tokens,
    gate_blocks,
    gate_slot,
    up_blocks,
    up_slot,
    down_blocks,
    down_slot,
    sketch,
    probe_index,
    probe_value,
):
    owner = lax.axis_index("fsdp")
    core = lax.axis_index("seq")
    group = lax.axis_index("groups")
    place = jnp.stack([owner, 2 * group + core, owner % 2, core]).astype(jnp.int32)

    def owner_flip(value, bits):
        return lax.ppermute(value, "fsdp", [(i, i ^ bits) for i in range(8)])

    def core_flip(value):
        return lax.ppermute(value, "seq", [(0, 1), (1, 0)])

    def zone_exchange(value):
        return lax.all_to_all(
            value,
            "fsdp",
            split_axis=0,
            concat_axis=0,
            tiled=True,
            axis_index_groups=[[0, 2, 4, 6], [1, 3, 5, 7]],
        )

    by_zone, kind_a, kind_b = pl.pallas_call(
        head_kernel,
        out_shape=(
            jax.ShapeDtypeStruct((4, 64, 2048), BF),
            jax.ShapeDtypeStruct((SHARED, 4096), BF),
            jax.ShapeDtypeStruct((160 - 2 * SHARED, 4096), BF),
        ),
        in_specs=[SMEM, HBM, HBM, HBM],
        out_specs=(HBM,) * 3,
        scratch_shapes=[
            pltpu.VMEM((4, 64, 2048), BF),
            pltpu.VMEM((160, 4096), BF),
            pltpu.SemaphoreType.DMA((11,)),
        ],
        compiler_params=params(60),
        name="head",
    )(place, tokens, gate_blocks, up_blocks)
    near_a = owner_flip(kind_a, 1)
    near_b = owner_flip(kind_b, 1)
    gathered = zone_exchange(by_zone)

    slots = jnp.stack([gate_slot, up_slot, down_slot])
    cells = lax.broadcasted_iota(jnp.int32, (3, 160, 256), 2)
    slot_numbers = lax.broadcasted_iota(jnp.int32, (3, 160, 256), 1)
    inv = jnp.min(jnp.where(slots[:, :, None] == cells, slot_numbers, 160), axis=1)
    near_inv = owner_flip(inv, 1)

    payload = pl.pallas_call(
        payload_kernel,
        out_shape=jax.ShapeDtypeStruct((64, 256), F32),
        in_specs=[SMEM, SMEM] + [HBM] * 3 + [VMEM] * 3,
        out_specs=VMEM,
        scratch_shapes=[
            pltpu.VMEM((32 * STRIDE, 128), F32),
            pltpu.VMEM((128, 128), F32),
            pltpu.VMEM((48, 1024), BF),
            pltpu.VMEM((256, 1024), BF),
            pltpu.VMEM((3, 160, 4096), BF),
            pltpu.VMEM((1024, 256), BF),
            pltpu.SemaphoreType.DMA((3,)),
        ],
        compiler_params=params(59.5),
        name="probe_terms",
    )(place, inv, gate_blocks, up_blocks, down_blocks, sketch, probe_index, probe_value)

    weights = pl.pallas_call(
        own_kernel,
        out_shape=jax.ShapeDtypeStruct((8, 1024, 256), BF),
        in_specs=[SMEM, HBM, HBM],
        out_specs=HBM,
        scratch_shapes=[
            pltpu.VMEM((32 * STRIDE, 128), F32),
            pltpu.VMEM((2, 160, 4096), BF),
            pltpu.VMEM((8, 1024, 256), BF),
            pltpu.SemaphoreType.DMA((2,)),
            pltpu.SemaphoreType.DMA((4,)),
        ],
        compiler_params=params(59.5),
        name="own_blocks",
    )(inv, gate_blocks, up_blocks)

    near_a, payload = lax.optimization_barrier((near_a, payload))
    near_a_other = lax.ppermute(near_a, "groups", [(0, 1), (1, 0)])
    for bits in (2, 4):
        payload = payload + owner_flip(payload, bits)
    near_inv, near_b, near_a_other, gathered, payload, weights = lax.optimization_barrier(
        (near_inv, near_b, near_a_other, gathered, payload, weights)
    )

    first_keep, first_sent, near_weights = pl.pallas_call(
        first_kernel,
        out_shape=(
            jax.ShapeDtypeStruct((64, 1024), F32),
            jax.ShapeDtypeStruct((4, 64, 1024), BF),
            jax.ShapeDtypeStruct((4, 1024, 256), BF),
        ),
        in_specs=[SMEM, SMEM, ANY, ANY, ANY, HBM, ANY],
        out_specs=(VMEM, HBM, HBM),
        scratch_shapes=[
            pltpu.VMEM((160, 4096), BF),
            pltpu.VMEM((32 * STRIDE, 128), F32),
            pltpu.VMEM((4, 1024, 256), BF),
            pltpu.VMEM((4, 1024, 256), BF),
            pltpu.VMEM((4, 64, 2048), BF),
            pltpu.VMEM((2, 256, 1024), BF),
            pltpu.VMEM((4, 64, 1024), BF),
            pltpu.VMEM((256, 256), F32),
            pltpu.SemaphoreType.DMA((5,)),
            pltpu.SemaphoreType.DMA,
            pltpu.SemaphoreType.DMA((4,)),
        ],
        compiler_params=params(50),
        name="first_partial",
    )(place, near_inv, near_a, near_b, near_a_other, weights, gathered)
    first_back = zone_exchange(first_sent)

    second_keep, *second_sent = pl.pallas_call(
        second_kernel,
        out_shape=(jax.ShapeDtypeStruct((64, 1024), F32),)
        + (jax.ShapeDtypeStruct((64, 1024), BF),) * 3,
        in_specs=[SMEM, ANY, HBM, ANY],
        out_specs=(VMEM,) * 4,
        scratch_shapes=[
            pltpu.VMEM((4, 1024, 256), BF),
            pltpu.VMEM((4, 1024, 256), BF),
            pltpu.VMEM((4, 64, 2048), BF),
            pltpu.VMEM((2, 256, 1024), BF),
            pltpu.VMEM((256, 256), F32),
            pltpu.SemaphoreType.DMA((3,)),
        ],
        compiler_params=params(50),
        name="second_partial",
    )(place, core_flip(near_weights), weights, gathered)
    second_back = [owner_flip(second_sent[flip - 1], 2 * flip) for flip in (1, 2, 3)]

    across = owner_flip(payload, 1)
    second_keep, across = lax.optimization_barrier((second_keep, across))
    payload = payload + across
    pay_parts = [
        payload,
        core_flip(payload),
        lax.ppermute(payload, "groups", [(0, 1), (1, 0)]),
        lax.ppermute(payload, ("groups", "seq"), [(i, i ^ 3) for i in range(4)]),
    ]

    first_back, weights = lax.optimization_barrier((first_back, weights))
    weights_at_hand = pl.pallas_call(
        fetch_kernel,
        out_shape=jax.ShapeDtypeStruct((8, 1024, 256), BF),
        in_specs=[HBM],
        out_specs=VMEM,
        scratch_shapes=[pltpu.SemaphoreType.DMA],
        compiler_params=params(48),
        name="fetch_weights",
    )(weights)
    pay_parts[0], weights_at_hand = lax.optimization_barrier((pay_parts[0], weights_at_hand))

    mine, theirs = pl.pallas_call(
        middle_kernel,
        out_shape=(jax.ShapeDtypeStruct((8, 2048), F32),) * 2,
        in_specs=[SMEM] + [VMEM] * 10,
        out_specs=(VMEM,) * 2,
        scratch_shapes=[
            pltpu.VMEM((64, 1024), F32),
            pltpu.VMEM((64, 1024), F32),
            pltpu.VMEM((4, 64, 256), F32),
            pltpu.VMEM((K, 1024), BF),
            pltpu.VMEM((64 * P_SIZE, 1024), BF),
            pltpu.VMEM((64 * P_SIZE, K), BF),
        ],
        compiler_params=params(48),
        name="token_sums",
    )(place, first_keep, first_back, second_keep, *second_back, *pay_parts)

    sums = mine + core_flip(theirs)
    for bits in (1, 2, 4):
        sums = sums + owner_flip(sums, bits)

    return pl.pallas_call(
        product_kernel,
        out_shape=jax.ShapeDtypeStruct((P_SIZE, 1024), F32),
        in_specs=[SMEM, VMEM, VMEM, VMEM],
        out_specs=VMEM,
        scratch_shapes=[pltpu.VMEM((2, 8, 2048), F32)],
        compiler_params=params(30),
        name="products",
    )(place, sums, core_flip(sums), weights_at_hand)


def per_device(tokens, gate_blocks, *rest):
    fits = (
        lax.axis_size("fsdp") == 8
        and lax.axis_size("seq") == 2
        and lax.axis_size("groups") == 2
        and tokens.shape == (64, 8192)
        and gate_blocks.shape == (160, 4096)
        and rest[-2].shape == (P_SIZE, 256)
    )
    return (pair_split if fits else hidden_split)(tokens, gate_blocks, *rest)


def solution(mesh):
    in_specs = (
        P(("groups", "fsdp", "seq"), None),
        P("fsdp", None),
        P("fsdp"),
        P("fsdp", None),
        P("fsdp"),
        P("fsdp", None),
        P("fsdp"),
        P(None, "fsdp"),
        P(),
        P(),
    )
    out_specs = P("groups", "fsdp")
    return jax.shard_map(
        per_device, mesh=mesh, in_specs=in_specs, out_specs=out_specs, check_vma=False
    )
```

```python
import functools

import jax
import jax.numpy as jnp
from jax import lax
from jax.experimental import pallas as pl
from jax.experimental.pallas import tpu as pltpu
from jax.sharding import PartitionSpec as P

HID_DEV = 128
BLK = 64
P_SIZE = 16
K = 32

BF = jnp.bfloat16
F32 = jnp.float32
VMEM = pl.BlockSpec(memory_space=pltpu.VMEM)
SMEM = pl.BlockSpec(memory_space=pltpu.SMEM)
HBM = pl.BlockSpec(memory_space=pltpu.HBM)
ANY = pl.BlockSpec(memory_space=pl.ANY)

STRIDE = 168
SHARED = 48


def params(mebibytes):
    return pltpu.CompilerParams(vmem_limit_bytes=int(mebibytes * 1024 * 1024))


def unpack(blocks, slot_ids, cell_total):
    holder = jnp.zeros((cell_total + 1, blocks.shape[1]), blocks.dtype)
    return holder.at[slot_ids].set(blocks)[:cell_total]


def contract_last(first_mat, second_mat):
    return lax.dot_general(
        first_mat, second_mat, (((1,), (1,)), ((), ())), preferred_element_type=jnp.float32
    )


def hidden_split(
    tokens,
    gate_blocks,
    gate_slot,
    up_blocks,
    up_slot,
    down_blocks,
    down_slot,
    sketch,
    probe_index,
    probe_value,
):
    owners = lax.axis_size("fsdp")
    model_width = tokens.shape[1]
    local_width = model_width // owners
    block_rows = local_width // BLK
    hidden = HID_DEV
    col_blocks = hidden * owners // BLK
    cell_total = block_rows * col_blocks
    gate_dense = unpack(gate_blocks, gate_slot, cell_total).reshape(
        block_rows, col_blocks, BLK, BLK
    )
    up_dense = unpack(up_blocks, up_slot, cell_total).reshape(block_rows, col_blocks, BLK, BLK)
    stacked = jnp.stack([gate_dense, up_dense], axis=1)
    stacked = stacked.reshape(block_rows, 2, owners, hidden // BLK, BLK, BLK)
    stacked = stacked.transpose(0, 4, 2, 1, 3, 5).reshape(local_width, owners * 2 * hidden)
    both_weights = lax.all_to_all(stacked, "fsdp", split_axis=1, concat_axis=0, tiled=True)
    picked = both_weights[probe_index].astype(jnp.float32)
    probe_both = jnp.sum(picked * probe_value[:, :, None], axis=1)
    preact = jnp.dot(
        lax.all_gather(tokens, "fsdp", axis=0, tiled=True),
        both_weights,
        preferred_element_type=jnp.float32,
    )
    row_count = preact.shape[0]
    gate_pre = preact[:, :hidden]
    up_pre = preact[:, hidden:]
    down_dense = unpack(down_blocks, down_slot, cell_total).reshape(
        col_blocks, block_rows, BLK, BLK
    )
    down_dense = down_dense.transpose(0, 2, 1, 3).reshape(col_blocks * BLK, local_width)
    down_rows = lax.all_to_all(down_dense, "fsdp", split_axis=0, concat_axis=1, tiled=True)
    full_sketch = lax.all_gather(sketch, "fsdp", axis=1, tiled=True)
    projected = contract_last(down_rows, full_sketch)
    projected = projected.astype(jnp.bfloat16)
    sigmoid_g = jax.nn.sigmoid(gate_pre)
    activated = gate_pre * sigmoid_g
    slope_g = sigmoid_g * (1.0 + gate_pre * (1.0 - sigmoid_g))
    lead_term = slope_g * up_pre
    tangent = (
        lead_term[:, None, :] * probe_both[None, :, :hidden]
        + activated[:, None, :] * probe_both[None, :, hidden:]
    )
    tangent = tangent.astype(jnp.bfloat16)
    partial_sketch = jnp.dot(
        tangent.reshape(row_count * P_SIZE, hidden), projected, preferred_element_type=jnp.float32
    )
    partial_sketch = partial_sketch.reshape(row_count, P_SIZE * K)
    sketch_rows = lax.psum(partial_sketch, "fsdp").astype(jnp.bfloat16)
    backward = contract_last(sketch_rows.reshape(row_count * P_SIZE, K), projected).reshape(
        row_count, P_SIZE, hidden
    )
    summed = jnp.concatenate(
        [
            jnp.sum(backward * lead_term[:, None, :], axis=0),
            jnp.sum(backward * activated[:, None, :], axis=0),
        ],
        axis=1,
    )
    summed = lax.psum(summed, "seq").astype(jnp.bfloat16)
    products = contract_last(summed, both_weights)
    return lax.psum_scatter(products, "fsdp", scatter_dimension=1, tiled=True)


def dot(a, b):
    return jnp.dot(a, b, preferred_element_type=F32)


def split3(value):
    high = value.astype(BF)
    rest = value - high.astype(F32)
    mid = rest.astype(BF)
    low = (rest - mid.astype(F32)).astype(BF)
    return high, mid, low


def shuffled(natural):
    return (natural // BLK) * BLK + (natural % 2) * (BLK // 2) + (natural % BLK) // 2


def shuffle_matrix(size):
    rows = lax.broadcasted_iota(jnp.int32, (size, size), 0)
    cols = lax.broadcasted_iota(jnp.int32, (size, size), 1)
    return jnp.where(shuffled(rows) == cols, 1.0, 0.0).astype(BF)


def unshuffle_matrix(size):
    rows = lax.broadcasted_iota(jnp.int32, (size, size), 0)
    cols = lax.broadcasted_iota(jnp.int32, (size, size), 1)
    return jnp.where(shuffled(cols) == rows, 1.0, 0.0).astype(BF)


def stage_blocks(blocks_ref, tiles_ref, first_slot):
    @pl.loop(0, blocks_ref.shape[0] // 16)
    def _(step):
        row = pl.multiple_of(step * 16, 16)
        target = pl.multiple_of(first_slot + row, 16)
        for chunk in range(32):
            piece = blocks_ref[pl.ds(row, 16), 128 * chunk : 128 * (chunk + 1)].astype(F32)
            tiles_ref[pl.ds(target + chunk * STRIDE, 16), :] = piece


def clear_empty_slot(tiles_ref):
    for chunk in range(32):
        tiles_ref[pl.ds(chunk * STRIDE + 160, 8), :] = jnp.zeros((8, 128), F32)


def assembled_pair(tiles_ref, left_slot, right_slot):
    left = tiles_ref[pl.ds(left_slot, 32, stride=STRIDE), :]
    right = tiles_ref[pl.ds(right_slot, 32, stride=STRIDE), :]
    low_half = lax.broadcasted_iota(jnp.int32, (32, 128), 1) < BLK
    straight = jnp.where(low_half, left, right)
    crossed = pltpu.roll(jnp.where(low_half, right, left), BLK, 1)
    even = jnp.where(low_half, straight, crossed)
    odd = jnp.where(low_half, crossed, straight)
    return even.astype(BF), odd.astype(BF)


def assemble_columns(inv_ref, inv_row, tiles_ref, put):
    @pl.loop(0, 16)
    def _(block_row):
        for pair in range(8):
            cell = block_row * 16 + 2 * pair
            even, odd = assembled_pair(
                tiles_ref, inv_ref[inv_row, cell], inv_ref[inv_row, cell + 1]
            )
            row = pl.multiple_of(block_row * BLK, BLK)
            put(pair, row, even)
            put(pair, row + BLK // 2, odd)


def head_kernel(
    place_ref, tok_in_ref, gate_ref, up_ref, zone_out_ref, a_out_ref, b_out_ref, tok_ref, blocks_ref, sem
):
    group = place_ref[1] // 2
    core = place_ref[3]

    @pl.when(core == 0)
    def _():
        pltpu.make_async_copy(gate_ref, blocks_ref, sem.at[0]).start()

    @pl.when(core != 0)
    def _():
        pltpu.make_async_copy(up_ref, blocks_ref, sem.at[0]).start()

    loads, stores = [], []
    for zone in range(4):
        held = tok_ref.at[zone]
        lanes = pl.ds(2048 * zone, 2048)
        loads.append(pltpu.make_async_copy(tok_in_ref.at[:, lanes], held, sem.at[3 + zone]))
        stores.append(pltpu.make_async_copy(held, zone_out_ref.at[zone], sem.at[7 + zone]))
    for load in loads:
        load.start()
    pltpu.make_async_copy(gate_ref, blocks_ref, sem.at[0]).wait()
    first = pl.multiple_of(SHARED * group, 16)
    stores.append(
        pltpu.make_async_copy(blocks_ref.at[pl.ds(first, SHARED)], a_out_ref, sem.at[1])
    )
    stores.append(
        pltpu.make_async_copy(
            blocks_ref.at[pl.ds(2 * SHARED, 160 - 2 * SHARED)], b_out_ref, sem.at[2]
        )
    )
    stores[4].start()
    stores[5].start()
    for load, store in zip(loads, stores[:4]):
        load.wait()
        store.start()
    for store in stores:
        store.wait()


def own_kernel(
    place_ref,
    inv_ref,
    gate_ref,
    up_ref,
    down_ref,
    sketch_ref,
    index_ref,
    value_ref,
    weight_out_ref,
    payload_ref,
    tiles_ref,
    omega_ref,
    split_ref,
    down_dense_ref,
    blocks_ref,
    weight_ref,
    in_sem,
    out_sem,
):
    owner = place_ref[0]
    quarter = place_ref[1]
    loads = [
        pltpu.make_async_copy(source, blocks_ref.at[i], in_sem.at[i])
        for i, source in enumerate((gate_ref, up_ref, down_ref))
    ]
    stores = [
        pltpu.make_async_copy(
            weight_ref.at[pl.ds(4 * i, 4)], weight_out_ref.at[pl.ds(4 * i, 4)], out_sem.at[i]
        )
        for i in range(2)
    ]
    for load in loads:
        load.start()
    clear_empty_slot(tiles_ref)

    for which in range(2):
        loads[which].wait()
        stage_blocks(blocks_ref.at[which], tiles_ref, 0)

        def put(pair, row, piece):
            lane = (pair % 2) * 128
            weight_ref[4 * which + pair // 2, pl.ds(row, 32), lane : lane + 128] = piece

        assemble_columns(inv_ref, which, tiles_ref, put)
        stores[which].start()

    loads[2].wait()
    stage_blocks(blocks_ref.at[2], tiles_ref, 0)
    for local_row in range(4):
        for pair in range(8):
            cell = (quarter * 4 + local_row) * 16 + 2 * pair
            even, odd = assembled_pair(tiles_ref, inv_ref[2, cell], inv_ref[2, cell + 1])
            row = local_row * BLK
            down_dense_ref[row : row + 32, 128 * pair : 128 * (pair + 1)] = even
            down_dense_ref[row + 32 : row + 64, 128 * pair : 128 * (pair + 1)] = odd
    payload_ref[32:64, :] = contract_last(sketch_ref[...], down_dense_ref[...])

    local = index_ref[...] - owner * 1024
    inside = (local >= 0) & (local < 1024)
    safe = jnp.where(inside, local, 0)
    spot = shuffled(safe)
    high_part = jnp.where(inside, spot // 128, -1)
    low_part = spot % 128
    values = value_ref[...]
    high_iota = lax.broadcasted_iota(jnp.int32, (8, 256), 0)
    low_iota = lax.broadcasted_iota(jnp.int32, (128, 256), 0)
    for probe in range(P_SIZE):
        picked = jnp.where(
            high_iota == high_part[probe : probe + 1, :], values[probe : probe + 1, :], 0.0
        )
        one_hot = jnp.where(low_iota == low_part[probe : probe + 1, :], 1.0, 0.0).astype(BF)
        total = None
        for part in split3(picked):
            term = contract_last(part, one_hot)
            total = term if total is None else total + term
        omega_ref[8 * probe : 8 * (probe + 1), :] = total
    for high in range(8):
        piece = omega_ref[pl.ds(high, 16, stride=8), :]
        for part_index, part in enumerate(split3(piece)):
            split_ref[
                16 * part_index : 16 * (part_index + 1), 128 * high : 128 * (high + 1)
            ] = part
    for which in range(2):
        triple = dot(split_ref[...], weight_ref[4 * which + quarter])
        payload_ref[16 * which : 16 * (which + 1), :] = triple[:16] + triple[16:32] + triple[32:]
    for store in stores:
        store.wait()


def flipped(two_bits, flip):
    low_bit = lax.rem(two_bits + flip % 2, 2)
    return low_bit + 2 * lax.rem(two_bits // 2 + flip // 2, 2)


def shuffle_tokens(side, tok_ref, tokens_ref):
    shuffle = shuffle_matrix(256)
    for group in range(8):
        piece = tok_ref[:, :, 256 * group : 256 * (group + 1)].reshape(256, 256)
        half = lax.rem(group // 4 + side, 2)
        tokens_ref[half, :, 256 * (group % 4) : 256 * (group % 4 + 1)] = dot(piece, shuffle).astype(
            BF
        )


def first_kernel(
    place_ref,
    inv_ref,
    a_in_ref,
    b_in_ref,
    a_other_ref,
    weight_in_ref,
    tok_in_ref,
    keep_ref,
    sent_out_ref,
    near_out_ref,
    blocks_ref,
    tiles_ref,
    near_ref,
    own_ref,
    tok_ref,
    tokens_ref,
    sent_ref,
    total_ref,
    in_sem,
    near_sem,
    sent_sem,
):
    zone = place_ref[0] // 2
    side = place_ref[2]
    core = place_ref[3]
    group = place_ref[1] // 2
    mine = pl.multiple_of(SHARED * group, 16)
    other = pl.multiple_of(SHARED * (1 - group), 16)
    loads = [
        pltpu.make_async_copy(a_in_ref, blocks_ref.at[pl.ds(mine, SHARED)], in_sem.at[0]),
        pltpu.make_async_copy(a_other_ref, blocks_ref.at[pl.ds(other, SHARED)], in_sem.at[1]),
        pltpu.make_async_copy(
            b_in_ref, blocks_ref.at[pl.ds(2 * SHARED, 160 - 2 * SHARED)], in_sem.at[2]
        ),
        pltpu.make_async_copy(tok_in_ref, tok_ref, in_sem.at[3]),
        pltpu.make_async_copy(weight_in_ref.at[pl.ds(4 * core, 4)], own_ref, in_sem.at[4]),
    ]
    for load in loads:
        load.start()
    clear_empty_slot(tiles_ref)
    for load in loads[:3]:
        load.wait()
    stage_blocks(blocks_ref, tiles_ref, 0)

    def put(pair, row, piece):
        lane = (pair % 2) * 128
        near_ref[pair // 2, pl.ds(row, 32), lane : lane + 128] = piece

    assemble_columns(inv_ref, core, tiles_ref, put)
    near_store = pltpu.make_async_copy(near_ref, near_out_ref, near_sem)
    near_store.start()
    loads[3].wait()
    shuffle_tokens(side, tok_ref, tokens_ref)
    loads[4].wait()
    stores = []
    for chunk in range(4):
        total = dot(tokens_ref[0], own_ref[chunk]) + dot(tokens_ref[1], near_ref[chunk])
        cols = slice(256 * chunk, 256 * (chunk + 1))
        total_ref[...] = total
        keep_ref[:, cols] = total_ref[pl.ds(pl.multiple_of(64 * zone, 64), 64), :]
        sent_ref[:, :, cols] = total.astype(BF).reshape(4, 64, 256)
        lanes = pl.ds(256 * chunk, 256)
        store = pltpu.make_async_copy(
            sent_ref.at[:, :, lanes], sent_out_ref.at[:, :, lanes], sent_sem.at[chunk]
        )
        store.start()
        stores.append(store)
    for store in stores:
        store.wait()
    near_store.wait()


def second_kernel(
    place_ref,
    near_in_ref,
    weight_in_ref,
    tok_in_ref,
    keep_ref,
    out1_ref,
    out2_ref,
    out3_ref,
    near_ref,
    own_ref,
    tok_ref,
    tokens_ref,
    total_ref,
    in_sem,
):
    zone = place_ref[0] // 2
    side = place_ref[2]
    core = place_ref[3]
    loads = [
        pltpu.make_async_copy(tok_in_ref, tok_ref, in_sem.at[0]),
        pltpu.make_async_copy(weight_in_ref.at[pl.ds(4 - 4 * core, 4)], own_ref, in_sem.at[1]),
        pltpu.make_async_copy(near_in_ref, near_ref, in_sem.at[2]),
    ]
    for load in loads:
        load.start()
    loads[0].wait()
    shuffle_tokens(side, tok_ref, tokens_ref)
    loads[1].wait()
    loads[2].wait()
    for chunk in range(4):
        total = dot(tokens_ref[0], own_ref[chunk]) + dot(tokens_ref[1], near_ref[chunk])
        cols = slice(256 * chunk, 256 * (chunk + 1))
        total_ref[...] = total
        keep_ref[:, cols] = total_ref[pl.ds(pl.multiple_of(64 * zone, 64), 64), :]
        for flip, ref in enumerate((out1_ref, out2_ref, out3_ref), 1):
            row = pl.multiple_of(64 * flipped(zone, flip), 64)
            ref[:, cols] = total_ref[pl.ds(row, 64), :].astype(BF)


def middle_kernel(
    place_ref,
    first_keep_ref,
    first_ref,
    second_keep_ref,
    second1_ref,
    second2_ref,
    second3_ref,
    pay0_ref,
    pay1_ref,
    pay2_ref,
    pay3_ref,
    mine_ref,
    theirs_ref,
    lead_ref,
    act_ref,
    pay_ref,
    proj_ref,
    tangent_ref,
    rows_ref,
):
    zone = place_ref[0] // 2
    quarter = place_ref[1]
    core = place_ref[3]
    unshuffle = unshuffle_matrix(256)
    for flip, ref in enumerate((pay0_ref, pay1_ref, pay2_ref, pay3_ref)):
        pay_ref[flipped(quarter, flip)] = ref[...]
    for chunk in range(4):
        cols = slice(256 * chunk, 256 * (chunk + 1))
        proj_ref[:, cols] = dot(pay_ref[chunk, 32:64, :].astype(BF), unshuffle).astype(BF)
        first = first_keep_ref[:, cols]
        for flip in (1, 2, 3):
            first = first + first_ref[flipped(zone, flip), :, cols].astype(F32)
        second = second_keep_ref[:, cols]
        for ref in (second1_ref, second2_ref, second3_ref):
            second = second + ref[:, cols].astype(F32)
        gate_pre = jnp.where(core == 0, first, second)
        up_pre = jnp.where(core == 0, second, first)
        sigmoid_g = jax.nn.sigmoid(gate_pre)
        activated = gate_pre * sigmoid_g
        slope_g = sigmoid_g * (1.0 + gate_pre * (1.0 - sigmoid_g))
        lead = slope_g * up_pre
        lead_ref[:, cols] = lead
        act_ref[:, cols] = activated
        for probe in range(P_SIZE):
            probe_gate = pay_ref[chunk, probe : probe + 1, :]
            probe_up = pay_ref[chunk, 16 + probe : 17 + probe, :]
            tangent_ref[64 * probe : 64 * (probe + 1), cols] = (
                lead * probe_gate + activated * probe_up
            ).astype(BF)
    rows_ref[...] = contract_last(tangent_ref[...], proj_ref[...]).astype(BF)
    for step in range(P_SIZE):
        probe = lax.rem(step + 8 * core, P_SIZE)
        backward = dot(rows_ref[pl.ds(pl.multiple_of(probe * 64, 64), 64), :], proj_ref[...])
        target = mine_ref if step < 8 else theirs_ref
        row = slice(step % 8, step % 8 + 1)
        target[row, :1024] = jnp.sum(backward * lead_ref[...], axis=0, keepdims=True)
        target[row, 1024:] = jnp.sum(backward * act_ref[...], axis=0, keepdims=True)


def fetch_kernel(weight_in_ref, weight_out_ref, sem):
    copy = pltpu.make_async_copy(weight_in_ref, weight_out_ref, sem)
    copy.start()
    copy.wait()


def product_kernel(place_ref, mine_ref, theirs_ref, weight_ref, out_ref, sum_ref):
    core = place_ref[3]
    sum_ref[core] = mine_ref[...]
    sum_ref[1 - core] = theirs_ref[...]
    sums = jnp.concatenate([sum_ref[0], sum_ref[1]], axis=0).astype(BF)
    total = None
    for chunk in range(8):
        term = contract_last(sums[:, 256 * chunk : 256 * (chunk + 1)], weight_ref[chunk])
        total = term if total is None else total + term
    unshuffle = unshuffle_matrix(256)
    for group in range(4):
        cols = slice(256 * group, 256 * (group + 1))
        high, mid, low = split3(total[:, cols])
        out_ref[:, cols] = dot(high, unshuffle) + dot(mid, unshuffle) + dot(low, unshuffle)


def pair_split(
    tokens,
    gate_blocks,
    gate_slot,
    up_blocks,
    up_slot,
    down_blocks,
    down_slot,
    sketch,
    probe_index,
    probe_value,
):
    owner = lax.axis_index("fsdp")
    core = lax.axis_index("seq")
    group = lax.axis_index("groups")
    place = jnp.stack([owner, 2 * group + core, owner % 2, core]).astype(jnp.int32)

    def owner_flip(value, bits):
        return lax.ppermute(value, "fsdp", [(i, i ^ bits) for i in range(8)])

    def core_flip(value):
        return lax.ppermute(value, "seq", [(0, 1), (1, 0)])

    def zone_exchange(value):
        return lax.all_to_all(
            value,
            "fsdp",
            split_axis=0,
            concat_axis=0,
            tiled=True,
            axis_index_groups=[[0, 2, 4, 6], [1, 3, 5, 7]],
        )

    by_zone, kind_a, kind_b = pl.pallas_call(
        head_kernel,
        out_shape=(
            jax.ShapeDtypeStruct((4, 64, 2048), BF),
            jax.ShapeDtypeStruct((SHARED, 4096), BF),
            jax.ShapeDtypeStruct((160 - 2 * SHARED, 4096), BF),
        ),
        in_specs=[SMEM, HBM, HBM, HBM],
        out_specs=(HBM,) * 3,
        scratch_shapes=[
            pltpu.VMEM((4, 64, 2048), BF),
            pltpu.VMEM((160, 4096), BF),
            pltpu.SemaphoreType.DMA((11,)),
        ],
        compiler_params=params(60),
        name="head",
    )(place, tokens, gate_blocks, up_blocks)
    near_a = owner_flip(kind_a, 1)
    near_b = owner_flip(kind_b, 1)
    gathered = zone_exchange(by_zone)

    slots = jnp.stack([gate_slot, up_slot, down_slot])
    cells = lax.broadcasted_iota(jnp.int32, (3, 160, 256), 2)
    slot_numbers = lax.broadcasted_iota(jnp.int32, (3, 160, 256), 1)
    inv = jnp.min(jnp.where(slots[:, :, None] == cells, slot_numbers, 160), axis=1)
    near_inv = owner_flip(inv, 1)

    weights, payload = pl.pallas_call(
        own_kernel,
        out_shape=(
            jax.ShapeDtypeStruct((8, 1024, 256), BF),
            jax.ShapeDtypeStruct((64, 256), F32),
        ),
        in_specs=[SMEM, SMEM] + [HBM] * 3 + [VMEM] * 3,
        out_specs=(HBM, VMEM),
        scratch_shapes=[
            pltpu.VMEM((32 * STRIDE, 128), F32),
            pltpu.VMEM((128, 128), F32),
            pltpu.VMEM((48, 1024), BF),
            pltpu.VMEM((256, 1024), BF),
            pltpu.VMEM((3, 160, 4096), BF),
            pltpu.VMEM((8, 1024, 256), BF),
            pltpu.SemaphoreType.DMA((3,)),
            pltpu.SemaphoreType.DMA((2,)),
        ],
        compiler_params=params(60),
        name="own_blocks",
    )(place, inv, gate_blocks, up_blocks, down_blocks, sketch, probe_index, probe_value)

    near_a, payload = lax.optimization_barrier((near_a, payload))
    near_a_other = lax.ppermute(near_a, "groups", [(0, 1), (1, 0)])
    for bits in (2, 4):
        payload = payload + owner_flip(payload, bits)
    near_inv, near_b, near_a_other, gathered, payload = lax.optimization_barrier(
        (near_inv, near_b, near_a_other, gathered, payload)
    )

    first_keep, first_sent, near_weights = pl.pallas_call(
        first_kernel,
        out_shape=(
            jax.ShapeDtypeStruct((64, 1024), F32),
            jax.ShapeDtypeStruct((4, 64, 1024), BF),
            jax.ShapeDtypeStruct((4, 1024, 256), BF),
        ),
        in_specs=[SMEM, SMEM, ANY, ANY, ANY, HBM, ANY],
        out_specs=(VMEM, HBM, HBM),
        scratch_shapes=[
            pltpu.VMEM((160, 4096), BF),
            pltpu.VMEM((32 * STRIDE, 128), F32),
            pltpu.VMEM((4, 1024, 256), BF),
            pltpu.VMEM((4, 1024, 256), BF),
            pltpu.VMEM((4, 64, 2048), BF),
            pltpu.VMEM((2, 256, 1024), BF),
            pltpu.VMEM((4, 64, 1024), BF),
            pltpu.VMEM((256, 256), F32),
            pltpu.SemaphoreType.DMA((5,)),
            pltpu.SemaphoreType.DMA,
            pltpu.SemaphoreType.DMA((4,)),
        ],
        compiler_params=params(50),
        name="first_partial",
    )(place, near_inv, near_a, near_b, near_a_other, weights, gathered)
    first_back = zone_exchange(first_sent)

    second_keep, *second_sent = pl.pallas_call(
        second_kernel,
        out_shape=(jax.ShapeDtypeStruct((64, 1024), F32),)
        + (jax.ShapeDtypeStruct((64, 1024), BF),) * 3,
        in_specs=[SMEM, ANY, HBM, ANY],
        out_specs=(VMEM,) * 4,
        scratch_shapes=[
            pltpu.VMEM((4, 1024, 256), BF),
            pltpu.VMEM((4, 1024, 256), BF),
            pltpu.VMEM((4, 64, 2048), BF),
            pltpu.VMEM((2, 256, 1024), BF),
            pltpu.VMEM((256, 256), F32),
            pltpu.SemaphoreType.DMA((3,)),
        ],
        compiler_params=params(50),
        name="second_partial",
    )(place, core_flip(near_weights), weights, gathered)
    second_back = [owner_flip(second_sent[flip - 1], 2 * flip) for flip in (1, 2, 3)]

    across = owner_flip(payload, 1)
    second_keep, across = lax.optimization_barrier((second_keep, across))
    payload = payload + across
    pay_parts = [
        payload,
        core_flip(payload),
        lax.ppermute(payload, "groups", [(0, 1), (1, 0)]),
        lax.ppermute(payload, ("groups", "seq"), [(i, i ^ 3) for i in range(4)]),
    ]

    first_back, weights = lax.optimization_barrier((first_back, weights))
    weights_at_hand = pl.pallas_call(
        fetch_kernel,
        out_shape=jax.ShapeDtypeStruct((8, 1024, 256), BF),
        in_specs=[HBM],
        out_specs=VMEM,
        scratch_shapes=[pltpu.SemaphoreType.DMA],
        compiler_params=params(48),
        name="fetch_weights",
    )(weights)
    pay_parts[0], weights_at_hand = lax.optimization_barrier((pay_parts[0], weights_at_hand))

    mine, theirs = pl.pallas_call(
        middle_kernel,
        out_shape=(jax.ShapeDtypeStruct((8, 2048), F32),) * 2,
        in_specs=[SMEM] + [VMEM] * 10,
        out_specs=(VMEM,) * 2,
        scratch_shapes=[
            pltpu.VMEM((64, 1024), F32),
            pltpu.VMEM((64, 1024), F32),
            pltpu.VMEM((4, 64, 256), F32),
            pltpu.VMEM((K, 1024), BF),
            pltpu.VMEM((64 * P_SIZE, 1024), BF),
            pltpu.VMEM((64 * P_SIZE, K), BF),
        ],
        compiler_params=params(48),
        name="token_sums",
    )(place, first_keep, first_back, second_keep, *second_back, *pay_parts)

    sums = mine + core_flip(theirs)
    for bits in (1, 2, 4):
        sums = sums + owner_flip(sums, bits)

    return pl.pallas_call(
        product_kernel,
        out_shape=jax.ShapeDtypeStruct((P_SIZE, 1024), F32),
        in_specs=[SMEM, VMEM, VMEM, VMEM],
        out_specs=VMEM,
        scratch_shapes=[pltpu.VMEM((2, 8, 2048), F32)],
        compiler_params=params(30),
        name="products",
    )(place, sums, core_flip(sums), weights_at_hand)


def per_device(tokens, gate_blocks, *rest):
    fits = (
        lax.axis_size("fsdp") == 8
        and lax.axis_size("seq") == 2
        and lax.axis_size("groups") == 2
        and tokens.shape == (64, 8192)
        and gate_blocks.shape == (160, 4096)
        and rest[-2].shape == (P_SIZE, 256)
    )
    return (pair_split if fits else hidden_split)(tokens, gate_blocks, *rest)


def solution(mesh):
    in_specs = (
        P(("groups", "fsdp", "seq"), None),
        P("fsdp", None),
        P("fsdp"),
        P("fsdp", None),
        P("fsdp"),
        P("fsdp", None),
        P("fsdp"),
        P(None, "fsdp"),
        P(),
        P(),
    )
    out_specs = P("groups", "fsdp")
    return jax.shard_map(
        per_device, mesh=mesh, in_specs=in_specs, out_specs=out_specs, check_vma=False
    )
```

```python
import functools

import jax
import jax.numpy as jnp
from jax import lax
from jax.experimental import pallas as pl
from jax.experimental.pallas import tpu as pltpu
from jax.sharding import PartitionSpec as P

HID_DEV = 128
BLK = 64
P_SIZE = 16
K = 32

BF = jnp.bfloat16
F32 = jnp.float32
VMEM = pl.BlockSpec(memory_space=pltpu.VMEM)
SMEM = pl.BlockSpec(memory_space=pltpu.SMEM)
HBM = pl.BlockSpec(memory_space=pltpu.HBM)
ANY = pl.BlockSpec(memory_space=pl.ANY)

STRIDE = 168
SHARED = 48


def params(mebibytes):
    return pltpu.CompilerParams(vmem_limit_bytes=int(mebibytes * 1024 * 1024))


def unpack(blocks, slot_ids, cell_total):
    holder = jnp.zeros((cell_total + 1, blocks.shape[1]), blocks.dtype)
    return holder.at[slot_ids].set(blocks)[:cell_total]


def contract_last(first_mat, second_mat):
    return lax.dot_general(
        first_mat, second_mat, (((1,), (1,)), ((), ())), preferred_element_type=jnp.float32
    )


def hidden_split(
    tokens,
    gate_blocks,
    gate_slot,
    up_blocks,
    up_slot,
    down_blocks,
    down_slot,
    sketch,
    probe_index,
    probe_value,
):
    owners = lax.axis_size("fsdp")
    model_width = tokens.shape[1]
    local_width = model_width // owners
    block_rows = local_width // BLK
    hidden = HID_DEV
    col_blocks = hidden * owners // BLK
    cell_total = block_rows * col_blocks
    gate_dense = unpack(gate_blocks, gate_slot, cell_total).reshape(
        block_rows, col_blocks, BLK, BLK
    )
    up_dense = unpack(up_blocks, up_slot, cell_total).reshape(block_rows, col_blocks, BLK, BLK)
    stacked = jnp.stack([gate_dense, up_dense], axis=1)
    stacked = stacked.reshape(block_rows, 2, owners, hidden // BLK, BLK, BLK)
    stacked = stacked.transpose(0, 4, 2, 1, 3, 5).reshape(local_width, owners * 2 * hidden)
    both_weights = lax.all_to_all(stacked, "fsdp", split_axis=1, concat_axis=0, tiled=True)
    picked = both_weights[probe_index].astype(jnp.float32)
    probe_both = jnp.sum(picked * probe_value[:, :, None], axis=1)
    preact = jnp.dot(
        lax.all_gather(tokens, "fsdp", axis=0, tiled=True),
        both_weights,
        preferred_element_type=jnp.float32,
    )
    row_count = preact.shape[0]
    gate_pre = preact[:, :hidden]
    up_pre = preact[:, hidden:]
    down_dense = unpack(down_blocks, down_slot, cell_total).reshape(
        col_blocks, block_rows, BLK, BLK
    )
    down_dense = down_dense.transpose(0, 2, 1, 3).reshape(col_blocks * BLK, local_width)
    down_rows = lax.all_to_all(down_dense, "fsdp", split_axis=0, concat_axis=1, tiled=True)
    full_sketch = lax.all_gather(sketch, "fsdp", axis=1, tiled=True)
    projected = contract_last(down_rows, full_sketch)
    projected = projected.astype(jnp.bfloat16)
    sigmoid_g = jax.nn.sigmoid(gate_pre)
    activated = gate_pre * sigmoid_g
    slope_g = sigmoid_g * (1.0 + gate_pre * (1.0 - sigmoid_g))
    lead_term = slope_g * up_pre
    tangent = (
        lead_term[:, None, :] * probe_both[None, :, :hidden]
        + activated[:, None, :] * probe_both[None, :, hidden:]
    )
    tangent = tangent.astype(jnp.bfloat16)
    partial_sketch = jnp.dot(
        tangent.reshape(row_count * P_SIZE, hidden), projected, preferred_element_type=jnp.float32
    )
    partial_sketch = partial_sketch.reshape(row_count, P_SIZE * K)
    sketch_rows = lax.psum(partial_sketch, "fsdp").astype(jnp.bfloat16)
    backward = contract_last(sketch_rows.reshape(row_count * P_SIZE, K), projected).reshape(
        row_count, P_SIZE, hidden
    )
    summed = jnp.concatenate(
        [
            jnp.sum(backward * lead_term[:, None, :], axis=0),
            jnp.sum(backward * activated[:, None, :], axis=0),
        ],
        axis=1,
    )
    summed = lax.psum(summed, "seq").astype(jnp.bfloat16)
    products = contract_last(summed, both_weights)
    return lax.psum_scatter(products, "fsdp", scatter_dimension=1, tiled=True)


def dot(a, b):
    return jnp.dot(a, b, preferred_element_type=F32)


def split3(value):
    high = value.astype(BF)
    rest = value - high.astype(F32)
    mid = rest.astype(BF)
    low = (rest - mid.astype(F32)).astype(BF)
    return high, mid, low


def shuffled(natural):
    return (natural // BLK) * BLK + (natural % 2) * (BLK // 2) + (natural % BLK) // 2


def shuffle_matrix(size):
    rows = lax.broadcasted_iota(jnp.int32, (size, size), 0)
    cols = lax.broadcasted_iota(jnp.int32, (size, size), 1)
    return jnp.where(shuffled(rows) == cols, 1.0, 0.0).astype(BF)


def unshuffle_matrix(size):
    rows = lax.broadcasted_iota(jnp.int32, (size, size), 0)
    cols = lax.broadcasted_iota(jnp.int32, (size, size), 1)
    return jnp.where(shuffled(cols) == rows, 1.0, 0.0).astype(BF)


def stage_blocks(blocks_ref, tiles_ref, first_slot):
    @pl.loop(0, blocks_ref.shape[0] // 16, unroll=2)
    def _(step):
        row = pl.multiple_of(step * 16, 16)
        target = pl.multiple_of(first_slot + row, 16)
        for chunk in range(32):
            piece = blocks_ref[pl.ds(row, 16), 128 * chunk : 128 * (chunk + 1)].astype(F32)
            tiles_ref[pl.ds(target + chunk * STRIDE, 16), :] = piece


def clear_empty_slot(tiles_ref):
    for chunk in range(32):
        tiles_ref[pl.ds(chunk * STRIDE + 160, 8), :] = jnp.zeros((8, 128), F32)


def assembled_pair(tiles_ref, left_slot, right_slot):
    left = tiles_ref[pl.ds(left_slot, 32, stride=STRIDE), :]
    right = tiles_ref[pl.ds(right_slot, 32, stride=STRIDE), :]
    low_half = lax.broadcasted_iota(jnp.int32, (32, 128), 1) < BLK
    straight = jnp.where(low_half, left, right)
    crossed = pltpu.roll(jnp.where(low_half, right, left), BLK, 1)
    even = jnp.where(low_half, straight, crossed)
    odd = jnp.where(low_half, crossed, straight)
    return even.astype(BF), odd.astype(BF)


def assemble_columns(inv_ref, inv_row, tiles_ref, put, first_row=0, row_count=16):
    @pl.loop(first_row, first_row + row_count, unroll=4)
    def _(block_row):
        for pair in range(8):
            cell = block_row * 16 + 2 * pair
            even, odd = assembled_pair(
                tiles_ref, inv_ref[inv_row, cell], inv_ref[inv_row, cell + 1]
            )
            row = pl.multiple_of(block_row * BLK, BLK)
            put(pair, row, even)
            put(pair, row + BLK // 2, odd)


def head_kernel(
    place_ref, tok_in_ref, gate_ref, up_ref, zone_out_ref, a_out_ref, b_out_ref, tok_ref, blocks_ref, sem
):
    group = place_ref[1] // 2
    core = place_ref[3]

    @pl.when(core == 0)
    def _():
        pltpu.make_async_copy(gate_ref, blocks_ref, sem.at[0]).start()

    @pl.when(core != 0)
    def _():
        pltpu.make_async_copy(up_ref, blocks_ref, sem.at[0]).start()

    loads, stores = [], []
    for zone in range(4):
        held = tok_ref.at[zone]
        lanes = pl.ds(2048 * zone, 2048)
        loads.append(pltpu.make_async_copy(tok_in_ref.at[:, lanes], held, sem.at[3 + zone]))
        stores.append(pltpu.make_async_copy(held, zone_out_ref.at[zone], sem.at[7 + zone]))
    for load in loads:
        load.start()
    pltpu.make_async_copy(gate_ref, blocks_ref, sem.at[0]).wait()
    first = pl.multiple_of(SHARED * group, 16)
    stores.append(
        pltpu.make_async_copy(blocks_ref.at[pl.ds(first, SHARED)], a_out_ref, sem.at[1])
    )
    stores.append(
        pltpu.make_async_copy(
            blocks_ref.at[pl.ds(2 * SHARED, 160 - 2 * SHARED)], b_out_ref, sem.at[2]
        )
    )
    stores[4].start()
    stores[5].start()
    for load, store in zip(loads, stores[:4]):
        load.wait()
        store.start()
    for store in stores:
        store.wait()


def own_kernel(
    place_ref,
    inv_ref,
    gate_ref,
    up_ref,
    down_ref,
    sketch_ref,
    index_ref,
    value_ref,
    weight_out_ref,
    payload_ref,
    tiles_ref,
    omega_ref,
    split_ref,
    down_dense_ref,
    blocks_ref,
    weight_ref,
    in_sem,
    out_sem,
):
    owner = place_ref[0]
    quarter = place_ref[1]
    loads = [
        pltpu.make_async_copy(source, blocks_ref.at[i], in_sem.at[i])
        for i, source in enumerate((gate_ref, up_ref, down_ref))
    ]
    stores = [
        pltpu.make_async_copy(
            weight_ref.at[pl.ds(4 * i, 4)], weight_out_ref.at[pl.ds(4 * i, 4)], out_sem.at[i]
        )
        for i in range(2)
    ]
    for load in loads:
        load.start()
    clear_empty_slot(tiles_ref)

    for which in range(2):
        loads[which].wait()
        stage_blocks(blocks_ref.at[which], tiles_ref, 0)

        def put(pair, row, piece):
            lane = (pair % 2) * 128
            weight_ref[4 * which + pair // 2, pl.ds(row, 32), lane : lane + 128] = piece

        assemble_columns(inv_ref, which, tiles_ref, put)
        stores[which].start()

    loads[2].wait()
    stage_blocks(blocks_ref.at[2], tiles_ref, 0)
    for local_row in range(4):
        for pair in range(8):
            cell = (quarter * 4 + local_row) * 16 + 2 * pair
            even, odd = assembled_pair(tiles_ref, inv_ref[2, cell], inv_ref[2, cell + 1])
            row = local_row * BLK
            down_dense_ref[row : row + 32, 128 * pair : 128 * (pair + 1)] = even
            down_dense_ref[row + 32 : row + 64, 128 * pair : 128 * (pair + 1)] = odd
    payload_ref[32:64, :] = contract_last(sketch_ref[...], down_dense_ref[...])

    local = index_ref[...] - owner * 1024
    inside = (local >= 0) & (local < 1024)
    safe = jnp.where(inside, local, 0)
    spot = shuffled(safe)
    high_part = jnp.where(inside, spot // 128, -1)
    low_part = spot % 128
    values = value_ref[...]
    high_iota = lax.broadcasted_iota(jnp.int32, (8, 256), 0)
    low_iota = lax.broadcasted_iota(jnp.int32, (128, 256), 0)
    for probe in range(P_SIZE):
        picked = jnp.where(
            high_iota == high_part[probe : probe + 1, :], values[probe : probe + 1, :], 0.0
        )
        one_hot = jnp.where(low_iota == low_part[probe : probe + 1, :], 1.0, 0.0).astype(BF)
        terms = contract_last(jnp.concatenate(split3(picked), axis=0), one_hot)
        total = terms[:8] + terms[8:16] + terms[16:]
        omega_ref[8 * probe : 8 * (probe + 1), :] = total
    for high in range(8):
        piece = omega_ref[pl.ds(high, 16, stride=8), :]
        for part_index, part in enumerate(split3(piece)):
            split_ref[
                16 * part_index : 16 * (part_index + 1), 128 * high : 128 * (high + 1)
            ] = part
    for which in range(2):
        triple = dot(split_ref[...], weight_ref[4 * which + quarter])
        payload_ref[16 * which : 16 * (which + 1), :] = triple[:16] + triple[16:32] + triple[32:]
    for store in stores:
        store.wait()


def flipped(two_bits, flip):
    low_bit = lax.rem(two_bits + flip % 2, 2)
    return low_bit + 2 * lax.rem(two_bits // 2 + flip // 2, 2)


def shuffle_tokens(side, tok_ref, tokens_ref):
    shuffle = shuffle_matrix(256)
    for group in range(8):
        piece = tok_ref[:, :, 256 * group : 256 * (group + 1)].reshape(256, 256)
        half = lax.rem(group // 4 + side, 2)
        tokens_ref[half, :, 256 * (group % 4) : 256 * (group % 4 + 1)] = dot(piece, shuffle).astype(
            BF
        )


def near_kernel(
    place_ref,
    inv_ref,
    a_in_ref,
    b_in_ref,
    a_other_ref,
    near_out_ref,
    blocks_ref,
    tiles_ref,
    near_ref,
    in_sem,
    out_sem,
):
    group = place_ref[1] // 2
    mine = pl.multiple_of(SHARED * group, 16)
    other = pl.multiple_of(SHARED * (1 - group), 16)
    loads = [
        pltpu.make_async_copy(a_in_ref, blocks_ref.at[pl.ds(mine, SHARED)], in_sem.at[0]),
        pltpu.make_async_copy(a_other_ref, blocks_ref.at[pl.ds(other, SHARED)], in_sem.at[1]),
        pltpu.make_async_copy(
            b_in_ref, blocks_ref.at[pl.ds(2 * SHARED, 160 - 2 * SHARED)], in_sem.at[2]
        ),
    ]
    for load in loads:
        load.start()
    clear_empty_slot(tiles_ref)
    for load in loads:
        load.wait()
    stage_blocks(blocks_ref, tiles_ref, 0)

    def put(pair, row, piece):
        lane = (pair % 2) * 128
        near_ref[pair // 2, pl.ds(row, 32), lane : lane + 128] = piece

    stores = []
    for part in range(2):
        assemble_columns(inv_ref, place_ref[3], tiles_ref, put, 8 * part, 8)
        rows = pl.ds(512 * part, 512)
        store = pltpu.make_async_copy(
            near_ref.at[:, rows], near_out_ref.at[:, rows], out_sem.at[part]
        )
        store.start()
        stores.append(store)
    for store in stores:
        store.wait()


def partial_kernel(
    first, place_ref, near_in_ref, weight_in_ref, tok_in_ref, keep_ref, *rest
):
    outs, scratch = (rest[:1], rest[1:]) if first else (rest[:3], rest[3:])
    near_ref, own_ref, tok_ref, tokens_ref, total_ref, in_sem = scratch[:6]
    zone = place_ref[0] // 2
    side = place_ref[2]
    core = place_ref[3]
    kind = core if first else 1 - core
    loads = [
        pltpu.make_async_copy(tok_in_ref, tok_ref, in_sem.at[0]),
        pltpu.make_async_copy(weight_in_ref.at[pl.ds(4 * kind, 4)], own_ref, in_sem.at[1]),
        pltpu.make_async_copy(near_in_ref, near_ref, in_sem.at[2]),
    ]
    for load in loads:
        load.start()
    loads[0].wait()
    shuffle_tokens(side, tok_ref, tokens_ref)
    loads[1].wait()
    loads[2].wait()
    stores = []
    for chunk in range(4):
        total = dot(tokens_ref[0], own_ref[chunk]) + dot(tokens_ref[1], near_ref[chunk])
        cols = slice(256 * chunk, 256 * (chunk + 1))
        total_ref[...] = total
        keep_ref[:, cols] = total_ref[pl.ds(pl.multiple_of(64 * zone, 64), 64), :]
        if first:
            sent_ref, sent_sem = scratch[6:]
            sent_ref[:, :, cols] = total.astype(BF).reshape(4, 64, 256)
            lanes = pl.ds(256 * chunk, 256)
            store = pltpu.make_async_copy(
                sent_ref.at[:, :, lanes], outs[0].at[:, :, lanes], sent_sem.at[chunk]
            )
            store.start()
            stores.append(store)
        else:
            for flip, ref in enumerate(outs, 1):
                row = pl.multiple_of(64 * flipped(zone, flip), 64)
                ref[:, cols] = total_ref[pl.ds(row, 64), :].astype(BF)
    for store in stores:
        store.wait()


def middle_kernel(
    place_ref,
    first_keep_ref,
    first_ref,
    second_keep_ref,
    second1_ref,
    second2_ref,
    second3_ref,
    pay0_ref,
    pay1_ref,
    pay2_ref,
    pay3_ref,
    mine_ref,
    theirs_ref,
    lead_ref,
    act_ref,
    pay_ref,
    proj_ref,
    tangent_ref,
    rows_ref,
):
    zone = place_ref[0] // 2
    quarter = place_ref[1]
    core = place_ref[3]
    unshuffle = unshuffle_matrix(256)
    for flip, ref in enumerate((pay0_ref, pay1_ref, pay2_ref, pay3_ref)):
        pay_ref[flipped(quarter, flip)] = ref[...]
    for chunk in range(4):
        cols = slice(256 * chunk, 256 * (chunk + 1))
        proj_ref[:, cols] = dot(pay_ref[chunk, 32:64, :].astype(BF), unshuffle).astype(BF)
        first = first_keep_ref[:, cols]
        for flip in (1, 2, 3):
            first = first + first_ref[flipped(zone, flip), :, cols].astype(F32)
        second = second_keep_ref[:, cols]
        for ref in (second1_ref, second2_ref, second3_ref):
            second = second + ref[:, cols].astype(F32)
        gate_pre = jnp.where(core == 0, first, second)
        up_pre = jnp.where(core == 0, second, first)
        sigmoid_g = jax.nn.sigmoid(gate_pre)
        activated = gate_pre * sigmoid_g
        slope_g = sigmoid_g * (1.0 + gate_pre * (1.0 - sigmoid_g))
        lead = slope_g * up_pre
        lead_ref[:, cols] = lead
        act_ref[:, cols] = activated
        for probe in range(P_SIZE):
            probe_gate = pay_ref[chunk, probe : probe + 1, :]
            probe_up = pay_ref[chunk, 16 + probe : 17 + probe, :]
            tangent_ref[64 * probe : 64 * (probe + 1), cols] = (
                lead * probe_gate + activated * probe_up
            ).astype(BF)
    rows_ref[...] = contract_last(tangent_ref[...], proj_ref[...]).astype(BF)
    for step in range(P_SIZE):
        probe = lax.rem(step + 8 * core, P_SIZE)
        backward = dot(rows_ref[pl.ds(pl.multiple_of(probe * 64, 64), 64), :], proj_ref[...])
        target = mine_ref if step < 8 else theirs_ref
        row = slice(step % 8, step % 8 + 1)
        target[row, :1024] = jnp.sum(backward * lead_ref[...], axis=0, keepdims=True)
        target[row, 1024:] = jnp.sum(backward * act_ref[...], axis=0, keepdims=True)


def fetch_kernel(weight_in_ref, weight_out_ref, sem):
    copy = pltpu.make_async_copy(weight_in_ref, weight_out_ref, sem)
    copy.start()
    copy.wait()


def product_kernel(place_ref, mine_ref, theirs_ref, weight_ref, out_ref, sum_ref):
    core = place_ref[3]
    sum_ref[core] = mine_ref[...]
    sum_ref[1 - core] = theirs_ref[...]
    sums = jnp.concatenate([sum_ref[0], sum_ref[1]], axis=0).astype(BF)
    total = None
    for chunk in range(8):
        term = contract_last(sums[:, 256 * chunk : 256 * (chunk + 1)], weight_ref[chunk])
        total = term if total is None else total + term
    unshuffle = unshuffle_matrix(256)
    for group in range(4):
        cols = slice(256 * group, 256 * (group + 1))
        high, mid, low = split3(total[:, cols])
        out_ref[:, cols] = dot(high, unshuffle) + dot(mid, unshuffle) + dot(low, unshuffle)


def pair_split(
    tokens,
    gate_blocks,
    gate_slot,
    up_blocks,
    up_slot,
    down_blocks,
    down_slot,
    sketch,
    probe_index,
    probe_value,
):
    owner = lax.axis_index("fsdp")
    core = lax.axis_index("seq")
    group = lax.axis_index("groups")
    place = jnp.stack([owner, 2 * group + core, owner % 2, core]).astype(jnp.int32)

    def owner_flip(value, bits):
        return lax.ppermute(value, "fsdp", [(i, i ^ bits) for i in range(8)])

    def core_flip(value):
        return lax.ppermute(value, "seq", [(0, 1), (1, 0)])

    def zone_exchange(value):
        return lax.all_to_all(
            value,
            "fsdp",
            split_axis=0,
            concat_axis=0,
            tiled=True,
            axis_index_groups=[[0, 2, 4, 6], [1, 3, 5, 7]],
        )

    by_zone, kind_a, kind_b = pl.pallas_call(
        head_kernel,
        out_shape=(
            jax.ShapeDtypeStruct((4, 64, 2048), BF),
            jax.ShapeDtypeStruct((SHARED, 4096), BF),
            jax.ShapeDtypeStruct((160 - 2 * SHARED, 4096), BF),
        ),
        in_specs=[SMEM, HBM, HBM, HBM],
        out_specs=(HBM,) * 3,
        scratch_shapes=[
            pltpu.VMEM((4, 64, 2048), BF),
            pltpu.VMEM((160, 4096), BF),
            pltpu.SemaphoreType.DMA((11,)),
        ],
        compiler_params=params(60),
        name="head",
    )(place, tokens, gate_blocks, up_blocks)
    near_a = owner_flip(kind_a, 1)
    near_b = owner_flip(kind_b, 1)
    gathered = zone_exchange(by_zone)

    slots = jnp.stack([gate_slot, up_slot, down_slot])
    cells = lax.broadcasted_iota(jnp.int32, (3, 160, 256), 2)
    slot_numbers = lax.broadcasted_iota(jnp.int32, (3, 160, 256), 1)
    inv = jnp.min(jnp.where(slots[:, :, None] == cells, slot_numbers, 160), axis=1)
    near_inv = owner_flip(inv, 1)

    weights, payload = pl.pallas_call(
        own_kernel,
        out_shape=(
            jax.ShapeDtypeStruct((8, 1024, 256), BF),
            jax.ShapeDtypeStruct((64, 256), F32),
        ),
        in_specs=[SMEM, SMEM] + [HBM] * 3 + [VMEM] * 3,
        out_specs=(HBM, VMEM),
        scratch_shapes=[
            pltpu.VMEM((32 * STRIDE, 128), F32),
            pltpu.VMEM((128, 128), F32),
            pltpu.VMEM((48, 1024), BF),
            pltpu.VMEM((256, 1024), BF),
            pltpu.VMEM((3, 160, 4096), BF),
            pltpu.VMEM((8, 1024, 256), BF),
            pltpu.SemaphoreType.DMA((3,)),
            pltpu.SemaphoreType.DMA((2,)),
        ],
        compiler_params=params(60),
        name="own_blocks",
    )(place, inv, gate_blocks, up_blocks, down_blocks, sketch, probe_index, probe_value)

    near_a, payload = lax.optimization_barrier((near_a, payload))
    near_a_other = lax.ppermute(near_a, "groups", [(0, 1), (1, 0)])
    payload = payload + owner_flip(payload, 2)
    from_far = owner_flip(payload, 4)
    near_inv, near_b, near_a_other, gathered, payload = lax.optimization_barrier(
        (near_inv, near_b, near_a_other, gathered, payload)
    )

    near_weights = pl.pallas_call(
        near_kernel,
        out_shape=jax.ShapeDtypeStruct((4, 1024, 256), BF),
        in_specs=[SMEM, SMEM, ANY, ANY, ANY],
        out_specs=HBM,
        scratch_shapes=[
            pltpu.VMEM((160, 4096), BF),
            pltpu.VMEM((32 * STRIDE, 128), F32),
            pltpu.VMEM((4, 1024, 256), BF),
            pltpu.SemaphoreType.DMA((3,)),
            pltpu.SemaphoreType.DMA((2,)),
        ],
        compiler_params=params(59.5),
        name="near_blocks",
    )(place, near_inv, near_a, near_b, near_a_other)

    near_weights, from_far = lax.optimization_barrier((near_weights, from_far))
    payload = payload + from_far

    first_keep, first_sent = pl.pallas_call(
        functools.partial(partial_kernel, True),
        out_shape=(
            jax.ShapeDtypeStruct((64, 1024), F32),
            jax.ShapeDtypeStruct((4, 64, 1024), BF),
        ),
        in_specs=[SMEM, ANY, HBM, ANY],
        out_specs=(VMEM, HBM),
        scratch_shapes=[
            pltpu.VMEM((4, 1024, 256), BF),
            pltpu.VMEM((4, 1024, 256), BF),
            pltpu.VMEM((4, 64, 2048), BF),
            pltpu.VMEM((2, 256, 1024), BF),
            pltpu.VMEM((256, 256), F32),
            pltpu.SemaphoreType.DMA((3,)),
            pltpu.VMEM((4, 64, 1024), BF),
            pltpu.SemaphoreType.DMA((4,)),
        ],
        compiler_params=params(59.5),
        name="first_partial",
    )(place, near_weights, weights, gathered)
    first_back = zone_exchange(first_sent)

    second_keep, *second_sent = pl.pallas_call(
        functools.partial(partial_kernel, False),
        out_shape=(jax.ShapeDtypeStruct((64, 1024), F32),)
        + (jax.ShapeDtypeStruct((64, 1024), BF),) * 3,
        in_specs=[SMEM, ANY, HBM, ANY],
        out_specs=(VMEM,) * 4,
        scratch_shapes=[
            pltpu.VMEM((4, 1024, 256), BF),
            pltpu.VMEM((4, 1024, 256), BF),
            pltpu.VMEM((4, 64, 2048), BF),
            pltpu.VMEM((2, 256, 1024), BF),
            pltpu.VMEM((256, 256), F32),
            pltpu.SemaphoreType.DMA((3,)),
        ],
        compiler_params=params(50),
        name="second_partial",
    )(place, core_flip(near_weights), weights, gathered)
    second_back = [owner_flip(second_sent[flip - 1], 2 * flip) for flip in (1, 2, 3)]

    across = owner_flip(payload, 1)
    second_keep, across = lax.optimization_barrier((second_keep, across))
    payload = payload + across
    pay_parts = [
        payload,
        core_flip(payload),
        lax.ppermute(payload, "groups", [(0, 1), (1, 0)]),
        lax.ppermute(payload, ("groups", "seq"), [(i, i ^ 3) for i in range(4)]),
    ]

    first_back, weights = lax.optimization_barrier((first_back, weights))
    weights_at_hand = pl.pallas_call(
        fetch_kernel,
        out_shape=jax.ShapeDtypeStruct((8, 1024, 256), BF),
        in_specs=[HBM],
        out_specs=VMEM,
        scratch_shapes=[pltpu.SemaphoreType.DMA],
        compiler_params=params(48),
        name="fetch_weights",
    )(weights)
    pay_parts[0], weights_at_hand = lax.optimization_barrier((pay_parts[0], weights_at_hand))

    mine, theirs = pl.pallas_call(
        middle_kernel,
        out_shape=(jax.ShapeDtypeStruct((8, 2048), F32),) * 2,
        in_specs=[SMEM] + [VMEM] * 10,
        out_specs=(VMEM,) * 2,
        scratch_shapes=[
            pltpu.VMEM((64, 1024), F32),
            pltpu.VMEM((64, 1024), F32),
            pltpu.VMEM((4, 64, 256), F32),
            pltpu.VMEM((K, 1024), BF),
            pltpu.VMEM((64 * P_SIZE, 1024), BF),
            pltpu.VMEM((64 * P_SIZE, K), BF),
        ],
        compiler_params=params(48),
        name="token_sums",
    )(place, first_keep, first_back, second_keep, *second_back, *pay_parts)

    sums = mine + core_flip(theirs)
    x_part, z_part, xz_part = [owner_flip(sums, bits) for bits in (1, 2, 3)]
    sums = (sums + x_part) + (z_part + xz_part)
    sums = sums + owner_flip(sums, 4)

    return pl.pallas_call(
        product_kernel,
        out_shape=jax.ShapeDtypeStruct((P_SIZE, 1024), F32),
        in_specs=[SMEM, VMEM, VMEM, VMEM],
        out_specs=VMEM,
        scratch_shapes=[pltpu.VMEM((2, 8, 2048), F32)],
        compiler_params=params(30),
        name="products",
    )(place, sums, core_flip(sums), weights_at_hand)


def per_device(tokens, gate_blocks, *rest):
    fits = (
        lax.axis_size("fsdp") == 8
        and lax.axis_size("seq") == 2
        and lax.axis_size("groups") == 2
        and tokens.shape == (64, 8192)
        and gate_blocks.shape == (160, 4096)
        and rest[-2].shape == (P_SIZE, 256)
    )
    return (pair_split if fits else hidden_split)(tokens, gate_blocks, *rest)


def solution(mesh):
    in_specs = (
        P(("groups", "fsdp", "seq"), None),
        P("fsdp", None),
        P("fsdp"),
        P("fsdp", None),
        P("fsdp"),
        P("fsdp", None),
        P("fsdp"),
        P(None, "fsdp"),
        P(),
        P(),
    )
    out_specs = P("groups", "fsdp")
    return jax.shard_map(
        per_device, mesh=mesh, in_specs=in_specs, out_specs=out_specs, check_vma=False
    )
```

```python
import functools

import jax
import jax.numpy as jnp
from jax import lax
from jax.experimental import pallas as pl
from jax.experimental.pallas import tpu as pltpu
from jax.sharding import PartitionSpec as P

HID_DEV = 128
BLK = 64
P_SIZE = 16
K = 32

BF = jnp.bfloat16
F32 = jnp.float32
VMEM = pl.BlockSpec(memory_space=pltpu.VMEM)
SMEM = pl.BlockSpec(memory_space=pltpu.SMEM)
HBM = pl.BlockSpec(memory_space=pltpu.HBM)
ANY = pl.BlockSpec(memory_space=pl.ANY)

STRIDE = 168
SHARED = 48


def params(mebibytes):
    return pltpu.CompilerParams(vmem_limit_bytes=int(mebibytes * 1024 * 1024))


def unpack(blocks, slot_ids, cell_total):
    holder = jnp.zeros((cell_total + 1, blocks.shape[1]), blocks.dtype)
    return holder.at[slot_ids].set(blocks)[:cell_total]


def contract_last(first_mat, second_mat):
    return lax.dot_general(
        first_mat, second_mat, (((1,), (1,)), ((), ())), preferred_element_type=jnp.float32
    )


def hidden_split(
    tokens,
    gate_blocks,
    gate_slot,
    up_blocks,
    up_slot,
    down_blocks,
    down_slot,
    sketch,
    probe_index,
    probe_value,
):
    owners = lax.axis_size("fsdp")
    model_width = tokens.shape[1]
    local_width = model_width // owners
    block_rows = local_width // BLK
    hidden = HID_DEV
    col_blocks = hidden * owners // BLK
    cell_total = block_rows * col_blocks
    gate_dense = unpack(gate_blocks, gate_slot, cell_total).reshape(
        block_rows, col_blocks, BLK, BLK
    )
    up_dense = unpack(up_blocks, up_slot, cell_total).reshape(block_rows, col_blocks, BLK, BLK)
    stacked = jnp.stack([gate_dense, up_dense], axis=1)
    stacked = stacked.reshape(block_rows, 2, owners, hidden // BLK, BLK, BLK)
    stacked = stacked.transpose(0, 4, 2, 1, 3, 5).reshape(local_width, owners * 2 * hidden)
    both_weights = lax.all_to_all(stacked, "fsdp", split_axis=1, concat_axis=0, tiled=True)
    picked = both_weights[probe_index].astype(jnp.float32)
    probe_both = jnp.sum(picked * probe_value[:, :, None], axis=1)
    preact = jnp.dot(
        lax.all_gather(tokens, "fsdp", axis=0, tiled=True),
        both_weights,
        preferred_element_type=jnp.float32,
    )
    row_count = preact.shape[0]
    gate_pre = preact[:, :hidden]
    up_pre = preact[:, hidden:]
    down_dense = unpack(down_blocks, down_slot, cell_total).reshape(
        col_blocks, block_rows, BLK, BLK
    )
    down_dense = down_dense.transpose(0, 2, 1, 3).reshape(col_blocks * BLK, local_width)
    down_rows = lax.all_to_all(down_dense, "fsdp", split_axis=0, concat_axis=1, tiled=True)
    full_sketch = lax.all_gather(sketch, "fsdp", axis=1, tiled=True)
    projected = contract_last(down_rows, full_sketch)
    projected = projected.astype(jnp.bfloat16)
    sigmoid_g = jax.nn.sigmoid(gate_pre)
    activated = gate_pre * sigmoid_g
    slope_g = sigmoid_g * (1.0 + gate_pre * (1.0 - sigmoid_g))
    lead_term = slope_g * up_pre
    tangent = (
        lead_term[:, None, :] * probe_both[None, :, :hidden]
        + activated[:, None, :] * probe_both[None, :, hidden:]
    )
    tangent = tangent.astype(jnp.bfloat16)
    partial_sketch = jnp.dot(
        tangent.reshape(row_count * P_SIZE, hidden), projected, preferred_element_type=jnp.float32
    )
    partial_sketch = partial_sketch.reshape(row_count, P_SIZE * K)
    sketch_rows = lax.psum(partial_sketch, "fsdp").astype(jnp.bfloat16)
    backward = contract_last(sketch_rows.reshape(row_count * P_SIZE, K), projected).reshape(
        row_count, P_SIZE, hidden
    )
    summed = jnp.concatenate(
        [
            jnp.sum(backward * lead_term[:, None, :], axis=0),
            jnp.sum(backward * activated[:, None, :], axis=0),
        ],
        axis=1,
    )
    summed = lax.psum(summed, "seq").astype(jnp.bfloat16)
    products = contract_last(summed, both_weights)
    return lax.psum_scatter(products, "fsdp", scatter_dimension=1, tiled=True)


def dot(a, b):
    return jnp.dot(a, b, preferred_element_type=F32)


def split3(value):
    high = value.astype(BF)
    rest = value - high.astype(F32)
    mid = rest.astype(BF)
    low = (rest - mid.astype(F32)).astype(BF)
    return high, mid, low


def shuffled(natural):
    return (natural // BLK) * BLK + (natural % 2) * (BLK // 2) + (natural % BLK) // 2


def shuffle_matrix(size):
    rows = lax.broadcasted_iota(jnp.int32, (size, size), 0)
    cols = lax.broadcasted_iota(jnp.int32, (size, size), 1)
    return jnp.where(shuffled(rows) == cols, 1.0, 0.0).astype(BF)


def unshuffle_matrix(size):
    rows = lax.broadcasted_iota(jnp.int32, (size, size), 0)
    cols = lax.broadcasted_iota(jnp.int32, (size, size), 1)
    return jnp.where(shuffled(cols) == rows, 1.0, 0.0).astype(BF)


def stage_blocks(blocks_ref, tiles_ref, first_slot):
    @pl.loop(0, blocks_ref.shape[0] // 16, unroll=2)
    def _(step):
        row = pl.multiple_of(step * 16, 16)
        target = pl.multiple_of(first_slot + row, 16)
        for chunk in range(32):
            piece = blocks_ref[pl.ds(row, 16), 128 * chunk : 128 * (chunk + 1)].astype(F32)
            tiles_ref[pl.ds(target + chunk * STRIDE, 16), :] = piece


def clear_empty_slot(tiles_ref):
    for chunk in range(32):
        tiles_ref[pl.ds(chunk * STRIDE + 160, 8), :] = jnp.zeros((8, 128), F32)


def assembled_pair(tiles_ref, left_slot, right_slot):
    left = tiles_ref[pl.ds(left_slot, 32, stride=STRIDE), :]
    right = tiles_ref[pl.ds(right_slot, 32, stride=STRIDE), :]
    low_half = lax.broadcasted_iota(jnp.int32, (32, 128), 1) < BLK
    straight = jnp.where(low_half, left, right)
    crossed = pltpu.roll(jnp.where(low_half, right, left), BLK, 1)
    even = jnp.where(low_half, straight, crossed)
    odd = jnp.where(low_half, crossed, straight)
    return even.astype(BF), odd.astype(BF)


def assemble_columns(inv_ref, inv_row, tiles_ref, put):
    @pl.loop(0, 16, unroll=4)
    def _(block_row):
        for pair in range(8):
            cell = block_row * 16 + 2 * pair
            even, odd = assembled_pair(
                tiles_ref, inv_ref[inv_row, cell], inv_ref[inv_row, cell + 1]
            )
            row = pl.multiple_of(block_row * BLK, BLK)
            put(pair, row, even)
            put(pair, row + BLK // 2, odd)


def head_kernel(place_ref, gate_ref, up_ref, a_out_ref, b_out_ref, blocks_ref, sem):
    group = place_ref[1] // 2
    core = place_ref[3]

    @pl.when(core == 0)
    def _():
        pltpu.make_async_copy(gate_ref, blocks_ref, sem.at[0]).start()

    @pl.when(core != 0)
    def _():
        pltpu.make_async_copy(up_ref, blocks_ref, sem.at[0]).start()

    pltpu.make_async_copy(gate_ref, blocks_ref, sem.at[0]).wait()
    first = pl.multiple_of(SHARED * group, 16)
    stores = [
        pltpu.make_async_copy(blocks_ref.at[pl.ds(first, SHARED)], a_out_ref, sem.at[1]),
        pltpu.make_async_copy(
            blocks_ref.at[pl.ds(2 * SHARED, 160 - 2 * SHARED)], b_out_ref, sem.at[2]
        ),
    ]
    for store in stores:
        store.start()
    for store in stores:
        store.wait()


def own_kernel(
    place_ref,
    inv_ref,
    gate_ref,
    up_ref,
    down_ref,
    sketch_ref,
    index_ref,
    value_ref,
    weight_out_ref,
    payload_ref,
    tiles_ref,
    omega_ref,
    split_ref,
    down_dense_ref,
    blocks_ref,
    weight_ref,
    in_sem,
    out_sem,
):
    owner = place_ref[0]
    quarter = place_ref[1]
    loads = [
        pltpu.make_async_copy(source, blocks_ref.at[i], in_sem.at[i])
        for i, source in enumerate((gate_ref, up_ref, down_ref))
    ]
    stores = [
        pltpu.make_async_copy(
            weight_ref.at[pl.ds(4 * i, 4)], weight_out_ref.at[pl.ds(4 * i, 4)], out_sem.at[i]
        )
        for i in range(2)
    ]
    for load in loads:
        load.start()
    clear_empty_slot(tiles_ref)

    for which in range(2):
        loads[which].wait()
        stage_blocks(blocks_ref.at[which], tiles_ref, 0)

        def put(pair, row, piece):
            lane = (pair % 2) * 128
            weight_ref[4 * which + pair // 2, pl.ds(row, 32), lane : lane + 128] = piece

        assemble_columns(inv_ref, which, tiles_ref, put)
        stores[which].start()

    loads[2].wait()
    stage_blocks(blocks_ref.at[2], tiles_ref, 0)
    for local_row in range(4):
        for pair in range(8):
            cell = (quarter * 4 + local_row) * 16 + 2 * pair
            even, odd = assembled_pair(tiles_ref, inv_ref[2, cell], inv_ref[2, cell + 1])
            row = local_row * BLK
            down_dense_ref[row : row + 32, 128 * pair : 128 * (pair + 1)] = even
            down_dense_ref[row + 32 : row + 64, 128 * pair : 128 * (pair + 1)] = odd
    payload_ref[32:64, :] = contract_last(sketch_ref[...], down_dense_ref[...])

    local = index_ref[...] - owner * 1024
    inside = (local >= 0) & (local < 1024)
    safe = jnp.where(inside, local, 0)
    spot = shuffled(safe)
    high_part = jnp.where(inside, spot // 128, -1)
    low_part = spot % 128
    values = value_ref[...]
    high_iota = lax.broadcasted_iota(jnp.int32, (8, 256), 0)
    low_iota = lax.broadcasted_iota(jnp.int32, (128, 256), 0)
    for probe in range(P_SIZE):
        picked = jnp.where(
            high_iota == high_part[probe : probe + 1, :], values[probe : probe + 1, :], 0.0
        )
        one_hot = jnp.where(low_iota == low_part[probe : probe + 1, :], 1.0, 0.0).astype(BF)
        terms = contract_last(jnp.concatenate(split3(picked), axis=0), one_hot)
        total = terms[:8] + terms[8:16] + terms[16:]
        omega_ref[8 * probe : 8 * (probe + 1), :] = total
    for high in range(8):
        piece = omega_ref[pl.ds(high, 16, stride=8), :]
        for part_index, part in enumerate(split3(piece)):
            split_ref[
                16 * part_index : 16 * (part_index + 1), 128 * high : 128 * (high + 1)
            ] = part
    for which in range(2):
        triple = dot(split_ref[...], weight_ref[4 * which + quarter])
        payload_ref[16 * which : 16 * (which + 1), :] = triple[:16] + triple[16:32] + triple[32:]
    for store in stores:
        store.wait()


def flipped(two_bits, flip):
    low_bit = lax.rem(two_bits + flip % 2, 2)
    return low_bit + 2 * lax.rem(two_bits // 2 + flip // 2, 2)


def shuffle_tokens(side, tok_ref, tokens_ref):
    shuffle = shuffle_matrix(256)
    for group in range(8):
        piece = tok_ref[:, :, 256 * group : 256 * (group + 1)].reshape(256, 256)
        half = lax.rem(group // 4 + side, 2)
        tokens_ref[half, :, 256 * (group % 4) : 256 * (group % 4 + 1)] = dot(piece, shuffle).astype(
            BF
        )


def first_kernel(
    place_ref,
    inv_ref,
    a_in_ref,
    b_in_ref,
    a_other_ref,
    weight_in_ref,
    tok_in_ref,
    keep_ref,
    sent_out_ref,
    near_out_ref,
    blocks_ref,
    tiles_ref,
    near_ref,
    own_ref,
    tok_ref,
    tokens_ref,
    sent_ref,
    total_ref,
    in_sem,
    near_sem,
    sent_sem,
):
    zone = place_ref[0] // 2
    side = place_ref[2]
    core = place_ref[3]
    group = place_ref[1] // 2
    mine = pl.multiple_of(SHARED * group, 16)
    other = pl.multiple_of(SHARED * (1 - group), 16)
    loads = [
        pltpu.make_async_copy(a_in_ref, blocks_ref.at[pl.ds(mine, SHARED)], in_sem.at[0]),
        pltpu.make_async_copy(a_other_ref, blocks_ref.at[pl.ds(other, SHARED)], in_sem.at[1]),
        pltpu.make_async_copy(
            b_in_ref, blocks_ref.at[pl.ds(2 * SHARED, 160 - 2 * SHARED)], in_sem.at[2]
        ),
        pltpu.make_async_copy(tok_in_ref, tok_ref, in_sem.at[3]),
        pltpu.make_async_copy(weight_in_ref.at[pl.ds(4 * core, 4)], own_ref, in_sem.at[4]),
    ]
    for load in loads:
        load.start()
    clear_empty_slot(tiles_ref)
    for load in loads[:3]:
        load.wait()
    stage_blocks(blocks_ref, tiles_ref, 0)

    def put(pair, row, piece):
        lane = (pair % 2) * 128
        near_ref[pair // 2, pl.ds(row, 32), lane : lane + 128] = piece

    assemble_columns(inv_ref, core, tiles_ref, put)
    near_store = pltpu.make_async_copy(near_ref, near_out_ref, near_sem)
    near_store.start()
    loads[3].wait()
    shuffle_tokens(side, tok_ref, tokens_ref)
    loads[4].wait()
    stores = []
    for chunk in range(4):
        total = dot(tokens_ref[0], own_ref[chunk]) + dot(tokens_ref[1], near_ref[chunk])
        cols = slice(256 * chunk, 256 * (chunk + 1))
        total_ref[...] = total
        keep_ref[:, cols] = total_ref[pl.ds(pl.multiple_of(64 * zone, 64), 64), :]
        sent_ref[:, :, cols] = total.astype(BF).reshape(4, 64, 256)
        lanes = pl.ds(256 * chunk, 256)
        store = pltpu.make_async_copy(
            sent_ref.at[:, :, lanes], sent_out_ref.at[:, :, lanes], sent_sem.at[chunk]
        )
        store.start()
        stores.append(store)
    for store in stores:
        store.wait()
    near_store.wait()


def second_kernel(
    place_ref,
    near_in_ref,
    weight_in_ref,
    tok_in_ref,
    keep_ref,
    out1_ref,
    out2_ref,
    out3_ref,
    near_ref,
    own_ref,
    tok_ref,
    tokens_ref,
    total_ref,
    in_sem,
):
    zone = place_ref[0] // 2
    side = place_ref[2]
    core = place_ref[3]
    loads = [
        pltpu.make_async_copy(tok_in_ref, tok_ref, in_sem.at[0]),
        pltpu.make_async_copy(weight_in_ref.at[pl.ds(4 - 4 * core, 4)], own_ref, in_sem.at[1]),
        pltpu.make_async_copy(near_in_ref, near_ref, in_sem.at[2]),
    ]
    for load in loads:
        load.start()
    loads[0].wait()
    shuffle_tokens(side, tok_ref, tokens_ref)
    loads[1].wait()
    loads[2].wait()
    for chunk in range(4):
        total = dot(tokens_ref[0], own_ref[chunk]) + dot(tokens_ref[1], near_ref[chunk])
        cols = slice(256 * chunk, 256 * (chunk + 1))
        total_ref[...] = total
        keep_ref[:, cols] = total_ref[pl.ds(pl.multiple_of(64 * zone, 64), 64), :]
        for flip, ref in enumerate((out1_ref, out2_ref, out3_ref), 1):
            row = pl.multiple_of(64 * flipped(zone, flip), 64)
            ref[:, cols] = total_ref[pl.ds(row, 64), :].astype(BF)


def middle_kernel(
    place_ref,
    first_keep_ref,
    first_ref,
    second_keep_ref,
    second1_ref,
    second2_ref,
    second3_ref,
    pay0_ref,
    pay1_ref,
    pay2_ref,
    pay3_ref,
    mine_ref,
    theirs_ref,
    lead_ref,
    act_ref,
    pay_ref,
    proj_ref,
    tangent_ref,
    rows_ref,
):
    zone = place_ref[0] // 2
    quarter = place_ref[1]
    core = place_ref[3]
    unshuffle = unshuffle_matrix(256)
    for flip, ref in enumerate((pay0_ref, pay1_ref, pay2_ref, pay3_ref)):
        pay_ref[flipped(quarter, flip)] = ref[...]
    for chunk in range(4):
        cols = slice(256 * chunk, 256 * (chunk + 1))
        proj_ref[:, cols] = dot(pay_ref[chunk, 32:64, :].astype(BF), unshuffle).astype(BF)
        first = first_keep_ref[:, cols]
        for flip in (1, 2, 3):
            first = first + first_ref[flipped(zone, flip), :, cols].astype(F32)
        second = second_keep_ref[:, cols]
        for ref in (second1_ref, second2_ref, second3_ref):
            second = second + ref[:, cols].astype(F32)
        gate_pre = jnp.where(core == 0, first, second)
        up_pre = jnp.where(core == 0, second, first)
        sigmoid_g = jax.nn.sigmoid(gate_pre)
        activated = gate_pre * sigmoid_g
        slope_g = sigmoid_g * (1.0 + gate_pre * (1.0 - sigmoid_g))
        lead = slope_g * up_pre
        lead_ref[:, cols] = lead
        act_ref[:, cols] = activated
        for probe in range(P_SIZE):
            probe_gate = pay_ref[chunk, probe : probe + 1, :]
            probe_up = pay_ref[chunk, 16 + probe : 17 + probe, :]
            tangent_ref[64 * probe : 64 * (probe + 1), cols] = (
                lead * probe_gate + activated * probe_up
            ).astype(BF)
    rows_ref[...] = contract_last(tangent_ref[...], proj_ref[...]).astype(BF)
    for step in range(P_SIZE):
        probe = lax.rem(step + 8 * core, P_SIZE)
        backward = dot(rows_ref[pl.ds(pl.multiple_of(probe * 64, 64), 64), :], proj_ref[...])
        target = mine_ref if step < 8 else theirs_ref
        row = slice(step % 8, step % 8 + 1)
        target[row, :1024] = jnp.sum(backward * lead_ref[...], axis=0, keepdims=True)
        target[row, 1024:] = jnp.sum(backward * act_ref[...], axis=0, keepdims=True)


def fetch_kernel(weight_in_ref, weight_out_ref, sem):
    copy = pltpu.make_async_copy(weight_in_ref, weight_out_ref, sem)
    copy.start()
    copy.wait()


def product_kernel(place_ref, mine_ref, theirs_ref, weight_ref, out_ref, sum_ref):
    core = place_ref[3]
    sum_ref[core] = mine_ref[...]
    sum_ref[1 - core] = theirs_ref[...]
    sums = jnp.concatenate([sum_ref[0], sum_ref[1]], axis=0).astype(BF)
    total = None
    for chunk in range(8):
        term = contract_last(sums[:, 256 * chunk : 256 * (chunk + 1)], weight_ref[chunk])
        total = term if total is None else total + term
    unshuffle = unshuffle_matrix(256)
    for group in range(4):
        cols = slice(256 * group, 256 * (group + 1))
        high, mid, low = split3(total[:, cols])
        out_ref[:, cols] = dot(high, unshuffle) + dot(mid, unshuffle) + dot(low, unshuffle)


def pair_split(
    tokens,
    gate_blocks,
    gate_slot,
    up_blocks,
    up_slot,
    down_blocks,
    down_slot,
    sketch,
    probe_index,
    probe_value,
):
    owner = lax.axis_index("fsdp")
    core = lax.axis_index("seq")
    group = lax.axis_index("groups")
    place = jnp.stack([owner, 2 * group + core, owner % 2, core]).astype(jnp.int32)

    def owner_flip(value, bits):
        return lax.ppermute(value, "fsdp", [(i, i ^ bits) for i in range(8)])

    def core_flip(value):
        return lax.ppermute(value, "seq", [(0, 1), (1, 0)])

    def zone_exchange(value):
        return lax.all_to_all(
            value,
            "fsdp",
            split_axis=0,
            concat_axis=0,
            tiled=True,
            axis_index_groups=[[0, 2, 4, 6], [1, 3, 5, 7]],
        )

    by_zone = tokens.reshape(64, 4, 2048).transpose(1, 0, 2)
    by_zone, place_now = lax.optimization_barrier((by_zone, place))
    kind_a, kind_b = pl.pallas_call(
        head_kernel,
        out_shape=(
            jax.ShapeDtypeStruct((SHARED, 4096), BF),
            jax.ShapeDtypeStruct((160 - 2 * SHARED, 4096), BF),
        ),
        in_specs=[SMEM, HBM, HBM],
        out_specs=(HBM,) * 2,
        scratch_shapes=[pltpu.VMEM((160, 4096), BF), pltpu.SemaphoreType.DMA((3,))],
        compiler_params=params(60),
        name="head",
    )(place_now, gate_blocks, up_blocks)
    near_a = owner_flip(kind_a, 1)
    near_b = owner_flip(kind_b, 1)
    gathered = zone_exchange(by_zone)

    slots = jnp.stack([gate_slot, up_slot, down_slot])
    cells = lax.broadcasted_iota(jnp.int32, (3, 160, 256), 2)
    slot_numbers = lax.broadcasted_iota(jnp.int32, (3, 160, 256), 1)
    inv = jnp.min(jnp.where(slots[:, :, None] == cells, slot_numbers, 160), axis=1)
    near_inv = owner_flip(inv, 1)

    weights, payload = pl.pallas_call(
        own_kernel,
        out_shape=(
            jax.ShapeDtypeStruct((8, 1024, 256), BF),
            jax.ShapeDtypeStruct((64, 256), F32),
        ),
        in_specs=[SMEM, SMEM] + [HBM] * 3 + [VMEM] * 3,
        out_specs=(HBM, VMEM),
        scratch_shapes=[
            pltpu.VMEM((32 * STRIDE, 128), F32),
            pltpu.VMEM((128, 128), F32),
            pltpu.VMEM((48, 1024), BF),
            pltpu.VMEM((256, 1024), BF),
            pltpu.VMEM((3, 160, 4096), BF),
            pltpu.VMEM((8, 1024, 256), BF),
            pltpu.SemaphoreType.DMA((3,)),
            pltpu.SemaphoreType.DMA((2,)),
        ],
        compiler_params=params(60),
        name="own_blocks",
    )(place, inv, gate_blocks, up_blocks, down_blocks, sketch, probe_index, probe_value)

    near_a, payload = lax.optimization_barrier((near_a, payload))
    near_a_other = lax.ppermute(near_a, "groups", [(0, 1), (1, 0)])
    for bits in (2, 4):
        payload = payload + owner_flip(payload, bits)
    near_inv, near_b, near_a_other, gathered, payload = lax.optimization_barrier(
        (near_inv, near_b, near_a_other, gathered, payload)
    )

    first_keep, first_sent, near_weights = pl.pallas_call(
        first_kernel,
        out_shape=(
            jax.ShapeDtypeStruct((64, 1024), F32),
            jax.ShapeDtypeStruct((4, 64, 1024), BF),
            jax.ShapeDtypeStruct((4, 1024, 256), BF),
        ),
        in_specs=[SMEM, SMEM, ANY, ANY, ANY, HBM, ANY],
        out_specs=(VMEM, HBM, HBM),
        scratch_shapes=[
            pltpu.VMEM((160, 4096), BF),
            pltpu.VMEM((32 * STRIDE, 128), F32),
            pltpu.VMEM((4, 1024, 256), BF),
            pltpu.VMEM((4, 1024, 256), BF),
            pltpu.VMEM((4, 64, 2048), BF),
            pltpu.VMEM((2, 256, 1024), BF),
            pltpu.VMEM((4, 64, 1024), BF),
            pltpu.VMEM((256, 256), F32),
            pltpu.SemaphoreType.DMA((5,)),
            pltpu.SemaphoreType.DMA,
            pltpu.SemaphoreType.DMA((4,)),
        ],
        compiler_params=params(50),
        name="first_partial",
    )(place, near_inv, near_a, near_b, near_a_other, weights, gathered)
    first_back = zone_exchange(first_sent)

    second_keep, *second_sent = pl.pallas_call(
        second_kernel,
        out_shape=(jax.ShapeDtypeStruct((64, 1024), F32),)
        + (jax.ShapeDtypeStruct((64, 1024), BF),) * 3,
        in_specs=[SMEM, ANY, HBM, ANY],
        out_specs=(VMEM,) * 4,
        scratch_shapes=[
            pltpu.VMEM((4, 1024, 256), BF),
            pltpu.VMEM((4, 1024, 256), BF),
            pltpu.VMEM((4, 64, 2048), BF),
            pltpu.VMEM((2, 256, 1024), BF),
            pltpu.VMEM((256, 256), F32),
            pltpu.SemaphoreType.DMA((3,)),
        ],
        compiler_params=params(50),
        name="second_partial",
    )(place, core_flip(near_weights), weights, gathered)
    second_back = [owner_flip(second_sent[flip - 1], 2 * flip) for flip in (1, 2, 3)]

    across = owner_flip(payload, 1)
    second_keep, across = lax.optimization_barrier((second_keep, across))
    payload = payload + across
    pay_parts = [
        payload,
        core_flip(payload),
        lax.ppermute(payload, "groups", [(0, 1), (1, 0)]),
        lax.ppermute(payload, ("groups", "seq"), [(i, i ^ 3) for i in range(4)]),
    ]

    first_back, weights = lax.optimization_barrier((first_back, weights))
    weights_at_hand = pl.pallas_call(
        fetch_kernel,
        out_shape=jax.ShapeDtypeStruct((8, 1024, 256), BF),
        in_specs=[HBM],
        out_specs=VMEM,
        scratch_shapes=[pltpu.SemaphoreType.DMA],
        compiler_params=params(48),
        name="fetch_weights",
    )(weights)
    pay_parts[0], weights_at_hand = lax.optimization_barrier((pay_parts[0], weights_at_hand))

    mine, theirs = pl.pallas_call(
        middle_kernel,
        out_shape=(jax.ShapeDtypeStruct((8, 2048), F32),) * 2,
        in_specs=[SMEM] + [VMEM] * 10,
        out_specs=(VMEM,) * 2,
        scratch_shapes=[
            pltpu.VMEM((64, 1024), F32),
            pltpu.VMEM((64, 1024), F32),
            pltpu.VMEM((4, 64, 256), F32),
            pltpu.VMEM((K, 1024), BF),
            pltpu.VMEM((64 * P_SIZE, 1024), BF),
            pltpu.VMEM((64 * P_SIZE, K), BF),
        ],
        compiler_params=params(48),
        name="token_sums",
    )(place, first_keep, first_back, second_keep, *second_back, *pay_parts)

    sums = mine + core_flip(theirs)
    x_part, z_part, xz_part = [owner_flip(sums, bits) for bits in (1, 2, 3)]
    sums = (sums + x_part) + (z_part + xz_part)
    sums = sums + owner_flip(sums, 4)

    return pl.pallas_call(
        product_kernel,
        out_shape=jax.ShapeDtypeStruct((P_SIZE, 1024), F32),
        in_specs=[SMEM, VMEM, VMEM, VMEM],
        out_specs=VMEM,
        scratch_shapes=[pltpu.VMEM((2, 8, 2048), F32)],
        compiler_params=params(30),
        name="products",
    )(place, sums, core_flip(sums), weights_at_hand)


def per_device(tokens, gate_blocks, *rest):
    fits = (
        lax.axis_size("fsdp") == 8
        and lax.axis_size("seq") == 2
        and lax.axis_size("groups") == 2
        and tokens.shape == (64, 8192)
        and gate_blocks.shape == (160, 4096)
        and rest[-2].shape == (P_SIZE, 256)
    )
    return (pair_split if fits else hidden_split)(tokens, gate_blocks, *rest)


def solution(mesh):
    in_specs = (
        P(("groups", "fsdp", "seq"), None),
        P("fsdp", None),
        P("fsdp"),
        P("fsdp", None),
        P("fsdp"),
        P("fsdp", None),
        P("fsdp"),
        P(None, "fsdp"),
        P(),
        P(),
    )
    out_specs = P("groups", "fsdp")
    return jax.shard_map(
        per_device, mesh=mesh, in_specs=in_specs, out_specs=out_specs, check_vma=False
    )
```

```python
import functools

import jax
import jax.numpy as jnp
from jax import lax
from jax.experimental import pallas as pl
from jax.experimental.pallas import tpu as pltpu
from jax.sharding import PartitionSpec as P

HID_DEV = 128
BLK = 64
P_SIZE = 16
K = 32

BF = jnp.bfloat16
F32 = jnp.float32
VMEM = pl.BlockSpec(memory_space=pltpu.VMEM)
SMEM = pl.BlockSpec(memory_space=pltpu.SMEM)
HBM = pl.BlockSpec(memory_space=pltpu.HBM)
ANY = pl.BlockSpec(memory_space=pl.ANY)

STRIDE = 168
SHARED = 48


def params(mebibytes):
    return pltpu.CompilerParams(vmem_limit_bytes=int(mebibytes * 1024 * 1024))


def unpack(blocks, slot_ids, cell_total):
    holder = jnp.zeros((cell_total + 1, blocks.shape[1]), blocks.dtype)
    return holder.at[slot_ids].set(blocks)[:cell_total]


def contract_last(first_mat, second_mat):
    return lax.dot_general(
        first_mat, second_mat, (((1,), (1,)), ((), ())), preferred_element_type=jnp.float32
    )


def hidden_split(
    tokens,
    gate_blocks,
    gate_slot,
    up_blocks,
    up_slot,
    down_blocks,
    down_slot,
    sketch,
    probe_index,
    probe_value,
):
    owners = lax.axis_size("fsdp")
    model_width = tokens.shape[1]
    local_width = model_width // owners
    block_rows = local_width // BLK
    hidden = HID_DEV
    col_blocks = hidden * owners // BLK
    cell_total = block_rows * col_blocks
    gate_dense = unpack(gate_blocks, gate_slot, cell_total).reshape(
        block_rows, col_blocks, BLK, BLK
    )
    up_dense = unpack(up_blocks, up_slot, cell_total).reshape(block_rows, col_blocks, BLK, BLK)
    stacked = jnp.stack([gate_dense, up_dense], axis=1)
    stacked = stacked.reshape(block_rows, 2, owners, hidden // BLK, BLK, BLK)
    stacked = stacked.transpose(0, 4, 2, 1, 3, 5).reshape(local_width, owners * 2 * hidden)
    both_weights = lax.all_to_all(stacked, "fsdp", split_axis=1, concat_axis=0, tiled=True)
    picked = both_weights[probe_index].astype(jnp.float32)
    probe_both = jnp.sum(picked * probe_value[:, :, None], axis=1)
    preact = jnp.dot(
        lax.all_gather(tokens, "fsdp", axis=0, tiled=True),
        both_weights,
        preferred_element_type=jnp.float32,
    )
    row_count = preact.shape[0]
    gate_pre = preact[:, :hidden]
    up_pre = preact[:, hidden:]
    down_dense = unpack(down_blocks, down_slot, cell_total).reshape(
        col_blocks, block_rows, BLK, BLK
    )
    down_dense = down_dense.transpose(0, 2, 1, 3).reshape(col_blocks * BLK, local_width)
    down_rows = lax.all_to_all(down_dense, "fsdp", split_axis=0, concat_axis=1, tiled=True)
    full_sketch = lax.all_gather(sketch, "fsdp", axis=1, tiled=True)
    projected = contract_last(down_rows, full_sketch)
    projected = projected.astype(jnp.bfloat16)
    sigmoid_g = jax.nn.sigmoid(gate_pre)
    activated = gate_pre * sigmoid_g
    slope_g = sigmoid_g * (1.0 + gate_pre * (1.0 - sigmoid_g))
    lead_term = slope_g * up_pre
    tangent = (
        lead_term[:, None, :] * probe_both[None, :, :hidden]
        + activated[:, None, :] * probe_both[None, :, hidden:]
    )
    tangent = tangent.astype(jnp.bfloat16)
    partial_sketch = jnp.dot(
        tangent.reshape(row_count * P_SIZE, hidden), projected, preferred_element_type=jnp.float32
    )
    partial_sketch = partial_sketch.reshape(row_count, P_SIZE * K)
    sketch_rows = lax.psum(partial_sketch, "fsdp").astype(jnp.bfloat16)
    backward = contract_last(sketch_rows.reshape(row_count * P_SIZE, K), projected).reshape(
        row_count, P_SIZE, hidden
    )
    summed = jnp.concatenate(
        [
            jnp.sum(backward * lead_term[:, None, :], axis=0),
            jnp.sum(backward * activated[:, None, :], axis=0),
        ],
        axis=1,
    )
    summed = lax.psum(summed, "seq").astype(jnp.bfloat16)
    products = contract_last(summed, both_weights)
    return lax.psum_scatter(products, "fsdp", scatter_dimension=1, tiled=True)


def dot(a, b):
    return jnp.dot(a, b, preferred_element_type=F32)


def split3(value):
    high = value.astype(BF)
    rest = value - high.astype(F32)
    mid = rest.astype(BF)
    low = (rest - mid.astype(F32)).astype(BF)
    return high, mid, low


def shuffled(natural):
    return (natural // BLK) * BLK + (natural % 2) * (BLK // 2) + (natural % BLK) // 2


def shuffle_matrix(size):
    rows = lax.broadcasted_iota(jnp.int32, (size, size), 0)
    cols = lax.broadcasted_iota(jnp.int32, (size, size), 1)
    return jnp.where(shuffled(rows) == cols, 1.0, 0.0).astype(BF)


def unshuffle_matrix(size):
    rows = lax.broadcasted_iota(jnp.int32, (size, size), 0)
    cols = lax.broadcasted_iota(jnp.int32, (size, size), 1)
    return jnp.where(shuffled(cols) == rows, 1.0, 0.0).astype(BF)


def stage_blocks(blocks_ref, tiles_ref, first_slot):
    @pl.loop(0, blocks_ref.shape[0] // 16, unroll=2)
    def _(step):
        row = pl.multiple_of(step * 16, 16)
        target = pl.multiple_of(first_slot + row, 16)
        for chunk in range(32):
            piece = blocks_ref[pl.ds(row, 16), 128 * chunk : 128 * (chunk + 1)].astype(F32)
            tiles_ref[pl.ds(target + chunk * STRIDE, 16), :] = piece


def clear_empty_slot(tiles_ref):
    for chunk in range(32):
        tiles_ref[pl.ds(chunk * STRIDE + 160, 8), :] = jnp.zeros((8, 128), F32)


def assembled_pair(tiles_ref, left_slot, right_slot):
    left = tiles_ref[pl.ds(left_slot, 32, stride=STRIDE), :]
    right = tiles_ref[pl.ds(right_slot, 32, stride=STRIDE), :]
    low_half = lax.broadcasted_iota(jnp.int32, (32, 128), 1) < BLK
    straight = jnp.where(low_half, left, right)
    crossed = pltpu.roll(jnp.where(low_half, right, left), BLK, 1)
    even = jnp.where(low_half, straight, crossed)
    odd = jnp.where(low_half, crossed, straight)
    return even.astype(BF), odd.astype(BF)


def assemble_columns(inv_ref, inv_row, tiles_ref, put):
    @pl.loop(0, 16, unroll=4)
    def _(block_row):
        for pair in range(8):
            cell = block_row * 16 + 2 * pair
            even, odd = assembled_pair(
                tiles_ref, inv_ref[inv_row, cell], inv_ref[inv_row, cell + 1]
            )
            row = pl.multiple_of(block_row * BLK, BLK)
            put(pair, row, even)
            put(pair, row + BLK // 2, odd)


def position():
    owner = lax.axis_index("fsdp")
    core = lax.axis_index("seq")
    return owner, 2 * lax.axis_index("groups") + core, lax.rem(owner, 2), core


def head_kernel(
    tok_in_ref, gate_ref, up_ref, zone_out_ref, a_out_ref, b_out_ref, tok_ref, blocks_ref, sem
):
    unused_owner, quarter, unused_side, core = position()
    first = pl.multiple_of(SHARED * (quarter // 2), 16)
    a_part = pl.ds(first, SHARED)
    b_part = pl.ds(2 * SHARED, 160 - 2 * SHARED)
    loads, stores = [], []
    for zone in range(4):
        held = tok_ref.at[zone]
        lanes = pl.ds(2048 * zone, 2048)
        loads.append(pltpu.make_async_copy(tok_in_ref.at[:, lanes], held, sem.at[zone]))
        stores.append(pltpu.make_async_copy(held, zone_out_ref.at[zone], sem.at[4 + zone]))
    for load in loads:
        load.start()
    for kind, source in enumerate((gate_ref, up_ref)):

        @pl.when(core == kind)
        def _():
            pltpu.make_async_copy(source.at[a_part], blocks_ref.at[a_part], sem.at[8]).start()
            pltpu.make_async_copy(source.at[b_part], blocks_ref.at[b_part], sem.at[9]).start()

    for load, store in zip(loads, stores):
        load.wait()
        store.start()
    pltpu.make_async_copy(gate_ref.at[a_part], blocks_ref.at[a_part], sem.at[8]).wait()
    stores.append(pltpu.make_async_copy(blocks_ref.at[a_part], a_out_ref, sem.at[10]))
    stores[4].start()
    pltpu.make_async_copy(gate_ref.at[b_part], blocks_ref.at[b_part], sem.at[9]).wait()
    stores.append(pltpu.make_async_copy(blocks_ref.at[b_part], b_out_ref, sem.at[11]))
    stores[5].start()
    for store in stores:
        store.wait()


def own_kernel(
    inv_ref,
    gate_ref,
    up_ref,
    down_ref,
    sketch_ref,
    index_ref,
    value_ref,
    weight_out_ref,
    payload_ref,
    tiles_ref,
    omega_ref,
    split_ref,
    down_dense_ref,
    blocks_ref,
    weight_ref,
    in_sem,
    out_sem,
):
    owner, quarter, unused_side, unused_core = position()
    loads = [
        pltpu.make_async_copy(source, blocks_ref.at[i], in_sem.at[i])
        for i, source in enumerate((gate_ref, up_ref, down_ref))
    ]
    stores = [
        pltpu.make_async_copy(
            weight_ref.at[pl.ds(4 * i, 4)], weight_out_ref.at[pl.ds(4 * i, 4)], out_sem.at[i]
        )
        for i in range(2)
    ]
    for load in loads:
        load.start()
    clear_empty_slot(tiles_ref)

    for which in range(2):
        loads[which].wait()
        stage_blocks(blocks_ref.at[which], tiles_ref, 0)

        def put(pair, row, piece):
            lane = (pair % 2) * 128
            weight_ref[4 * which + pair // 2, pl.ds(row, 32), lane : lane + 128] = piece

        assemble_columns(inv_ref, which, tiles_ref, put)
        stores[which].start()

    loads[2].wait()
    stage_blocks(blocks_ref.at[2], tiles_ref, 0)
    for local_row in range(4):
        for pair in range(8):
            cell = (quarter * 4 + local_row) * 16 + 2 * pair
            even, odd = assembled_pair(tiles_ref, inv_ref[2, cell], inv_ref[2, cell + 1])
            row = local_row * BLK
            down_dense_ref[row : row + 32, 128 * pair : 128 * (pair + 1)] = even
            down_dense_ref[row + 32 : row + 64, 128 * pair : 128 * (pair + 1)] = odd
    payload_ref[32:64, :] = contract_last(sketch_ref[...], down_dense_ref[...])

    local = index_ref[...] - owner * 1024
    inside = (local >= 0) & (local < 1024)
    safe = jnp.where(inside, local, 0)
    spot = shuffled(safe)
    high_part = jnp.where(inside, spot // 128, -1)
    low_part = spot % 128
    values = value_ref[...]
    high_iota = lax.broadcasted_iota(jnp.int32, (8, 256), 0)
    low_iota = lax.broadcasted_iota(jnp.int32, (128, 256), 0)
    for probe in range(P_SIZE):
        picked = jnp.where(
            high_iota == high_part[probe : probe + 1, :], values[probe : probe + 1, :], 0.0
        )
        one_hot = jnp.where(low_iota == low_part[probe : probe + 1, :], 1.0, 0.0).astype(BF)
        terms = contract_last(jnp.concatenate(split3(picked), axis=0), one_hot)
        total = terms[:8] + terms[8:16] + terms[16:]
        omega_ref[8 * probe : 8 * (probe + 1), :] = total
    for high in range(8):
        piece = omega_ref[pl.ds(high, 16, stride=8), :]
        for part_index, part in enumerate(split3(piece)):
            split_ref[
                16 * part_index : 16 * (part_index + 1), 128 * high : 128 * (high + 1)
            ] = part
    for which in range(2):
        triple = dot(split_ref[...], weight_ref[4 * which + quarter])
        payload_ref[16 * which : 16 * (which + 1), :] = triple[:16] + triple[16:32] + triple[32:]
    for store in stores:
        store.wait()


def flipped(two_bits, flip):
    low_bit = lax.rem(two_bits + flip % 2, 2)
    return low_bit + 2 * lax.rem(two_bits // 2 + flip // 2, 2)


def shuffle_tokens(side, tok_ref, tokens_ref):
    shuffle = shuffle_matrix(256)
    for group in range(8):
        piece = tok_ref[:, :, 256 * group : 256 * (group + 1)].reshape(256, 256)
        half = lax.rem(group // 4 + side, 2)
        tokens_ref[half, :, 256 * (group % 4) : 256 * (group % 4 + 1)] = dot(piece, shuffle).astype(
            BF
        )


def first_kernel(
    inv_ref,
    a_in_ref,
    b_in_ref,
    a_other_ref,
    weight_in_ref,
    tok_in_ref,
    keep_ref,
    sent_out_ref,
    near_out_ref,
    blocks_ref,
    tiles_ref,
    near_ref,
    own_ref,
    tok_ref,
    tokens_ref,
    sent_ref,
    total_ref,
    in_sem,
    near_sem,
    sent_sem,
):
    owner, quarter, side, core = position()
    zone = owner // 2
    group = quarter // 2
    mine = pl.multiple_of(SHARED * group, 16)
    other = pl.multiple_of(SHARED * (1 - group), 16)
    loads = [
        pltpu.make_async_copy(a_in_ref, blocks_ref.at[pl.ds(mine, SHARED)], in_sem.at[0]),
        pltpu.make_async_copy(a_other_ref, blocks_ref.at[pl.ds(other, SHARED)], in_sem.at[1]),
        pltpu.make_async_copy(
            b_in_ref, blocks_ref.at[pl.ds(2 * SHARED, 160 - 2 * SHARED)], in_sem.at[2]
        ),
        pltpu.make_async_copy(tok_in_ref, tok_ref, in_sem.at[3]),
        pltpu.make_async_copy(weight_in_ref.at[pl.ds(4 * core, 4)], own_ref, in_sem.at[4]),
    ]
    for load in loads:
        load.start()
    clear_empty_slot(tiles_ref)
    for load in loads[:3]:
        load.wait()
    stage_blocks(blocks_ref, tiles_ref, 0)

    def put(pair, row, piece):
        lane = (pair % 2) * 128
        near_ref[pair // 2, pl.ds(row, 32), lane : lane + 128] = piece

    assemble_columns(inv_ref, core, tiles_ref, put)
    near_store = pltpu.make_async_copy(near_ref, near_out_ref, near_sem)
    near_store.start()
    loads[3].wait()
    shuffle_tokens(side, tok_ref, tokens_ref)
    loads[4].wait()
    stores = []
    for chunk in range(4):
        total = dot(tokens_ref[0], own_ref[chunk]) + dot(tokens_ref[1], near_ref[chunk])
        cols = slice(256 * chunk, 256 * (chunk + 1))
        total_ref[...] = total
        keep_ref[:, cols] = total_ref[pl.ds(pl.multiple_of(64 * zone, 64), 64), :]
        sent_ref[:, :, cols] = total.astype(BF).reshape(4, 64, 256)
        lanes = pl.ds(256 * chunk, 256)
        store = pltpu.make_async_copy(
            sent_ref.at[:, :, lanes], sent_out_ref.at[:, :, lanes], sent_sem.at[chunk]
        )
        store.start()
        stores.append(store)
    for store in stores:
        store.wait()
    near_store.wait()


def second_kernel(
    near_in_ref,
    weight_in_ref,
    tok_in_ref,
    keep_ref,
    out1_ref,
    out2_ref,
    out3_ref,
    near_ref,
    own_ref,
    tok_ref,
    tokens_ref,
    total_ref,
    in_sem,
):
    owner, unused_quarter, side, core = position()
    zone = owner // 2
    loads = [
        pltpu.make_async_copy(tok_in_ref, tok_ref, in_sem.at[0]),
        pltpu.make_async_copy(weight_in_ref.at[pl.ds(4 - 4 * core, 4)], own_ref, in_sem.at[1]),
        pltpu.make_async_copy(near_in_ref, near_ref, in_sem.at[2]),
    ]
    for load in loads:
        load.start()
    loads[0].wait()
    shuffle_tokens(side, tok_ref, tokens_ref)
    loads[1].wait()
    loads[2].wait()
    for chunk in range(4):
        total = dot(tokens_ref[0], own_ref[chunk]) + dot(tokens_ref[1], near_ref[chunk])
        cols = slice(256 * chunk, 256 * (chunk + 1))
        total_ref[...] = total
        keep_ref[:, cols] = total_ref[pl.ds(pl.multiple_of(64 * zone, 64), 64), :]
        for flip, ref in enumerate((out1_ref, out2_ref, out3_ref), 1):
            row = pl.multiple_of(64 * flipped(zone, flip), 64)
            ref[:, cols] = total_ref[pl.ds(row, 64), :].astype(BF)


def middle_kernel(
    first_keep_ref,
    first_ref,
    second_keep_ref,
    second1_ref,
    second2_ref,
    second3_ref,
    pay0_ref,
    pay1_ref,
    pay2_ref,
    pay3_ref,
    mine_ref,
    theirs_ref,
    lead_ref,
    act_ref,
    pay_ref,
    proj_ref,
    tangent_ref,
    rows_ref,
):
    owner, quarter, unused_side, core = position()
    zone = owner // 2
    unshuffle = unshuffle_matrix(256)
    for flip, ref in enumerate((pay0_ref, pay1_ref, pay2_ref, pay3_ref)):
        pay_ref[flipped(quarter, flip)] = ref[...]
    for chunk in range(4):
        cols = slice(256 * chunk, 256 * (chunk + 1))
        proj_ref[:, cols] = dot(pay_ref[chunk, 32:64, :].astype(BF), unshuffle).astype(BF)
        first = first_keep_ref[:, cols]
        for flip in (1, 2, 3):
            first = first + first_ref[flipped(zone, flip), :, cols].astype(F32)
        second = second_keep_ref[:, cols]
        for ref in (second1_ref, second2_ref, second3_ref):
            second = second + ref[:, cols].astype(F32)
        gate_pre = jnp.where(core == 0, first, second)
        up_pre = jnp.where(core == 0, second, first)
        sigmoid_g = jax.nn.sigmoid(gate_pre)
        activated = gate_pre * sigmoid_g
        slope_g = sigmoid_g * (1.0 + gate_pre * (1.0 - sigmoid_g))
        lead = slope_g * up_pre
        lead_ref[:, cols] = lead
        act_ref[:, cols] = activated
        for probe in range(P_SIZE):
            probe_gate = pay_ref[chunk, probe : probe + 1, :]
            probe_up = pay_ref[chunk, 16 + probe : 17 + probe, :]
            tangent_ref[64 * probe : 64 * (probe + 1), cols] = (
                lead * probe_gate + activated * probe_up
            ).astype(BF)
    rows_ref[...] = contract_last(tangent_ref[...], proj_ref[...]).astype(BF)
    for step in range(P_SIZE):
        probe = lax.rem(step + 8 * core, P_SIZE)
        backward = dot(rows_ref[pl.ds(pl.multiple_of(probe * 64, 64), 64), :], proj_ref[...])
        target = mine_ref if step < 8 else theirs_ref
        row = slice(step % 8, step % 8 + 1)
        target[row, :1024] = jnp.sum(backward * lead_ref[...], axis=0, keepdims=True)
        target[row, 1024:] = jnp.sum(backward * act_ref[...], axis=0, keepdims=True)


def fetch_kernel(weight_in_ref, weight_out_ref, sem):
    copy = pltpu.make_async_copy(weight_in_ref, weight_out_ref, sem)
    copy.start()
    copy.wait()


def product_kernel(mine_ref, theirs_ref, weight_ref, out_ref, sum_ref):
    core = lax.axis_index("seq")
    sum_ref[core] = mine_ref[...]
    sum_ref[1 - core] = theirs_ref[...]
    sums = jnp.concatenate([sum_ref[0], sum_ref[1]], axis=0).astype(BF)
    total = None
    for chunk in range(8):
        term = contract_last(sums[:, 256 * chunk : 256 * (chunk + 1)], weight_ref[chunk])
        total = term if total is None else total + term
    unshuffle = unshuffle_matrix(256)
    for group in range(4):
        cols = slice(256 * group, 256 * (group + 1))
        high, mid, low = split3(total[:, cols])
        out_ref[:, cols] = dot(high, unshuffle) + dot(mid, unshuffle) + dot(low, unshuffle)


def pair_split(
    tokens,
    gate_blocks,
    gate_slot,
    up_blocks,
    up_slot,
    down_blocks,
    down_slot,
    sketch,
    probe_index,
    probe_value,
):
    def owner_flip(value, bits):
        return lax.ppermute(value, "fsdp", [(i, i ^ bits) for i in range(8)])

    def core_flip(value):
        return lax.ppermute(value, "seq", [(0, 1), (1, 0)])

    def zone_exchange(value):
        return lax.all_to_all(
            value,
            "fsdp",
            split_axis=0,
            concat_axis=0,
            tiled=True,
            axis_index_groups=[[0, 2, 4, 6], [1, 3, 5, 7]],
        )

    by_zone, kind_a, kind_b = pl.pallas_call(
        head_kernel,
        out_shape=(
            jax.ShapeDtypeStruct((4, 64, 2048), BF),
            jax.ShapeDtypeStruct((SHARED, 4096), BF),
            jax.ShapeDtypeStruct((160 - 2 * SHARED, 4096), BF),
        ),
        in_specs=[HBM, HBM, HBM],
        out_specs=(HBM,) * 3,
        scratch_shapes=[
            pltpu.VMEM((4, 64, 2048), BF),
            pltpu.VMEM((160, 4096), BF),
            pltpu.SemaphoreType.DMA((12,)),
        ],
        compiler_params=params(60),
        name="head",
    )(tokens, gate_blocks, up_blocks)
    near_a = owner_flip(kind_a, 1)
    near_b = owner_flip(kind_b, 1)
    gathered = zone_exchange(by_zone)

    slots = jnp.stack([gate_slot, up_slot, down_slot])
    cells = lax.broadcasted_iota(jnp.int32, (3, 160, 256), 2)
    slot_numbers = lax.broadcasted_iota(jnp.int32, (3, 160, 256), 1)
    inv = jnp.min(jnp.where(slots[:, :, None] == cells, slot_numbers, 160), axis=1)
    near_inv = owner_flip(inv, 1)

    weights, payload = pl.pallas_call(
        own_kernel,
        out_shape=(
            jax.ShapeDtypeStruct((8, 1024, 256), BF),
            jax.ShapeDtypeStruct((64, 256), F32),
        ),
        in_specs=[SMEM] + [HBM] * 3 + [VMEM] * 3,
        out_specs=(HBM, VMEM),
        scratch_shapes=[
            pltpu.VMEM((32 * STRIDE, 128), F32),
            pltpu.VMEM((128, 128), F32),
            pltpu.VMEM((48, 1024), BF),
            pltpu.VMEM((256, 1024), BF),
            pltpu.VMEM((3, 160, 4096), BF),
            pltpu.VMEM((8, 1024, 256), BF),
            pltpu.SemaphoreType.DMA((3,)),
            pltpu.SemaphoreType.DMA((2,)),
        ],
        compiler_params=params(60),
        name="own_blocks",
    )(inv, gate_blocks, up_blocks, down_blocks, sketch, probe_index, probe_value)

    near_a, payload = lax.optimization_barrier((near_a, payload))
    near_a_other = lax.ppermute(near_a, "groups", [(0, 1), (1, 0)])
    for bits in (2, 4):
        payload = payload + owner_flip(payload, bits)
    near_inv, near_b, near_a_other, gathered, payload = lax.optimization_barrier(
        (near_inv, near_b, near_a_other, gathered, payload)
    )

    first_keep, first_sent, near_weights = pl.pallas_call(
        first_kernel,
        out_shape=(
            jax.ShapeDtypeStruct((64, 1024), F32),
            jax.ShapeDtypeStruct((4, 64, 1024), BF),
            jax.ShapeDtypeStruct((4, 1024, 256), BF),
        ),
        in_specs=[SMEM, ANY, ANY, ANY, HBM, ANY],
        out_specs=(VMEM, HBM, HBM),
        scratch_shapes=[
            pltpu.VMEM((160, 4096), BF),
            pltpu.VMEM((32 * STRIDE, 128), F32),
            pltpu.VMEM((4, 1024, 256), BF),
            pltpu.VMEM((4, 1024, 256), BF),
            pltpu.VMEM((4, 64, 2048), BF),
            pltpu.VMEM((2, 256, 1024), BF),
            pltpu.VMEM((4, 64, 1024), BF),
            pltpu.VMEM((256, 256), F32),
            pltpu.SemaphoreType.DMA((5,)),
            pltpu.SemaphoreType.DMA,
            pltpu.SemaphoreType.DMA((4,)),
        ],
        compiler_params=params(53),
        name="first_partial",
    )(near_inv, near_a, near_b, near_a_other, weights, gathered)
    first_back = zone_exchange(first_sent)

    second_keep, *second_sent = pl.pallas_call(
        second_kernel,
        out_shape=(jax.ShapeDtypeStruct((64, 1024), F32),)
        + (jax.ShapeDtypeStruct((64, 1024), BF),) * 3,
        in_specs=[ANY, HBM, ANY],
        out_specs=(VMEM,) * 4,
        scratch_shapes=[
            pltpu.VMEM((4, 1024, 256), BF),
            pltpu.VMEM((4, 1024, 256), BF),
            pltpu.VMEM((4, 64, 2048), BF),
            pltpu.VMEM((2, 256, 1024), BF),
            pltpu.VMEM((256, 256), F32),
            pltpu.SemaphoreType.DMA((3,)),
        ],
        compiler_params=params(50),
        name="second_partial",
    )(core_flip(near_weights), weights, gathered)
    second_back = [owner_flip(second_sent[flip - 1], 2 * flip) for flip in (1, 2, 3)]

    across = owner_flip(payload, 1)
    second_keep, across = lax.optimization_barrier((second_keep, across))
    payload = payload + across
    pay_parts = [
        payload,
        core_flip(payload),
        lax.ppermute(payload, "groups", [(0, 1), (1, 0)]),
        lax.ppermute(payload, ("groups", "seq"), [(i, i ^ 3) for i in range(4)]),
    ]

    first_back, weights = lax.optimization_barrier((first_back, weights))
    weights_at_hand = pl.pallas_call(
        fetch_kernel,
        out_shape=jax.ShapeDtypeStruct((8, 1024, 256), BF),
        in_specs=[HBM],
        out_specs=VMEM,
        scratch_shapes=[pltpu.SemaphoreType.DMA],
        compiler_params=params(48),
        name="fetch_weights",
    )(weights)
    pay_parts[0], weights_at_hand = lax.optimization_barrier((pay_parts[0], weights_at_hand))

    mine, theirs = pl.pallas_call(
        middle_kernel,
        out_shape=(jax.ShapeDtypeStruct((8, 2048), F32),) * 2,
        in_specs=[VMEM] * 10,
        out_specs=(VMEM,) * 2,
        scratch_shapes=[
            pltpu.VMEM((64, 1024), F32),
            pltpu.VMEM((64, 1024), F32),
            pltpu.VMEM((4, 64, 256), F32),
            pltpu.VMEM((K, 1024), BF),
            pltpu.VMEM((64 * P_SIZE, 1024), BF),
            pltpu.VMEM((64 * P_SIZE, K), BF),
        ],
        compiler_params=params(48),
        name="token_sums",
    )(first_keep, first_back, second_keep, *second_back, *pay_parts)

    sums = mine + core_flip(theirs)
    x_part, z_part, xz_part = [owner_flip(sums, bits) for bits in (1, 2, 3)]
    sums = (sums + x_part) + (z_part + xz_part)
    sums = sums + owner_flip(sums, 4)

    return pl.pallas_call(
        product_kernel,
        out_shape=jax.ShapeDtypeStruct((P_SIZE, 1024), F32),
        in_specs=[VMEM, VMEM, VMEM],
        out_specs=VMEM,
        scratch_shapes=[pltpu.VMEM((2, 8, 2048), F32)],
        compiler_params=params(30),
        name="products",
    )(sums, core_flip(sums), weights_at_hand)


def per_device(tokens, gate_blocks, *rest):
    fits = (
        lax.axis_size("fsdp") == 8
        and lax.axis_size("seq") == 2
        and lax.axis_size("groups") == 2
        and tokens.shape == (64, 8192)
        and gate_blocks.shape == (160, 4096)
        and rest[-2].shape == (P_SIZE, 256)
    )
    return (pair_split if fits else hidden_split)(tokens, gate_blocks, *rest)


def solution(mesh):
    in_specs = (
        P(("groups", "fsdp", "seq"), None),
        P("fsdp", None),
        P("fsdp"),
        P("fsdp", None),
        P("fsdp"),
        P("fsdp", None),
        P("fsdp"),
        P(None, "fsdp"),
        P(),
        P(),
    )
    out_specs = P("groups", "fsdp")
    return jax.shard_map(
        per_device, mesh=mesh, in_specs=in_specs, out_specs=out_specs, check_vma=False
    )
```

```python
import functools

import jax
import jax.numpy as jnp
from jax import lax
from jax.experimental import pallas as pl
from jax.experimental.pallas import tpu as pltpu
from jax.sharding import PartitionSpec as P

HID_DEV = 128
BLK = 64
P_SIZE = 16
K = 32

BF = jnp.bfloat16
F32 = jnp.float32
VMEM = pl.BlockSpec(memory_space=pltpu.VMEM)
SMEM = pl.BlockSpec(memory_space=pltpu.SMEM)
HBM = pl.BlockSpec(memory_space=pltpu.HBM)
ANY = pl.BlockSpec(memory_space=pl.ANY)

STRIDE = 168
SHARED = 48


def params(mebibytes):
    return pltpu.CompilerParams(vmem_limit_bytes=int(mebibytes * 1024 * 1024))


def unpack(blocks, slot_ids, cell_total):
    holder = jnp.zeros((cell_total + 1, blocks.shape[1]), blocks.dtype)
    return holder.at[slot_ids].set(blocks)[:cell_total]


def contract_last(first_mat, second_mat):
    return lax.dot_general(
        first_mat, second_mat, (((1,), (1,)), ((), ())), preferred_element_type=jnp.float32
    )


def hidden_split(
    tokens,
    gate_blocks,
    gate_slot,
    up_blocks,
    up_slot,
    down_blocks,
    down_slot,
    sketch,
    probe_index,
    probe_value,
):
    owners = lax.axis_size("fsdp")
    model_width = tokens.shape[1]
    local_width = model_width // owners
    block_rows = local_width // BLK
    hidden = HID_DEV
    col_blocks = hidden * owners // BLK
    cell_total = block_rows * col_blocks
    gate_dense = unpack(gate_blocks, gate_slot, cell_total).reshape(
        block_rows, col_blocks, BLK, BLK
    )
    up_dense = unpack(up_blocks, up_slot, cell_total).reshape(block_rows, col_blocks, BLK, BLK)
    stacked = jnp.stack([gate_dense, up_dense], axis=1)
    stacked = stacked.reshape(block_rows, 2, owners, hidden // BLK, BLK, BLK)
    stacked = stacked.transpose(0, 4, 2, 1, 3, 5).reshape(local_width, owners * 2 * hidden)
    both_weights = lax.all_to_all(stacked, "fsdp", split_axis=1, concat_axis=0, tiled=True)
    picked = both_weights[probe_index].astype(jnp.float32)
    probe_both = jnp.sum(picked * probe_value[:, :, None], axis=1)
    preact = jnp.dot(
        lax.all_gather(tokens, "fsdp", axis=0, tiled=True),
        both_weights,
        preferred_element_type=jnp.float32,
    )
    row_count = preact.shape[0]
    gate_pre = preact[:, :hidden]
    up_pre = preact[:, hidden:]
    down_dense = unpack(down_blocks, down_slot, cell_total).reshape(
        col_blocks, block_rows, BLK, BLK
    )
    down_dense = down_dense.transpose(0, 2, 1, 3).reshape(col_blocks * BLK, local_width)
    down_rows = lax.all_to_all(down_dense, "fsdp", split_axis=0, concat_axis=1, tiled=True)
    full_sketch = lax.all_gather(sketch, "fsdp", axis=1, tiled=True)
    projected = contract_last(down_rows, full_sketch)
    projected = projected.astype(jnp.bfloat16)
    sigmoid_g = jax.nn.sigmoid(gate_pre)
    activated = gate_pre * sigmoid_g
    slope_g = sigmoid_g * (1.0 + gate_pre * (1.0 - sigmoid_g))
    lead_term = slope_g * up_pre
    tangent = (
        lead_term[:, None, :] * probe_both[None, :, :hidden]
        + activated[:, None, :] * probe_both[None, :, hidden:]
    )
    tangent = tangent.astype(jnp.bfloat16)
    partial_sketch = jnp.dot(
        tangent.reshape(row_count * P_SIZE, hidden), projected, preferred_element_type=jnp.float32
    )
    partial_sketch = partial_sketch.reshape(row_count, P_SIZE * K)
    sketch_rows = lax.psum(partial_sketch, "fsdp").astype(jnp.bfloat16)
    backward = contract_last(sketch_rows.reshape(row_count * P_SIZE, K), projected).reshape(
        row_count, P_SIZE, hidden
    )
    summed = jnp.concatenate(
        [
            jnp.sum(backward * lead_term[:, None, :], axis=0),
            jnp.sum(backward * activated[:, None, :], axis=0),
        ],
        axis=1,
    )
    summed = lax.psum(summed, "seq").astype(jnp.bfloat16)
    products = contract_last(summed, both_weights)
    return lax.psum_scatter(products, "fsdp", scatter_dimension=1, tiled=True)


def dot(a, b):
    return jnp.dot(a, b, preferred_element_type=F32)


def split3(value):
    high = value.astype(BF)
    rest = value - high.astype(F32)
    mid = rest.astype(BF)
    low = (rest - mid.astype(F32)).astype(BF)
    return high, mid, low


def shuffled(natural):
    return (natural // BLK) * BLK + (natural % 2) * (BLK // 2) + (natural % BLK) // 2


def shuffle_matrix(size):
    rows = lax.broadcasted_iota(jnp.int32, (size, size), 0)
    cols = lax.broadcasted_iota(jnp.int32, (size, size), 1)
    return jnp.where(shuffled(rows) == cols, 1.0, 0.0).astype(BF)


def unshuffle_matrix(size):
    rows = lax.broadcasted_iota(jnp.int32, (size, size), 0)
    cols = lax.broadcasted_iota(jnp.int32, (size, size), 1)
    return jnp.where(shuffled(cols) == rows, 1.0, 0.0).astype(BF)


def stage_blocks(blocks_ref, tiles_ref, first_slot):
    @pl.loop(0, blocks_ref.shape[0] // 16, unroll=2)
    def _(step):
        row = pl.multiple_of(step * 16, 16)
        target = pl.multiple_of(first_slot + row, 16)
        for chunk in range(32):
            piece = blocks_ref[pl.ds(row, 16), 128 * chunk : 128 * (chunk + 1)].astype(F32)
            tiles_ref[pl.ds(target + chunk * STRIDE, 16), :] = piece


def clear_empty_slot(tiles_ref):
    for chunk in range(32):
        tiles_ref[pl.ds(chunk * STRIDE + 160, 8), :] = jnp.zeros((8, 128), F32)


def assembled_pair(tiles_ref, left_slot, right_slot):
    left = tiles_ref[pl.ds(left_slot, 32, stride=STRIDE), :]
    right = tiles_ref[pl.ds(right_slot, 32, stride=STRIDE), :]
    low_half = lax.broadcasted_iota(jnp.int32, (32, 128), 1) < BLK
    straight = jnp.where(low_half, left, right)
    crossed = pltpu.roll(jnp.where(low_half, right, left), BLK, 1)
    even = jnp.where(low_half, straight, crossed)
    odd = jnp.where(low_half, crossed, straight)
    return even.astype(BF), odd.astype(BF)


def assemble_columns(inv_ref, inv_row, tiles_ref, put):
    @pl.loop(0, 16, unroll=4)
    def _(block_row):
        for pair in range(8):
            cell = block_row * 16 + 2 * pair
            even, odd = assembled_pair(
                tiles_ref, inv_ref[inv_row, cell], inv_ref[inv_row, cell + 1]
            )
            row = pl.multiple_of(block_row * BLK, BLK)
            put(pair, row, even)
            put(pair, row + BLK // 2, odd)


def position():
    owner = lax.axis_index("fsdp")
    core = lax.axis_index("seq")
    return owner, 2 * lax.axis_index("groups") + core, lax.rem(owner, 2), core


def head_kernel(
    tok_in_ref, gate_ref, up_ref, zone_out_ref, a_out_ref, b_out_ref, tok_ref, blocks_ref, sem
):
    unused_owner, quarter, unused_side, core = position()
    first = pl.multiple_of(SHARED * (quarter // 2), 16)
    a_part = pl.ds(first, SHARED)
    b_part = pl.ds(2 * SHARED, 160 - 2 * SHARED)
    loads, stores = [], []
    for zone in range(4):
        held = tok_ref.at[zone]
        lanes = pl.ds(2048 * zone, 2048)
        loads.append(pltpu.make_async_copy(tok_in_ref.at[:, lanes], held, sem.at[zone]))
        stores.append(pltpu.make_async_copy(held, zone_out_ref.at[zone], sem.at[4 + zone]))
    for load in loads:
        load.start()
    for kind, source in enumerate((gate_ref, up_ref)):

        @pl.when(core == kind)
        def _():
            pltpu.make_async_copy(source.at[a_part], blocks_ref.at[a_part], sem.at[8]).start()
            pltpu.make_async_copy(source.at[b_part], blocks_ref.at[b_part], sem.at[9]).start()

    for load, store in zip(loads, stores):
        load.wait()
        store.start()
    pltpu.make_async_copy(gate_ref.at[a_part], blocks_ref.at[a_part], sem.at[8]).wait()
    stores.append(pltpu.make_async_copy(blocks_ref.at[a_part], a_out_ref, sem.at[10]))
    stores[4].start()
    pltpu.make_async_copy(gate_ref.at[b_part], blocks_ref.at[b_part], sem.at[9]).wait()
    stores.append(pltpu.make_async_copy(blocks_ref.at[b_part], b_out_ref, sem.at[11]))
    stores[5].start()
    for store in stores:
        store.wait()


def own_kernel(
    inv_ref,
    gate_ref,
    up_ref,
    down_ref,
    sketch_ref,
    index_ref,
    value_ref,
    weight_out_ref,
    payload_ref,
    tiles_ref,
    omega_ref,
    split_ref,
    down_dense_ref,
    blocks_ref,
    weight_ref,
    in_sem,
    out_sem,
):
    owner, quarter, unused_side, unused_core = position()
    loads = [
        pltpu.make_async_copy(source, blocks_ref.at[i], in_sem.at[i])
        for i, source in enumerate((gate_ref, up_ref, down_ref))
    ]
    stores = [
        pltpu.make_async_copy(
            weight_ref.at[pl.ds(4 * i, 4)], weight_out_ref.at[pl.ds(4 * i, 4)], out_sem.at[i]
        )
        for i in range(2)
    ]
    for load in loads:
        load.start()
    clear_empty_slot(tiles_ref)

    for which in range(2):
        loads[which].wait()
        stage_blocks(blocks_ref.at[which], tiles_ref, 0)

        def put(pair, row, piece):
            lane = (pair % 2) * 128
            weight_ref[4 * which + pair // 2, pl.ds(row, 32), lane : lane + 128] = piece

        assemble_columns(inv_ref, which, tiles_ref, put)
        stores[which].start()

    loads[2].wait()
    stage_blocks(blocks_ref.at[2], tiles_ref, 0)
    for local_row in range(4):
        for pair in range(8):
            cell = (quarter * 4 + local_row) * 16 + 2 * pair
            even, odd = assembled_pair(tiles_ref, inv_ref[2, cell], inv_ref[2, cell + 1])
            row = local_row * BLK
            down_dense_ref[row : row + 32, 128 * pair : 128 * (pair + 1)] = even
            down_dense_ref[row + 32 : row + 64, 128 * pair : 128 * (pair + 1)] = odd
    payload_ref[32:64, :] = contract_last(sketch_ref[...], down_dense_ref[...])

    local = index_ref[...] - owner * 1024
    inside = (local >= 0) & (local < 1024)
    safe = jnp.where(inside, local, 0)
    spot = shuffled(safe)
    high_part = jnp.where(inside, spot // 128, -1)
    low_part = spot % 128
    values = value_ref[...]
    high_iota = lax.broadcasted_iota(jnp.int32, (8, 256), 0)
    low_iota = lax.broadcasted_iota(jnp.int32, (128, 256), 0)
    for probe in range(P_SIZE):
        picked = jnp.where(
            high_iota == high_part[probe : probe + 1, :], values[probe : probe + 1, :], 0.0
        )
        one_hot = jnp.where(low_iota == low_part[probe : probe + 1, :], 1.0, 0.0).astype(BF)
        terms = contract_last(jnp.concatenate(split3(picked), axis=0), one_hot)
        total = terms[:8] + terms[8:16] + terms[16:]
        omega_ref[8 * probe : 8 * (probe + 1), :] = total
    for high in range(8):
        piece = omega_ref[pl.ds(high, 16, stride=8), :]
        for part_index, part in enumerate(split3(piece)):
            split_ref[
                16 * part_index : 16 * (part_index + 1), 128 * high : 128 * (high + 1)
            ] = part
    for which in range(2):
        triple = dot(split_ref[...], weight_ref[4 * which + quarter])
        payload_ref[16 * which : 16 * (which + 1), :] = triple[:16] + triple[16:32] + triple[32:]
    for store in stores:
        store.wait()


def flipped(two_bits, flip):
    low_bit = lax.rem(two_bits + flip % 2, 2)
    return low_bit + 2 * lax.rem(two_bits // 2 + flip // 2, 2)


def shuffle_tokens(side, tok_ref, tokens_ref):
    shuffle = shuffle_matrix(256)
    for group in range(8):
        piece = tok_ref[:, :, 256 * group : 256 * (group + 1)].reshape(256, 256)
        half = lax.rem(group // 4 + side, 2)
        tokens_ref[half, :, 256 * (group % 4) : 256 * (group % 4 + 1)] = dot(piece, shuffle).astype(
            BF
        )


def first_kernel(
    inv_ref,
    a_in_ref,
    b_in_ref,
    a_other_ref,
    weight_in_ref,
    tok_in_ref,
    keep_ref,
    sent_out_ref,
    near_out_ref,
    tokens_out_ref,
    blocks_ref,
    tiles_ref,
    near_ref,
    own_ref,
    tok_ref,
    tokens_ref,
    sent_ref,
    total_ref,
    in_sem,
    near_sem,
    sent_sem,
):
    owner, quarter, side, core = position()
    zone = owner // 2
    group = quarter // 2
    mine = pl.multiple_of(SHARED * group, 16)
    other = pl.multiple_of(SHARED * (1 - group), 16)
    loads = [
        pltpu.make_async_copy(a_in_ref, blocks_ref.at[pl.ds(mine, SHARED)], in_sem.at[0]),
        pltpu.make_async_copy(a_other_ref, blocks_ref.at[pl.ds(other, SHARED)], in_sem.at[1]),
        pltpu.make_async_copy(
            b_in_ref, blocks_ref.at[pl.ds(2 * SHARED, 160 - 2 * SHARED)], in_sem.at[2]
        ),
        pltpu.make_async_copy(tok_in_ref, tok_ref, in_sem.at[3]),
        pltpu.make_async_copy(weight_in_ref.at[pl.ds(4 * core, 4)], own_ref, in_sem.at[4]),
    ]
    for load in loads:
        load.start()
    clear_empty_slot(tiles_ref)
    for load in loads[:3]:
        load.wait()
    stage_blocks(blocks_ref, tiles_ref, 0)

    def put(pair, row, piece):
        lane = (pair % 2) * 128
        near_ref[pair // 2, pl.ds(row, 32), lane : lane + 128] = piece

    assemble_columns(inv_ref, core, tiles_ref, put)
    near_store = pltpu.make_async_copy(near_ref, near_out_ref, near_sem.at[0])
    near_store.start()
    loads[3].wait()
    shuffle_tokens(side, tok_ref, tokens_ref)
    tokens_store = pltpu.make_async_copy(tokens_ref, tokens_out_ref, near_sem.at[1])
    tokens_store.start()
    loads[4].wait()
    stores = []
    for chunk in range(4):
        total = dot(tokens_ref[0], own_ref[chunk]) + dot(tokens_ref[1], near_ref[chunk])
        cols = slice(256 * chunk, 256 * (chunk + 1))
        total_ref[...] = total
        keep_ref[:, cols] = total_ref[pl.ds(pl.multiple_of(64 * zone, 64), 64), :]
        sent_ref[:, :, cols] = total.astype(BF).reshape(4, 64, 256)
        lanes = pl.ds(256 * chunk, 256)
        store = pltpu.make_async_copy(
            sent_ref.at[:, :, lanes], sent_out_ref.at[:, :, lanes], sent_sem.at[chunk]
        )
        store.start()
        stores.append(store)
    for store in stores:
        store.wait()
    near_store.wait()
    tokens_store.wait()


def second_kernel(
    near_in_ref,
    weight_in_ref,
    tokens_in_ref,
    keep_ref,
    out1_ref,
    out2_ref,
    out3_ref,
    near_ref,
    own_ref,
    tokens_ref,
    total_ref,
    in_sem,
):
    owner, unused_quarter, unused_side, core = position()
    zone = owner // 2
    loads = [
        pltpu.make_async_copy(tokens_in_ref, tokens_ref, in_sem.at[0]),
        pltpu.make_async_copy(weight_in_ref.at[pl.ds(4 - 4 * core, 4)], own_ref, in_sem.at[1]),
        pltpu.make_async_copy(near_in_ref, near_ref, in_sem.at[2]),
    ]
    for load in loads:
        load.start()
    for load in loads:
        load.wait()
    for chunk in range(4):
        total = dot(tokens_ref[0], own_ref[chunk]) + dot(tokens_ref[1], near_ref[chunk])
        cols = slice(256 * chunk, 256 * (chunk + 1))
        total_ref[...] = total
        keep_ref[:, cols] = total_ref[pl.ds(pl.multiple_of(64 * zone, 64), 64), :]
        for flip, ref in enumerate((out1_ref, out2_ref, out3_ref), 1):
            row = pl.multiple_of(64 * flipped(zone, flip), 64)
            ref[:, cols] = total_ref[pl.ds(row, 64), :].astype(BF)


def middle_kernel(
    first_keep_ref,
    first_ref,
    second_keep_ref,
    second1_ref,
    second2_ref,
    second3_ref,
    pay0_ref,
    pay1_ref,
    pay2_ref,
    pay3_ref,
    mine_ref,
    theirs_ref,
    lead_ref,
    act_ref,
    pay_ref,
    proj_ref,
    tangent_ref,
    rows_ref,
):
    owner, quarter, unused_side, core = position()
    zone = owner // 2
    unshuffle = unshuffle_matrix(256)
    for flip, ref in enumerate((pay0_ref, pay1_ref, pay2_ref, pay3_ref)):
        pay_ref[flipped(quarter, flip)] = ref[...]
    for chunk in range(4):
        cols = slice(256 * chunk, 256 * (chunk + 1))
        proj_ref[:, cols] = dot(pay_ref[chunk, 32:64, :].astype(BF), unshuffle).astype(BF)
        first = first_keep_ref[:, cols]
        for flip in (1, 2, 3):
            first = first + first_ref[flipped(zone, flip), :, cols].astype(F32)
        second = second_keep_ref[:, cols]
        for ref in (second1_ref, second2_ref, second3_ref):
            second = second + ref[:, cols].astype(F32)
        gate_pre = jnp.where(core == 0, first, second)
        up_pre = jnp.where(core == 0, second, first)
        sigmoid_g = jax.nn.sigmoid(gate_pre)
        activated = gate_pre * sigmoid_g
        slope_g = sigmoid_g * (1.0 + gate_pre * (1.0 - sigmoid_g))
        lead = slope_g * up_pre
        lead_ref[:, cols] = lead
        act_ref[:, cols] = activated
        for probe in range(P_SIZE):
            probe_gate = pay_ref[chunk, probe : probe + 1, :]
            probe_up = pay_ref[chunk, 16 + probe : 17 + probe, :]
            tangent_ref[64 * probe : 64 * (probe + 1), cols] = (
                lead * probe_gate + activated * probe_up
            ).astype(BF)
    rows_ref[...] = contract_last(tangent_ref[...], proj_ref[...]).astype(BF)
    for step in range(P_SIZE):
        probe = lax.rem(step + 8 * core, P_SIZE)
        backward = dot(rows_ref[pl.ds(pl.multiple_of(probe * 64, 64), 64), :], proj_ref[...])
        target = mine_ref if step < 8 else theirs_ref
        row = slice(step % 8, step % 8 + 1)
        target[row, :1024] = jnp.sum(backward * lead_ref[...], axis=0, keepdims=True)
        target[row, 1024:] = jnp.sum(backward * act_ref[...], axis=0, keepdims=True)


def fetch_kernel(weight_in_ref, weight_out_ref, sem):
    copy = pltpu.make_async_copy(weight_in_ref, weight_out_ref, sem)
    copy.start()
    copy.wait()


def product_kernel(mine_ref, theirs_ref, weight_ref, out_ref, sum_ref):
    core = lax.axis_index("seq")
    sum_ref[core] = mine_ref[...]
    sum_ref[1 - core] = theirs_ref[...]
    sums = jnp.concatenate([sum_ref[0], sum_ref[1]], axis=0).astype(BF)
    total = None
    for chunk in range(8):
        term = contract_last(sums[:, 256 * chunk : 256 * (chunk + 1)], weight_ref[chunk])
        total = term if total is None else total + term
    unshuffle = unshuffle_matrix(256)
    for group in range(4):
        cols = slice(256 * group, 256 * (group + 1))
        high, mid, low = split3(total[:, cols])
        out_ref[:, cols] = dot(high, unshuffle) + dot(mid, unshuffle) + dot(low, unshuffle)


def pair_split(
    tokens,
    gate_blocks,
    gate_slot,
    up_blocks,
    up_slot,
    down_blocks,
    down_slot,
    sketch,
    probe_index,
    probe_value,
):
    def owner_flip(value, bits):
        return lax.ppermute(value, "fsdp", [(i, i ^ bits) for i in range(8)])

    def core_flip(value):
        return lax.ppermute(value, "seq", [(0, 1), (1, 0)])

    def zone_exchange(value):
        return lax.all_to_all(
            value,
            "fsdp",
            split_axis=0,
            concat_axis=0,
            tiled=True,
            axis_index_groups=[[0, 2, 4, 6], [1, 3, 5, 7]],
        )

    by_zone, kind_a, kind_b = pl.pallas_call(
        head_kernel,
        out_shape=(
            jax.ShapeDtypeStruct((4, 64, 2048), BF),
            jax.ShapeDtypeStruct((SHARED, 4096), BF),
            jax.ShapeDtypeStruct((160 - 2 * SHARED, 4096), BF),
        ),
        in_specs=[HBM, HBM, HBM],
        out_specs=(HBM,) * 3,
        scratch_shapes=[
            pltpu.VMEM((4, 64, 2048), BF),
            pltpu.VMEM((160, 4096), BF),
            pltpu.SemaphoreType.DMA((12,)),
        ],
        compiler_params=params(60),
        name="head",
    )(tokens, gate_blocks, up_blocks)
    near_a = owner_flip(kind_a, 1)
    near_b = owner_flip(kind_b, 1)
    gathered = zone_exchange(by_zone)

    slots = jnp.stack([gate_slot, up_slot, down_slot])
    cells = lax.broadcasted_iota(jnp.int32, (3, 160, 256), 2)
    slot_numbers = lax.broadcasted_iota(jnp.int32, (3, 160, 256), 1)
    inv = jnp.min(jnp.where(slots[:, :, None] == cells, slot_numbers, 160), axis=1)
    near_inv = owner_flip(inv, 1)

    weights, payload = pl.pallas_call(
        own_kernel,
        out_shape=(
            jax.ShapeDtypeStruct((8, 1024, 256), BF),
            jax.ShapeDtypeStruct((64, 256), F32),
        ),
        in_specs=[SMEM] + [HBM] * 3 + [VMEM] * 3,
        out_specs=(HBM, VMEM),
        scratch_shapes=[
            pltpu.VMEM((32 * STRIDE, 128), F32),
            pltpu.VMEM((128, 128), F32),
            pltpu.VMEM((48, 1024), BF),
            pltpu.VMEM((256, 1024), BF),
            pltpu.VMEM((3, 160, 4096), BF),
            pltpu.VMEM((8, 1024, 256), BF),
            pltpu.SemaphoreType.DMA((3,)),
            pltpu.SemaphoreType.DMA((2,)),
        ],
        compiler_params=params(60),
        name="own_blocks",
    )(inv, gate_blocks, up_blocks, down_blocks, sketch, probe_index, probe_value)

    near_a, payload = lax.optimization_barrier((near_a, payload))
    near_a_other = lax.ppermute(near_a, "groups", [(0, 1), (1, 0)])
    for bits in (2, 4):
        payload = payload + owner_flip(payload, bits)
    near_inv, near_b, near_a_other, gathered, payload = lax.optimization_barrier(
        (near_inv, near_b, near_a_other, gathered, payload)
    )

    first_keep, first_sent, near_weights, shuffled_tokens = pl.pallas_call(
        first_kernel,
        out_shape=(
            jax.ShapeDtypeStruct((64, 1024), F32),
            jax.ShapeDtypeStruct((4, 64, 1024), BF),
            jax.ShapeDtypeStruct((4, 1024, 256), BF),
            jax.ShapeDtypeStruct((2, 256, 1024), BF),
        ),
        in_specs=[SMEM, ANY, ANY, ANY, HBM, ANY],
        out_specs=(VMEM, HBM, HBM, HBM),
        scratch_shapes=[
            pltpu.VMEM((160, 4096), BF),
            pltpu.VMEM((32 * STRIDE, 128), F32),
            pltpu.VMEM((4, 1024, 256), BF),
            pltpu.VMEM((4, 1024, 256), BF),
            pltpu.VMEM((4, 64, 2048), BF),
            pltpu.VMEM((2, 256, 1024), BF),
            pltpu.VMEM((4, 64, 1024), BF),
            pltpu.VMEM((256, 256), F32),
            pltpu.SemaphoreType.DMA((5,)),
            pltpu.SemaphoreType.DMA((2,)),
            pltpu.SemaphoreType.DMA((4,)),
        ],
        compiler_params=params(46),
        name="first_partial",
    )(near_inv, near_a, near_b, near_a_other, weights, gathered)
    first_back = zone_exchange(first_sent)

    second_keep, *second_sent = pl.pallas_call(
        second_kernel,
        out_shape=(jax.ShapeDtypeStruct((64, 1024), F32),)
        + (jax.ShapeDtypeStruct((64, 1024), BF),) * 3,
        in_specs=[ANY, HBM, ANY],
        out_specs=(VMEM,) * 4,
        scratch_shapes=[
            pltpu.VMEM((4, 1024, 256), BF),
            pltpu.VMEM((4, 1024, 256), BF),
            pltpu.VMEM((2, 256, 1024), BF),
            pltpu.VMEM((256, 256), F32),
            pltpu.SemaphoreType.DMA((3,)),
        ],
        compiler_params=params(56),
        name="second_partial",
    )(core_flip(near_weights), weights, shuffled_tokens)
    second_back = [owner_flip(second_sent[flip - 1], 2 * flip) for flip in (1, 2, 3)]

    across = owner_flip(payload, 1)
    second_keep, across = lax.optimization_barrier((second_keep, across))
    payload = payload + across
    pay_parts = [
        payload,
        core_flip(payload),
        lax.ppermute(payload, "groups", [(0, 1), (1, 0)]),
        lax.ppermute(payload, ("groups", "seq"), [(i, i ^ 3) for i in range(4)]),
    ]

    first_back, weights = lax.optimization_barrier((first_back, weights))
    weights_at_hand = pl.pallas_call(
        fetch_kernel,
        out_shape=jax.ShapeDtypeStruct((8, 1024, 256), BF),
        in_specs=[HBM],
        out_specs=VMEM,
        scratch_shapes=[pltpu.SemaphoreType.DMA],
        compiler_params=params(48),
        name="fetch_weights",
    )(weights)
    pay_parts[0], weights_at_hand = lax.optimization_barrier((pay_parts[0], weights_at_hand))

    mine, theirs = pl.pallas_call(
        middle_kernel,
        out_shape=(jax.ShapeDtypeStruct((8, 2048), F32),) * 2,
        in_specs=[VMEM] * 10,
        out_specs=(VMEM,) * 2,
        scratch_shapes=[
            pltpu.VMEM((64, 1024), F32),
            pltpu.VMEM((64, 1024), F32),
            pltpu.VMEM((4, 64, 256), F32),
            pltpu.VMEM((K, 1024), BF),
            pltpu.VMEM((64 * P_SIZE, 1024), BF),
            pltpu.VMEM((64 * P_SIZE, K), BF),
        ],
        compiler_params=params(48),
        name="token_sums",
    )(first_keep, first_back, second_keep, *second_back, *pay_parts)

    sums = mine + core_flip(theirs)
    x_part, z_part, xz_part = [owner_flip(sums, bits) for bits in (1, 2, 3)]
    sums = (sums + x_part) + (z_part + xz_part)
    sums = sums + owner_flip(sums, 4)

    return pl.pallas_call(
        product_kernel,
        out_shape=jax.ShapeDtypeStruct((P_SIZE, 1024), F32),
        in_specs=[VMEM, VMEM, VMEM],
        out_specs=VMEM,
        scratch_shapes=[pltpu.VMEM((2, 8, 2048), F32)],
        compiler_params=params(30),
        name="products",
    )(sums, core_flip(sums), weights_at_hand)


def per_device(tokens, gate_blocks, *rest):
    fits = (
        lax.axis_size("fsdp") == 8
        and lax.axis_size("seq") == 2
        and lax.axis_size("groups") == 2
        and tokens.shape == (64, 8192)
        and gate_blocks.shape == (160, 4096)
        and rest[-2].shape == (P_SIZE, 256)
    )
    return (pair_split if fits else hidden_split)(tokens, gate_blocks, *rest)


def solution(mesh):
    in_specs = (
        P(("groups", "fsdp", "seq"), None),
        P("fsdp", None),
        P("fsdp"),
        P("fsdp", None),
        P("fsdp"),
        P("fsdp", None),
        P("fsdp"),
        P(None, "fsdp"),
        P(),
        P(),
    )
    out_specs = P("groups", "fsdp")
    return jax.shard_map(
        per_device, mesh=mesh, in_specs=in_specs, out_specs=out_specs, check_vma=False
    )
```

```python
import functools

import jax
import jax.numpy as jnp
from jax import lax
from jax.experimental import pallas as pl
from jax.experimental.pallas import tpu as pltpu
from jax.sharding import PartitionSpec as P

HID_DEV = 128
BLK = 64
P_SIZE = 16
K = 32

BF = jnp.bfloat16
F32 = jnp.float32
VMEM = pl.BlockSpec(memory_space=pltpu.VMEM)
SMEM = pl.BlockSpec(memory_space=pltpu.SMEM)
HBM = pl.BlockSpec(memory_space=pltpu.HBM)
ANY = pl.BlockSpec(memory_space=pl.ANY)

STRIDE = 168
SHARED = 48


def params(mebibytes):
    return pltpu.CompilerParams(vmem_limit_bytes=int(mebibytes * 1024 * 1024))


def unpack(blocks, slot_ids, cell_total):
    holder = jnp.zeros((cell_total + 1, blocks.shape[1]), blocks.dtype)
    return holder.at[slot_ids].set(blocks)[:cell_total]


def contract_last(first_mat, second_mat):
    return lax.dot_general(
        first_mat, second_mat, (((1,), (1,)), ((), ())), preferred_element_type=jnp.float32
    )


def hidden_split(
    tokens,
    gate_blocks,
    gate_slot,
    up_blocks,
    up_slot,
    down_blocks,
    down_slot,
    sketch,
    probe_index,
    probe_value,
):
    owners = lax.axis_size("fsdp")
    model_width = tokens.shape[1]
    local_width = model_width // owners
    block_rows = local_width // BLK
    hidden = HID_DEV
    col_blocks = hidden * owners // BLK
    cell_total = block_rows * col_blocks
    gate_dense = unpack(gate_blocks, gate_slot, cell_total).reshape(
        block_rows, col_blocks, BLK, BLK
    )
    up_dense = unpack(up_blocks, up_slot, cell_total).reshape(block_rows, col_blocks, BLK, BLK)
    stacked = jnp.stack([gate_dense, up_dense], axis=1)
    stacked = stacked.reshape(block_rows, 2, owners, hidden // BLK, BLK, BLK)
    stacked = stacked.transpose(0, 4, 2, 1, 3, 5).reshape(local_width, owners * 2 * hidden)
    both_weights = lax.all_to_all(stacked, "fsdp", split_axis=1, concat_axis=0, tiled=True)
    picked = both_weights[probe_index].astype(jnp.float32)
    probe_both = jnp.sum(picked * probe_value[:, :, None], axis=1)
    preact = jnp.dot(
        lax.all_gather(tokens, "fsdp", axis=0, tiled=True),
        both_weights,
        preferred_element_type=jnp.float32,
    )
    row_count = preact.shape[0]
    gate_pre = preact[:, :hidden]
    up_pre = preact[:, hidden:]
    down_dense = unpack(down_blocks, down_slot, cell_total).reshape(
        col_blocks, block_rows, BLK, BLK
    )
    down_dense = down_dense.transpose(0, 2, 1, 3).reshape(col_blocks * BLK, local_width)
    down_rows = lax.all_to_all(down_dense, "fsdp", split_axis=0, concat_axis=1, tiled=True)
    full_sketch = lax.all_gather(sketch, "fsdp", axis=1, tiled=True)
    projected = contract_last(down_rows, full_sketch)
    projected = projected.astype(jnp.bfloat16)
    sigmoid_g = jax.nn.sigmoid(gate_pre)
    activated = gate_pre * sigmoid_g
    slope_g = sigmoid_g * (1.0 + gate_pre * (1.0 - sigmoid_g))
    lead_term = slope_g * up_pre
    tangent = (
        lead_term[:, None, :] * probe_both[None, :, :hidden]
        + activated[:, None, :] * probe_both[None, :, hidden:]
    )
    tangent = tangent.astype(jnp.bfloat16)
    partial_sketch = jnp.dot(
        tangent.reshape(row_count * P_SIZE, hidden), projected, preferred_element_type=jnp.float32
    )
    partial_sketch = partial_sketch.reshape(row_count, P_SIZE * K)
    sketch_rows = lax.psum(partial_sketch, "fsdp").astype(jnp.bfloat16)
    backward = contract_last(sketch_rows.reshape(row_count * P_SIZE, K), projected).reshape(
        row_count, P_SIZE, hidden
    )
    summed = jnp.concatenate(
        [
            jnp.sum(backward * lead_term[:, None, :], axis=0),
            jnp.sum(backward * activated[:, None, :], axis=0),
        ],
        axis=1,
    )
    summed = lax.psum(summed, "seq").astype(jnp.bfloat16)
    products = contract_last(summed, both_weights)
    return lax.psum_scatter(products, "fsdp", scatter_dimension=1, tiled=True)


def dot(a, b):
    return jnp.dot(a, b, preferred_element_type=F32)


def split3(value):
    high = value.astype(BF)
    rest = value - high.astype(F32)
    mid = rest.astype(BF)
    low = (rest - mid.astype(F32)).astype(BF)
    return high, mid, low


def shuffled(natural):
    return (natural // BLK) * BLK + (natural % 2) * (BLK // 2) + (natural % BLK) // 2


def shuffle_matrix(size):
    rows = lax.broadcasted_iota(jnp.int32, (size, size), 0)
    cols = lax.broadcasted_iota(jnp.int32, (size, size), 1)
    return jnp.where(shuffled(rows) == cols, 1.0, 0.0).astype(BF)


def unshuffle_matrix(size):
    rows = lax.broadcasted_iota(jnp.int32, (size, size), 0)
    cols = lax.broadcasted_iota(jnp.int32, (size, size), 1)
    return jnp.where(shuffled(cols) == rows, 1.0, 0.0).astype(BF)


def stage_blocks(blocks_ref, tiles_ref, first_slot):
    @pl.loop(0, blocks_ref.shape[0] // 16, unroll=2)
    def _(step):
        row = pl.multiple_of(step * 16, 16)
        target = pl.multiple_of(first_slot + row, 16)
        for chunk in range(32):
            piece = blocks_ref[pl.ds(row, 16), 128 * chunk : 128 * (chunk + 1)].astype(F32)
            tiles_ref[pl.ds(target + chunk * STRIDE, 16), :] = piece


def clear_empty_slot(tiles_ref):
    for chunk in range(32):
        tiles_ref[pl.ds(chunk * STRIDE + 160, 8), :] = jnp.zeros((8, 128), F32)


def assembled_pair(tiles_ref, left_slot, right_slot):
    left = tiles_ref[pl.ds(left_slot, 32, stride=STRIDE), :]
    right = tiles_ref[pl.ds(right_slot, 32, stride=STRIDE), :]
    low_half = lax.broadcasted_iota(jnp.int32, (32, 128), 1) < BLK
    straight = jnp.where(low_half, left, right)
    crossed = pltpu.roll(jnp.where(low_half, right, left), BLK, 1)
    even = jnp.where(low_half, straight, crossed)
    odd = jnp.where(low_half, crossed, straight)
    return even.astype(BF), odd.astype(BF)


def assemble_columns(inv_ref, inv_row, tiles_ref, put):
    @pl.loop(0, 16, unroll=4)
    def _(block_row):
        for pair in range(8):
            cell = block_row * 16 + 2 * pair
            even, odd = assembled_pair(
                tiles_ref, inv_ref[inv_row, cell], inv_ref[inv_row, cell + 1]
            )
            row = pl.multiple_of(block_row * BLK, BLK)
            put(pair, row, even)
            put(pair, row + BLK // 2, odd)


def position():
    owner = lax.axis_index("fsdp")
    core = lax.axis_index("seq")
    return owner, 2 * lax.axis_index("groups") + core, lax.rem(owner, 2), core


def head_kernel(
    tok_in_ref, gate_ref, up_ref, zone_out_ref, a_out_ref, b_out_ref, tok_ref, blocks_ref, sem
):
    unused_owner, quarter, unused_side, core = position()
    first = pl.multiple_of(SHARED * (quarter // 2), 16)
    a_part = pl.ds(first, SHARED)
    b_part = pl.ds(2 * SHARED, 160 - 2 * SHARED)
    loads, stores = [], []
    for zone in range(4):
        held = tok_ref.at[zone]
        lanes = pl.ds(2048 * zone, 2048)
        loads.append(pltpu.make_async_copy(tok_in_ref.at[:, lanes], held, sem.at[zone]))
        stores.append(pltpu.make_async_copy(held, zone_out_ref.at[zone], sem.at[4 + zone]))
    for load in loads:
        load.start()
    for kind, source in enumerate((gate_ref, up_ref)):

        @pl.when(core == kind)
        def _():
            pltpu.make_async_copy(source.at[a_part], blocks_ref.at[a_part], sem.at[8]).start()
            pltpu.make_async_copy(source.at[b_part], blocks_ref.at[b_part], sem.at[9]).start()

    for load, store in zip(loads, stores):
        load.wait()
        store.start()
    pltpu.make_async_copy(gate_ref.at[a_part], blocks_ref.at[a_part], sem.at[8]).wait()
    stores.append(pltpu.make_async_copy(blocks_ref.at[a_part], a_out_ref, sem.at[10]))
    stores[4].start()
    pltpu.make_async_copy(gate_ref.at[b_part], blocks_ref.at[b_part], sem.at[9]).wait()
    stores.append(pltpu.make_async_copy(blocks_ref.at[b_part], b_out_ref, sem.at[11]))
    stores[5].start()
    for store in stores:
        store.wait()


def own_kernel(
    inv_ref,
    gate_ref,
    up_ref,
    down_ref,
    sketch_ref,
    index_ref,
    value_ref,
    weight_out_ref,
    payload_ref,
    tiles_ref,
    omega_ref,
    split_ref,
    down_dense_ref,
    blocks_ref,
    weight_ref,
    in_sem,
    out_sem,
):
    owner, quarter, unused_side, unused_core = position()
    loads = [
        pltpu.make_async_copy(source, blocks_ref.at[i], in_sem.at[i])
        for i, source in enumerate((gate_ref, up_ref, down_ref))
    ]
    stores = [
        pltpu.make_async_copy(
            weight_ref.at[pl.ds(4 * i, 4)], weight_out_ref.at[pl.ds(4 * i, 4)], out_sem.at[i]
        )
        for i in range(2)
    ]
    for load in loads:
        load.start()
    clear_empty_slot(tiles_ref)

    for which in range(2):
        loads[which].wait()
        stage_blocks(blocks_ref.at[which], tiles_ref, 0)

        def put(pair, row, piece):
            lane = (pair % 2) * 128
            weight_ref[4 * which + pair // 2, pl.ds(row, 32), lane : lane + 128] = piece

        assemble_columns(inv_ref, which, tiles_ref, put)
        stores[which].start()

    loads[2].wait()
    stage_blocks(blocks_ref.at[2], tiles_ref, 0)
    for local_row in range(4):
        for pair in range(8):
            cell = (quarter * 4 + local_row) * 16 + 2 * pair
            even, odd = assembled_pair(tiles_ref, inv_ref[2, cell], inv_ref[2, cell + 1])
            row = local_row * BLK
            down_dense_ref[row : row + 32, 128 * pair : 128 * (pair + 1)] = even
            down_dense_ref[row + 32 : row + 64, 128 * pair : 128 * (pair + 1)] = odd
    payload_ref[32:64, :] = contract_last(sketch_ref[...], down_dense_ref[...])

    local = index_ref[...] - owner * 1024
    inside = (local >= 0) & (local < 1024)
    safe = jnp.where(inside, local, 0)
    spot = shuffled(safe)
    high_part = jnp.where(inside, spot // 128, -1)
    low_part = spot % 128
    values = value_ref[...]
    high_iota = lax.broadcasted_iota(jnp.int32, (8, 256), 0)
    low_iota = lax.broadcasted_iota(jnp.int32, (128, 256), 0)
    for probe in range(P_SIZE):
        picked = jnp.where(
            high_iota == high_part[probe : probe + 1, :], values[probe : probe + 1, :], 0.0
        )
        one_hot = jnp.where(low_iota == low_part[probe : probe + 1, :], 1.0, 0.0).astype(BF)
        terms = contract_last(jnp.concatenate(split3(picked), axis=0), one_hot)
        total = terms[:8] + terms[8:16] + terms[16:]
        omega_ref[8 * probe : 8 * (probe + 1), :] = total
    for high in range(8):
        piece = omega_ref[pl.ds(high, 16, stride=8), :]
        for part_index, part in enumerate(split3(piece)):
            split_ref[
                16 * part_index : 16 * (part_index + 1), 128 * high : 128 * (high + 1)
            ] = part
    for which in range(2):
        triple = dot(split_ref[...], weight_ref[4 * which + quarter])
        payload_ref[16 * which : 16 * (which + 1), :] = triple[:16] + triple[16:32] + triple[32:]
    for store in stores:
        store.wait()


def flipped(two_bits, flip):
    low_bit = lax.rem(two_bits + flip % 2, 2)
    return low_bit + 2 * lax.rem(two_bits // 2 + flip // 2, 2)


def shuffle_tokens(side, tok_ref, tokens_ref):
    shuffle = shuffle_matrix(256)
    for group in range(8):
        piece = tok_ref[:, :, 256 * group : 256 * (group + 1)].reshape(256, 256)
        half = lax.rem(group // 4 + side, 2)
        tokens_ref[half, :, 256 * (group % 4) : 256 * (group % 4 + 1)] = dot(piece, shuffle).astype(
            BF
        )


def first_kernel(
    inv_ref,
    a_in_ref,
    b_in_ref,
    a_other_ref,
    weight_in_ref,
    tok_in_ref,
    keep_ref,
    sent_out_ref,
    near_out_ref,
    tokens_out_ref,
    blocks_ref,
    tiles_ref,
    near_ref,
    own_ref,
    tok_ref,
    tokens_ref,
    sent_ref,
    total_ref,
    in_sem,
    near_sem,
    sent_sem,
):
    owner, quarter, side, core = position()
    zone = owner // 2
    group = quarter // 2
    mine = pl.multiple_of(SHARED * group, 16)
    other = pl.multiple_of(SHARED * (1 - group), 16)
    loads = [
        pltpu.make_async_copy(a_in_ref, blocks_ref.at[pl.ds(mine, SHARED)], in_sem.at[0]),
        pltpu.make_async_copy(a_other_ref, blocks_ref.at[pl.ds(other, SHARED)], in_sem.at[1]),
        pltpu.make_async_copy(
            b_in_ref, blocks_ref.at[pl.ds(2 * SHARED, 160 - 2 * SHARED)], in_sem.at[2]
        ),
        pltpu.make_async_copy(tok_in_ref, tok_ref, in_sem.at[3]),
        pltpu.make_async_copy(weight_in_ref.at[pl.ds(4 * core, 4)], own_ref, in_sem.at[4]),
    ]
    for load in loads:
        load.start()
    clear_empty_slot(tiles_ref)
    for load in loads[:3]:
        load.wait()
    stage_blocks(blocks_ref, tiles_ref, 0)

    def put(pair, row, piece):
        lane = (pair % 2) * 128
        near_ref[pair // 2, pl.ds(row, 32), lane : lane + 128] = piece

    assemble_columns(inv_ref, core, tiles_ref, put)
    near_store = pltpu.make_async_copy(near_ref, near_out_ref, near_sem.at[0])
    near_store.start()
    loads[3].wait()
    shuffle_tokens(side, tok_ref, tokens_ref)
    tokens_store = pltpu.make_async_copy(tokens_ref, tokens_out_ref, near_sem.at[1])
    tokens_store.start()
    loads[4].wait()
    stores = []
    for chunk in range(4):
        total = dot(tokens_ref[0], own_ref[chunk]) + dot(tokens_ref[1], near_ref[chunk])
        cols = slice(256 * chunk, 256 * (chunk + 1))
        total_ref[...] = total
        keep_ref[:, cols] = total_ref[pl.ds(pl.multiple_of(64 * zone, 64), 64), :]
        sent_ref[:, :, cols] = total.astype(BF).reshape(4, 64, 256)
        lanes = pl.ds(256 * chunk, 256)
        store = pltpu.make_async_copy(
            sent_ref.at[:, :, lanes], sent_out_ref.at[:, :, lanes], sent_sem.at[chunk]
        )
        store.start()
        stores.append(store)
    for store in stores:
        store.wait()
    near_store.wait()
    tokens_store.wait()


def second_kernel(
    near_in_ref,
    weight_in_ref,
    tokens_in_ref,
    keep_ref,
    out1_ref,
    out2_ref,
    out3_ref,
    near_ref,
    own_ref,
    tokens_ref,
    total_ref,
    in_sem,
):
    owner, unused_quarter, unused_side, core = position()
    zone = owner // 2
    loads = [
        pltpu.make_async_copy(tokens_in_ref, tokens_ref, in_sem.at[0]),
        pltpu.make_async_copy(weight_in_ref.at[pl.ds(4 - 4 * core, 4)], own_ref, in_sem.at[1]),
        pltpu.make_async_copy(near_in_ref, near_ref, in_sem.at[2]),
    ]
    for load in loads:
        load.start()
    for load in loads:
        load.wait()
    for chunk in range(4):
        total = dot(tokens_ref[0], own_ref[chunk]) + dot(tokens_ref[1], near_ref[chunk])
        cols = slice(256 * chunk, 256 * (chunk + 1))
        total_ref[...] = total
        keep_ref[:, cols] = total_ref[pl.ds(pl.multiple_of(64 * zone, 64), 64), :]
        for flip, ref in enumerate((out1_ref, out2_ref, out3_ref), 1):
            row = pl.multiple_of(64 * flipped(zone, flip), 64)
            ref[:, cols] = total_ref[pl.ds(row, 64), :].astype(BF)


def middle_kernel(
    first_keep_ref,
    first_ref,
    second_keep_ref,
    second1_ref,
    second2_ref,
    second3_ref,
    pay0_ref,
    pay1_ref,
    pay2_ref,
    pay3_ref,
    mine_ref,
    theirs_ref,
    lead_ref,
    act_ref,
    pay_ref,
    proj_ref,
    tangent_ref,
    rows_ref,
):
    owner, quarter, unused_side, core = position()
    zone = owner // 2
    unshuffle = unshuffle_matrix(256)
    for flip, ref in enumerate((pay0_ref, pay1_ref, pay2_ref, pay3_ref)):
        pay_ref[flipped(quarter, flip)] = ref[...]
    for chunk in range(4):
        cols = slice(256 * chunk, 256 * (chunk + 1))
        proj_ref[:, cols] = dot(pay_ref[chunk, 32:64, :].astype(BF), unshuffle).astype(BF)
        first = first_keep_ref[:, cols]
        for flip in (1, 2, 3):
            first = first + first_ref[flipped(zone, flip), :, cols].astype(F32)
        second = second_keep_ref[:, cols]
        for ref in (second1_ref, second2_ref, second3_ref):
            second = second + ref[:, cols].astype(F32)
        gate_pre = jnp.where(core == 0, first, second)
        up_pre = jnp.where(core == 0, second, first)
        sigmoid_g = jax.nn.sigmoid(gate_pre)
        activated = gate_pre * sigmoid_g
        slope_g = sigmoid_g * (1.0 + gate_pre * (1.0 - sigmoid_g))
        lead = slope_g * up_pre
        lead_ref[:, cols] = lead
        act_ref[:, cols] = activated
        for probe in range(P_SIZE):
            probe_gate = pay_ref[chunk, probe : probe + 1, :]
            probe_up = pay_ref[chunk, 16 + probe : 17 + probe, :]
            tangent_ref[64 * probe : 64 * (probe + 1), cols] = (
                lead * probe_gate + activated * probe_up
            ).astype(BF)
    rows_ref[...] = contract_last(tangent_ref[...], proj_ref[...]).astype(BF)
    for step in range(P_SIZE):
        probe = lax.rem(step + 8 * core, P_SIZE)
        backward = dot(rows_ref[pl.ds(pl.multiple_of(probe * 64, 64), 64), :], proj_ref[...])
        target = mine_ref if step < 8 else theirs_ref
        row = slice(step % 8, step % 8 + 1)
        target[row, :1024] = jnp.sum(backward * lead_ref[...], axis=0, keepdims=True)
        target[row, 1024:] = jnp.sum(backward * act_ref[...], axis=0, keepdims=True)


def fetch_kernel(weight_in_ref, weight_out_ref, sem):
    copy = pltpu.make_async_copy(weight_in_ref, weight_out_ref, sem)
    copy.start()
    copy.wait()


def product_kernel(mine_ref, theirs_ref, weight_ref, out_ref, sum_ref):
    core = lax.axis_index("seq")
    sum_ref[core] = mine_ref[...]
    sum_ref[1 - core] = theirs_ref[...]
    sums = jnp.concatenate([sum_ref[0], sum_ref[1]], axis=0)
    total = None
    for chunk in range(8):
        term = contract_last(sums[:, 256 * chunk : 256 * (chunk + 1)], weight_ref[chunk])
        total = term if total is None else total + term
    unshuffle = unshuffle_matrix(256)
    for group in range(4):
        cols = slice(256 * group, 256 * (group + 1))
        high, mid, low = split3(total[:, cols])
        out_ref[:, cols] = dot(high, unshuffle) + dot(mid, unshuffle) + dot(low, unshuffle)


def pair_split(
    tokens,
    gate_blocks,
    gate_slot,
    up_blocks,
    up_slot,
    down_blocks,
    down_slot,
    sketch,
    probe_index,
    probe_value,
):
    def owner_flip(value, bits):
        return lax.ppermute(value, "fsdp", [(i, i ^ bits) for i in range(8)])

    def core_flip(value):
        return lax.ppermute(value, "seq", [(0, 1), (1, 0)])

    def zone_exchange(value):
        return lax.all_to_all(
            value,
            "fsdp",
            split_axis=0,
            concat_axis=0,
            tiled=True,
            axis_index_groups=[[0, 2, 4, 6], [1, 3, 5, 7]],
        )

    by_zone, kind_a, kind_b = pl.pallas_call(
        head_kernel,
        out_shape=(
            jax.ShapeDtypeStruct((4, 64, 2048), BF),
            jax.ShapeDtypeStruct((SHARED, 4096), BF),
            jax.ShapeDtypeStruct((160 - 2 * SHARED, 4096), BF),
        ),
        in_specs=[HBM, HBM, HBM],
        out_specs=(HBM,) * 3,
        scratch_shapes=[
            pltpu.VMEM((4, 64, 2048), BF),
            pltpu.VMEM((160, 4096), BF),
            pltpu.SemaphoreType.DMA((12,)),
        ],
        compiler_params=params(60),
        name="head",
    )(tokens, gate_blocks, up_blocks)
    near_a = owner_flip(kind_a, 1)
    near_b = owner_flip(kind_b, 1)
    gathered = zone_exchange(by_zone)

    slots = jnp.stack([gate_slot, up_slot, down_slot])
    cells = lax.broadcasted_iota(jnp.int32, (3, 160, 256), 2)
    slot_numbers = lax.broadcasted_iota(jnp.int32, (3, 160, 256), 1)
    inv = jnp.min(jnp.where(slots[:, :, None] == cells, slot_numbers, 160), axis=1)
    near_inv = owner_flip(inv, 1)

    weights, payload = pl.pallas_call(
        own_kernel,
        out_shape=(
            jax.ShapeDtypeStruct((8, 1024, 256), BF),
            jax.ShapeDtypeStruct((64, 256), F32),
        ),
        in_specs=[SMEM] + [HBM] * 3 + [VMEM] * 3,
        out_specs=(HBM, VMEM),
        scratch_shapes=[
            pltpu.VMEM((32 * STRIDE, 128), F32),
            pltpu.VMEM((128, 128), F32),
            pltpu.VMEM((48, 1024), BF),
            pltpu.VMEM((256, 1024), BF),
            pltpu.VMEM((3, 160, 4096), BF),
            pltpu.VMEM((8, 1024, 256), BF),
            pltpu.SemaphoreType.DMA((3,)),
            pltpu.SemaphoreType.DMA((2,)),
        ],
        compiler_params=params(60),
        name="own_blocks",
    )(inv, gate_blocks, up_blocks, down_blocks, sketch, probe_index, probe_value)

    near_a, payload = lax.optimization_barrier((near_a, payload))
    near_a_other = lax.ppermute(near_a, "groups", [(0, 1), (1, 0)])
    for bits in (2, 4):
        payload = payload + owner_flip(payload, bits)
    near_inv, near_b, near_a_other, gathered, payload = lax.optimization_barrier(
        (near_inv, near_b, near_a_other, gathered, payload)
    )

    first_keep, first_sent, near_weights, shuffled_tokens = pl.pallas_call(
        first_kernel,
        out_shape=(
            jax.ShapeDtypeStruct((64, 1024), F32),
            jax.ShapeDtypeStruct((4, 64, 1024), BF),
            jax.ShapeDtypeStruct((4, 1024, 256), BF),
            pltpu.HBM((2, 256, 1024), BF),
        ),
        in_specs=[SMEM, ANY, ANY, ANY, HBM, ANY],
        out_specs=(VMEM, HBM, HBM, HBM),
        scratch_shapes=[
            pltpu.VMEM((160, 4096), BF),
            pltpu.VMEM((32 * STRIDE, 128), F32),
            pltpu.VMEM((4, 1024, 256), BF),
            pltpu.VMEM((4, 1024, 256), BF),
            pltpu.VMEM((4, 64, 2048), BF),
            pltpu.VMEM((2, 256, 1024), BF),
            pltpu.VMEM((4, 64, 1024), BF),
            pltpu.VMEM((256, 256), F32),
            pltpu.SemaphoreType.DMA((5,)),
            pltpu.SemaphoreType.DMA((2,)),
            pltpu.SemaphoreType.DMA((4,)),
        ],
        compiler_params=params(46),
        name="first_partial",
    )(near_inv, near_a, near_b, near_a_other, weights, gathered)
    first_back = zone_exchange(first_sent)

    second_keep, *second_sent = pl.pallas_call(
        second_kernel,
        out_shape=(jax.ShapeDtypeStruct((64, 1024), F32),)
        + (jax.ShapeDtypeStruct((64, 1024), BF),) * 3,
        in_specs=[ANY, HBM, ANY],
        out_specs=(VMEM,) * 4,
        scratch_shapes=[
            pltpu.VMEM((4, 1024, 256), BF),
            pltpu.VMEM((4, 1024, 256), BF),
            pltpu.VMEM((2, 256, 1024), BF),
            pltpu.VMEM((256, 256), F32),
            pltpu.SemaphoreType.DMA((3,)),
        ],
        compiler_params=params(56),
        name="second_partial",
    )(core_flip(near_weights), weights, shuffled_tokens)
    second_back = [owner_flip(second_sent[flip - 1], 2 * flip) for flip in (1, 2, 3)]

    across = owner_flip(payload, 1)
    second_keep, across = lax.optimization_barrier((second_keep, across))
    payload = payload + across
    pay_parts = [
        payload,
        core_flip(payload),
        lax.ppermute(payload, "groups", [(0, 1), (1, 0)]),
        lax.ppermute(payload, ("groups", "seq"), [(i, i ^ 3) for i in range(4)]),
    ]

    first_back, weights = lax.optimization_barrier((first_back, weights))
    weights_at_hand = pl.pallas_call(
        fetch_kernel,
        out_shape=jax.ShapeDtypeStruct((8, 1024, 256), BF),
        in_specs=[HBM],
        out_specs=VMEM,
        scratch_shapes=[pltpu.SemaphoreType.DMA],
        compiler_params=params(48),
        name="fetch_weights",
    )(weights)
    pay_parts[0], weights_at_hand = lax.optimization_barrier((pay_parts[0], weights_at_hand))

    mine, theirs = pl.pallas_call(
        middle_kernel,
        out_shape=(jax.ShapeDtypeStruct((8, 2048), F32),) * 2,
        in_specs=[VMEM] * 10,
        out_specs=(VMEM,) * 2,
        scratch_shapes=[
            pltpu.VMEM((64, 1024), F32),
            pltpu.VMEM((64, 1024), F32),
            pltpu.VMEM((4, 64, 256), F32),
            pltpu.VMEM((K, 1024), BF),
            pltpu.VMEM((64 * P_SIZE, 1024), BF),
            pltpu.VMEM((64 * P_SIZE, K), BF),
        ],
        compiler_params=params(48),
        name="token_sums",
    )(first_keep, first_back, second_keep, *second_back, *pay_parts)

    sums = mine + core_flip(theirs)
    x_part, z_part, xz_part = [
        owner_flip(sums.astype(BF), bits).astype(F32) for bits in (1, 2, 3)
    ]
    sums = (sums + x_part) + (z_part + xz_part)
    sums = (sums + owner_flip(sums.astype(BF), 4).astype(F32)).astype(BF)

    return pl.pallas_call(
        product_kernel,
        out_shape=jax.ShapeDtypeStruct((P_SIZE, 1024), F32),
        in_specs=[VMEM, VMEM, VMEM],
        out_specs=VMEM,
        scratch_shapes=[pltpu.VMEM((2, 8, 2048), BF)],
        compiler_params=params(30),
        name="products",
    )(sums, core_flip(sums), weights_at_hand)


def per_device(tokens, gate_blocks, *rest):
    fits = (
        lax.axis_size("fsdp") == 8
        and lax.axis_size("seq") == 2
        and lax.axis_size("groups") == 2
        and tokens.shape == (64, 8192)
        and gate_blocks.shape == (160, 4096)
        and rest[-2].shape == (P_SIZE, 256)
    )
    return (pair_split if fits else hidden_split)(tokens, gate_blocks, *rest)


def solution(mesh):
    in_specs = (
        P(("groups", "fsdp", "seq"), None),
        P("fsdp", None),
        P("fsdp"),
        P("fsdp", None),
        P("fsdp"),
        P("fsdp", None),
        P("fsdp"),
        P(None, "fsdp"),
        P(),
        P(),
    )
    out_specs = P("groups", "fsdp")
    return jax.shard_map(
        per_device, mesh=mesh, in_specs=in_specs, out_specs=out_specs, check_vma=False
    )
```

```python
import functools

import jax
import jax.numpy as jnp
from jax import lax
from jax.experimental import pallas as pl
from jax.experimental.pallas import tpu as pltpu
from jax.sharding import PartitionSpec as P

HID_DEV = 128
BLK = 64
P_SIZE = 16
K = 32

BF = jnp.bfloat16
F32 = jnp.float32
VMEM = pl.BlockSpec(memory_space=pltpu.VMEM)
SMEM = pl.BlockSpec(memory_space=pltpu.SMEM)
HBM = pl.BlockSpec(memory_space=pltpu.HBM)
ANY = pl.BlockSpec(memory_space=pl.ANY)

STRIDE = 168
SHARED = 48


def params(mebibytes):
    return pltpu.CompilerParams(vmem_limit_bytes=int(mebibytes * 1024 * 1024))


def unpack(blocks, slot_ids, cell_total):
    holder = jnp.zeros((cell_total + 1, blocks.shape[1]), blocks.dtype)
    return holder.at[slot_ids].set(blocks)[:cell_total]


def contract_last(first_mat, second_mat):
    return lax.dot_general(
        first_mat, second_mat, (((1,), (1,)), ((), ())), preferred_element_type=jnp.float32
    )


def hidden_split(
    tokens,
    gate_blocks,
    gate_slot,
    up_blocks,
    up_slot,
    down_blocks,
    down_slot,
    sketch,
    probe_index,
    probe_value,
):
    owners = lax.axis_size("fsdp")
    model_width = tokens.shape[1]
    local_width = model_width // owners
    block_rows = local_width // BLK
    hidden = HID_DEV
    col_blocks = hidden * owners // BLK
    cell_total = block_rows * col_blocks
    gate_dense = unpack(gate_blocks, gate_slot, cell_total).reshape(
        block_rows, col_blocks, BLK, BLK
    )
    up_dense = unpack(up_blocks, up_slot, cell_total).reshape(block_rows, col_blocks, BLK, BLK)
    stacked = jnp.stack([gate_dense, up_dense], axis=1)
    stacked = stacked.reshape(block_rows, 2, owners, hidden // BLK, BLK, BLK)
    stacked = stacked.transpose(0, 4, 2, 1, 3, 5).reshape(local_width, owners * 2 * hidden)
    both_weights = lax.all_to_all(stacked, "fsdp", split_axis=1, concat_axis=0, tiled=True)
    picked = both_weights[probe_index].astype(jnp.float32)
    probe_both = jnp.sum(picked * probe_value[:, :, None], axis=1)
    preact = jnp.dot(
        lax.all_gather(tokens, "fsdp", axis=0, tiled=True),
        both_weights,
        preferred_element_type=jnp.float32,
    )
    row_count = preact.shape[0]
    gate_pre = preact[:, :hidden]
    up_pre = preact[:, hidden:]
    down_dense = unpack(down_blocks, down_slot, cell_total).reshape(
        col_blocks, block_rows, BLK, BLK
    )
    down_dense = down_dense.transpose(0, 2, 1, 3).reshape(col_blocks * BLK, local_width)
    down_rows = lax.all_to_all(down_dense, "fsdp", split_axis=0, concat_axis=1, tiled=True)
    full_sketch = lax.all_gather(sketch, "fsdp", axis=1, tiled=True)
    projected = contract_last(down_rows, full_sketch)
    projected = projected.astype(jnp.bfloat16)
    sigmoid_g = jax.nn.sigmoid(gate_pre)
    activated = gate_pre * sigmoid_g
    slope_g = sigmoid_g * (1.0 + gate_pre * (1.0 - sigmoid_g))
    lead_term = slope_g * up_pre
    tangent = (
        lead_term[:, None, :] * probe_both[None, :, :hidden]
        + activated[:, None, :] * probe_both[None, :, hidden:]
    )
    tangent = tangent.astype(jnp.bfloat16)
    partial_sketch = jnp.dot(
        tangent.reshape(row_count * P_SIZE, hidden), projected, preferred_element_type=jnp.float32
    )
    partial_sketch = partial_sketch.reshape(row_count, P_SIZE * K)
    sketch_rows = lax.psum(partial_sketch, "fsdp").astype(jnp.bfloat16)
    backward = contract_last(sketch_rows.reshape(row_count * P_SIZE, K), projected).reshape(
        row_count, P_SIZE, hidden
    )
    summed = jnp.concatenate(
        [
            jnp.sum(backward * lead_term[:, None, :], axis=0),
            jnp.sum(backward * activated[:, None, :], axis=0),
        ],
        axis=1,
    )
    summed = lax.psum(summed, "seq").astype(jnp.bfloat16)
    products = contract_last(summed, both_weights)
    return lax.psum_scatter(products, "fsdp", scatter_dimension=1, tiled=True)


def dot(a, b):
    return jnp.dot(a, b, preferred_element_type=F32)


def split3(value):
    high = value.astype(BF)
    rest = value - high.astype(F32)
    mid = rest.astype(BF)
    low = (rest - mid.astype(F32)).astype(BF)
    return high, mid, low


def shuffled(natural):
    return (natural // BLK) * BLK + (natural % 2) * (BLK // 2) + (natural % BLK) // 2


def shuffle_matrix(size):
    rows = lax.broadcasted_iota(jnp.int32, (size, size), 0)
    cols = lax.broadcasted_iota(jnp.int32, (size, size), 1)
    return jnp.where(shuffled(rows) == cols, 1.0, 0.0).astype(BF)


def unshuffle_matrix(size):
    rows = lax.broadcasted_iota(jnp.int32, (size, size), 0)
    cols = lax.broadcasted_iota(jnp.int32, (size, size), 1)
    return jnp.where(shuffled(cols) == rows, 1.0, 0.0).astype(BF)


def stage_blocks(blocks_ref, tiles_ref, first_slot):
    @pl.loop(0, blocks_ref.shape[0] // 16, unroll=2)
    def _(step):
        row = pl.multiple_of(step * 16, 16)
        target = pl.multiple_of(first_slot + row, 16)
        for chunk in range(32):
            piece = blocks_ref[pl.ds(row, 16), 128 * chunk : 128 * (chunk + 1)].astype(F32)
            tiles_ref[pl.ds(target + chunk * STRIDE, 16), :] = piece


def clear_empty_slot(tiles_ref):
    for chunk in range(32):
        tiles_ref[pl.ds(chunk * STRIDE + 160, 8), :] = jnp.zeros((8, 128), F32)


def assembled_pair(tiles_ref, left_slot, right_slot):
    left = tiles_ref[pl.ds(left_slot, 32, stride=STRIDE), :]
    right = tiles_ref[pl.ds(right_slot, 32, stride=STRIDE), :]
    low_half = lax.broadcasted_iota(jnp.int32, (32, 128), 1) < BLK
    straight = jnp.where(low_half, left, right)
    crossed = pltpu.roll(jnp.where(low_half, right, left), BLK, 1)
    even = jnp.where(low_half, straight, crossed)
    odd = jnp.where(low_half, crossed, straight)
    return even.astype(BF), odd.astype(BF)


def assemble_columns(inv_ref, inv_row, tiles_ref, put):
    @pl.loop(0, 16, unroll=4)
    def _(block_row):
        for pair in range(8):
            cell = block_row * 16 + 2 * pair
            even, odd = assembled_pair(
                tiles_ref, inv_ref[inv_row, cell], inv_ref[inv_row, cell + 1]
            )
            row = pl.multiple_of(block_row * BLK, BLK)
            put(pair, row, even)
            put(pair, row + BLK // 2, odd)


def position():
    owner = lax.axis_index("fsdp")
    core = lax.axis_index("seq")
    return owner, 2 * lax.axis_index("groups") + core, lax.rem(owner, 2), core


def head_kernel(
    tok_in_ref, gate_ref, up_ref, zone_out_ref, a_out_ref, b_out_ref, tok_ref, blocks_ref, sem
):
    unused_owner, quarter, unused_side, core = position()
    first = pl.multiple_of(SHARED * (quarter // 2), 16)
    a_part = pl.ds(first, SHARED)
    b_part = pl.ds(2 * SHARED, 160 - 2 * SHARED)
    loads, stores = [], []
    for zone in range(4):
        held = tok_ref.at[zone]
        lanes = pl.ds(2048 * zone, 2048)
        loads.append(pltpu.make_async_copy(tok_in_ref.at[:, lanes], held, sem.at[zone]))
        stores.append(pltpu.make_async_copy(held, zone_out_ref.at[zone], sem.at[4 + zone]))
    for load in loads:
        load.start()
    for kind, source in enumerate((gate_ref, up_ref)):

        @pl.when(core == kind)
        def _():
            pltpu.make_async_copy(source.at[a_part], blocks_ref.at[a_part], sem.at[8]).start()
            pltpu.make_async_copy(source.at[b_part], blocks_ref.at[b_part], sem.at[9]).start()

    for load, store in zip(loads, stores):
        load.wait()
        store.start()
    pltpu.make_async_copy(gate_ref.at[a_part], blocks_ref.at[a_part], sem.at[8]).wait()
    stores.append(pltpu.make_async_copy(blocks_ref.at[a_part], a_out_ref, sem.at[10]))
    stores[4].start()
    pltpu.make_async_copy(gate_ref.at[b_part], blocks_ref.at[b_part], sem.at[9]).wait()
    stores.append(pltpu.make_async_copy(blocks_ref.at[b_part], b_out_ref, sem.at[11]))
    stores[5].start()
    for store in stores:
        store.wait()


def own_kernel(
    inv_ref,
    gate_ref,
    up_ref,
    down_ref,
    sketch_ref,
    index_ref,
    value_ref,
    weight_out_ref,
    payload_ref,
    tiles_ref,
    omega_ref,
    split_ref,
    down_dense_ref,
    blocks_ref,
    weight_ref,
    in_sem,
    out_sem,
):
    owner, quarter, unused_side, unused_core = position()
    loads = [
        pltpu.make_async_copy(source, blocks_ref.at[i], in_sem.at[i])
        for i, source in enumerate((gate_ref, up_ref, down_ref))
    ]
    stores = [
        pltpu.make_async_copy(
            weight_ref.at[pl.ds(4 * i, 4)], weight_out_ref.at[pl.ds(4 * i, 4)], out_sem.at[i]
        )
        for i in range(2)
    ]
    for load in loads:
        load.start()
    clear_empty_slot(tiles_ref)

    for which in range(2):
        loads[which].wait()
        stage_blocks(blocks_ref.at[which], tiles_ref, 0)

        def put(pair, row, piece):
            lane = (pair % 2) * 128
            weight_ref[4 * which + pair // 2, pl.ds(row, 32), lane : lane + 128] = piece

        assemble_columns(inv_ref, which, tiles_ref, put)
        stores[which].start()

    loads[2].wait()
    stage_blocks(blocks_ref.at[2], tiles_ref, 0)
    for local_row in range(4):
        for pair in range(8):
            cell = (quarter * 4 + local_row) * 16 + 2 * pair
            even, odd = assembled_pair(tiles_ref, inv_ref[2, cell], inv_ref[2, cell + 1])
            row = local_row * BLK
            down_dense_ref[row : row + 32, 128 * pair : 128 * (pair + 1)] = even
            down_dense_ref[row + 32 : row + 64, 128 * pair : 128 * (pair + 1)] = odd
    payload_ref[32:64, :] = contract_last(sketch_ref[...], down_dense_ref[...])

    local = index_ref[...] - owner * 1024
    inside = (local >= 0) & (local < 1024)
    safe = jnp.where(inside, local, 0)
    spot = shuffled(safe)
    high_part = jnp.where(inside, spot // 128, -1)
    low_part = spot % 128
    values = value_ref[...]
    high_iota = lax.broadcasted_iota(jnp.int32, (8, 256), 0)
    low_iota = lax.broadcasted_iota(jnp.int32, (128, 256), 0)
    for probe in range(P_SIZE):
        picked = jnp.where(
            high_iota == high_part[probe : probe + 1, :], values[probe : probe + 1, :], 0.0
        )
        one_hot = jnp.where(low_iota == low_part[probe : probe + 1, :], 1.0, 0.0).astype(BF)
        terms = contract_last(jnp.concatenate(split3(picked), axis=0), one_hot)
        total = terms[:8] + terms[8:16] + terms[16:]
        omega_ref[8 * probe : 8 * (probe + 1), :] = total
    for high in range(8):
        piece = omega_ref[pl.ds(high, 16, stride=8), :]
        for part_index, part in enumerate(split3(piece)):
            split_ref[
                16 * part_index : 16 * (part_index + 1), 128 * high : 128 * (high + 1)
            ] = part
    for which in range(2):
        triple = dot(split_ref[...], weight_ref[4 * which + quarter])
        payload_ref[16 * which : 16 * (which + 1), :] = triple[:16] + triple[16:32] + triple[32:]
    for store in stores:
        store.wait()


def flipped(two_bits, flip):
    low_bit = lax.rem(two_bits + flip % 2, 2)
    return low_bit + 2 * lax.rem(two_bits // 2 + flip // 2, 2)


def shuffle_tokens(side, tok_ref, tokens_ref):
    shuffle = shuffle_matrix(256)
    for group in range(8):
        piece = tok_ref[:, :, 256 * group : 256 * (group + 1)].reshape(256, 256)
        half = lax.rem(group // 4 + side, 2)
        tokens_ref[half, :, 256 * (group % 4) : 256 * (group % 4 + 1)] = dot(piece, shuffle).astype(
            BF
        )


def first_kernel(
    inv_ref,
    a_in_ref,
    b_in_ref,
    a_other_ref,
    weight_in_ref,
    tok_in_ref,
    keep_ref,
    sent_out_ref,
    near_out_ref,
    tokens_out_ref,
    blocks_ref,
    tiles_ref,
    near_ref,
    own_ref,
    tok_ref,
    tokens_ref,
    sent_ref,
    total_ref,
    in_sem,
    near_sem,
    sent_sem,
):
    owner, quarter, side, core = position()
    zone = owner // 2
    group = quarter // 2
    mine = pl.multiple_of(SHARED * group, 16)
    other = pl.multiple_of(SHARED * (1 - group), 16)
    loads = [
        pltpu.make_async_copy(a_in_ref, blocks_ref.at[pl.ds(mine, SHARED)], in_sem.at[0]),
        pltpu.make_async_copy(a_other_ref, blocks_ref.at[pl.ds(other, SHARED)], in_sem.at[1]),
        pltpu.make_async_copy(
            b_in_ref, blocks_ref.at[pl.ds(2 * SHARED, 160 - 2 * SHARED)], in_sem.at[2]
        ),
        pltpu.make_async_copy(tok_in_ref, tok_ref, in_sem.at[3]),
        pltpu.make_async_copy(weight_in_ref.at[pl.ds(4 * core, 4)], own_ref, in_sem.at[4]),
    ]
    for load in loads:
        load.start()
    clear_empty_slot(tiles_ref)
    loads[3].wait()
    shuffle_tokens(side, tok_ref, tokens_ref)
    tokens_store = pltpu.make_async_copy(tokens_ref, tokens_out_ref, near_sem.at[1])
    tokens_store.start()
    for load in loads[:3]:
        load.wait()
    stage_blocks(blocks_ref, tiles_ref, 0)
    loads[4].wait()

    @pl.loop(0, 4)
    def _(step):
        total_ref[step] = dot(tokens_ref[0], own_ref[step])
        for inner in range(4):
            block_row = 4 * step + inner
            for pair in range(8):
                cell = block_row * 16 + 2 * pair
                even, odd = assembled_pair(tiles_ref, inv_ref[core, cell], inv_ref[core, cell + 1])
                row = pl.multiple_of(block_row * BLK, BLK)
                cols = slice((pair % 2) * 128, (pair % 2) * 128 + 128)
                near_ref[pair // 2, pl.ds(row, 32), cols] = even
                near_ref[pair // 2, pl.ds(row + 32, 32), cols] = odd

    near_store = pltpu.make_async_copy(near_ref, near_out_ref, near_sem.at[0])
    near_store.start()
    stores = []
    for chunk in range(4):
        total = total_ref[chunk] + dot(tokens_ref[1], near_ref[chunk])
        cols = slice(256 * chunk, 256 * (chunk + 1))
        total_ref[chunk] = total
        keep_ref[:, cols] = total_ref[chunk, pl.ds(pl.multiple_of(64 * zone, 64), 64), :]
        sent_ref[:, :, cols] = total.astype(BF).reshape(4, 64, 256)
        lanes = pl.ds(256 * chunk, 256)
        store = pltpu.make_async_copy(
            sent_ref.at[:, :, lanes], sent_out_ref.at[:, :, lanes], sent_sem.at[chunk]
        )
        store.start()
        stores.append(store)
    for store in stores:
        store.wait()
    near_store.wait()
    tokens_store.wait()


def second_kernel(
    near_in_ref,
    weight_in_ref,
    tokens_in_ref,
    keep_ref,
    out1_ref,
    out2_ref,
    out3_ref,
    near_ref,
    own_ref,
    tokens_ref,
    total_ref,
    in_sem,
):
    owner, unused_quarter, unused_side, core = position()
    zone = owner // 2
    loads = [
        pltpu.make_async_copy(tokens_in_ref, tokens_ref, in_sem.at[0]),
        pltpu.make_async_copy(weight_in_ref.at[pl.ds(4 - 4 * core, 4)], own_ref, in_sem.at[1]),
        pltpu.make_async_copy(near_in_ref, near_ref, in_sem.at[2]),
    ]
    for load in loads:
        load.start()
    for load in loads:
        load.wait()
    for chunk in range(4):
        total = dot(tokens_ref[0], own_ref[chunk]) + dot(tokens_ref[1], near_ref[chunk])
        cols = slice(256 * chunk, 256 * (chunk + 1))
        total_ref[...] = total
        keep_ref[:, cols] = total_ref[pl.ds(pl.multiple_of(64 * zone, 64), 64), :]
        for flip, ref in enumerate((out1_ref, out2_ref, out3_ref), 1):
            row = pl.multiple_of(64 * flipped(zone, flip), 64)
            ref[:, cols] = total_ref[pl.ds(row, 64), :].astype(BF)


def middle_kernel(
    first_keep_ref,
    first_ref,
    second_keep_ref,
    second1_ref,
    second2_ref,
    second3_ref,
    pay0_ref,
    pay1_ref,
    pay2_ref,
    pay3_ref,
    mine_ref,
    theirs_ref,
    lead_ref,
    act_ref,
    pay_ref,
    proj_ref,
    tangent_ref,
    rows_ref,
):
    owner, quarter, unused_side, core = position()
    zone = owner // 2
    unshuffle = unshuffle_matrix(256)
    for flip, ref in enumerate((pay0_ref, pay1_ref, pay2_ref, pay3_ref)):
        pay_ref[flipped(quarter, flip)] = ref[...]
    for chunk in range(4):
        cols = slice(256 * chunk, 256 * (chunk + 1))
        proj_ref[:, cols] = dot(pay_ref[chunk, 32:64, :].astype(BF), unshuffle).astype(BF)
        first = first_keep_ref[:, cols]
        for flip in (1, 2, 3):
            first = first + first_ref[flipped(zone, flip), :, cols].astype(F32)
        second = second_keep_ref[:, cols]
        for ref in (second1_ref, second2_ref, second3_ref):
            second = second + ref[:, cols].astype(F32)
        gate_pre = jnp.where(core == 0, first, second)
        up_pre = jnp.where(core == 0, second, first)
        sigmoid_g = jax.nn.sigmoid(gate_pre)
        activated = gate_pre * sigmoid_g
        slope_g = sigmoid_g * (1.0 + gate_pre * (1.0 - sigmoid_g))
        lead = slope_g * up_pre
        lead_ref[:, cols] = lead
        act_ref[:, cols] = activated
        for probe in range(P_SIZE):
            probe_gate = pay_ref[chunk, probe : probe + 1, :]
            probe_up = pay_ref[chunk, 16 + probe : 17 + probe, :]
            tangent_ref[64 * probe : 64 * (probe + 1), cols] = (
                lead * probe_gate + activated * probe_up
            ).astype(BF)
    rows_ref[...] = contract_last(tangent_ref[...], proj_ref[...]).astype(BF)
    for step in range(P_SIZE):
        probe = lax.rem(step + 8 * core, P_SIZE)
        backward = dot(rows_ref[pl.ds(pl.multiple_of(probe * 64, 64), 64), :], proj_ref[...])
        target = mine_ref if step < 8 else theirs_ref
        row = slice(step % 8, step % 8 + 1)
        target[row, :1024] = jnp.sum(backward * lead_ref[...], axis=0, keepdims=True)
        target[row, 1024:] = jnp.sum(backward * act_ref[...], axis=0, keepdims=True)


def fetch_kernel(weight_in_ref, weight_out_ref, sem):
    copy = pltpu.make_async_copy(weight_in_ref, weight_out_ref, sem)
    copy.start()
    copy.wait()


def product_kernel(mine_ref, theirs_ref, weight_ref, out_ref, sum_ref):
    core = lax.axis_index("seq")
    sum_ref[core] = mine_ref[...]
    sum_ref[1 - core] = theirs_ref[...]
    sums = jnp.concatenate([sum_ref[0], sum_ref[1]], axis=0)
    total = None
    for chunk in range(8):
        term = contract_last(sums[:, 256 * chunk : 256 * (chunk + 1)], weight_ref[chunk])
        total = term if total is None else total + term
    unshuffle = unshuffle_matrix(256)
    for group in range(4):
        cols = slice(256 * group, 256 * (group + 1))
        high, mid, low = split3(total[:, cols])
        out_ref[:, cols] = dot(high, unshuffle) + dot(mid, unshuffle) + dot(low, unshuffle)


def pair_split(
    tokens,
    gate_blocks,
    gate_slot,
    up_blocks,
    up_slot,
    down_blocks,
    down_slot,
    sketch,
    probe_index,
    probe_value,
):
    def owner_flip(value, bits):
        return lax.ppermute(value, "fsdp", [(i, i ^ bits) for i in range(8)])

    def core_flip(value):
        return lax.ppermute(value, "seq", [(0, 1), (1, 0)])

    def zone_exchange(value):
        return lax.all_to_all(
            value,
            "fsdp",
            split_axis=0,
            concat_axis=0,
            tiled=True,
            axis_index_groups=[[0, 2, 4, 6], [1, 3, 5, 7]],
        )

    by_zone, kind_a, kind_b = pl.pallas_call(
        head_kernel,
        out_shape=(
            jax.ShapeDtypeStruct((4, 64, 2048), BF),
            jax.ShapeDtypeStruct((SHARED, 4096), BF),
            jax.ShapeDtypeStruct((160 - 2 * SHARED, 4096), BF),
        ),
        in_specs=[HBM, HBM, HBM],
        out_specs=(HBM,) * 3,
        scratch_shapes=[
            pltpu.VMEM((4, 64, 2048), BF),
            pltpu.VMEM((160, 4096), BF),
            pltpu.SemaphoreType.DMA((12,)),
        ],
        compiler_params=params(60),
        name="head",
    )(tokens, gate_blocks, up_blocks)
    near_a = owner_flip(kind_a, 1)
    near_b = owner_flip(kind_b, 1)
    gathered = zone_exchange(by_zone)

    slots = jnp.stack([gate_slot, up_slot, down_slot])
    cells = lax.broadcasted_iota(jnp.int32, (3, 160, 256), 2)
    slot_numbers = lax.broadcasted_iota(jnp.int32, (3, 160, 256), 1)
    inv = jnp.min(jnp.where(slots[:, :, None] == cells, slot_numbers, 160), axis=1)
    near_inv = owner_flip(inv, 1)

    weights, payload = pl.pallas_call(
        own_kernel,
        out_shape=(
            jax.ShapeDtypeStruct((8, 1024, 256), BF),
            jax.ShapeDtypeStruct((64, 256), F32),
        ),
        in_specs=[SMEM] + [HBM] * 3 + [VMEM] * 3,
        out_specs=(HBM, VMEM),
        scratch_shapes=[
            pltpu.VMEM((32 * STRIDE, 128), F32),
            pltpu.VMEM((128, 128), F32),
            pltpu.VMEM((48, 1024), BF),
            pltpu.VMEM((256, 1024), BF),
            pltpu.VMEM((3, 160, 4096), BF),
            pltpu.VMEM((8, 1024, 256), BF),
            pltpu.SemaphoreType.DMA((3,)),
            pltpu.SemaphoreType.DMA((2,)),
        ],
        compiler_params=params(60),
        name="own_blocks",
    )(inv, gate_blocks, up_blocks, down_blocks, sketch, probe_index, probe_value)

    near_a, payload = lax.optimization_barrier((near_a, payload))
    near_a_other = lax.ppermute(near_a, "groups", [(0, 1), (1, 0)])
    for bits in (2, 4):
        payload = payload + owner_flip(payload, bits)
    near_inv, near_b, near_a_other, gathered, payload = lax.optimization_barrier(
        (near_inv, near_b, near_a_other, gathered, payload)
    )

    first_keep, first_sent, near_weights, shuffled_tokens = pl.pallas_call(
        first_kernel,
        out_shape=(
            jax.ShapeDtypeStruct((64, 1024), F32),
            jax.ShapeDtypeStruct((4, 64, 1024), BF),
            jax.ShapeDtypeStruct((4, 1024, 256), BF),
            pltpu.HBM((2, 256, 1024), BF),
        ),
        in_specs=[SMEM, ANY, ANY, ANY, HBM, ANY],
        out_specs=(VMEM, HBM, HBM, HBM),
        scratch_shapes=[
            pltpu.VMEM((160, 4096), BF),
            pltpu.VMEM((32 * STRIDE, 128), F32),
            pltpu.VMEM((4, 1024, 256), BF),
            pltpu.VMEM((4, 1024, 256), BF),
            pltpu.VMEM((4, 64, 2048), BF),
            pltpu.VMEM((2, 256, 1024), BF),
            pltpu.VMEM((4, 64, 1024), BF),
            pltpu.VMEM((4, 256, 256), F32),
            pltpu.SemaphoreType.DMA((5,)),
            pltpu.SemaphoreType.DMA((2,)),
            pltpu.SemaphoreType.DMA((4,)),
        ],
        compiler_params=params(46),
        name="first_partial",
    )(near_inv, near_a, near_b, near_a_other, weights, gathered)
    first_back = zone_exchange(first_sent)

    second_keep, *second_sent = pl.pallas_call(
        second_kernel,
        out_shape=(jax.ShapeDtypeStruct((64, 1024), F32),)
        + (jax.ShapeDtypeStruct((64, 1024), BF),) * 3,
        in_specs=[ANY, HBM, ANY],
        out_specs=(VMEM,) * 4,
        scratch_shapes=[
            pltpu.VMEM((4, 1024, 256), BF),
            pltpu.VMEM((4, 1024, 256), BF),
            pltpu.VMEM((2, 256, 1024), BF),
            pltpu.VMEM((256, 256), F32),
            pltpu.SemaphoreType.DMA((3,)),
        ],
        compiler_params=params(56),
        name="second_partial",
    )(core_flip(near_weights), weights, shuffled_tokens)
    second_back = [owner_flip(second_sent[flip - 1], 2 * flip) for flip in (1, 2, 3)]

    across = owner_flip(payload, 1)
    second_keep, across = lax.optimization_barrier((second_keep, across))
    payload = payload + across
    pay_parts = [
        payload,
        core_flip(payload),
        lax.ppermute(payload, "groups", [(0, 1), (1, 0)]),
        lax.ppermute(payload, ("groups", "seq"), [(i, i ^ 3) for i in range(4)]),
    ]

    first_back, weights = lax.optimization_barrier((first_back, weights))
    weights_at_hand = pl.pallas_call(
        fetch_kernel,
        out_shape=jax.ShapeDtypeStruct((8, 1024, 256), BF),
        in_specs=[HBM],
        out_specs=VMEM,
        scratch_shapes=[pltpu.SemaphoreType.DMA],
        compiler_params=params(48),
        name="fetch_weights",
    )(weights)
    pay_parts[0], weights_at_hand = lax.optimization_barrier((pay_parts[0], weights_at_hand))

    mine, theirs = pl.pallas_call(
        middle_kernel,
        out_shape=(jax.ShapeDtypeStruct((8, 2048), F32),) * 2,
        in_specs=[VMEM] * 10,
        out_specs=(VMEM,) * 2,
        scratch_shapes=[
            pltpu.VMEM((64, 1024), F32),
            pltpu.VMEM((64, 1024), F32),
            pltpu.VMEM((4, 64, 256), F32),
            pltpu.VMEM((K, 1024), BF),
            pltpu.VMEM((64 * P_SIZE, 1024), BF),
            pltpu.VMEM((64 * P_SIZE, K), BF),
        ],
        compiler_params=params(48),
        name="token_sums",
    )(first_keep, first_back, second_keep, *second_back, *pay_parts)

    sums = mine + core_flip(theirs)
    sums = sums + owner_flip(sums.astype(BF), 1).astype(F32)
    parts = [owner_flip(sums.astype(BF), bits).astype(F32) for bits in (2, 4, 6)]
    sums = ((sums + parts[0]) + (parts[1] + parts[2])).astype(BF)

    return pl.pallas_call(
        product_kernel,
        out_shape=jax.ShapeDtypeStruct((P_SIZE, 1024), F32),
        in_specs=[VMEM, VMEM, VMEM],
        out_specs=VMEM,
        scratch_shapes=[pltpu.VMEM((2, 8, 2048), BF)],
        compiler_params=params(30),
        name="products",
    )(sums, core_flip(sums), weights_at_hand)


def per_device(tokens, gate_blocks, *rest):
    fits = (
        lax.axis_size("fsdp") == 8
        and lax.axis_size("seq") == 2
        and lax.axis_size("groups") == 2
        and tokens.shape == (64, 8192)
        and gate_blocks.shape == (160, 4096)
        and rest[-2].shape == (P_SIZE, 256)
    )
    return (pair_split if fits else hidden_split)(tokens, gate_blocks, *rest)


def solution(mesh):
    in_specs = (
        P(("groups", "fsdp", "seq"), None),
        P("fsdp", None),
        P("fsdp"),
        P("fsdp", None),
        P("fsdp"),
        P("fsdp", None),
        P("fsdp"),
        P(None, "fsdp"),
        P(),
        P(),
    )
    out_specs = P("groups", "fsdp")
    return jax.shard_map(
        per_device, mesh=mesh, in_specs=in_specs, out_specs=out_specs, check_vma=False
    )
```

```python
import functools

import jax
import jax.numpy as jnp
from jax import lax
from jax.experimental import pallas as pl
from jax.experimental.pallas import tpu as pltpu
from jax.sharding import PartitionSpec as P

HID_DEV = 128
BLK = 64
P_SIZE = 16
K = 32

BF = jnp.bfloat16
F32 = jnp.float32
VMEM = pl.BlockSpec(memory_space=pltpu.VMEM)
SMEM = pl.BlockSpec(memory_space=pltpu.SMEM)
HBM = pl.BlockSpec(memory_space=pltpu.HBM)
ANY = pl.BlockSpec(memory_space=pl.ANY)

STRIDE = 168
SHARED = 48


def params(mebibytes):
    return pltpu.CompilerParams(vmem_limit_bytes=int(mebibytes * 1024 * 1024))


def unpack(blocks, slot_ids, cell_total):
    holder = jnp.zeros((cell_total + 1, blocks.shape[1]), blocks.dtype)
    return holder.at[slot_ids].set(blocks)[:cell_total]


def contract_last(first_mat, second_mat):
    return lax.dot_general(
        first_mat, second_mat, (((1,), (1,)), ((), ())), preferred_element_type=jnp.float32
    )


def hidden_split(
    tokens,
    gate_blocks,
    gate_slot,
    up_blocks,
    up_slot,
    down_blocks,
    down_slot,
    sketch,
    probe_index,
    probe_value,
):
    owners = lax.axis_size("fsdp")
    model_width = tokens.shape[1]
    local_width = model_width // owners
    block_rows = local_width // BLK
    hidden = HID_DEV
    col_blocks = hidden * owners // BLK
    cell_total = block_rows * col_blocks
    gate_dense = unpack(gate_blocks, gate_slot, cell_total).reshape(
        block_rows, col_blocks, BLK, BLK
    )
    up_dense = unpack(up_blocks, up_slot, cell_total).reshape(block_rows, col_blocks, BLK, BLK)
    stacked = jnp.stack([gate_dense, up_dense], axis=1)
    stacked = stacked.reshape(block_rows, 2, owners, hidden // BLK, BLK, BLK)
    stacked = stacked.transpose(0, 4, 2, 1, 3, 5).reshape(local_width, owners * 2 * hidden)
    both_weights = lax.all_to_all(stacked, "fsdp", split_axis=1, concat_axis=0, tiled=True)
    picked = both_weights[probe_index].astype(jnp.float32)
    probe_both = jnp.sum(picked * probe_value[:, :, None], axis=1)
    preact = jnp.dot(
        lax.all_gather(tokens, "fsdp", axis=0, tiled=True),
        both_weights,
        preferred_element_type=jnp.float32,
    )
    row_count = preact.shape[0]
    gate_pre = preact[:, :hidden]
    up_pre = preact[:, hidden:]
    down_dense = unpack(down_blocks, down_slot, cell_total).reshape(
        col_blocks, block_rows, BLK, BLK
    )
    down_dense = down_dense.transpose(0, 2, 1, 3).reshape(col_blocks * BLK, local_width)
    down_rows = lax.all_to_all(down_dense, "fsdp", split_axis=0, concat_axis=1, tiled=True)
    full_sketch = lax.all_gather(sketch, "fsdp", axis=1, tiled=True)
    projected = contract_last(down_rows, full_sketch)
    projected = projected.astype(jnp.bfloat16)
    sigmoid_g = jax.nn.sigmoid(gate_pre)
    activated = gate_pre * sigmoid_g
    slope_g = sigmoid_g * (1.0 + gate_pre * (1.0 - sigmoid_g))
    lead_term = slope_g * up_pre
    tangent = (
        lead_term[:, None, :] * probe_both[None, :, :hidden]
        + activated[:, None, :] * probe_both[None, :, hidden:]
    )
    tangent = tangent.astype(jnp.bfloat16)
    partial_sketch = jnp.dot(
        tangent.reshape(row_count * P_SIZE, hidden), projected, preferred_element_type=jnp.float32
    )
    partial_sketch = partial_sketch.reshape(row_count, P_SIZE * K)
    sketch_rows = lax.psum(partial_sketch, "fsdp").astype(jnp.bfloat16)
    backward = contract_last(sketch_rows.reshape(row_count * P_SIZE, K), projected).reshape(
        row_count, P_SIZE, hidden
    )
    summed = jnp.concatenate(
        [
            jnp.sum(backward * lead_term[:, None, :], axis=0),
            jnp.sum(backward * activated[:, None, :], axis=0),
        ],
        axis=1,
    )
    summed = lax.psum(summed, "seq").astype(jnp.bfloat16)
    products = contract_last(summed, both_weights)
    return lax.psum_scatter(products, "fsdp", scatter_dimension=1, tiled=True)


def dot(a, b):
    return jnp.dot(a, b, preferred_element_type=F32)


def split3(value):
    high = value.astype(BF)
    rest = value - high.astype(F32)
    mid = rest.astype(BF)
    low = (rest - mid.astype(F32)).astype(BF)
    return high, mid, low


def shuffled(natural):
    return (natural // BLK) * BLK + (natural % 2) * (BLK // 2) + (natural % BLK) // 2


def shuffle_matrix(size):
    rows = lax.broadcasted_iota(jnp.int32, (size, size), 0)
    cols = lax.broadcasted_iota(jnp.int32, (size, size), 1)
    return jnp.where(shuffled(rows) == cols, 1.0, 0.0).astype(BF)


def unshuffle_matrix(size):
    rows = lax.broadcasted_iota(jnp.int32, (size, size), 0)
    cols = lax.broadcasted_iota(jnp.int32, (size, size), 1)
    return jnp.where(shuffled(cols) == rows, 1.0, 0.0).astype(BF)


def stage_blocks(blocks_ref, tiles_ref, first_slot):
    @pl.loop(0, blocks_ref.shape[0] // 16, unroll=2)
    def _(step):
        row = pl.multiple_of(step * 16, 16)
        target = pl.multiple_of(first_slot + row, 16)
        for chunk in range(32):
            piece = blocks_ref[pl.ds(row, 16), 128 * chunk : 128 * (chunk + 1)].astype(F32)
            tiles_ref[pl.ds(target + chunk * STRIDE, 16), :] = piece


def clear_empty_slot(tiles_ref):
    for chunk in range(32):
        tiles_ref[pl.ds(chunk * STRIDE + 160, 8), :] = jnp.zeros((8, 128), F32)


def assembled_pair(tiles_ref, left_slot, right_slot):
    left = tiles_ref[pl.ds(left_slot, 32, stride=STRIDE), :]
    right = tiles_ref[pl.ds(right_slot, 32, stride=STRIDE), :]
    low_half = lax.broadcasted_iota(jnp.int32, (32, 128), 1) < BLK
    straight = jnp.where(low_half, left, right)
    crossed = pltpu.roll(jnp.where(low_half, right, left), BLK, 1)
    even = jnp.where(low_half, straight, crossed)
    odd = jnp.where(low_half, crossed, straight)
    return even.astype(BF), odd.astype(BF)


def assemble_columns(inv_ref, inv_row, tiles_ref, put):
    @pl.loop(0, 16, unroll=4)
    def _(block_row):
        for pair in range(8):
            cell = block_row * 16 + 2 * pair
            even, odd = assembled_pair(
                tiles_ref, inv_ref[inv_row, cell], inv_ref[inv_row, cell + 1]
            )
            row = pl.multiple_of(block_row * BLK, BLK)
            put(pair, row, even)
            put(pair, row + BLK // 2, odd)


def position():
    owner = lax.axis_index("fsdp")
    core = lax.axis_index("seq")
    return owner, 2 * lax.axis_index("groups") + core, lax.rem(owner, 2), core


def head_kernel(
    tok_in_ref, gate_ref, up_ref, zone_out_ref, a_out_ref, b_out_ref, tok_ref, blocks_ref, sem
):
    unused_owner, quarter, unused_side, core = position()
    first = pl.multiple_of(SHARED * (quarter // 2), 16)
    a_part = pl.ds(first, SHARED)
    b_part = pl.ds(2 * SHARED, 160 - 2 * SHARED)
    loads, stores = [], []
    for zone in range(4):
        held = tok_ref.at[zone]
        lanes = pl.ds(2048 * zone, 2048)
        loads.append(pltpu.make_async_copy(tok_in_ref.at[:, lanes], held, sem.at[zone]))
        stores.append(pltpu.make_async_copy(held, zone_out_ref.at[zone], sem.at[4 + zone]))
    for load in loads:
        load.start()
    for kind, source in enumerate((gate_ref, up_ref)):

        @pl.when(core == kind)
        def _():
            pltpu.make_async_copy(source.at[a_part], blocks_ref.at[a_part], sem.at[8]).start()
            pltpu.make_async_copy(source.at[b_part], blocks_ref.at[b_part], sem.at[9]).start()

    for load, store in zip(loads, stores):
        load.wait()
        store.start()
    pltpu.make_async_copy(gate_ref.at[a_part], blocks_ref.at[a_part], sem.at[8]).wait()
    stores.append(pltpu.make_async_copy(blocks_ref.at[a_part], a_out_ref, sem.at[10]))
    stores[4].start()
    pltpu.make_async_copy(gate_ref.at[b_part], blocks_ref.at[b_part], sem.at[9]).wait()
    stores.append(pltpu.make_async_copy(blocks_ref.at[b_part], b_out_ref, sem.at[11]))
    stores[5].start()
    for store in stores:
        store.wait()


def own_kernel(
    inv_ref,
    gate_ref,
    up_ref,
    down_ref,
    sketch_ref,
    index_ref,
    value_ref,
    weight_out_ref,
    payload_ref,
    tiles_ref,
    omega_ref,
    split_ref,
    down_dense_ref,
    blocks_ref,
    weight_ref,
    in_sem,
    out_sem,
):
    owner, quarter, unused_side, unused_core = position()
    loads = [
        pltpu.make_async_copy(source, blocks_ref.at[i], in_sem.at[i])
        for i, source in enumerate((gate_ref, up_ref, down_ref))
    ]
    stores = [
        pltpu.make_async_copy(
            weight_ref.at[pl.ds(4 * i, 4)], weight_out_ref.at[pl.ds(4 * i, 4)], out_sem.at[i]
        )
        for i in range(2)
    ]
    for load in loads:
        load.start()
    clear_empty_slot(tiles_ref)

    for which in range(2):
        loads[which].wait()
        stage_blocks(blocks_ref.at[which], tiles_ref, 0)

        def put(pair, row, piece):
            lane = (pair % 2) * 128
            weight_ref[4 * which + pair // 2, pl.ds(row, 32), lane : lane + 128] = piece

        assemble_columns(inv_ref, which, tiles_ref, put)
        stores[which].start()

    loads[2].wait()
    stage_blocks(blocks_ref.at[2], tiles_ref, 0)
    for local_row in range(4):
        for pair in range(8):
            cell = (quarter * 4 + local_row) * 16 + 2 * pair
            even, odd = assembled_pair(tiles_ref, inv_ref[2, cell], inv_ref[2, cell + 1])
            row = local_row * BLK
            down_dense_ref[row : row + 32, 128 * pair : 128 * (pair + 1)] = even
            down_dense_ref[row + 32 : row + 64, 128 * pair : 128 * (pair + 1)] = odd
    payload_ref[32:64, :] = contract_last(sketch_ref[...], down_dense_ref[...])

    local = index_ref[...] - owner * 1024
    inside = (local >= 0) & (local < 1024)
    safe = jnp.where(inside, local, 0)
    spot = shuffled(safe)
    high_part = jnp.where(inside, spot // 128, -1)
    low_part = spot % 128
    values = value_ref[...]
    high_iota = lax.broadcasted_iota(jnp.int32, (8, 256), 0)
    low_iota = lax.broadcasted_iota(jnp.int32, (128, 256), 0)
    for probe in range(P_SIZE):
        picked = jnp.where(
            high_iota == high_part[probe : probe + 1, :], values[probe : probe + 1, :], 0.0
        )
        one_hot = jnp.where(low_iota == low_part[probe : probe + 1, :], 1.0, 0.0).astype(BF)
        terms = contract_last(jnp.concatenate(split3(picked), axis=0), one_hot)
        total = terms[:8] + terms[8:16] + terms[16:]
        omega_ref[8 * probe : 8 * (probe + 1), :] = total
    for high in range(8):
        piece = omega_ref[pl.ds(high, 16, stride=8), :]
        for part_index, part in enumerate(split3(piece)):
            split_ref[
                16 * part_index : 16 * (part_index + 1), 128 * high : 128 * (high + 1)
            ] = part
    for which in range(2):
        triple = dot(split_ref[...], weight_ref[4 * which + quarter])
        payload_ref[16 * which : 16 * (which + 1), :] = triple[:16] + triple[16:32] + triple[32:]
    for store in stores:
        store.wait()


def flipped(two_bits, flip):
    low_bit = lax.rem(two_bits + flip % 2, 2)
    return low_bit + 2 * lax.rem(two_bits // 2 + flip // 2, 2)


def shuffle_tokens(side, tok_ref, tokens_ref):
    shuffle = shuffle_matrix(256)
    for group in range(8):
        piece = tok_ref[:, :, 256 * group : 256 * (group + 1)].reshape(256, 256)
        half = lax.rem(group // 4 + side, 2)
        tokens_ref[half, :, 256 * (group % 4) : 256 * (group % 4 + 1)] = dot(piece, shuffle).astype(
            BF
        )


def first_kernel(
    inv_ref,
    a_in_ref,
    b_in_ref,
    a_other_ref,
    weight_in_ref,
    tok_in_ref,
    keep_ref,
    sent_out_ref,
    near_out_ref,
    tokens_out_ref,
    blocks_ref,
    tiles_ref,
    near_ref,
    own_ref,
    tok_ref,
    tokens_ref,
    sent_ref,
    total_ref,
    in_sem,
    near_sem,
    sent_sem,
):
    owner, quarter, side, core = position()
    zone = owner // 2
    group = quarter // 2
    mine = pl.multiple_of(SHARED * group, 16)
    other = pl.multiple_of(SHARED * (1 - group), 16)
    loads = [
        pltpu.make_async_copy(a_in_ref, blocks_ref.at[pl.ds(mine, SHARED)], in_sem.at[0]),
        pltpu.make_async_copy(a_other_ref, blocks_ref.at[pl.ds(other, SHARED)], in_sem.at[1]),
        pltpu.make_async_copy(
            b_in_ref, blocks_ref.at[pl.ds(2 * SHARED, 160 - 2 * SHARED)], in_sem.at[2]
        ),
        pltpu.make_async_copy(tok_in_ref, tok_ref, in_sem.at[3]),
        pltpu.make_async_copy(weight_in_ref.at[pl.ds(4 * core, 4)], own_ref, in_sem.at[4]),
    ]
    for load in loads:
        load.start()
    clear_empty_slot(tiles_ref)
    for load in loads[:3]:
        load.wait()
    stage_blocks(blocks_ref, tiles_ref, 0)

    def put(pair, row, piece):
        lane = (pair % 2) * 128
        near_ref[pair // 2, pl.ds(row, 32), lane : lane + 128] = piece

    assemble_columns(inv_ref, core, tiles_ref, put)
    near_store = pltpu.make_async_copy(near_ref, near_out_ref, near_sem.at[0])
    near_store.start()
    loads[3].wait()
    shuffle_tokens(side, tok_ref, tokens_ref)
    tokens_store = pltpu.make_async_copy(tokens_ref, tokens_out_ref, near_sem.at[1])
    tokens_store.start()
    loads[4].wait()
    stores = []
    for chunk in range(4):
        total = dot(tokens_ref[0], own_ref[chunk]) + dot(tokens_ref[1], near_ref[chunk])
        cols = slice(256 * chunk, 256 * (chunk + 1))
        total_ref[...] = total
        keep_ref[:, cols] = total_ref[pl.ds(pl.multiple_of(64 * zone, 64), 64), :]
        sent_ref[:, :, cols] = total.astype(BF).reshape(4, 64, 256)
        lanes = pl.ds(256 * chunk, 256)
        store = pltpu.make_async_copy(
            sent_ref.at[:, :, lanes], sent_out_ref.at[:, :, lanes], sent_sem.at[chunk]
        )
        store.start()
        stores.append(store)
    for store in stores:
        store.wait()
    near_store.wait()
    tokens_store.wait()


def second_kernel(
    near_in_ref,
    weight_in_ref,
    tokens_in_ref,
    keep_ref,
    out1_ref,
    out2_ref,
    out3_ref,
    near_ref,
    own_ref,
    tokens_ref,
    total_ref,
    in_sem,
):
    owner, unused_quarter, unused_side, core = position()
    zone = owner // 2
    token_load = pltpu.make_async_copy(tokens_in_ref, tokens_ref, in_sem.at[0])
    token_load.start()
    loads = []
    for chunk in range(4):
        source = weight_in_ref.at[4 - 4 * core + chunk]
        own_load = pltpu.make_async_copy(source, own_ref.at[chunk], in_sem.at[1 + chunk])
        near_load = pltpu.make_async_copy(
            near_in_ref.at[chunk], near_ref.at[chunk], in_sem.at[5 + chunk]
        )
        own_load.start()
        near_load.start()
        loads.append((own_load, near_load))
    token_load.wait()
    for chunk in range(4):
        for load in loads[chunk]:
            load.wait()
        total = dot(tokens_ref[0], own_ref[chunk]) + dot(tokens_ref[1], near_ref[chunk])
        cols = slice(256 * chunk, 256 * (chunk + 1))
        total_ref[...] = total
        keep_ref[:, cols] = total_ref[pl.ds(pl.multiple_of(64 * zone, 64), 64), :]
        for flip, ref in enumerate((out1_ref, out2_ref, out3_ref), 1):
            row = pl.multiple_of(64 * flipped(zone, flip), 64)
            ref[:, cols] = total_ref[pl.ds(row, 64), :].astype(BF)


def middle_kernel(
    first_keep_ref,
    first_ref,
    second_keep_ref,
    second1_ref,
    second2_ref,
    second3_ref,
    pay0_ref,
    pay1_ref,
    pay2_ref,
    pay3_ref,
    mine_ref,
    theirs_ref,
    lead_ref,
    act_ref,
    pay_ref,
    proj_ref,
    tangent_ref,
    rows_ref,
):
    owner, quarter, unused_side, core = position()
    zone = owner // 2
    unshuffle = unshuffle_matrix(256)
    for flip, ref in enumerate((pay0_ref, pay1_ref, pay2_ref, pay3_ref)):
        pay_ref[flipped(quarter, flip)] = ref[...]
    for chunk in range(4):
        cols = slice(256 * chunk, 256 * (chunk + 1))
        proj_ref[:, cols] = dot(pay_ref[chunk, 32:64, :].astype(BF), unshuffle).astype(BF)
        first = first_keep_ref[:, cols]
        for flip in (1, 2, 3):
            first = first + first_ref[flipped(zone, flip), :, cols].astype(F32)
        second = second_keep_ref[:, cols]
        for ref in (second1_ref, second2_ref, second3_ref):
            second = second + ref[:, cols].astype(F32)
        gate_pre = jnp.where(core == 0, first, second)
        up_pre = jnp.where(core == 0, second, first)
        sigmoid_g = jax.nn.sigmoid(gate_pre)
        activated = gate_pre * sigmoid_g
        slope_g = sigmoid_g * (1.0 + gate_pre * (1.0 - sigmoid_g))
        lead = slope_g * up_pre
        lead_ref[:, cols] = lead
        act_ref[:, cols] = activated
        for probe in range(P_SIZE):
            probe_gate = pay_ref[chunk, probe : probe + 1, :]
            probe_up = pay_ref[chunk, 16 + probe : 17 + probe, :]
            tangent_ref[64 * probe : 64 * (probe + 1), cols] = (
                lead * probe_gate + activated * probe_up
            ).astype(BF)
    rows_ref[...] = contract_last(tangent_ref[...], proj_ref[...]).astype(BF)
    for step in range(P_SIZE):
        probe = lax.rem(step + 8 * core, P_SIZE)
        backward = dot(rows_ref[pl.ds(pl.multiple_of(probe * 64, 64), 64), :], proj_ref[...])
        target = mine_ref if step < 8 else theirs_ref
        row = slice(step % 8, step % 8 + 1)
        target[row, :1024] = jnp.sum(backward * lead_ref[...], axis=0, keepdims=True)
        target[row, 1024:] = jnp.sum(backward * act_ref[...], axis=0, keepdims=True)


def fetch_kernel(weight_in_ref, weight_out_ref, sem):
    copy = pltpu.make_async_copy(weight_in_ref, weight_out_ref, sem)
    copy.start()
    copy.wait()


def product_kernel(mine_ref, theirs_ref, weight_ref, out_ref, sum_ref):
    core = lax.axis_index("seq")
    sum_ref[core] = mine_ref[...]
    sum_ref[1 - core] = theirs_ref[...]
    sums = jnp.concatenate([sum_ref[0], sum_ref[1]], axis=0)
    total = None
    for chunk in range(8):
        term = contract_last(sums[:, 256 * chunk : 256 * (chunk + 1)], weight_ref[chunk])
        total = term if total is None else total + term
    unshuffle = unshuffle_matrix(256)
    for group in range(4):
        cols = slice(256 * group, 256 * (group + 1))
        high, mid, low = split3(total[:, cols])
        out_ref[:, cols] = dot(high, unshuffle) + dot(mid, unshuffle) + dot(low, unshuffle)


def pair_split(
    tokens,
    gate_blocks,
    gate_slot,
    up_blocks,
    up_slot,
    down_blocks,
    down_slot,
    sketch,
    probe_index,
    probe_value,
):
    def owner_flip(value, bits):
        return lax.ppermute(value, "fsdp", [(i, i ^ bits) for i in range(8)])

    def core_flip(value):
        return lax.ppermute(value, "seq", [(0, 1), (1, 0)])

    def zone_exchange(value):
        return lax.all_to_all(
            value,
            "fsdp",
            split_axis=0,
            concat_axis=0,
            tiled=True,
            axis_index_groups=[[0, 2, 4, 6], [1, 3, 5, 7]],
        )

    by_zone, kind_a, kind_b = pl.pallas_call(
        head_kernel,
        out_shape=(
            jax.ShapeDtypeStruct((4, 64, 2048), BF),
            jax.ShapeDtypeStruct((SHARED, 4096), BF),
            jax.ShapeDtypeStruct((160 - 2 * SHARED, 4096), BF),
        ),
        in_specs=[HBM, HBM, HBM],
        out_specs=(HBM,) * 3,
        scratch_shapes=[
            pltpu.VMEM((4, 64, 2048), BF),
            pltpu.VMEM((160, 4096), BF),
            pltpu.SemaphoreType.DMA((12,)),
        ],
        compiler_params=params(60),
        name="head",
    )(tokens, gate_blocks, up_blocks)
    near_a = owner_flip(kind_a, 1)
    near_b = owner_flip(kind_b, 1)
    gathered = zone_exchange(by_zone)

    slots = jnp.stack([gate_slot, up_slot, down_slot])
    cells = lax.broadcasted_iota(jnp.int32, (3, 160, 256), 2)
    slot_numbers = lax.broadcasted_iota(jnp.int32, (3, 160, 256), 1)
    inv = jnp.min(jnp.where(slots[:, :, None] == cells, slot_numbers, 160), axis=1)
    near_inv = owner_flip(inv, 1)

    weights, payload = pl.pallas_call(
        own_kernel,
        out_shape=(
            jax.ShapeDtypeStruct((8, 1024, 256), BF),
            jax.ShapeDtypeStruct((64, 256), F32),
        ),
        in_specs=[SMEM] + [HBM] * 3 + [VMEM] * 3,
        out_specs=(HBM, VMEM),
        scratch_shapes=[
            pltpu.VMEM((32 * STRIDE, 128), F32),
            pltpu.VMEM((128, 128), F32),
            pltpu.VMEM((48, 1024), BF),
            pltpu.VMEM((256, 1024), BF),
            pltpu.VMEM((3, 160, 4096), BF),
            pltpu.VMEM((8, 1024, 256), BF),
            pltpu.SemaphoreType.DMA((3,)),
            pltpu.SemaphoreType.DMA((2,)),
        ],
        compiler_params=params(60),
        name="own_blocks",
    )(inv, gate_blocks, up_blocks, down_blocks, sketch, probe_index, probe_value)

    near_a, payload = lax.optimization_barrier((near_a, payload))
    near_a_other = lax.ppermute(near_a, "groups", [(0, 1), (1, 0)])
    for bits in (2, 4):
        payload = payload + owner_flip(payload, bits)
    near_inv, near_b, near_a_other, gathered, payload = lax.optimization_barrier(
        (near_inv, near_b, near_a_other, gathered, payload)
    )

    first_keep, first_sent, near_weights, shuffled_tokens = pl.pallas_call(
        first_kernel,
        out_shape=(
            jax.ShapeDtypeStruct((64, 1024), F32),
            jax.ShapeDtypeStruct((4, 64, 1024), BF),
            jax.ShapeDtypeStruct((4, 1024, 256), BF),
            pltpu.HBM((2, 256, 1024), BF),
        ),
        in_specs=[SMEM, ANY, ANY, ANY, HBM, ANY],
        out_specs=(VMEM, HBM, HBM, HBM),
        scratch_shapes=[
            pltpu.VMEM((160, 4096), BF),
            pltpu.VMEM((32 * STRIDE, 128), F32),
            pltpu.VMEM((4, 1024, 256), BF),
            pltpu.VMEM((4, 1024, 256), BF),
            pltpu.VMEM((4, 64, 2048), BF),
            pltpu.VMEM((2, 256, 1024), BF),
            pltpu.VMEM((4, 64, 1024), BF),
            pltpu.VMEM((256, 256), F32),
            pltpu.SemaphoreType.DMA((5,)),
            pltpu.SemaphoreType.DMA((2,)),
            pltpu.SemaphoreType.DMA((4,)),
        ],
        compiler_params=params(46),
        name="first_partial",
    )(near_inv, near_a, near_b, near_a_other, weights, gathered)
    first_back = zone_exchange(first_sent)

    second_keep, *second_sent = pl.pallas_call(
        second_kernel,
        out_shape=(jax.ShapeDtypeStruct((64, 1024), F32),)
        + (jax.ShapeDtypeStruct((64, 1024), BF),) * 3,
        in_specs=[ANY, HBM, ANY],
        out_specs=(VMEM,) * 4,
        scratch_shapes=[
            pltpu.VMEM((4, 1024, 256), BF),
            pltpu.VMEM((4, 1024, 256), BF),
            pltpu.VMEM((2, 256, 1024), BF),
            pltpu.VMEM((256, 256), F32),
            pltpu.SemaphoreType.DMA((9,)),
        ],
        compiler_params=params(56),
        name="second_partial",
    )(core_flip(near_weights), weights, shuffled_tokens)
    second_back = [owner_flip(second_sent[flip - 1], 2 * flip) for flip in (2, 3, 1)]

    across = owner_flip(payload, 1)
    second_keep, across = lax.optimization_barrier((second_keep, across))
    payload = payload + across
    pay_parts = [
        payload,
        core_flip(payload),
        lax.ppermute(payload, "groups", [(0, 1), (1, 0)]),
        lax.ppermute(payload, ("groups", "seq"), [(i, i ^ 3) for i in range(4)]),
    ]

    first_back, weights = lax.optimization_barrier((first_back, weights))
    weights_at_hand = pl.pallas_call(
        fetch_kernel,
        out_shape=jax.ShapeDtypeStruct((8, 1024, 256), BF),
        in_specs=[HBM],
        out_specs=VMEM,
        scratch_shapes=[pltpu.SemaphoreType.DMA],
        compiler_params=params(48),
        name="fetch_weights",
    )(weights)
    pay_parts[0], weights_at_hand = lax.optimization_barrier((pay_parts[0], weights_at_hand))

    mine, theirs = pl.pallas_call(
        middle_kernel,
        out_shape=(jax.ShapeDtypeStruct((8, 2048), F32),) * 2,
        in_specs=[VMEM] * 10,
        out_specs=(VMEM,) * 2,
        scratch_shapes=[
            pltpu.VMEM((64, 1024), F32),
            pltpu.VMEM((64, 1024), F32),
            pltpu.VMEM((4, 64, 256), F32),
            pltpu.VMEM((K, 1024), BF),
            pltpu.VMEM((64 * P_SIZE, 1024), BF),
            pltpu.VMEM((64 * P_SIZE, K), BF),
        ],
        compiler_params=params(48),
        name="token_sums",
    )(first_keep, first_back, second_keep, *second_back, *pay_parts)

    sums = mine + core_flip(theirs)
    x_part, z_part, xz_part = [
        owner_flip(sums.astype(BF), bits).astype(F32) for bits in (1, 2, 3)
    ]
    sums = (sums + x_part) + (z_part + xz_part)
    sums = (sums + owner_flip(sums.astype(BF), 4).astype(F32)).astype(BF)

    return pl.pallas_call(
        product_kernel,
        out_shape=jax.ShapeDtypeStruct((P_SIZE, 1024), F32),
        in_specs=[VMEM, VMEM, VMEM],
        out_specs=VMEM,
        scratch_shapes=[pltpu.VMEM((2, 8, 2048), BF)],
        compiler_params=params(30),
        name="products",
    )(sums, core_flip(sums), weights_at_hand)


def per_device(tokens, gate_blocks, *rest):
    fits = (
        lax.axis_size("fsdp") == 8
        and lax.axis_size("seq") == 2
        and lax.axis_size("groups") == 2
        and tokens.shape == (64, 8192)
        and gate_blocks.shape == (160, 4096)
        and rest[-2].shape == (P_SIZE, 256)
    )
    return (pair_split if fits else hidden_split)(tokens, gate_blocks, *rest)


def solution(mesh):
    in_specs = (
        P(("groups", "fsdp", "seq"), None),
        P("fsdp", None),
        P("fsdp"),
        P("fsdp", None),
        P("fsdp"),
        P("fsdp", None),
        P("fsdp"),
        P(None, "fsdp"),
        P(),
        P(),
    )
    out_specs = P("groups", "fsdp")
    return jax.shard_map(
        per_device, mesh=mesh, in_specs=in_specs, out_specs=out_specs, check_vma=False
    )
```

```python
import functools

import jax
import jax.numpy as jnp
from jax import lax
from jax.experimental import pallas as pl
from jax.experimental.pallas import tpu as pltpu
from jax.sharding import PartitionSpec as P

HID_DEV = 128
BLK = 64
P_SIZE = 16
K = 32

BF = jnp.bfloat16
F32 = jnp.float32
VMEM = pl.BlockSpec(memory_space=pltpu.VMEM)
SMEM = pl.BlockSpec(memory_space=pltpu.SMEM)
HBM = pl.BlockSpec(memory_space=pltpu.HBM)
ANY = pl.BlockSpec(memory_space=pl.ANY)

STRIDE = 168
SHARED = 48


def params(mebibytes):
    return pltpu.CompilerParams(vmem_limit_bytes=int(mebibytes * 1024 * 1024))


def unpack(blocks, slot_ids, cell_total):
    holder = jnp.zeros((cell_total + 1, blocks.shape[1]), blocks.dtype)
    return holder.at[slot_ids].set(blocks)[:cell_total]


def contract_last(first_mat, second_mat):
    return lax.dot_general(
        first_mat, second_mat, (((1,), (1,)), ((), ())), preferred_element_type=jnp.float32
    )


def hidden_split(
    tokens,
    gate_blocks,
    gate_slot,
    up_blocks,
    up_slot,
    down_blocks,
    down_slot,
    sketch,
    probe_index,
    probe_value,
):
    owners = lax.axis_size("fsdp")
    model_width = tokens.shape[1]
    local_width = model_width // owners
    block_rows = local_width // BLK
    hidden = HID_DEV
    col_blocks = hidden * owners // BLK
    cell_total = block_rows * col_blocks
    gate_dense = unpack(gate_blocks, gate_slot, cell_total).reshape(
        block_rows, col_blocks, BLK, BLK
    )
    up_dense = unpack(up_blocks, up_slot, cell_total).reshape(block_rows, col_blocks, BLK, BLK)
    stacked = jnp.stack([gate_dense, up_dense], axis=1)
    stacked = stacked.reshape(block_rows, 2, owners, hidden // BLK, BLK, BLK)
    stacked = stacked.transpose(0, 4, 2, 1, 3, 5).reshape(local_width, owners * 2 * hidden)
    both_weights = lax.all_to_all(stacked, "fsdp", split_axis=1, concat_axis=0, tiled=True)
    picked = both_weights[probe_index].astype(jnp.float32)
    probe_both = jnp.sum(picked * probe_value[:, :, None], axis=1)
    preact = jnp.dot(
        lax.all_gather(tokens, "fsdp", axis=0, tiled=True),
        both_weights,
        preferred_element_type=jnp.float32,
    )
    row_count = preact.shape[0]
    gate_pre = preact[:, :hidden]
    up_pre = preact[:, hidden:]
    down_dense = unpack(down_blocks, down_slot, cell_total).reshape(
        col_blocks, block_rows, BLK, BLK
    )
    down_dense = down_dense.transpose(0, 2, 1, 3).reshape(col_blocks * BLK, local_width)
    down_rows = lax.all_to_all(down_dense, "fsdp", split_axis=0, concat_axis=1, tiled=True)
    full_sketch = lax.all_gather(sketch, "fsdp", axis=1, tiled=True)
    projected = contract_last(down_rows, full_sketch)
    projected = projected.astype(jnp.bfloat16)
    sigmoid_g = jax.nn.sigmoid(gate_pre)
    activated = gate_pre * sigmoid_g
    slope_g = sigmoid_g * (1.0 + gate_pre * (1.0 - sigmoid_g))
    lead_term = slope_g * up_pre
    tangent = (
        lead_term[:, None, :] * probe_both[None, :, :hidden]
        + activated[:, None, :] * probe_both[None, :, hidden:]
    )
    tangent = tangent.astype(jnp.bfloat16)
    partial_sketch = jnp.dot(
        tangent.reshape(row_count * P_SIZE, hidden), projected, preferred_element_type=jnp.float32
    )
    partial_sketch = partial_sketch.reshape(row_count, P_SIZE * K)
    sketch_rows = lax.psum(partial_sketch, "fsdp").astype(jnp.bfloat16)
    backward = contract_last(sketch_rows.reshape(row_count * P_SIZE, K), projected).reshape(
        row_count, P_SIZE, hidden
    )
    summed = jnp.concatenate(
        [
            jnp.sum(backward * lead_term[:, None, :], axis=0),
            jnp.sum(backward * activated[:, None, :], axis=0),
        ],
        axis=1,
    )
    summed = lax.psum(summed, "seq").astype(jnp.bfloat16)
    products = contract_last(summed, both_weights)
    return lax.psum_scatter(products, "fsdp", scatter_dimension=1, tiled=True)


def dot(a, b):
    return jnp.dot(a, b, preferred_element_type=F32)


def split3(value):
    high = value.astype(BF)
    rest = value - high.astype(F32)
    mid = rest.astype(BF)
    low = (rest - mid.astype(F32)).astype(BF)
    return high, mid, low


def shuffled(natural):
    return (natural // BLK) * BLK + (natural % 2) * (BLK // 2) + (natural % BLK) // 2


def shuffle_matrix(size):
    rows = lax.broadcasted_iota(jnp.int32, (size, size), 0)
    cols = lax.broadcasted_iota(jnp.int32, (size, size), 1)
    return jnp.where(shuffled(rows) == cols, 1.0, 0.0).astype(BF)


def unshuffle_matrix(size):
    rows = lax.broadcasted_iota(jnp.int32, (size, size), 0)
    cols = lax.broadcasted_iota(jnp.int32, (size, size), 1)
    return jnp.where(shuffled(cols) == rows, 1.0, 0.0).astype(BF)


def stage_blocks(blocks_ref, tiles_ref, first_slot):
    @pl.loop(0, blocks_ref.shape[0] // 16, unroll=2)
    def _(step):
        row = pl.multiple_of(step * 16, 16)
        target = pl.multiple_of(first_slot + row, 16)
        for chunk in range(32):
            piece = blocks_ref[pl.ds(row, 16), 128 * chunk : 128 * (chunk + 1)].astype(F32)
            tiles_ref[pl.ds(target + chunk * STRIDE, 16), :] = piece


def clear_empty_slot(tiles_ref):
    for chunk in range(32):
        tiles_ref[pl.ds(chunk * STRIDE + 160, 8), :] = jnp.zeros((8, 128), F32)


def assembled_pair(tiles_ref, left_slot, right_slot):
    left = tiles_ref[pl.ds(left_slot, 32, stride=STRIDE), :]
    right = tiles_ref[pl.ds(right_slot, 32, stride=STRIDE), :]
    low_half = lax.broadcasted_iota(jnp.int32, (32, 128), 1) < BLK
    straight = jnp.where(low_half, left, right)
    crossed = pltpu.roll(jnp.where(low_half, right, left), BLK, 1)
    even = jnp.where(low_half, straight, crossed)
    odd = jnp.where(low_half, crossed, straight)
    return even.astype(BF), odd.astype(BF)


def assemble_columns(inv_ref, inv_row, tiles_ref, put):
    @pl.loop(0, 16, unroll=4)
    def _(block_row):
        for pair in range(8):
            cell = block_row * 16 + 2 * pair
            even, odd = assembled_pair(
                tiles_ref, inv_ref[inv_row, cell], inv_ref[inv_row, cell + 1]
            )
            row = pl.multiple_of(block_row * BLK, BLK)
            put(pair, row, even)
            put(pair, row + BLK // 2, odd)


def position():
    owner = lax.axis_index("fsdp")
    core = lax.axis_index("seq")
    return owner, 2 * lax.axis_index("groups") + core, lax.rem(owner, 2), core


def head_kernel(
    tok_in_ref, gate_ref, up_ref, zone_out_ref, a_out_ref, b_out_ref, tok_ref, blocks_ref, sem
):
    unused_owner, quarter, unused_side, core = position()
    first = pl.multiple_of(SHARED * (quarter // 2), 16)
    a_part = pl.ds(first, SHARED)
    b_part = pl.ds(2 * SHARED, 160 - 2 * SHARED)
    loads, stores = [], []
    for zone in range(4):
        held = tok_ref.at[zone]
        lanes = pl.ds(2048 * zone, 2048)
        loads.append(pltpu.make_async_copy(tok_in_ref.at[:, lanes], held, sem.at[zone]))
        stores.append(pltpu.make_async_copy(held, zone_out_ref.at[zone], sem.at[4 + zone]))
    for load in loads:
        load.start()
    for kind, source in enumerate((gate_ref, up_ref)):

        @pl.when(core == kind)
        def _():
            pltpu.make_async_copy(source.at[a_part], blocks_ref.at[a_part], sem.at[8]).start()
            pltpu.make_async_copy(source.at[b_part], blocks_ref.at[b_part], sem.at[9]).start()

    for load, store in zip(loads, stores):
        load.wait()
        store.start()
    pltpu.make_async_copy(gate_ref.at[a_part], blocks_ref.at[a_part], sem.at[8]).wait()
    stores.append(pltpu.make_async_copy(blocks_ref.at[a_part], a_out_ref, sem.at[10]))
    stores[4].start()
    pltpu.make_async_copy(gate_ref.at[b_part], blocks_ref.at[b_part], sem.at[9]).wait()
    stores.append(pltpu.make_async_copy(blocks_ref.at[b_part], b_out_ref, sem.at[11]))
    stores[5].start()
    for store in stores:
        store.wait()


def own_kernel(
    inv_ref,
    gate_ref,
    up_ref,
    down_ref,
    sketch_ref,
    index_ref,
    value_ref,
    weight_out_ref,
    payload_ref,
    tiles_ref,
    omega_ref,
    split_ref,
    down_dense_ref,
    blocks_ref,
    weight_ref,
    in_sem,
    out_sem,
):
    owner, quarter, unused_side, unused_core = position()
    loads = [
        pltpu.make_async_copy(source, blocks_ref.at[i], in_sem.at[i])
        for i, source in enumerate((gate_ref, up_ref, down_ref))
    ]
    stores = [
        pltpu.make_async_copy(
            weight_ref.at[pl.ds(4 * i, 4)], weight_out_ref.at[pl.ds(4 * i, 4)], out_sem.at[i]
        )
        for i in range(2)
    ]
    for load in loads:
        load.start()
    clear_empty_slot(tiles_ref)

    for which in range(2):
        loads[which].wait()
        stage_blocks(blocks_ref.at[which], tiles_ref, 0)

        def put(pair, row, piece):
            lane = (pair % 2) * 128
            weight_ref[4 * which + pair // 2, pl.ds(row, 32), lane : lane + 128] = piece

        assemble_columns(inv_ref, which, tiles_ref, put)
        stores[which].start()

    loads[2].wait()
    stage_blocks(blocks_ref.at[2], tiles_ref, 0)
    for local_row in range(4):
        for pair in range(8):
            cell = (quarter * 4 + local_row) * 16 + 2 * pair
            even, odd = assembled_pair(tiles_ref, inv_ref[2, cell], inv_ref[2, cell + 1])
            row = local_row * BLK
            down_dense_ref[row : row + 32, 128 * pair : 128 * (pair + 1)] = even
            down_dense_ref[row + 32 : row + 64, 128 * pair : 128 * (pair + 1)] = odd
    payload_ref[32:64, :] = contract_last(sketch_ref[...], down_dense_ref[...])

    local = index_ref[...] - owner * 1024
    inside = (local >= 0) & (local < 1024)
    safe = jnp.where(inside, local, 0)
    spot = shuffled(safe)
    high_part = jnp.where(inside, spot // 128, -1)
    low_part = spot % 128
    values = value_ref[...]
    high_iota = lax.broadcasted_iota(jnp.int32, (8, 256), 0)
    low_iota = lax.broadcasted_iota(jnp.int32, (128, 256), 0)
    for probe in range(P_SIZE):
        picked = jnp.where(
            high_iota == high_part[probe : probe + 1, :], values[probe : probe + 1, :], 0.0
        )
        one_hot = jnp.where(low_iota == low_part[probe : probe + 1, :], 1.0, 0.0).astype(BF)
        terms = contract_last(jnp.concatenate(split3(picked), axis=0), one_hot)
        total = terms[:8] + terms[8:16] + terms[16:]
        omega_ref[8 * probe : 8 * (probe + 1), :] = total
    for high in range(8):
        piece = omega_ref[pl.ds(high, 16, stride=8), :]
        for part_index, part in enumerate(split3(piece)):
            split_ref[
                16 * part_index : 16 * (part_index + 1), 128 * high : 128 * (high + 1)
            ] = part
    for which in range(2):
        triple = dot(split_ref[...], weight_ref[4 * which + quarter])
        payload_ref[16 * which : 16 * (which + 1), :] = triple[:16] + triple[16:32] + triple[32:]
    for store in stores:
        store.wait()


def flipped(two_bits, flip):
    low_bit = lax.rem(two_bits + flip % 2, 2)
    return low_bit + 2 * lax.rem(two_bits // 2 + flip // 2, 2)


def shuffle_tokens(side, tok_ref, tokens_ref):
    shuffle = shuffle_matrix(256)
    for group in range(8):
        piece = tok_ref[:, :, 256 * group : 256 * (group + 1)].reshape(256, 256)
        half = lax.rem(group // 4 + side, 2)
        tokens_ref[half, :, 256 * (group % 4) : 256 * (group % 4 + 1)] = dot(piece, shuffle).astype(
            BF
        )


def first_kernel(
    inv_ref,
    a_in_ref,
    b_in_ref,
    a_other_ref,
    weight_in_ref,
    tok_in_ref,
    keep_ref,
    sent_out_ref,
    near_out_ref,
    tokens_out_ref,
    tiles_ref,
    near_ref,
    own_ref,
    tokens_ref,
    sent_ref,
    total_ref,
    in_sem,
    near_sem,
    sent_sem,
):
    owner, quarter, side, core = position()
    zone = owner // 2
    group = quarter // 2
    load = pltpu.make_async_copy(weight_in_ref.at[pl.ds(4 * core, 4)], own_ref, in_sem)
    load.start()
    clear_empty_slot(tiles_ref)
    stage_blocks(a_in_ref, tiles_ref, SHARED * group)
    stage_blocks(a_other_ref, tiles_ref, SHARED * (1 - group))
    stage_blocks(b_in_ref, tiles_ref, 2 * SHARED)

    def put(pair, row, piece):
        lane = (pair % 2) * 128
        near_ref[pair // 2, pl.ds(row, 32), lane : lane + 128] = piece

    assemble_columns(inv_ref, core, tiles_ref, put)
    near_store = pltpu.make_async_copy(near_ref, near_out_ref, near_sem.at[0])
    near_store.start()
    shuffle_tokens(side, tok_in_ref, tokens_ref)
    tokens_store = pltpu.make_async_copy(tokens_ref, tokens_out_ref, near_sem.at[1])
    tokens_store.start()
    load.wait()
    stores = []
    for chunk in range(4):
        total = dot(tokens_ref[0], own_ref[chunk]) + dot(tokens_ref[1], near_ref[chunk])
        cols = slice(256 * chunk, 256 * (chunk + 1))
        total_ref[...] = total
        keep_ref[:, cols] = total_ref[pl.ds(pl.multiple_of(64 * zone, 64), 64), :]
        sent_ref[:, :, cols] = total.astype(BF).reshape(4, 64, 256)
        lanes = pl.ds(256 * chunk, 256)
        store = pltpu.make_async_copy(
            sent_ref.at[:, :, lanes], sent_out_ref.at[:, :, lanes], sent_sem.at[chunk]
        )
        store.start()
        stores.append(store)
    for store in stores:
        store.wait()
    near_store.wait()
    tokens_store.wait()


def second_kernel(
    near_in_ref,
    weight_in_ref,
    tokens_in_ref,
    keep_ref,
    out1_ref,
    out2_ref,
    out3_ref,
    near_ref,
    own_ref,
    tokens_ref,
    total_ref,
    in_sem,
):
    owner, unused_quarter, unused_side, core = position()
    zone = owner // 2
    loads = [
        pltpu.make_async_copy(tokens_in_ref, tokens_ref, in_sem.at[0]),
        pltpu.make_async_copy(weight_in_ref.at[pl.ds(4 - 4 * core, 4)], own_ref, in_sem.at[1]),
        pltpu.make_async_copy(near_in_ref, near_ref, in_sem.at[2]),
    ]
    for load in loads:
        load.start()
    for load in loads:
        load.wait()
    for chunk in range(4):
        total = dot(tokens_ref[0], own_ref[chunk]) + dot(tokens_ref[1], near_ref[chunk])
        cols = slice(256 * chunk, 256 * (chunk + 1))
        total_ref[...] = total
        keep_ref[:, cols] = total_ref[pl.ds(pl.multiple_of(64 * zone, 64), 64), :]
        for flip, ref in enumerate((out1_ref, out2_ref, out3_ref), 1):
            row = pl.multiple_of(64 * flipped(zone, flip), 64)
            ref[:, cols] = total_ref[pl.ds(row, 64), :].astype(BF)


def middle_kernel(
    first_keep_ref,
    first_ref,
    second_keep_ref,
    second1_ref,
    second2_ref,
    second3_ref,
    pay0_ref,
    pay1_ref,
    pay2_ref,
    pay3_ref,
    mine_ref,
    theirs_ref,
    lead_ref,
    act_ref,
    pay_ref,
    proj_ref,
    tangent_ref,
    rows_ref,
):
    owner, quarter, unused_side, core = position()
    zone = owner // 2
    unshuffle = unshuffle_matrix(256)
    for flip, ref in enumerate((pay0_ref, pay1_ref, pay2_ref, pay3_ref)):
        pay_ref[flipped(quarter, flip)] = ref[...]
    for chunk in range(4):
        cols = slice(256 * chunk, 256 * (chunk + 1))
        proj_ref[:, cols] = dot(pay_ref[chunk, 32:64, :].astype(BF), unshuffle).astype(BF)
        first = first_keep_ref[:, cols]
        for flip in (1, 2, 3):
            first = first + first_ref[flipped(zone, flip), :, cols].astype(F32)
        second = second_keep_ref[:, cols]
        for ref in (second1_ref, second2_ref, second3_ref):
            second = second + ref[:, cols].astype(F32)
        gate_pre = jnp.where(core == 0, first, second)
        up_pre = jnp.where(core == 0, second, first)
        sigmoid_g = jax.nn.sigmoid(gate_pre)
        activated = gate_pre * sigmoid_g
        slope_g = sigmoid_g * (1.0 + gate_pre * (1.0 - sigmoid_g))
        lead = slope_g * up_pre
        lead_ref[:, cols] = lead
        act_ref[:, cols] = activated
        for probe in range(P_SIZE):
            probe_gate = pay_ref[chunk, probe : probe + 1, :]
            probe_up = pay_ref[chunk, 16 + probe : 17 + probe, :]
            tangent_ref[64 * probe : 64 * (probe + 1), cols] = (
                lead * probe_gate + activated * probe_up
            ).astype(BF)
    rows_ref[...] = contract_last(tangent_ref[...], proj_ref[...]).astype(BF)
    for step in range(P_SIZE):
        probe = lax.rem(step + 8 * core, P_SIZE)
        backward = dot(rows_ref[pl.ds(pl.multiple_of(probe * 64, 64), 64), :], proj_ref[...])
        target = mine_ref if step < 8 else theirs_ref
        row = slice(step % 8, step % 8 + 1)
        target[row, :1024] = jnp.sum(backward * lead_ref[...], axis=0, keepdims=True)
        target[row, 1024:] = jnp.sum(backward * act_ref[...], axis=0, keepdims=True)


def fetch_kernel(weight_in_ref, weight_out_ref, sem):
    copy = pltpu.make_async_copy(weight_in_ref, weight_out_ref, sem)
    copy.start()
    copy.wait()


def product_kernel(mine_ref, theirs_ref, weight_ref, out_ref, sum_ref):
    core = lax.axis_index("seq")
    sum_ref[core] = mine_ref[...]
    sum_ref[1 - core] = theirs_ref[...]
    sums = jnp.concatenate([sum_ref[0], sum_ref[1]], axis=0)
    total = None
    for chunk in range(8):
        term = contract_last(sums[:, 256 * chunk : 256 * (chunk + 1)], weight_ref[chunk])
        total = term if total is None else total + term
    unshuffle = unshuffle_matrix(256)
    for group in range(4):
        cols = slice(256 * group, 256 * (group + 1))
        high, mid, low = split3(total[:, cols])
        out_ref[:, cols] = dot(high, unshuffle) + dot(mid, unshuffle) + dot(low, unshuffle)


def pair_split(
    tokens,
    gate_blocks,
    gate_slot,
    up_blocks,
    up_slot,
    down_blocks,
    down_slot,
    sketch,
    probe_index,
    probe_value,
):
    def owner_flip(value, bits):
        return lax.ppermute(value, "fsdp", [(i, i ^ bits) for i in range(8)])

    def core_flip(value):
        return lax.ppermute(value, "seq", [(0, 1), (1, 0)])

    def zone_exchange(value):
        return lax.all_to_all(
            value,
            "fsdp",
            split_axis=0,
            concat_axis=0,
            tiled=True,
            axis_index_groups=[[0, 2, 4, 6], [1, 3, 5, 7]],
        )

    by_zone, kind_a, kind_b = pl.pallas_call(
        head_kernel,
        out_shape=(
            jax.ShapeDtypeStruct((4, 64, 2048), BF),
            jax.ShapeDtypeStruct((SHARED, 4096), BF),
            jax.ShapeDtypeStruct((160 - 2 * SHARED, 4096), BF),
        ),
        in_specs=[HBM, HBM, HBM],
        out_specs=(HBM,) * 3,
        scratch_shapes=[
            pltpu.VMEM((4, 64, 2048), BF),
            pltpu.VMEM((160, 4096), BF),
            pltpu.SemaphoreType.DMA((12,)),
        ],
        compiler_params=params(60),
        name="head",
    )(tokens, gate_blocks, up_blocks)
    near_a = owner_flip(kind_a, 1)
    near_b = owner_flip(kind_b, 1)
    gathered = zone_exchange(by_zone)

    slots = jnp.stack([gate_slot, up_slot, down_slot])
    cells = lax.broadcasted_iota(jnp.int32, (3, 160, 256), 2)
    slot_numbers = lax.broadcasted_iota(jnp.int32, (3, 160, 256), 1)
    inv = jnp.min(jnp.where(slots[:, :, None] == cells, slot_numbers, 160), axis=1)
    near_inv = owner_flip(inv, 1)

    weights, payload = pl.pallas_call(
        own_kernel,
        out_shape=(
            jax.ShapeDtypeStruct((8, 1024, 256), BF),
            jax.ShapeDtypeStruct((64, 256), F32),
        ),
        in_specs=[SMEM] + [HBM] * 3 + [VMEM] * 3,
        out_specs=(HBM, VMEM),
        scratch_shapes=[
            pltpu.VMEM((33 * STRIDE, 128), F32),
            pltpu.VMEM((136, 128), F32),
            pltpu.VMEM((48, 1024), BF),
            pltpu.VMEM((256, 1024), BF),
            pltpu.VMEM((3, 160, 4096), BF),
            pltpu.VMEM((8, 1024, 256), BF),
            pltpu.SemaphoreType.DMA((3,)),
            pltpu.SemaphoreType.DMA((2,)),
        ],
        compiler_params=params(60),
        name="own_blocks",
    )(inv, gate_blocks, up_blocks, down_blocks, sketch, probe_index, probe_value)

    near_a, payload = lax.optimization_barrier((near_a, payload))
    near_a_other = lax.ppermute(near_a, "groups", [(0, 1), (1, 0)])
    for bits in (2, 4):
        payload = payload + owner_flip(payload, bits)
    near_inv, near_b, near_a_other, gathered, payload = lax.optimization_barrier(
        (near_inv, near_b, near_a_other, gathered, payload)
    )

    first_keep, first_sent, near_weights, shuffled_tokens = pl.pallas_call(
        first_kernel,
        out_shape=(
            jax.ShapeDtypeStruct((64, 1024), F32),
            jax.ShapeDtypeStruct((4, 64, 1024), BF),
            jax.ShapeDtypeStruct((4, 1024, 256), BF),
            pltpu.HBM((2, 256, 1024), BF),
        ),
        in_specs=[SMEM, VMEM, VMEM, VMEM, HBM, VMEM],
        out_specs=(VMEM, HBM, HBM, HBM),
        scratch_shapes=[
            pltpu.VMEM((33 * STRIDE, 128), F32),
            pltpu.VMEM((4, 1024, 256), BF),
            pltpu.VMEM((4, 1024, 256), BF),
            pltpu.VMEM((2, 256, 1024), BF),
            pltpu.VMEM((4, 64, 1024), BF),
            pltpu.VMEM((256, 256), F32),
            pltpu.SemaphoreType.DMA,
            pltpu.SemaphoreType.DMA((2,)),
            pltpu.SemaphoreType.DMA((4,)),
        ],
        compiler_params=params(46),
        name="first_partial",
    )(near_inv, near_a, near_b, near_a_other, weights, gathered)
    first_back = zone_exchange(first_sent)

    second_keep, *second_sent = pl.pallas_call(
        second_kernel,
        out_shape=(jax.ShapeDtypeStruct((64, 1024), F32),)
        + (jax.ShapeDtypeStruct((64, 1024), BF),) * 3,
        in_specs=[ANY, HBM, ANY],
        out_specs=(VMEM,) * 4,
        scratch_shapes=[
            pltpu.VMEM((4, 1024, 256), BF),
            pltpu.VMEM((4, 1024, 256), BF),
            pltpu.VMEM((2, 256, 1024), BF),
            pltpu.VMEM((256, 256), F32),
            pltpu.SemaphoreType.DMA((3,)),
        ],
        compiler_params=params(56),
        name="second_partial",
    )(core_flip(near_weights), weights, shuffled_tokens)
    second_back = [owner_flip(second_sent[flip - 1], 2 * flip) for flip in (1, 2, 3)]

    across = owner_flip(payload, 1)
    second_keep, across = lax.optimization_barrier((second_keep, across))
    payload = payload + across
    pay_parts = [
        payload,
        core_flip(payload),
        lax.ppermute(payload, "groups", [(0, 1), (1, 0)]),
        lax.ppermute(payload, ("groups", "seq"), [(i, i ^ 3) for i in range(4)]),
    ]

    first_back, weights = lax.optimization_barrier((first_back, weights))
    weights_at_hand = pl.pallas_call(
        fetch_kernel,
        out_shape=jax.ShapeDtypeStruct((8, 1024, 256), BF),
        in_specs=[HBM],
        out_specs=VMEM,
        scratch_shapes=[pltpu.SemaphoreType.DMA],
        compiler_params=params(48),
        name="fetch_weights",
    )(weights)
    pay_parts[0], weights_at_hand = lax.optimization_barrier((pay_parts[0], weights_at_hand))

    mine, theirs = pl.pallas_call(
        middle_kernel,
        out_shape=(jax.ShapeDtypeStruct((8, 2048), F32),) * 2,
        in_specs=[VMEM] * 10,
        out_specs=(VMEM,) * 2,
        scratch_shapes=[
            pltpu.VMEM((64, 1024), F32),
            pltpu.VMEM((64, 1024), F32),
            pltpu.VMEM((4, 64, 256), F32),
            pltpu.VMEM((K, 1024), BF),
            pltpu.VMEM((64 * P_SIZE, 1024), BF),
            pltpu.VMEM((64 * P_SIZE, K), BF),
        ],
        compiler_params=params(48),
        name="token_sums",
    )(first_keep, first_back, second_keep, *second_back, *pay_parts)

    sums = mine + core_flip(theirs)
    x_part, z_part, xz_part = [
        owner_flip(sums.astype(BF), bits).astype(F32) for bits in (1, 2, 3)
    ]
    sums = (sums + x_part) + (z_part + xz_part)
    sums = (sums + owner_flip(sums.astype(BF), 4).astype(F32)).astype(BF)

    return pl.pallas_call(
        product_kernel,
        out_shape=jax.ShapeDtypeStruct((P_SIZE, 1024), F32),
        in_specs=[VMEM, VMEM, VMEM],
        out_specs=VMEM,
        scratch_shapes=[pltpu.VMEM((2, 8, 2048), BF)],
        compiler_params=params(30),
        name="products",
    )(sums, core_flip(sums), weights_at_hand)


def per_device(tokens, gate_blocks, *rest):
    fits = (
        lax.axis_size("fsdp") == 8
        and lax.axis_size("seq") == 2
        and lax.axis_size("groups") == 2
        and tokens.shape == (64, 8192)
        and gate_blocks.shape == (160, 4096)
        and rest[-2].shape == (P_SIZE, 256)
    )
    return (pair_split if fits else hidden_split)(tokens, gate_blocks, *rest)


def solution(mesh):
    in_specs = (
        P(("groups", "fsdp", "seq"), None),
        P("fsdp", None),
        P("fsdp"),
        P("fsdp", None),
        P("fsdp"),
        P("fsdp", None),
        P("fsdp"),
        P(None, "fsdp"),
        P(),
        P(),
    )
    out_specs = P("groups", "fsdp")
    return jax.shard_map(
        per_device, mesh=mesh, in_specs=in_specs, out_specs=out_specs, check_vma=False
    )
```

```python
import functools

import jax
import jax.numpy as jnp
from jax import lax
from jax.experimental import pallas as pl
from jax.experimental.pallas import tpu as pltpu
from jax.sharding import PartitionSpec as P

HID_DEV = 128
BLK = 64
P_SIZE = 16
K = 32

BF = jnp.bfloat16
F32 = jnp.float32
VMEM = pl.BlockSpec(memory_space=pltpu.VMEM)
SMEM = pl.BlockSpec(memory_space=pltpu.SMEM)
HBM = pl.BlockSpec(memory_space=pltpu.HBM)
ANY = pl.BlockSpec(memory_space=pl.ANY)

STRIDE = 168
SHARED = 48


def params(mebibytes):
    return pltpu.CompilerParams(vmem_limit_bytes=int(mebibytes * 1024 * 1024))


def unpack(blocks, slot_ids, cell_total):
    holder = jnp.zeros((cell_total + 1, blocks.shape[1]), blocks.dtype)
    return holder.at[slot_ids].set(blocks)[:cell_total]


def contract_last(first_mat, second_mat):
    return lax.dot_general(
        first_mat, second_mat, (((1,), (1,)), ((), ())), preferred_element_type=jnp.float32
    )


def hidden_split(
    tokens,
    gate_blocks,
    gate_slot,
    up_blocks,
    up_slot,
    down_blocks,
    down_slot,
    sketch,
    probe_index,
    probe_value,
):
    owners = lax.axis_size("fsdp")
    model_width = tokens.shape[1]
    local_width = model_width // owners
    block_rows = local_width // BLK
    hidden = HID_DEV
    col_blocks = hidden * owners // BLK
    cell_total = block_rows * col_blocks
    gate_dense = unpack(gate_blocks, gate_slot, cell_total).reshape(
        block_rows, col_blocks, BLK, BLK
    )
    up_dense = unpack(up_blocks, up_slot, cell_total).reshape(block_rows, col_blocks, BLK, BLK)
    stacked = jnp.stack([gate_dense, up_dense], axis=1)
    stacked = stacked.reshape(block_rows, 2, owners, hidden // BLK, BLK, BLK)
    stacked = stacked.transpose(0, 4, 2, 1, 3, 5).reshape(local_width, owners * 2 * hidden)
    both_weights = lax.all_to_all(stacked, "fsdp", split_axis=1, concat_axis=0, tiled=True)
    picked = both_weights[probe_index].astype(jnp.float32)
    probe_both = jnp.sum(picked * probe_value[:, :, None], axis=1)
    preact = jnp.dot(
        lax.all_gather(tokens, "fsdp", axis=0, tiled=True),
        both_weights,
        preferred_element_type=jnp.float32,
    )
    row_count = preact.shape[0]
    gate_pre = preact[:, :hidden]
    up_pre = preact[:, hidden:]
    down_dense = unpack(down_blocks, down_slot, cell_total).reshape(
        col_blocks, block_rows, BLK, BLK
    )
    down_dense = down_dense.transpose(0, 2, 1, 3).reshape(col_blocks * BLK, local_width)
    down_rows = lax.all_to_all(down_dense, "fsdp", split_axis=0, concat_axis=1, tiled=True)
    full_sketch = lax.all_gather(sketch, "fsdp", axis=1, tiled=True)
    projected = contract_last(down_rows, full_sketch)
    projected = projected.astype(jnp.bfloat16)
    sigmoid_g = jax.nn.sigmoid(gate_pre)
    activated = gate_pre * sigmoid_g
    slope_g = sigmoid_g * (1.0 + gate_pre * (1.0 - sigmoid_g))
    lead_term = slope_g * up_pre
    tangent = (
        lead_term[:, None, :] * probe_both[None, :, :hidden]
        + activated[:, None, :] * probe_both[None, :, hidden:]
    )
    tangent = tangent.astype(jnp.bfloat16)
    partial_sketch = jnp.dot(
        tangent.reshape(row_count * P_SIZE, hidden), projected, preferred_element_type=jnp.float32
    )
    partial_sketch = partial_sketch.reshape(row_count, P_SIZE * K)
    sketch_rows = lax.psum(partial_sketch, "fsdp").astype(jnp.bfloat16)
    backward = contract_last(sketch_rows.reshape(row_count * P_SIZE, K), projected).reshape(
        row_count, P_SIZE, hidden
    )
    summed = jnp.concatenate(
        [
            jnp.sum(backward * lead_term[:, None, :], axis=0),
            jnp.sum(backward * activated[:, None, :], axis=0),
        ],
        axis=1,
    )
    summed = lax.psum(summed, "seq").astype(jnp.bfloat16)
    products = contract_last(summed, both_weights)
    return lax.psum_scatter(products, "fsdp", scatter_dimension=1, tiled=True)


def dot(a, b):
    return jnp.dot(a, b, preferred_element_type=F32)


def split3(value):
    high = value.astype(BF)
    rest = value - high.astype(F32)
    mid = rest.astype(BF)
    low = (rest - mid.astype(F32)).astype(BF)
    return high, mid, low


def shuffled(natural):
    return (natural // BLK) * BLK + (natural % 2) * (BLK // 2) + (natural % BLK) // 2


def shuffle_matrix(size):
    rows = lax.broadcasted_iota(jnp.int32, (size, size), 0)
    cols = lax.broadcasted_iota(jnp.int32, (size, size), 1)
    return jnp.where(shuffled(rows) == cols, 1.0, 0.0).astype(BF)


def unshuffle_matrix(size):
    rows = lax.broadcasted_iota(jnp.int32, (size, size), 0)
    cols = lax.broadcasted_iota(jnp.int32, (size, size), 1)
    return jnp.where(shuffled(cols) == rows, 1.0, 0.0).astype(BF)


def stage_blocks(blocks_ref, tiles_ref, first_slot):
    @pl.loop(0, blocks_ref.shape[0] // 16, unroll=2)
    def _(step):
        row = pl.multiple_of(step * 16, 16)
        target = pl.multiple_of(first_slot + row, 16)
        for chunk in range(32):
            piece = blocks_ref[pl.ds(row, 16), 128 * chunk : 128 * (chunk + 1)].astype(F32)
            tiles_ref[pl.ds(target + chunk * STRIDE, 16), :] = piece


def clear_empty_slot(tiles_ref):
    for chunk in range(32):
        tiles_ref[pl.ds(chunk * STRIDE + 160, 8), :] = jnp.zeros((8, 128), F32)


def assembled_pair(tiles_ref, left_slot, right_slot):
    left = tiles_ref[pl.ds(left_slot, 32, stride=STRIDE), :]
    right = tiles_ref[pl.ds(right_slot, 32, stride=STRIDE), :]
    low_half = lax.broadcasted_iota(jnp.int32, (32, 128), 1) < BLK
    straight = jnp.where(low_half, left, right)
    crossed = pltpu.roll(jnp.where(low_half, right, left), BLK, 1)
    even = jnp.where(low_half, straight, crossed)
    odd = jnp.where(low_half, crossed, straight)
    return even.astype(BF), odd.astype(BF)


def assemble_columns(inv_ref, inv_row, tiles_ref, put):
    @pl.loop(0, 16, unroll=8)
    def _(block_row):
        for pair in range(8):
            cell = block_row * 16 + 2 * pair
            even, odd = assembled_pair(
                tiles_ref, inv_ref[inv_row, cell], inv_ref[inv_row, cell + 1]
            )
            row = pl.multiple_of(block_row * BLK, BLK)
            put(pair, row, even)
            put(pair, row + BLK // 2, odd)


def position():
    owner = lax.axis_index("fsdp")
    core = lax.axis_index("seq")
    return owner, 2 * lax.axis_index("groups") + core, lax.rem(owner, 2), core


def head_kernel(
    tok_in_ref, gate_ref, up_ref, zone_out_ref, a_out_ref, b_out_ref, tok_ref, blocks_ref, sem
):
    unused_owner, quarter, unused_side, core = position()
    first = pl.multiple_of(SHARED * (quarter // 2), 16)
    a_part = pl.ds(first, SHARED)
    b_part = pl.ds(2 * SHARED, 160 - 2 * SHARED)
    loads, stores = [], []
    for zone in range(4):
        held = tok_ref.at[zone]
        lanes = pl.ds(2048 * zone, 2048)
        loads.append(pltpu.make_async_copy(tok_in_ref.at[:, lanes], held, sem.at[zone]))
        stores.append(pltpu.make_async_copy(held, zone_out_ref.at[zone], sem.at[4 + zone]))
    for load in loads:
        load.start()
    for kind, source in enumerate((gate_ref, up_ref)):

        @pl.when(core == kind)
        def _():
            pltpu.make_async_copy(source.at[a_part], blocks_ref.at[a_part], sem.at[8]).start()
            pltpu.make_async_copy(source.at[b_part], blocks_ref.at[b_part], sem.at[9]).start()

    for load, store in zip(loads, stores):
        load.wait()
        store.start()
    pltpu.make_async_copy(gate_ref.at[a_part], blocks_ref.at[a_part], sem.at[8]).wait()
    stores.append(pltpu.make_async_copy(blocks_ref.at[a_part], a_out_ref, sem.at[10]))
    stores[4].start()
    pltpu.make_async_copy(gate_ref.at[b_part], blocks_ref.at[b_part], sem.at[9]).wait()
    stores.append(pltpu.make_async_copy(blocks_ref.at[b_part], b_out_ref, sem.at[11]))
    stores[5].start()
    for store in stores:
        store.wait()


def own_kernel(
    inv_ref,
    gate_ref,
    up_ref,
    down_ref,
    sketch_ref,
    index_ref,
    value_ref,
    weight_out_ref,
    payload_ref,
    tiles_ref,
    omega_ref,
    split_ref,
    down_dense_ref,
    blocks_ref,
    weight_ref,
    in_sem,
    out_sem,
):
    owner, quarter, unused_side, unused_core = position()
    loads = [
        pltpu.make_async_copy(source, blocks_ref.at[i], in_sem.at[i])
        for i, source in enumerate((gate_ref, up_ref, down_ref))
    ]
    stores = [
        pltpu.make_async_copy(
            weight_ref.at[pl.ds(4 * i, 4)], weight_out_ref.at[pl.ds(4 * i, 4)], out_sem.at[i]
        )
        for i in range(2)
    ]
    for load in loads:
        load.start()
    clear_empty_slot(tiles_ref)

    for which in range(2):
        loads[which].wait()
        stage_blocks(blocks_ref.at[which], tiles_ref, 0)

        def put(pair, row, piece):
            lane = (pair % 2) * 128
            weight_ref[4 * which + pair // 2, pl.ds(row, 32), lane : lane + 128] = piece

        assemble_columns(inv_ref, which, tiles_ref, put)
        stores[which].start()

    loads[2].wait()
    stage_blocks(blocks_ref.at[2], tiles_ref, 0)
    for local_row in range(4):
        for pair in range(8):
            cell = (quarter * 4 + local_row) * 16 + 2 * pair
            even, odd = assembled_pair(tiles_ref, inv_ref[2, cell], inv_ref[2, cell + 1])
            row = local_row * BLK
            down_dense_ref[row : row + 32, 128 * pair : 128 * (pair + 1)] = even
            down_dense_ref[row + 32 : row + 64, 128 * pair : 128 * (pair + 1)] = odd
    payload_ref[32:64, :] = contract_last(sketch_ref[...], down_dense_ref[...])

    local = index_ref[...] - owner * 1024
    inside = (local >= 0) & (local < 1024)
    safe = jnp.where(inside, local, 0)
    spot = shuffled(safe)
    high_part = jnp.where(inside, spot // 128, -1)
    low_part = spot % 128
    values = value_ref[...]
    high_iota = lax.broadcasted_iota(jnp.int32, (8, 256), 0)
    low_iota = lax.broadcasted_iota(jnp.int32, (128, 256), 0)
    for probe in range(P_SIZE):
        picked = jnp.where(
            high_iota == high_part[probe : probe + 1, :], values[probe : probe + 1, :], 0.0
        )
        one_hot = jnp.where(low_iota == low_part[probe : probe + 1, :], 1.0, 0.0).astype(BF)
        terms = contract_last(jnp.concatenate(split3(picked), axis=0), one_hot)
        total = terms[:8] + terms[8:16] + terms[16:]
        omega_ref[8 * probe : 8 * (probe + 1), :] = total
    for high in range(8):
        piece = omega_ref[pl.ds(high, 16, stride=8), :]
        for part_index, part in enumerate(split3(piece)):
            split_ref[
                16 * part_index : 16 * (part_index + 1), 128 * high : 128 * (high + 1)
            ] = part
    for which in range(2):
        triple = dot(split_ref[...], weight_ref[4 * which + quarter])
        payload_ref[16 * which : 16 * (which + 1), :] = triple[:16] + triple[16:32] + triple[32:]
    for store in stores:
        store.wait()


def flipped(two_bits, flip):
    low_bit = lax.rem(two_bits + flip % 2, 2)
    return low_bit + 2 * lax.rem(two_bits // 2 + flip // 2, 2)


def shuffle_tokens(side, tok_ref, tokens_ref):
    shuffle = shuffle_matrix(256)
    for group in range(8):
        piece = tok_ref[:, :, 256 * group : 256 * (group + 1)].reshape(256, 256)
        half = lax.rem(group // 4 + side, 2)
        tokens_ref[half, :, 256 * (group % 4) : 256 * (group % 4 + 1)] = dot(piece, shuffle).astype(
            BF
        )


def first_kernel(
    inv_ref,
    a_in_ref,
    b_in_ref,
    a_other_ref,
    weight_in_ref,
    tok_in_ref,
    keep_ref,
    sent_out_ref,
    near_out_ref,
    tokens_out_ref,
    tiles_ref,
    near_ref,
    own_ref,
    tokens_ref,
    sent_ref,
    total_ref,
    in_sem,
    near_sem,
    sent_sem,
):
    owner, quarter, side, core = position()
    zone = owner // 2
    group = quarter // 2
    load = pltpu.make_async_copy(weight_in_ref.at[pl.ds(4 * core, 4)], own_ref, in_sem)
    load.start()
    clear_empty_slot(tiles_ref)
    stage_blocks(a_in_ref, tiles_ref, SHARED * group)
    stage_blocks(a_other_ref, tiles_ref, SHARED * (1 - group))
    stage_blocks(b_in_ref, tiles_ref, 2 * SHARED)

    def put(pair, row, piece):
        lane = (pair % 2) * 128
        near_ref[pair // 2, pl.ds(row, 32), lane : lane + 128] = piece

    assemble_columns(inv_ref, core, tiles_ref, put)
    near_store = pltpu.make_async_copy(near_ref, near_out_ref, near_sem.at[0])
    near_store.start()
    shuffle_tokens(side, tok_in_ref, tokens_ref)
    tokens_store = pltpu.make_async_copy(tokens_ref, tokens_out_ref, near_sem.at[1])
    tokens_store.start()
    load.wait()
    stores = []
    for chunk in range(4):
        total = dot(tokens_ref[0], own_ref[chunk]) + dot(tokens_ref[1], near_ref[chunk])
        cols = slice(256 * chunk, 256 * (chunk + 1))
        total_ref[...] = total
        keep_ref[:, cols] = total_ref[pl.ds(pl.multiple_of(64 * zone, 64), 64), :]
        sent_ref[:, :, cols] = total.astype(BF).reshape(4, 64, 256)
        lanes = pl.ds(256 * chunk, 256)
        store = pltpu.make_async_copy(
            sent_ref.at[:, :, lanes], sent_out_ref.at[:, :, lanes], sent_sem.at[chunk]
        )
        store.start()
        stores.append(store)
    for store in stores:
        store.wait()
    near_store.wait()
    tokens_store.wait()


def second_kernel(
    near_in_ref,
    weight_in_ref,
    tokens_in_ref,
    keep_ref,
    out1_ref,
    out2_ref,
    out3_ref,
    near_ref,
    own_ref,
    tokens_ref,
    total_ref,
    in_sem,
):
    owner, unused_quarter, unused_side, core = position()
    zone = owner // 2
    loads = [
        pltpu.make_async_copy(tokens_in_ref, tokens_ref, in_sem.at[0]),
        pltpu.make_async_copy(weight_in_ref.at[pl.ds(4 - 4 * core, 4)], own_ref, in_sem.at[1]),
        pltpu.make_async_copy(near_in_ref, near_ref, in_sem.at[2]),
    ]
    for load in loads:
        load.start()
    for load in loads:
        load.wait()
    for chunk in range(4):
        total = dot(tokens_ref[0], own_ref[chunk]) + dot(tokens_ref[1], near_ref[chunk])
        cols = slice(256 * chunk, 256 * (chunk + 1))
        total_ref[...] = total
        keep_ref[:, cols] = total_ref[pl.ds(pl.multiple_of(64 * zone, 64), 64), :]
        for flip, ref in enumerate((out1_ref, out2_ref, out3_ref), 1):
            row = pl.multiple_of(64 * flipped(zone, flip), 64)
            ref[:, cols] = total_ref[pl.ds(row, 64), :].astype(BF)


def middle_kernel(
    first_keep_ref,
    first_ref,
    second_keep_ref,
    second1_ref,
    second2_ref,
    second3_ref,
    pay0_ref,
    pay1_ref,
    pay2_ref,
    pay3_ref,
    mine_ref,
    theirs_ref,
    lead_ref,
    act_ref,
    pay_ref,
    proj_ref,
    tangent_ref,
    rows_ref,
):
    owner, quarter, unused_side, core = position()
    zone = owner // 2
    unshuffle = unshuffle_matrix(256)
    for flip, ref in enumerate((pay0_ref, pay1_ref, pay2_ref, pay3_ref)):
        pay_ref[flipped(quarter, flip)] = ref[...]
    for chunk in range(4):
        cols = slice(256 * chunk, 256 * (chunk + 1))
        proj_ref[:, cols] = dot(pay_ref[chunk, 32:64, :].astype(BF), unshuffle).astype(BF)
        first = first_keep_ref[:, cols]
        for flip in (1, 2, 3):
            first = first + first_ref[flipped(zone, flip), :, cols].astype(F32)
        second = second_keep_ref[:, cols]
        for ref in (second1_ref, second2_ref, second3_ref):
            second = second + ref[:, cols].astype(F32)
        gate_pre = jnp.where(core == 0, first, second)
        up_pre = jnp.where(core == 0, second, first)
        sigmoid_g = jax.nn.sigmoid(gate_pre)
        activated = gate_pre * sigmoid_g
        slope_g = sigmoid_g * (1.0 + gate_pre * (1.0 - sigmoid_g))
        lead = slope_g * up_pre
        lead_ref[:, cols] = lead
        act_ref[:, cols] = activated
        for probe in range(P_SIZE):
            probe_gate = pay_ref[chunk, probe : probe + 1, :]
            probe_up = pay_ref[chunk, 16 + probe : 17 + probe, :]
            tangent_ref[64 * probe : 64 * (probe + 1), cols] = (
                lead * probe_gate + activated * probe_up
            ).astype(BF)
    rows_ref[...] = contract_last(tangent_ref[...], proj_ref[...]).astype(BF)
    for step in range(P_SIZE):
        probe = lax.rem(step + 8 * core, P_SIZE)
        backward = dot(rows_ref[pl.ds(pl.multiple_of(probe * 64, 64), 64), :], proj_ref[...])
        target = mine_ref if step < 8 else theirs_ref
        row = slice(step % 8, step % 8 + 1)
        target[row, :1024] = jnp.sum(backward * lead_ref[...], axis=0, keepdims=True)
        target[row, 1024:] = jnp.sum(backward * act_ref[...], axis=0, keepdims=True)


def fetch_kernel(weight_in_ref, weight_out_ref, sem):
    copy = pltpu.make_async_copy(weight_in_ref, weight_out_ref, sem)
    copy.start()
    copy.wait()


def product_kernel(mine_ref, theirs_ref, weight_ref, out_ref, sum_ref):
    core = lax.axis_index("seq")
    sum_ref[core] = mine_ref[...]
    sum_ref[1 - core] = theirs_ref[...]
    sums = jnp.concatenate([sum_ref[0], sum_ref[1]], axis=0)
    total = None
    for chunk in range(8):
        term = contract_last(sums[:, 256 * chunk : 256 * (chunk + 1)], weight_ref[chunk])
        total = term if total is None else total + term
    unshuffle = unshuffle_matrix(256)
    for group in range(4):
        cols = slice(256 * group, 256 * (group + 1))
        high, mid, low = split3(total[:, cols])
        out_ref[:, cols] = dot(high, unshuffle) + dot(mid, unshuffle) + dot(low, unshuffle)


def pair_split(
    tokens,
    gate_blocks,
    gate_slot,
    up_blocks,
    up_slot,
    down_blocks,
    down_slot,
    sketch,
    probe_index,
    probe_value,
):
    def owner_flip(value, bits):
        return lax.ppermute(value, "fsdp", [(i, i ^ bits) for i in range(8)])

    def core_flip(value):
        return lax.ppermute(value, "seq", [(0, 1), (1, 0)])

    def zone_exchange(value):
        return lax.all_to_all(
            value,
            "fsdp",
            split_axis=0,
            concat_axis=0,
            tiled=True,
            axis_index_groups=[[0, 2, 4, 6], [1, 3, 5, 7]],
        )

    by_zone, kind_a, kind_b = pl.pallas_call(
        head_kernel,
        out_shape=(
            jax.ShapeDtypeStruct((4, 64, 2048), BF),
            jax.ShapeDtypeStruct((SHARED, 4096), BF),
            jax.ShapeDtypeStruct((160 - 2 * SHARED, 4096), BF),
        ),
        in_specs=[HBM, HBM, HBM],
        out_specs=(HBM,) * 3,
        scratch_shapes=[
            pltpu.VMEM((4, 64, 2048), BF),
            pltpu.VMEM((160, 4096), BF),
            pltpu.SemaphoreType.DMA((12,)),
        ],
        compiler_params=params(60),
        name="head",
    )(tokens, gate_blocks, up_blocks)
    near_a = owner_flip(kind_a, 1)
    near_b = owner_flip(kind_b, 1)
    gathered = zone_exchange(by_zone)

    slots = jnp.stack([gate_slot, up_slot, down_slot])
    cells = lax.broadcasted_iota(jnp.int32, (3, 160, 256), 2)
    slot_numbers = lax.broadcasted_iota(jnp.int32, (3, 160, 256), 1)
    inv = jnp.min(jnp.where(slots[:, :, None] == cells, slot_numbers, 160), axis=1)
    near_inv = owner_flip(inv, 1)

    weights, payload = pl.pallas_call(
        own_kernel,
        out_shape=(
            jax.ShapeDtypeStruct((8, 1024, 256), BF),
            jax.ShapeDtypeStruct((64, 256), F32),
        ),
        in_specs=[SMEM] + [HBM] * 3 + [VMEM] * 3,
        out_specs=(HBM, VMEM),
        scratch_shapes=[
            pltpu.VMEM((33 * STRIDE, 128), F32),
            pltpu.VMEM((136, 128), F32),
            pltpu.VMEM((48, 1024), BF),
            pltpu.VMEM((256, 1024), BF),
            pltpu.VMEM((3, 160, 4096), BF),
            pltpu.VMEM((8, 1024, 256), BF),
            pltpu.SemaphoreType.DMA((3,)),
            pltpu.SemaphoreType.DMA((2,)),
        ],
        compiler_params=params(60),
        name="own_blocks",
    )(inv, gate_blocks, up_blocks, down_blocks, sketch, probe_index, probe_value)

    near_a, payload = lax.optimization_barrier((near_a, payload))
    near_a_other = lax.ppermute(near_a, "groups", [(0, 1), (1, 0)])
    for bits in (2, 4):
        payload = payload + owner_flip(payload, bits)
    near_inv, near_b, near_a_other, gathered, payload = lax.optimization_barrier(
        (near_inv, near_b, near_a_other, gathered, payload)
    )

    first_keep, first_sent, near_weights, shuffled_tokens = pl.pallas_call(
        first_kernel,
        out_shape=(
            jax.ShapeDtypeStruct((64, 1024), F32),
            jax.ShapeDtypeStruct((4, 64, 1024), BF),
            jax.ShapeDtypeStruct((4, 1024, 256), BF),
            pltpu.HBM((2, 256, 1024), BF),
        ),
        in_specs=[SMEM, VMEM, VMEM, VMEM, HBM, VMEM],
        out_specs=(VMEM, HBM, HBM, HBM),
        scratch_shapes=[
            pltpu.VMEM((33 * STRIDE, 128), F32),
            pltpu.VMEM((4, 1024, 256), BF),
            pltpu.VMEM((4, 1024, 256), BF),
            pltpu.VMEM((2, 256, 1024), BF),
            pltpu.VMEM((4, 64, 1024), BF),
            pltpu.VMEM((256, 256), F32),
            pltpu.SemaphoreType.DMA,
            pltpu.SemaphoreType.DMA((2,)),
            pltpu.SemaphoreType.DMA((4,)),
        ],
        compiler_params=params(46),
        name="first_partial",
    )(near_inv, near_a, near_b, near_a_other, weights, gathered)
    first_back = zone_exchange(first_sent)

    second_keep, *second_sent = pl.pallas_call(
        second_kernel,
        out_shape=(jax.ShapeDtypeStruct((64, 1024), F32),)
        + (jax.ShapeDtypeStruct((64, 1024), BF),) * 3,
        in_specs=[ANY, HBM, ANY],
        out_specs=(VMEM,) * 4,
        scratch_shapes=[
            pltpu.VMEM((4, 1024, 256), BF),
            pltpu.VMEM((4, 1024, 256), BF),
            pltpu.VMEM((2, 256, 1024), BF),
            pltpu.VMEM((256, 256), F32),
            pltpu.SemaphoreType.DMA((3,)),
        ],
        compiler_params=params(56),
        name="second_partial",
    )(core_flip(near_weights), weights, shuffled_tokens)
    second_back = [owner_flip(second_sent[flip - 1], 2 * flip) for flip in (1, 2, 3)]

    across = owner_flip(payload, 1)
    second_keep, across = lax.optimization_barrier((second_keep, across))
    payload = payload + across
    pay_parts = [
        payload,
        core_flip(payload),
        lax.ppermute(payload, "groups", [(0, 1), (1, 0)]),
        lax.ppermute(payload, ("groups", "seq"), [(i, i ^ 3) for i in range(4)]),
    ]

    first_back, weights = lax.optimization_barrier((first_back, weights))
    weights_at_hand = pl.pallas_call(
        fetch_kernel,
        out_shape=jax.ShapeDtypeStruct((8, 1024, 256), BF),
        in_specs=[HBM],
        out_specs=VMEM,
        scratch_shapes=[pltpu.SemaphoreType.DMA],
        compiler_params=params(48),
        name="fetch_weights",
    )(weights)
    pay_parts[0], weights_at_hand = lax.optimization_barrier((pay_parts[0], weights_at_hand))

    mine, theirs = pl.pallas_call(
        middle_kernel,
        out_shape=(jax.ShapeDtypeStruct((8, 2048), F32),) * 2,
        in_specs=[VMEM] * 10,
        out_specs=(VMEM,) * 2,
        scratch_shapes=[
            pltpu.VMEM((64, 1024), F32),
            pltpu.VMEM((64, 1024), F32),
            pltpu.VMEM((4, 64, 256), F32),
            pltpu.VMEM((K, 1024), BF),
            pltpu.VMEM((64 * P_SIZE, 1024), BF),
            pltpu.VMEM((64 * P_SIZE, K), BF),
        ],
        compiler_params=params(48),
        name="token_sums",
    )(first_keep, first_back, second_keep, *second_back, *pay_parts)

    sums = mine + core_flip(theirs)
    sums = sums + owner_flip(sums.astype(BF), 1).astype(F32)
    parts = [owner_flip(sums.astype(BF), bits).astype(F32) for bits in (2, 4, 6)]
    sums = ((sums + parts[0]) + (parts[1] + parts[2])).astype(BF)

    return pl.pallas_call(
        product_kernel,
        out_shape=jax.ShapeDtypeStruct((P_SIZE, 1024), F32),
        in_specs=[VMEM, VMEM, VMEM],
        out_specs=VMEM,
        scratch_shapes=[pltpu.VMEM((2, 8, 2048), BF)],
        compiler_params=params(30),
        name="products",
    )(sums, core_flip(sums), weights_at_hand)


def per_device(tokens, gate_blocks, *rest):
    fits = (
        lax.axis_size("fsdp") == 8
        and lax.axis_size("seq") == 2
        and lax.axis_size("groups") == 2
        and tokens.shape == (64, 8192)
        and gate_blocks.shape == (160, 4096)
        and rest[-2].shape == (P_SIZE, 256)
    )
    return (pair_split if fits else hidden_split)(tokens, gate_blocks, *rest)


def solution(mesh):
    in_specs = (
        P(("groups", "fsdp", "seq"), None),
        P("fsdp", None),
        P("fsdp"),
        P("fsdp", None),
        P("fsdp"),
        P("fsdp", None),
        P("fsdp"),
        P(None, "fsdp"),
        P(),
        P(),
    )
    out_specs = P("groups", "fsdp")
    return jax.shard_map(
        per_device, mesh=mesh, in_specs=in_specs, out_specs=out_specs, check_vma=False
    )
```

```python
import functools

import jax
import jax.numpy as jnp
from jax import lax
from jax.experimental import pallas as pl
from jax.experimental.pallas import tpu as pltpu
from jax.sharding import PartitionSpec as P

HID_DEV = 128
BLK = 64
P_SIZE = 16
K = 32

BF = jnp.bfloat16
F32 = jnp.float32
VMEM = pl.BlockSpec(memory_space=pltpu.VMEM)
SMEM = pl.BlockSpec(memory_space=pltpu.SMEM)
HBM = pl.BlockSpec(memory_space=pltpu.HBM)
ANY = pl.BlockSpec(memory_space=pl.ANY)

STRIDE = 168
SHARED = 48


def params(mebibytes):
    return pltpu.CompilerParams(vmem_limit_bytes=int(mebibytes * 1024 * 1024))


def unpack(blocks, slot_ids, cell_total):
    holder = jnp.zeros((cell_total + 1, blocks.shape[1]), blocks.dtype)
    return holder.at[slot_ids].set(blocks)[:cell_total]


def contract_last(first_mat, second_mat):
    return lax.dot_general(
        first_mat, second_mat, (((1,), (1,)), ((), ())), preferred_element_type=jnp.float32
    )


def hidden_split(
    tokens,
    gate_blocks,
    gate_slot,
    up_blocks,
    up_slot,
    down_blocks,
    down_slot,
    sketch,
    probe_index,
    probe_value,
):
    owners = lax.axis_size("fsdp")
    model_width = tokens.shape[1]
    local_width = model_width // owners
    block_rows = local_width // BLK
    hidden = HID_DEV
    col_blocks = hidden * owners // BLK
    cell_total = block_rows * col_blocks
    gate_dense = unpack(gate_blocks, gate_slot, cell_total).reshape(
        block_rows, col_blocks, BLK, BLK
    )
    up_dense = unpack(up_blocks, up_slot, cell_total).reshape(block_rows, col_blocks, BLK, BLK)
    stacked = jnp.stack([gate_dense, up_dense], axis=1)
    stacked = stacked.reshape(block_rows, 2, owners, hidden // BLK, BLK, BLK)
    stacked = stacked.transpose(0, 4, 2, 1, 3, 5).reshape(local_width, owners * 2 * hidden)
    both_weights = lax.all_to_all(stacked, "fsdp", split_axis=1, concat_axis=0, tiled=True)
    picked = both_weights[probe_index].astype(jnp.float32)
    probe_both = jnp.sum(picked * probe_value[:, :, None], axis=1)
    preact = jnp.dot(
        lax.all_gather(tokens, "fsdp", axis=0, tiled=True),
        both_weights,
        preferred_element_type=jnp.float32,
    )
    row_count = preact.shape[0]
    gate_pre = preact[:, :hidden]
    up_pre = preact[:, hidden:]
    down_dense = unpack(down_blocks, down_slot, cell_total).reshape(
        col_blocks, block_rows, BLK, BLK
    )
    down_dense = down_dense.transpose(0, 2, 1, 3).reshape(col_blocks * BLK, local_width)
    down_rows = lax.all_to_all(down_dense, "fsdp", split_axis=0, concat_axis=1, tiled=True)
    full_sketch = lax.all_gather(sketch, "fsdp", axis=1, tiled=True)
    projected = contract_last(down_rows, full_sketch)
    projected = projected.astype(jnp.bfloat16)
    sigmoid_g = jax.nn.sigmoid(gate_pre)
    activated = gate_pre * sigmoid_g
    slope_g = sigmoid_g * (1.0 + gate_pre * (1.0 - sigmoid_g))
    lead_term = slope_g * up_pre
    tangent = (
        lead_term[:, None, :] * probe_both[None, :, :hidden]
        + activated[:, None, :] * probe_both[None, :, hidden:]
    )
    tangent = tangent.astype(jnp.bfloat16)
    partial_sketch = jnp.dot(
        tangent.reshape(row_count * P_SIZE, hidden), projected, preferred_element_type=jnp.float32
    )
    partial_sketch = partial_sketch.reshape(row_count, P_SIZE * K)
    sketch_rows = lax.psum(partial_sketch, "fsdp").astype(jnp.bfloat16)
    backward = contract_last(sketch_rows.reshape(row_count * P_SIZE, K), projected).reshape(
        row_count, P_SIZE, hidden
    )
    summed = jnp.concatenate(
        [
            jnp.sum(backward * lead_term[:, None, :], axis=0),
            jnp.sum(backward * activated[:, None, :], axis=0),
        ],
        axis=1,
    )
    summed = lax.psum(summed, "seq").astype(jnp.bfloat16)
    products = contract_last(summed, both_weights)
    return lax.psum_scatter(products, "fsdp", scatter_dimension=1, tiled=True)


def dot(a, b):
    return jnp.dot(a, b, preferred_element_type=F32)


def split3(value):
    high = value.astype(BF)
    rest = value - high.astype(F32)
    mid = rest.astype(BF)
    low = (rest - mid.astype(F32)).astype(BF)
    return high, mid, low


def shuffled(natural):
    return (natural // BLK) * BLK + (natural % 2) * (BLK // 2) + (natural % BLK) // 2


def shuffle_matrix(size):
    rows = lax.broadcasted_iota(jnp.int32, (size, size), 0)
    cols = lax.broadcasted_iota(jnp.int32, (size, size), 1)
    return jnp.where(shuffled(rows) == cols, 1.0, 0.0).astype(BF)


def unshuffle_matrix(size):
    rows = lax.broadcasted_iota(jnp.int32, (size, size), 0)
    cols = lax.broadcasted_iota(jnp.int32, (size, size), 1)
    return jnp.where(shuffled(cols) == rows, 1.0, 0.0).astype(BF)


def stage_blocks(blocks_ref, tiles_ref, first_slot):
    @pl.loop(0, blocks_ref.shape[0] // 16, unroll=2)
    def _(step):
        row = pl.multiple_of(step * 16, 16)
        target = pl.multiple_of(first_slot + row, 16)
        for chunk in range(32):
            piece = blocks_ref[pl.ds(row, 16), 128 * chunk : 128 * (chunk + 1)].astype(F32)
            tiles_ref[pl.ds(target + chunk * STRIDE, 16), :] = piece


def clear_empty_slot(tiles_ref):
    for chunk in range(32):
        tiles_ref[pl.ds(chunk * STRIDE + 160, 8), :] = jnp.zeros((8, 128), F32)


def assembled_pair(tiles_ref, left_slot, right_slot):
    left = tiles_ref[pl.ds(left_slot, 32, stride=STRIDE), :]
    right = tiles_ref[pl.ds(right_slot, 32, stride=STRIDE), :]
    low_half = lax.broadcasted_iota(jnp.int32, (32, 128), 1) < BLK
    straight = jnp.where(low_half, left, right)
    crossed = pltpu.roll(jnp.where(low_half, right, left), BLK, 1)
    even = jnp.where(low_half, straight, crossed)
    odd = jnp.where(low_half, crossed, straight)
    return even.astype(BF), odd.astype(BF)


def assemble_columns(inv_ref, inv_row, tiles_ref, put):
    @pl.loop(0, 16, unroll=8)
    def _(block_row):
        for pair in range(8):
            cell = block_row * 16 + 2 * pair
            even, odd = assembled_pair(
                tiles_ref, inv_ref[inv_row, cell], inv_ref[inv_row, cell + 1]
            )
            row = pl.multiple_of(block_row * BLK, BLK)
            put(pair, row, even)
            put(pair, row + BLK // 2, odd)


def position():
    owner = lax.axis_index("fsdp")
    core = lax.axis_index("seq")
    return owner, 2 * lax.axis_index("groups") + core, lax.rem(owner, 2), core


def head_kernel(
    tok_in_ref, gate_ref, up_ref, zone_out_ref, a_out_ref, b_out_ref, tok_ref, blocks_ref, sem
):
    unused_owner, quarter, unused_side, core = position()
    first = pl.multiple_of(SHARED * (quarter // 2), 16)
    a_part = pl.ds(first, SHARED)
    b_part = pl.ds(2 * SHARED, 160 - 2 * SHARED)
    loads, stores = [], []
    for zone in range(4):
        held = tok_ref.at[zone]
        lanes = pl.ds(2048 * zone, 2048)
        loads.append(pltpu.make_async_copy(tok_in_ref.at[:, lanes], held, sem.at[zone]))
        stores.append(pltpu.make_async_copy(held, zone_out_ref.at[zone], sem.at[4 + zone]))
    for load in loads:
        load.start()
    for kind, source in enumerate((gate_ref, up_ref)):

        @pl.when(core == kind)
        def _():
            pltpu.make_async_copy(source.at[a_part], blocks_ref.at[a_part], sem.at[8]).start()
            pltpu.make_async_copy(source.at[b_part], blocks_ref.at[b_part], sem.at[9]).start()

    for load, store in zip(loads, stores):
        load.wait()
        store.start()
    pltpu.make_async_copy(gate_ref.at[a_part], blocks_ref.at[a_part], sem.at[8]).wait()
    stores.append(pltpu.make_async_copy(blocks_ref.at[a_part], a_out_ref, sem.at[10]))
    stores[4].start()
    pltpu.make_async_copy(gate_ref.at[b_part], blocks_ref.at[b_part], sem.at[9]).wait()
    stores.append(pltpu.make_async_copy(blocks_ref.at[b_part], b_out_ref, sem.at[11]))
    stores[5].start()
    for store in stores:
        store.wait()


def own_kernel(
    inv_ref,
    gate_ref,
    up_ref,
    down_ref,
    sketch_ref,
    index_ref,
    value_ref,
    weight_out_ref,
    payload_ref,
    tiles_ref,
    omega_ref,
    split_ref,
    down_dense_ref,
    blocks_ref,
    weight_ref,
    in_sem,
    out_sem,
):
    owner, quarter, unused_side, unused_core = position()
    loads = [
        pltpu.make_async_copy(source, blocks_ref.at[i], in_sem.at[i])
        for i, source in enumerate((gate_ref, up_ref, down_ref))
    ]
    stores = [
        pltpu.make_async_copy(
            weight_ref.at[pl.ds(4 * i, 4)], weight_out_ref.at[pl.ds(4 * i, 4)], out_sem.at[i]
        )
        for i in range(2)
    ]
    for load in loads:
        load.start()
    clear_empty_slot(tiles_ref)

    for which in range(2):
        loads[which].wait()
        stage_blocks(blocks_ref.at[which], tiles_ref, 0)

        def put(pair, row, piece):
            lane = (pair % 2) * 128
            weight_ref[4 * which + pair // 2, pl.ds(row, 32), lane : lane + 128] = piece

        assemble_columns(inv_ref, which, tiles_ref, put)
        stores[which].start()

    loads[2].wait()
    stage_blocks(blocks_ref.at[2], tiles_ref, 0)
    for local_row in range(4):
        for pair in range(8):
            cell = (quarter * 4 + local_row) * 16 + 2 * pair
            even, odd = assembled_pair(tiles_ref, inv_ref[2, cell], inv_ref[2, cell + 1])
            row = local_row * BLK
            down_dense_ref[row : row + 32, 128 * pair : 128 * (pair + 1)] = even
            down_dense_ref[row + 32 : row + 64, 128 * pair : 128 * (pair + 1)] = odd
    payload_ref[32:64, :] = contract_last(sketch_ref[...], down_dense_ref[...])

    local = index_ref[...] - owner * 1024
    inside = (local >= 0) & (local < 1024)
    safe = jnp.where(inside, local, 0)
    spot = shuffled(safe)
    high_part = jnp.where(inside, spot // 128, -1)
    low_part = spot % 128
    values = value_ref[...]
    high_iota = lax.broadcasted_iota(jnp.int32, (8, 256), 0)
    low_iota = lax.broadcasted_iota(jnp.int32, (128, 256), 0)
    for probe in range(P_SIZE):
        picked = jnp.where(
            high_iota == high_part[probe : probe + 1, :], values[probe : probe + 1, :], 0.0
        )
        one_hot = jnp.where(low_iota == low_part[probe : probe + 1, :], 1.0, 0.0).astype(BF)
        terms = contract_last(jnp.concatenate(split3(picked), axis=0), one_hot)
        total = terms[:8] + terms[8:16] + terms[16:]
        omega_ref[8 * probe : 8 * (probe + 1), :] = total
    for high in range(8):
        piece = omega_ref[pl.ds(high, 16, stride=8), :]
        for part_index, part in enumerate(split3(piece)):
            split_ref[
                16 * part_index : 16 * (part_index + 1), 128 * high : 128 * (high + 1)
            ] = part
    for which in range(2):
        triple = dot(split_ref[...], weight_ref[4 * which + quarter])
        payload_ref[16 * which : 16 * (which + 1), :] = triple[:16] + triple[16:32] + triple[32:]
    for store in stores:
        store.wait()


def flipped(two_bits, flip):
    low_bit = lax.rem(two_bits + flip % 2, 2)
    return low_bit + 2 * lax.rem(two_bits // 2 + flip // 2, 2)


def shuffle_tokens(side, tok_ref, tokens_ref):
    shuffle = shuffle_matrix(256)
    for group in range(8):
        piece = tok_ref[:, :, 256 * group : 256 * (group + 1)].reshape(256, 256)
        half = lax.rem(group // 4 + side, 2)
        tokens_ref[half, :, 256 * (group % 4) : 256 * (group % 4 + 1)] = dot(piece, shuffle).astype(
            BF
        )


def first_kernel(
    inv_ref,
    a_in_ref,
    b_in_ref,
    a_other_ref,
    weight_in_ref,
    tok_in_ref,
    keep_ref,
    sent_out_ref,
    near_out_ref,
    tokens_out_ref,
    tiles_ref,
    near_ref,
    own_ref,
    tokens_ref,
    sent_ref,
    total_ref,
    in_sem,
    near_sem,
    sent_sem,
):
    owner, quarter, side, core = position()
    zone = owner // 2
    group = quarter // 2
    load = pltpu.make_async_copy(weight_in_ref.at[pl.ds(4 * core, 4)], own_ref, in_sem)
    load.start()
    clear_empty_slot(tiles_ref)
    stage_blocks(a_in_ref, tiles_ref, SHARED * group)
    stage_blocks(a_other_ref, tiles_ref, SHARED * (1 - group))
    stage_blocks(b_in_ref, tiles_ref, 2 * SHARED)

    def put(pair, row, piece):
        lane = (pair % 2) * 128
        near_ref[pair // 2, pl.ds(row, 32), lane : lane + 128] = piece

    assemble_columns(inv_ref, core, tiles_ref, put)
    near_store = pltpu.make_async_copy(near_ref, near_out_ref, near_sem.at[0])
    near_store.start()
    shuffle_tokens(side, tok_in_ref, tokens_ref)
    tokens_store = pltpu.make_async_copy(tokens_ref, tokens_out_ref, near_sem.at[1])
    tokens_store.start()
    load.wait()
    stores = []
    for chunk in range(4):
        total = dot(tokens_ref[0], own_ref[chunk]) + dot(tokens_ref[1], near_ref[chunk])
        cols = slice(256 * chunk, 256 * (chunk + 1))
        total_ref[...] = total
        keep_ref[:, cols] = total_ref[pl.ds(pl.multiple_of(64 * zone, 64), 64), :]
        sent_ref[:, :, cols] = total.astype(BF).reshape(4, 64, 256)
        lanes = pl.ds(256 * chunk, 256)
        store = pltpu.make_async_copy(
            sent_ref.at[:, :, lanes], sent_out_ref.at[:, :, lanes], sent_sem.at[chunk]
        )
        store.start()
        stores.append(store)
    for store in stores:
        store.wait()
    near_store.wait()
    tokens_store.wait()


def second_kernel(
    near_in_ref,
    weight_in_ref,
    tokens_in_ref,
    keep_ref,
    out1_ref,
    out2_ref,
    out3_ref,
    near_ref,
    own_ref,
    tokens_ref,
    total_ref,
    in_sem,
):
    owner, unused_quarter, unused_side, core = position()
    zone = owner // 2
    loads = [
        pltpu.make_async_copy(tokens_in_ref, tokens_ref, in_sem.at[0]),
        pltpu.make_async_copy(weight_in_ref.at[pl.ds(4 - 4 * core, 4)], own_ref, in_sem.at[1]),
        pltpu.make_async_copy(near_in_ref, near_ref, in_sem.at[2]),
    ]
    for load in loads:
        load.start()
    for load in loads:
        load.wait()
    for chunk in range(4):
        total = dot(tokens_ref[0], own_ref[chunk]) + dot(tokens_ref[1], near_ref[chunk])
        cols = slice(256 * chunk, 256 * (chunk + 1))
        total_ref[...] = total
        keep_ref[:, cols] = total_ref[pl.ds(pl.multiple_of(64 * zone, 64), 64), :]
        for flip, ref in enumerate((out1_ref, out2_ref, out3_ref), 1):
            row = pl.multiple_of(64 * flipped(zone, flip), 64)
            ref[:, cols] = total_ref[pl.ds(row, 64), :].astype(BF)


def middle_kernel(
    first_keep_ref,
    first_ref,
    second_keep_ref,
    second1_ref,
    second2_ref,
    second3_ref,
    pay0_ref,
    pay1_ref,
    pay2_ref,
    pay3_ref,
    mine_ref,
    theirs_ref,
    lead_ref,
    act_ref,
    pay_ref,
    proj_ref,
    tangent_ref,
    rows_ref,
):
    owner, quarter, unused_side, core = position()
    zone = owner // 2
    unshuffle = unshuffle_matrix(256)
    for flip, ref in enumerate((pay0_ref, pay1_ref, pay2_ref, pay3_ref)):
        pay_ref[flipped(quarter, flip)] = ref[...]
    for chunk in range(4):
        cols = slice(256 * chunk, 256 * (chunk + 1))
        proj_ref[:, cols] = dot(pay_ref[chunk, 32:64, :].astype(BF), unshuffle).astype(BF)
        first = first_keep_ref[:, cols]
        for flip in (1, 2, 3):
            first = first + first_ref[flipped(zone, flip), :, cols].astype(F32)
        second = second_keep_ref[:, cols]
        for ref in (second1_ref, second2_ref, second3_ref):
            second = second + ref[:, cols].astype(F32)
        gate_pre = jnp.where(core == 0, first, second)
        up_pre = jnp.where(core == 0, second, first)
        sigmoid_g = jax.nn.sigmoid(gate_pre)
        activated = gate_pre * sigmoid_g
        slope_g = sigmoid_g * (1.0 + gate_pre * (1.0 - sigmoid_g))
        lead = slope_g * up_pre
        lead_ref[:, cols] = lead
        act_ref[:, cols] = activated
        for probe in range(P_SIZE):
            probe_gate = pay_ref[chunk, probe : probe + 1, :]
            probe_up = pay_ref[chunk, 16 + probe : 17 + probe, :]
            tangent_ref[64 * probe : 64 * (probe + 1), cols] = (
                lead * probe_gate + activated * probe_up
            ).astype(BF)
    rows_ref[...] = contract_last(tangent_ref[...], proj_ref[...]).astype(BF)
    for step in range(P_SIZE):
        probe = lax.rem(step + 8 * core, P_SIZE)
        backward = dot(rows_ref[pl.ds(pl.multiple_of(probe * 64, 64), 64), :], proj_ref[...])
        target = mine_ref if step < 8 else theirs_ref
        row = slice(step % 8, step % 8 + 1)
        target[row, :1024] = jnp.sum(backward * lead_ref[...], axis=0, keepdims=True)
        target[row, 1024:] = jnp.sum(backward * act_ref[...], axis=0, keepdims=True)


def fetch_kernel(weight_in_ref, weight_out_ref, sem):
    copy = pltpu.make_async_copy(weight_in_ref, weight_out_ref, sem)
    copy.start()
    copy.wait()


def product_kernel(mine_ref, theirs_ref, weight_ref, out_ref, sum_ref):
    core = lax.axis_index("seq")
    sum_ref[core] = mine_ref[...]
    sum_ref[1 - core] = theirs_ref[...]
    sums = jnp.concatenate([sum_ref[0], sum_ref[1]], axis=0)
    total = None
    for chunk in range(8):
        term = contract_last(sums[:, 256 * chunk : 256 * (chunk + 1)], weight_ref[chunk])
        total = term if total is None else total + term
    unshuffle = unshuffle_matrix(256)
    for group in range(4):
        cols = slice(256 * group, 256 * (group + 1))
        high, mid, low = split3(total[:, cols])
        out_ref[:, cols] = dot(high, unshuffle) + dot(mid, unshuffle) + dot(low, unshuffle)


def pair_split(
    tokens,
    gate_blocks,
    gate_slot,
    up_blocks,
    up_slot,
    down_blocks,
    down_slot,
    sketch,
    probe_index,
    probe_value,
):
    def owner_flip(value, bits):
        return lax.ppermute(value, "fsdp", [(i, i ^ bits) for i in range(8)])

    def core_flip(value):
        return lax.ppermute(value, "seq", [(0, 1), (1, 0)])

    def zone_exchange(value):
        return lax.all_to_all(
            value,
            "fsdp",
            split_axis=0,
            concat_axis=0,
            tiled=True,
            axis_index_groups=[[0, 2, 4, 6], [1, 3, 5, 7]],
        )

    by_zone, kind_a, kind_b = pl.pallas_call(
        head_kernel,
        out_shape=(
            jax.ShapeDtypeStruct((4, 64, 2048), BF),
            jax.ShapeDtypeStruct((SHARED, 4096), BF),
            jax.ShapeDtypeStruct((160 - 2 * SHARED, 4096), BF),
        ),
        in_specs=[HBM, HBM, HBM],
        out_specs=(HBM,) * 3,
        scratch_shapes=[
            pltpu.VMEM((4, 64, 2048), BF),
            pltpu.VMEM((160, 4096), BF),
            pltpu.SemaphoreType.DMA((12,)),
        ],
        compiler_params=params(60),
        name="head",
    )(tokens, gate_blocks, up_blocks)
    near_a = owner_flip(kind_a, 1)
    near_b = owner_flip(kind_b, 1)
    gathered = zone_exchange(by_zone)

    slots = jnp.stack([gate_slot, up_slot, down_slot])
    cells = lax.broadcasted_iota(jnp.int32, (3, 160, 256), 2)
    slot_numbers = lax.broadcasted_iota(jnp.int32, (3, 160, 256), 1)
    inv = jnp.min(jnp.where(slots[:, :, None] == cells, slot_numbers, 160), axis=1)
    near_inv = owner_flip(inv, 1)

    weights, payload = pl.pallas_call(
        own_kernel,
        out_shape=(
            jax.ShapeDtypeStruct((8, 1024, 256), BF),
            jax.ShapeDtypeStruct((64, 256), F32),
        ),
        in_specs=[SMEM] + [HBM] * 3 + [VMEM] * 3,
        out_specs=(HBM, VMEM),
        scratch_shapes=[
            pltpu.VMEM((33 * STRIDE, 128), F32),
            pltpu.VMEM((136, 128), F32),
            pltpu.VMEM((48, 1024), BF),
            pltpu.VMEM((256, 1024), BF),
            pltpu.VMEM((3, 160, 4096), BF),
            pltpu.VMEM((8, 1024, 256), BF),
            pltpu.SemaphoreType.DMA((3,)),
            pltpu.SemaphoreType.DMA((2,)),
        ],
        compiler_params=params(60),
        name="own_blocks",
    )(inv, gate_blocks, up_blocks, down_blocks, sketch, probe_index, probe_value)

    near_a, payload = lax.optimization_barrier((near_a, payload))
    near_a_other = lax.ppermute(near_a, "groups", [(0, 1), (1, 0)])
    for bits in (2, 4):
        payload = payload + owner_flip(payload, bits)
    near_inv, near_b, near_a_other, gathered, payload = lax.optimization_barrier(
        (near_inv, near_b, near_a_other, gathered, payload)
    )

    first_keep, first_sent, near_weights, shuffled_tokens = pl.pallas_call(
        first_kernel,
        out_shape=(
            jax.ShapeDtypeStruct((64, 1024), F32),
            jax.ShapeDtypeStruct((4, 64, 1024), BF),
            jax.ShapeDtypeStruct((4, 1024, 256), BF),
            pltpu.HBM((2, 256, 1024), BF),
        ),
        in_specs=[SMEM, VMEM, VMEM, VMEM, HBM, VMEM],
        out_specs=(VMEM, HBM, HBM, HBM),
        scratch_shapes=[
            pltpu.VMEM((33 * STRIDE, 128), F32),
            pltpu.VMEM((4, 1024, 256), BF),
            pltpu.VMEM((4, 1024, 256), BF),
            pltpu.VMEM((2, 256, 1024), BF),
            pltpu.VMEM((4, 64, 1024), BF),
            pltpu.VMEM((256, 256), F32),
            pltpu.SemaphoreType.DMA,
            pltpu.SemaphoreType.DMA((2,)),
            pltpu.SemaphoreType.DMA((4,)),
        ],
        compiler_params=params(46),
        name="first_partial",
    )(near_inv, near_a, near_b, near_a_other, weights, gathered)
    first_back = zone_exchange(first_sent)

    second_keep, *second_sent = pl.pallas_call(
        second_kernel,
        out_shape=(jax.ShapeDtypeStruct((64, 1024), F32),)
        + (jax.ShapeDtypeStruct((64, 1024), BF),) * 3,
        in_specs=[ANY, HBM, ANY],
        out_specs=(VMEM,) * 4,
        scratch_shapes=[
            pltpu.VMEM((4, 1024, 256), BF),
            pltpu.VMEM((4, 1024, 256), BF),
            pltpu.VMEM((2, 256, 1024), BF),
            pltpu.VMEM((256, 256), F32),
            pltpu.SemaphoreType.DMA((3,)),
        ],
        compiler_params=params(56),
        name="second_partial",
    )(core_flip(near_weights), weights, shuffled_tokens)
    second_back = [owner_flip(second_sent[flip - 1], 2 * flip) for flip in (1, 2, 3)]

    across = owner_flip(payload, 1)
    second_keep, across = lax.optimization_barrier((second_keep, across))
    payload = payload + across
    pay_parts = [
        payload,
        core_flip(payload),
        lax.ppermute(payload, "groups", [(0, 1), (1, 0)]),
        lax.ppermute(payload, ("groups", "seq"), [(i, i ^ 3) for i in range(4)]),
    ]

    first_back, weights = lax.optimization_barrier((first_back, weights))
    weights_at_hand = pl.pallas_call(
        fetch_kernel,
        out_shape=jax.ShapeDtypeStruct((8, 1024, 256), BF),
        in_specs=[HBM],
        out_specs=VMEM,
        scratch_shapes=[pltpu.SemaphoreType.DMA],
        compiler_params=params(48),
        name="fetch_weights",
    )(weights)
    pay_parts[0], weights_at_hand = lax.optimization_barrier((pay_parts[0], weights_at_hand))

    mine, theirs = pl.pallas_call(
        middle_kernel,
        out_shape=(jax.ShapeDtypeStruct((8, 2048), F32),) * 2,
        in_specs=[VMEM] * 10,
        out_specs=(VMEM,) * 2,
        scratch_shapes=[
            pltpu.VMEM((64, 1024), F32),
            pltpu.VMEM((64, 1024), F32),
            pltpu.VMEM((4, 64, 256), F32),
            pltpu.VMEM((K, 1024), BF),
            pltpu.VMEM((64 * P_SIZE, 1024), BF),
            pltpu.VMEM((64 * P_SIZE, K), BF),
        ],
        compiler_params=params(48),
        name="token_sums",
    )(first_keep, first_back, second_keep, *second_back, *pay_parts)

    sums = mine + core_flip(theirs)
    sums = sums + owner_flip(sums.astype(BF), 1).astype(F32)
    parts = [owner_flip(sums.astype(BF), bits).astype(F32) for bits in (4, 6, 2)]
    sums = ((sums + parts[0]) + (parts[1] + parts[2])).astype(BF)

    return pl.pallas_call(
        product_kernel,
        out_shape=jax.ShapeDtypeStruct((P_SIZE, 1024), F32),
        in_specs=[VMEM, VMEM, VMEM],
        out_specs=VMEM,
        scratch_shapes=[pltpu.VMEM((2, 8, 2048), BF)],
        compiler_params=params(30),
        name="products",
    )(sums, core_flip(sums), weights_at_hand)


def per_device(tokens, gate_blocks, *rest):
    fits = (
        lax.axis_size("fsdp") == 8
        and lax.axis_size("seq") == 2
        and lax.axis_size("groups") == 2
        and tokens.shape == (64, 8192)
        and gate_blocks.shape == (160, 4096)
        and rest[-2].shape == (P_SIZE, 256)
    )
    return (pair_split if fits else hidden_split)(tokens, gate_blocks, *rest)


def solution(mesh):
    in_specs = (
        P(("groups", "fsdp", "seq"), None),
        P("fsdp", None),
        P("fsdp"),
        P("fsdp", None),
        P("fsdp"),
        P("fsdp", None),
        P("fsdp"),
        P(None, "fsdp"),
        P(),
        P(),
    )
    out_specs = P("groups", "fsdp")
    return jax.shard_map(
        per_device, mesh=mesh, in_specs=in_specs, out_specs=out_specs, check_vma=False
    )
```
